32 devices in a mesh: batch: 4 (over y, x), rows: 8 (over z, core).
Axes of the slice: x: 2, y: 2, z: 4, core: 2. Of those that a mesh axis runs over, the one named last changes fastest.
Arguments:
- features: bfloat16 [256, 8, 16, 2048], P('batch', 'rows'), may hold values from -6 to 6
- w_reduce: bfloat16 [2048, 512], P('rows'), may hold values from -0.125 to 0.125
- w_spatial: bfloat16 [4608, 512], P('rows'), may hold values from -0.09375 to 0.09375
- w_expand: bfloat16 [512, 2048], P('rows'), may hold values from -0.25 to 0.25
- query_weight: bfloat16 [2048, 512], P('rows'), may hold values from -0.125 to 0.125
- w_key: bfloat16 [2048, 512], P('rows'), may hold values from -0.125 to 0.125
- w_value: bfloat16 [2048, 512], P('rows'), may hold values from -0.125 to 0.125
- w_out: bfloat16 [512, 2048], P('rows'), may hold values from -0.5 to 0.5
- w_head: bfloat16 [4096, 80], P('rows'), may hold values from -0.09375 to 0.09375
- gain_a: float32 [512], replicated, may hold values from 0.1 to 1.9
- bias_a: float32 [512], replicated, may hold values from -0.5 to 0.5
- gain_b: float32 [512], replicated, may hold values from 0.1 to 1.9
- bias_b: float32 [512], replicated, may hold values from -0.5 to 0.5
- gain_c: float32 [2048], replicated, may hold values from 0.1 to 1.9
- bias_c: float32 [2048], replicated, may hold values from -0.5 to 0.5
- ln_gain: float32 [512], replicated, may hold values from 0.1 to 1.9
- ln_bias: float32 [512], replicated, may hold values from -0.5 to 0.5
- head_bias: float32 [80], replicated, may hold values from -1 to 1
- bank: bfloat16 [320, 2048], P(('batch', 'rows')), may hold values from -6 to 6
- piece_box: int32 [256, 8], P(('batch', 'rows')), may hold values from 0 to 127
- piece_clip: int32 [256, 8], P(('batch', 'rows')), may hold values from 0 to 63
- send_count: int32 [256], P(('batch', 'rows')), may hold values from 0 to 8, as said below
- sample_pos: int32 [256, 224], P(('batch', 'rows')), may hold values from 0 to 15
- sample_weight: float32 [256, 224], P(('batch', 'rows')), may hold values from 0.01 to 0.06
- win_start: int32 [4096], P(('batch', 'rows')), may hold values from 0 to 60, as said below
- win_len: int32 [4096], P(('batch', 'rows')), may hold values from 20 to 40, as said below
- prob_cotangent: float32 [4096, 80], P(('batch', 'rows')), may hold values from -6 to 6
Outputs:
- probs: float32 [4096, 80], P(('batch', 'rows'))
- features_grad: bfloat16 [256, 8, 16, 2048], P('batch', 'rows')
- w_reduce_grad: float32 [2048, 512], P('rows', 'batch')
- w_spatial_grad: float32 [4608, 512], P('rows', 'batch')
- w_expand_grad: float32 [512, 2048], P('rows', 'batch')
- w_query_grad: float32 [2048, 512], P('rows', 'batch')
- w_key_grad: float32 [2048, 512], P('rows', 'batch')
- w_value_grad: float32 [2048, 512], P('rows', 'batch')
- w_out_grad: float32 [512, 2048], P('rows', 'batch')
- w_head_grad: float32 [4096, 80], P('rows', 'batch')
- gain_a_grad: float32 [512], replicated
- bias_a_grad: float32 [512], replicated
- gain_b_grad: float32 [512], replicated
- bias_b_grad: float32 [512], replicated
- gain_c_grad: float32 [2048], replicated
- bias_c_grad: float32 [2048], replicated
- ln_gain_grad: float32 [512], replicated
- ln_bias_grad: float32 [512], replicated
- classifier_bias_gradient: float32 [80], replicated
The draws below stay inside these ranges and needn't reach their ends.
Inputs may be any that keep to these rules, and one draw needn't show every extreme that they name: `send_count`: at most 8 live slots from one device to one owner; some device sends exactly 8 to some owner in every draw. `win_len`: every window holds 20 to 40 entries, some box's exactly 40. win_start + win_len <= 80.
All inputs are finite; a program needn't handle non-finite values.
Results may differ from the reference program's by a relative error of at most 0.024.
Values may be sent and summed in bfloat16 or wider, within the bound.
A program may use at most 256 MiB of HBM per device.

```python
import math
import jax
import jax.numpy as jnp
from jax import lax

D_IN = 2048
D_MID = 512
CLASSES = 80
KERNEL = 9
CLIP_DEV = 64
ROW_DEV = 1
COLS = 16
BOX_DEV = 128
CAP = 8
SAMP = 28
GROUPS = 4
RANKS = 8
CLIPS = 256
ROWS_ALL = 8
CELLS = 1024
BOXES = 4096
BANK = 80
SENDERS = 256


def window_draw(key):
    base = jax.random.fold_in(key, 41)
    key_len, key_spot, key_start = jax.random.split(base, 3)
    lengths = jax.random.randint(key_len, (BOXES,), BANK // 4, BANK // 2 + 1)
    chosen = jax.random.randint(key_spot, (), 0, BOXES)
    lengths = jnp.where(jnp.arange(BOXES) == chosen, BANK // 2, lengths)
    starts = jax.random.randint(key_start, (BOXES,), 0, BANK - lengths + 1)
    return (starts.astype(jnp.int32), lengths.astype(jnp.int32))


def draw_win_start(key, part):
    return window_draw(key)[0]


def draw_win_len(key, part):
    return window_draw(key)[1]


def draw_send_count(key, part):
    base = jax.random.fold_in(key, 23)
    key_demand, key_reduce, key_spot = jax.random.split(base, 3)
    demand = jax.random.randint(key_demand, (GROUPS, 1, RANKS), 1, CAP + 1)
    reduce_by = jax.random.randint(key_reduce, (GROUPS, RANKS, RANKS), 0, 3)
    counts = jnp.maximum(demand - reduce_by, 0).reshape(SENDERS)
    chosen = jax.random.randint(key_spot, (), 0, SENDERS)
    return jnp.where(jnp.arange(SENDERS) == chosen, CAP, counts).astype(jnp.int32)


def with_ends(result, key, low, largest):
    longest = result.shape.index(max(result.shape))
    spots = []
    for shift in (0, 1):
        where = [jax.random.randint(jax.random.fold_in(key, axis), (), 0, length) for axis, length in enumerate(result.shape)]
        where[longest] = (where[longest] + shift) % result.shape[longest]
        spots.append(tuple(where))
    return result.at[spots[0]].set(low).at[spots[1]].set(largest)


def block_scale(stream_key, dims, shards, smallest, largest):
    def one(dim, parts):
        draws = jax.random.uniform(jax.random.fold_in(jax.random.fold_in(stream_key, 6), dim), (parts,), jnp.float32, smallest / len(shards), largest / len(shards))
        return jnp.repeat(jnp.exp(draws), dims[dim] // parts).reshape((-1,) + (1,) * (len(dims) - dim - 1))

    level = one(*shards[0])
    for cut in shards[1:]:
        level = level * one(*cut)
    return level


def gaussian(own_key, shape, deviation, most, cuts=(), kind=jnp.bfloat16):
    level = block_scale(own_key, shape, cuts, -0.22, 0.18) if cuts else 1.0
    entries = jax.random.normal(own_key, shape, jnp.float32) * deviation * level
    return jnp.minimum(jnp.maximum(entries, -most), most).astype(kind)


def setup_inputs(seed: int = 0) -> dict:
    seeds = jax.random.split(jax.random.key(seed), 28)
    return {
        "features": gaussian(seeds[0], (CLIPS, ROWS_ALL, COLS, D_IN), 1.0, 6.0, ((0, 4), (1, 8))),
        "w_reduce": gaussian(seeds[1], (D_IN, D_MID), D_IN ** -0.5, 0.125, ((0, 8),)),
        "w_spatial": gaussian(seeds[2], (KERNEL * D_MID, D_MID), (KERNEL * D_MID) ** -0.5, 0.09375, ((0, 8),)),
        "w_expand": gaussian(seeds[3], (D_MID, D_IN), D_MID ** -0.5, 0.25, ((0, 8),)),
        "query_weight": gaussian(seeds[4], (D_IN, D_MID), D_IN ** -0.5, 0.125, ((0, 8),)),
        "w_key": gaussian(seeds[5], (D_IN, D_MID), D_IN ** -0.5, 0.125, ((0, 8),)),
        "w_value": gaussian(seeds[6], (D_IN, D_MID), D_IN ** -0.5, 0.125, ((0, 8),)),
        "w_out": gaussian(seeds[7], (D_MID, D_IN), (D_MID // 4) ** -0.5, 0.5, ((0, 8),)),
        "w_head": gaussian(seeds[8], (2 * D_IN, CLASSES), (2 * D_IN) ** -0.5, 0.09375, ((0, 8),)),
        "gain_a": jnp.clip(1.0 + 0.18 * jax.random.normal(seeds[9], (D_MID,), jnp.float32), 0.1, 1.9),
        "bias_a": jnp.clip(jax.random.uniform(seeds[10], (D_MID,), jnp.float32, -0.5, 0.5), -0.5, 0.5),
        "gain_b": jnp.clip(1.0 + 0.18 * jax.random.normal(seeds[11], (D_MID,), jnp.float32), 0.1, 1.9),
        "bias_b": jnp.clip(jax.random.uniform(seeds[12], (D_MID,), jnp.float32, -0.5, 0.5), -0.5, 0.5),
        "gain_c": jnp.clip(1.0 + 0.18 * jax.random.normal(seeds[13], (D_IN,), jnp.float32), 0.1, 1.9),
        "bias_c": jnp.clip(jax.random.uniform(seeds[14], (D_IN,), jnp.float32, -0.5, 0.5), -0.5, 0.5),
        "ln_gain": jnp.clip(1.0 + 0.18 * jax.random.normal(seeds[15], (D_MID,), jnp.float32), 0.1, 1.9),
        "ln_bias": jnp.clip(jax.random.uniform(seeds[16], (D_MID,), jnp.float32, -0.5, 0.5), -0.5, 0.5),
        "head_bias": jnp.clip(jax.random.uniform(seeds[17], (CLASSES,), jnp.float32, -1.0, 1.0), -1.0, 1.0),
        "bank": gaussian(seeds[18], (GROUPS * BANK, D_IN), 1.0, 6.0, ((0, 32),)),
        "piece_box": with_ends(jax.random.randint(seeds[19], (SENDERS, CAP), 0, BOX_DEV), jax.random.fold_in(seeds[19], 1), 0, BOX_DEV - 1).astype(jnp.int32),
        "piece_clip": with_ends(jax.random.randint(seeds[20], (SENDERS, CAP), 0, CLIP_DEV), jax.random.fold_in(seeds[20], 1), 0, CLIP_DEV - 1).astype(jnp.int32),
        "send_count": draw_send_count(jax.random.fold_in(seeds[27], 71), 0),
        "sample_pos": with_ends(jax.random.randint(seeds[22], (SENDERS, CAP * SAMP), 0, ROW_DEV * COLS), jax.random.fold_in(seeds[22], 1), 0, (ROW_DEV * COLS) - 1).astype(jnp.int32),
        "sample_weight": jnp.clip(jnp.exp(math.log(0.06) - 1.7917595 * jax.random.uniform(seeds[23], (SENDERS, CAP * SAMP), jnp.float32) ** block_scale(seeds[23], (SENDERS, CAP * SAMP), ((0, 32),), -0.2, 0.2)), 0.01, 0.06),
        "win_start": draw_win_start(jax.random.fold_in(seeds[27], 71), 0),
        "win_len": draw_win_len(jax.random.fold_in(seeds[27], 71), 0),
        "prob_cotangent": gaussian(seeds[26], (BOXES, CLASSES), 1.0, 6.0, ((0, 32),), jnp.float32),
    }


@jax.custom_vjp
def low(v):
    return lax.optimization_barrier(v.astype(jnp.bfloat16)).astype(jnp.float32)

@jax.custom_vjp
def low_back(v):
    return v

def low_keep(v):
    return (low(v), None)

def low_pass(kept, grad):
    return (grad,)

def back_keep(v):
    return (v, None)

def back_low(kept, grad):
    return (low(grad),)
low.defvjp(low_keep, low_pass)
low_back.defvjp(back_keep, back_low)

def batch_norm(field, gain, shift):
    centre_value = lax.optimization_barrier(jnp.mean(field, axis=(0, 1, 2)))
    square_mean = lax.optimization_barrier(jnp.mean(field * field, axis=(0, 1, 2)))
    return gain * ((field - centre_value) * lax.rsqrt(square_mean - centre_value * centre_value + 1e-05)) + shift

def conv_spatial(field, weight):
    width = field.shape[3]
    padded = jnp.pad(field, ((0, 0), (1, 1), (1, 1), (0, 0)))
    total = jnp.zeros(field.shape[:3] + (weight.shape[1],), jnp.float32)
    for tap_index in range(9):
        row_step = tap_index // 3
        col_step = tap_index % 3
        window = padded[:, row_step:row_step + field.shape[1], col_step:col_step + field.shape[2]]
        total = total + jnp.einsum('nrcd,de->nrce', window, weight[tap_index * width:(tap_index + 1) * width], precision=lax.Precision.HIGHEST)
    return total

def forward(params, bank_wide, interpolated_value, box_index, window_mask):
    inputs, w_a, w_b, w_c, w_q, w_k, w_v, w_o, w_h, gain_a, bias_a, gain_b, bias_b, gain_c, bias_c, ln_gain, ln_bias, head_bias = params
    pre_a = low_back(jnp.einsum('nrcd,de->nrce', inputs, w_a, precision=lax.Precision.HIGHEST))
    low_a = low(jax.nn.silu(batch_norm(pre_a, gain_a, bias_a)))
    pre_b = low_back(conv_spatial(low_a, w_b))
    low_b = low(jax.nn.silu(batch_norm(pre_b, gain_b, bias_b)))
    pre_c = low_back(jnp.einsum('nrcd,de->nrce', low_b, w_c, precision=lax.Precision.HIGHEST))
    fmap = low(jax.nn.silu(batch_norm(pre_c, gain_c, bias_c) + inputs))
    device_share = fmap.reshape(GROUPS, CLIP_DEV, RANKS, ROW_DEV, COLS, D_IN).transpose(0, 2, 1, 3, 4, 5).reshape(GROUPS * RANKS, CELLS, D_IN)
    region_parts = jnp.einsum('mrh,mhz->mrz', interpolated_value, device_share, precision=lax.Precision.HIGHEST)
    arrived = low_back(low(region_parts))
    pooled = jax.ops.segment_sum(arrived.reshape(SENDERS * CAP, D_IN), box_index, num_segments=BOXES)
    pooled_low = low(pooled)
    key_rows = low(low_back(jnp.dot(bank_wide, w_k, precision=lax.Precision.HIGHEST))).reshape(GROUPS, BANK, D_MID)
    value_rows = low(low_back(jnp.dot(bank_wide, w_v, precision=lax.Precision.HIGHEST))).reshape(GROUPS, BANK, D_MID)
    queries = low(low_back(jnp.dot(pooled_low, w_q, precision=lax.Precision.HIGHEST))).reshape(GROUPS, RANKS * BOX_DEV, D_MID)
    scores = low_back(jnp.einsum('gqd,gkd->gqk', queries, key_rows, precision=lax.Precision.HIGHEST) * D_MID ** (-0.5))
    scores = jnp.where(window_mask, scores, -1e+30)
    attend = low(jax.nn.softmax(scores, axis=-1))
    mixture = low_back(jnp.einsum('gqk,gkd->gqd', attend, value_rows, precision=lax.Precision.HIGHEST)).reshape(BOXES, D_MID)
    centre_value = lax.optimization_barrier(jnp.mean(mixture, axis=-1, keepdims=True))
    centred = mixture - centre_value
    spread_value = lax.optimization_barrier(jnp.mean(centred * centred, axis=-1, keepdims=True))
    hat_z = centred * lax.rsqrt(spread_value + 1e-05)
    low_r = low(jax.nn.silu(ln_gain * hat_z + ln_bias))
    branch = low_back(jnp.dot(low_r, w_o, precision=lax.Precision.HIGHEST))
    joined = low(jnp.concatenate([pooled, pooled + branch], axis=1))
    logits = low_back(jnp.dot(joined, w_h, precision=lax.Precision.HIGHEST) + head_bias)
    return jax.nn.sigmoid(logits)

def reference(features, w_reduce, w_spatial, w_expand, query_weight, w_key, w_value, w_out, w_head, gain_a, bias_a, gain_b, bias_b, gain_c, bias_c, ln_gain, ln_bias, head_bias, bank, piece_box, piece_clip, send_count, sample_pos, sample_weight, win_start, win_len, prob_cotangent):
    sample_cells = (piece_clip[:, :, None] * (ROW_DEV * COLS) + sample_pos.reshape(SENDERS, CAP, SAMP)).reshape(SENDERS * CAP, SAMP).astype(jnp.int32)
    is_live = (jnp.arange(CAP, dtype=jnp.int32)[None, :] < send_count[:, None]).reshape(SENDERS * CAP)
    slot_weights = sample_weight.reshape(SENDERS * CAP, SAMP) * is_live[:, None].astype(jnp.float32)
    slot_index = jnp.broadcast_to(jnp.arange(SENDERS * CAP, dtype=jnp.int32)[:, None], (SENDERS * CAP, SAMP))
    interpolated_value = jnp.zeros((SENDERS * CAP, CELLS), jnp.float32).at[slot_index, sample_cells].add(slot_weights)
    interpolated_value = low(interpolated_value.reshape(GROUPS * RANKS, RANKS * CAP, CELLS))
    sender = jnp.arange(SENDERS, dtype=jnp.int32)
    owner_base = (sender // (RANKS * RANKS) * RANKS + sender % RANKS) * BOX_DEV
    box_index = (owner_base[:, None] + piece_box).reshape(SENDERS * CAP).astype(jnp.int32)
    positions = jnp.arange(BANK, dtype=jnp.int32)[None, :]
    window_mask = ((positions >= win_start[:, None]) & (positions < (win_start + win_len)[:, None])).reshape(GROUPS, RANKS * BOX_DEV, BANK)
    bank_wide = bank.astype(jnp.float32)
    params = tuple((item.astype(jnp.float32) for item in (features, w_reduce, w_spatial, w_expand, query_weight, w_key, w_value, w_out, w_head, gain_a, bias_a, gain_b, bias_b, gain_c, bias_c, ln_gain, ln_bias, head_bias)))

    def forward_result(*values):
        return forward(values, bank_wide, interpolated_value, box_index, window_mask)
    probs, pullback = jax.vjp(forward_result, *params)
    grads = pullback(prob_cotangent.astype(jnp.float32))
    return (probs, grads[0].astype(jnp.bfloat16), grads[1], grads[2], grads[3], grads[4], grads[5], grads[6], grads[7], grads[8], grads[9], grads[10], grads[11], grads[12], grads[13], grads[14], grads[15], grads[16], grads[17])
```

```python
import jax
import jax.numpy as jnp
from jax import lax
from jax.experimental import pallas as pl
from jax.experimental.pallas import tpu as pltpu
from jax.sharding import PartitionSpec as P


def padded(cells, sides, width):
    for axis, dim in sides:
        count = lax.axis_size(axis)
        ends = count - 1
        head = lax.slice_in_dim(cells, 0, width, axis=dim)
        tail = lax.slice_in_dim(cells, cells.shape[dim] - width, cells.shape[dim], axis=dim)
        cells = jnp.concatenate(
            [
                lax.ppermute(tail, axis, [(i, (i + 1) % count) for i in range(ends)]),
                cells,
                lax.ppermute(head, axis, [((i + 1) % count, i) for i in range(ends)]),
            ],
            axis=dim,
        )
    return cells


def split_up(value, dim, peers):
    shape = value.shape
    parts = value.reshape(*shape[:dim], peers, shape[dim] // peers, *shape[dim + 1 :])
    return jnp.moveaxis(parts, dim, 0)


def sum_at_owner(value, axis, dim):
    peers = lax.axis_size(axis)
    parts = lax.all_to_all(split_up(value, dim, peers), axis, 0, 0, tiled=True)
    return jnp.sum(parts.astype(jnp.float32), axis=0)


def side_by_side(arrays, axis, dim, along):
    ends, at = ([], 0)
    for a in arrays[:-1]:
        at += a.shape[along]
        ends.append(at)
    both = jnp.concatenate(arrays, axis=along)
    return tuple(jnp.split(sum_at_owner(both, axis, dim), ends, axis=along))


def total_kernel(part, result, held, from_rows, from_batch, send_rows, recv_rows, send_batch, recv_batch):
    groups, ranks = lax.axis_size("batch"), lax.axis_size("rows")
    here_g, here_r = lax.axis_index("batch"), lax.axis_index("rows")
    along_rows = [(here_g, lax.rem(here_r + k, ranks)) for k in range(1, ranks)]
    along_batch = [(lax.rem(here_g + k, groups), here_r) for k in range(1, groups)]
    barrier = pltpu.get_barrier_semaphore()
    for peer in along_rows + along_batch:
        pl.semaphore_signal(
            barrier, inc=1, device_id=peer, device_id_type=pl.DeviceIdType.MESH
        )
    pl.semaphore_wait(barrier, len(along_rows) + len(along_batch))
    held[...] = part[...]
    for peers, landing, send, recv in (
        (along_rows, from_rows, send_rows, recv_rows),
        (along_batch, from_batch, send_batch, recv_batch),
    ):
        copies = [
            pltpu.make_async_remote_copy(
                src_ref=held,
                dst_ref=landing.at[k],
                send_sem=send.at[k],
                recv_sem=recv.at[k],
                device_id=peer,
                device_id_type=pl.DeviceIdType.MESH,
            )
            for k, peer in enumerate(peers)
        ]
        for copy in copies:
            copy.start()
        for copy in copies:
            copy.wait()
        total = held[...]
        for k in range(len(peers)):
            total = total + landing[k]
        held[...] = total
    result[...] = held[...]


def total_over_all(arrays, channel):
    groups, ranks = lax.axis_size("batch"), lax.axis_size("rows")
    flat = jnp.concatenate([a.reshape(-1) for a in arrays])
    width = -(-flat.shape[0] // 1024) * 128
    packed = jnp.pad(flat, (0, 8 * width - flat.shape[0])).reshape(8, width)
    dma = pltpu.SemaphoreType.DMA
    summed = pl.pallas_call(
        total_kernel,
        out_shape=jax.ShapeDtypeStruct((8, width), jnp.float32),
        in_specs=[pl.BlockSpec(memory_space=pltpu.VMEM)],
        out_specs=pl.BlockSpec(memory_space=pltpu.VMEM),
        scratch_shapes=[
            pltpu.VMEM((8, width), jnp.float32),
            pltpu.VMEM((ranks - 1, 8, width), jnp.float32),
            pltpu.VMEM((groups - 1, 8, width), jnp.float32),
            dma((ranks - 1,)),
            dma((ranks - 1,)),
            dma((groups - 1,)),
            dma((groups - 1,)),
        ],
        compiler_params=pltpu.CompilerParams(collective_id=channel, has_side_effects=True),
    )(packed).reshape(-1)
    results, at = [], 0
    for a in arrays:
        results.append(summed[at : at + a.size].reshape(a.shape))
        at += a.size
    return tuple(results)


def tdot(left, right):
    return lax.dot_general(
        left, right, (((0,), (0,)), ((), ())), preferred_element_type=jnp.float32
    )


def ndot(left, right):
    return lax.dot_general(
        left, right, (((1,), (1,)), ((), ())), preferred_element_type=jnp.float32
    )


def silu_slope(value):
    sig = jax.nn.sigmoid(value)
    return sig * (1.0 + value * (1.0 - sig))


def normalize(field, total_count):
    sums, squares = total_over_all(
        (jnp.sum(field, 0), jnp.sum(field * field, 0)), field.shape[1] // 512
    )
    centre_value = sums / total_count
    inverse = lax.rsqrt(squares / total_count - centre_value * centre_value + 1e-05)
    return ((field - centre_value) * inverse, inverse)


def segment_totals(grad, normed):
    return total_over_all(
        (jnp.sum(grad, 0), jnp.sum(grad * normed, 0)), grad.shape[1] // 512
    )


def norm_back(grad, normed, inverse, gain, shift_sum, gain_total_grad, total_count):
    return (
        gain * inverse * (grad - shift_sum / total_count - normed * gain_total_grad / total_count)
    )


def on_device(
    features,
    w_reduce,
    w_spatial,
    w_expand,
    query_weight,
    w_key,
    w_value,
    w_out,
    w_head,
    gain_a,
    bias_a,
    gain_b,
    bias_b,
    gain_c,
    bias_c,
    ln_gain,
    ln_bias,
    head_bias,
    bank,
    piece_box,
    piece_clip,
    send_count,
    sample_pos,
    sample_weight,
    win_start,
    win_len,
    prob_cotangent,
):
    owners = lax.axis_size("rows")
    clip_dev, row_dev, col_count, d_in = features.shape
    cell_count = clip_dev * row_dev * col_count
    total_count = cell_count * owners * lax.axis_size("batch")
    w_a, w_b, w_c, w_q, w_k, w_v, w_o, w_h = (
        lax.all_gather(w_reduce, "rows", axis=0, tiled=True),
        lax.all_gather(w_spatial, "rows", axis=0, tiled=True),
        lax.all_gather(w_expand, "rows", axis=0, tiled=True),
        lax.all_gather(query_weight, "rows", axis=0, tiled=True),
        lax.all_gather(w_key, "rows", axis=0, tiled=True),
        lax.all_gather(w_value, "rows", axis=0, tiled=True),
        lax.all_gather(w_out, "rows", axis=0, tiled=True),
        lax.all_gather(w_head, "rows", axis=0, tiled=True),
    )
    d_mid = w_a.shape[1]
    flat_x = features.reshape(cell_count, d_in)
    pre_a = jnp.dot(flat_x, w_a, preferred_element_type=jnp.float32)
    hat_a, inverse_a = normalize(pre_a, total_count)
    act_a = gain_a * hat_a + bias_a
    low_a = jax.nn.silu(act_a).astype(jnp.bfloat16)
    halo_a = padded(low_a.reshape(clip_dev, row_dev, col_count, d_mid), (("rows", 1),), 1)
    halo_a = jnp.pad(halo_a, ((0, 0), (0, 0), (1, 1), (0, 0)))
    window_a = jnp.concatenate(
        [
            halo_a[:, row_step : row_step + row_dev, col_step : col_step + col_count]
            for row_step in range(3)
            for col_step in range(3)
        ],
        axis=3,
    ).reshape(cell_count, 9 * d_mid)
    pre_b = jnp.dot(window_a, w_b, preferred_element_type=jnp.float32)
    hat_b, inverse_b = normalize(pre_b, total_count)
    act_b = gain_b * hat_b + bias_b
    low_b = jax.nn.silu(act_b).astype(jnp.bfloat16)
    pre_c = jnp.dot(low_b, w_c, preferred_element_type=jnp.float32)
    hat_c, inverse_c = normalize(pre_c, total_count)
    pre_out = gain_c * hat_c + bias_c + flat_x.astype(jnp.float32)
    fmap = jax.nn.silu(pre_out).astype(jnp.bfloat16)
    capacity = piece_box.shape[1]
    samples = sample_pos.shape[1] // capacity
    slot_count = owners * capacity
    sample_cells = (
        piece_clip[:, :, None] * (row_dev * col_count)
        + sample_pos.reshape(owners, capacity, samples)
    ).reshape(slot_count, samples)
    is_live = (jnp.arange(capacity)[None, :] < send_count[:, None]).reshape(slot_count)
    slot_weights = sample_weight.reshape(slot_count, samples) * is_live[:, None].astype(jnp.float32)
    cell_ids = jnp.arange(cell_count)[None, :]
    interp_sum = jnp.zeros((slot_count, cell_count), jnp.float32)
    for sample_index in range(samples):
        interp_sum = interp_sum + jnp.where(
            sample_cells[:, sample_index, None] == cell_ids,
            slot_weights[:, sample_index, None],
            0.0,
        )
    interpolated_value = interp_sum.astype(jnp.bfloat16)
    region_parts = (
        jnp.dot(interpolated_value, fmap, preferred_element_type=jnp.float32)
        .astype(jnp.bfloat16)
        .reshape(owners, capacity, d_in)
    )
    arrived, arrived_box = (
        lax.all_to_all(region_parts, "rows", split_axis=0, concat_axis=0, tiled=True),
        lax.all_to_all(piece_box, "rows", split_axis=0, concat_axis=0, tiled=True),
    )
    box_dev = win_start.shape[0]
    flat_box = arrived_box.reshape(slot_count)
    owner_hits = (flat_box[None, :] == jnp.arange(box_dev)[:, None]).astype(jnp.bfloat16)
    pooled = jnp.dot(
        owner_hits, arrived.reshape(slot_count, d_in), preferred_element_type=jnp.float32
    )
    pooled_low = pooled.astype(jnp.bfloat16)
    keys_own = jnp.dot(bank, w_k, preferred_element_type=jnp.float32).astype(jnp.bfloat16)
    values_own = jnp.dot(bank, w_v, preferred_element_type=jnp.float32).astype(jnp.bfloat16)
    key_rows, value_rows = (
        lax.all_gather(keys_own, "rows", axis=0, tiled=True),
        lax.all_gather(values_own, "rows", axis=0, tiled=True),
    )
    bank_length = key_rows.shape[0]
    queries = jnp.dot(pooled_low, w_q, preferred_element_type=jnp.float32).astype(jnp.bfloat16)
    score_scale = d_mid ** (-0.5)
    scores = ndot(queries, key_rows) * score_scale
    positions = jnp.arange(bank_length)[None, :]
    window_mask = (positions >= win_start[:, None]) & (positions < (win_start + win_len)[:, None])
    attend = jax.nn.softmax(jnp.where(window_mask, scores, -1e30), axis=-1)
    attend_low = attend.astype(jnp.bfloat16)
    mixture = jnp.dot(attend_low, value_rows, preferred_element_type=jnp.float32)
    centred = mixture - jnp.mean(mixture, axis=-1, keepdims=True)
    inverse_z = lax.rsqrt(jnp.mean(centred * centred, axis=-1, keepdims=True) + 1e-05)
    hat_z = centred * inverse_z
    pre_ln = ln_gain * hat_z + ln_bias
    low_r = jax.nn.silu(pre_ln).astype(jnp.bfloat16)
    branch = jnp.dot(low_r, w_o, preferred_element_type=jnp.float32)
    joined = jnp.concatenate([pooled, pooled + branch], axis=1).astype(jnp.bfloat16)
    logits = jnp.dot(joined, w_h, preferred_element_type=jnp.float32) + head_bias
    likely = jax.nn.sigmoid(logits)
    d_logit = (prob_cotangent * (likely * (1.0 - likely))).astype(jnp.bfloat16)
    grad_head_bias = jnp.sum(d_logit.astype(jnp.float32), 0)
    grad_wh = tdot(joined, d_logit)
    d_joined = ndot(d_logit, w_h)
    d_pooled = d_joined[:, :d_in] + d_joined[:, d_in:]
    d_branch = d_joined[:, d_in:].astype(jnp.bfloat16)
    grad_wo = tdot(low_r, d_branch)
    d_ln = ndot(d_branch, w_o) * silu_slope(pre_ln)
    grad_ln_gain = jnp.sum(d_ln * hat_z, 0)
    grad_ln_bias = jnp.sum(d_ln, 0)
    d_hat = d_ln * ln_gain
    d_mixture = (
        inverse_z
        * (
            d_hat
            - jnp.mean(d_hat, axis=-1, keepdims=True)
            - hat_z * jnp.mean(d_hat * hat_z, axis=-1, keepdims=True)
        )
    ).astype(jnp.bfloat16)
    d_attend = ndot(d_mixture, value_rows)
    d_values = tdot(attend_low, d_mixture)
    d_scores = (attend * (d_attend - jnp.sum(d_attend * attend, axis=-1, keepdims=True))).astype(
        jnp.bfloat16
    )
    d_queries = (
        jnp.dot(d_scores, key_rows, preferred_element_type=jnp.float32) * score_scale
    ).astype(jnp.bfloat16)
    d_keys = tdot(d_scores, queries) * score_scale
    grad_wq = tdot(pooled_low, d_queries)
    d_pooled = d_pooled + ndot(d_queries, w_q)
    key_sum, value_sum = side_by_side(
        (d_keys.astype(jnp.bfloat16), d_values.astype(jnp.bfloat16)), "rows", 0, 1
    )
    grad_wk = tdot(bank, key_sum.astype(jnp.bfloat16))
    grad_wv = tdot(bank, value_sum.astype(jnp.bfloat16))
    back_pieces = jnp.take(d_pooled.astype(jnp.bfloat16), flat_box, axis=0).reshape(
        owners, capacity, d_in
    )
    returned = lax.all_to_all(back_pieces, "rows", split_axis=0, concat_axis=0, tiled=True)
    d_fmap = tdot(interpolated_value, returned.reshape(slot_count, d_in))
    d_pre = d_fmap * silu_slope(pre_out)
    head_sums = total_over_all(
        (jnp.sum(d_pre, 0), jnp.sum(d_pre * hat_c, 0), grad_ln_gain, grad_ln_bias, grad_head_bias),
        9,
    )
    d_c = norm_back(
        d_pre, hat_c, inverse_c, gain_c, head_sums[0], head_sums[1], total_count
    ).astype(jnp.bfloat16)
    grad_wc = tdot(low_b, d_c)
    d_act_b = ndot(d_c, w_c) * silu_slope(act_b)
    shift_b_sum, gain_b_sum = segment_totals(d_act_b, hat_b)
    d_b = norm_back(d_act_b, hat_b, inverse_b, gain_b, shift_b_sum, gain_b_sum, total_count).astype(
        jnp.bfloat16
    )
    grad_wb = tdot(window_a, d_b)
    halo_d = padded(d_b.reshape(clip_dev, row_dev, col_count, d_mid), (("rows", 1),), 1)
    halo_d = jnp.pad(halo_d, ((0, 0), (0, 0), (1, 1), (0, 0)))
    window_d = jnp.concatenate(
        [
            halo_d[
                :, 2 - row_step : 2 - row_step + row_dev, 2 - col_step : 2 - col_step + col_count
            ]
            for row_step in range(3)
            for col_step in range(3)
        ],
        axis=3,
    ).reshape(cell_count, 9 * d_mid)
    flipped = w_b.reshape(9, d_mid, d_mid).transpose(0, 2, 1).reshape(9 * d_mid, d_mid)
    d_act_a = jnp.dot(window_d, flipped, preferred_element_type=jnp.float32) * silu_slope(act_a)
    shift_a_sum, gain_a_sum = segment_totals(d_act_a, hat_a)
    d_a = norm_back(d_act_a, hat_a, inverse_a, gain_a, shift_a_sum, gain_a_sum, total_count).astype(
        jnp.bfloat16
    )
    grad_wa = tdot(flat_x, d_a)
    grad_input = (ndot(d_a, w_a) + d_pre).astype(jnp.bfloat16).reshape(features.shape)
    partial_sums = (
        lax.psum_scatter(grad_wa, "rows", scatter_dimension=0, tiled=True),
        lax.psum_scatter(grad_wb, "rows", scatter_dimension=0, tiled=True),
        lax.psum_scatter(grad_wc, "rows", scatter_dimension=0, tiled=True),
        lax.psum_scatter(grad_wq, "rows", scatter_dimension=0, tiled=True),
        lax.psum_scatter(grad_wk, "rows", scatter_dimension=0, tiled=True),
        lax.psum_scatter(grad_wv, "rows", scatter_dimension=0, tiled=True),
        lax.psum_scatter(grad_wo, "rows", scatter_dimension=0, tiled=True),
        lax.psum_scatter(grad_wh, "rows", scatter_dimension=0, tiled=True),
    )
    finished = (
        lax.psum_scatter(
            partial_sums[0].astype(jnp.bfloat16), "batch", scatter_dimension=1, tiled=True
        ).astype(jnp.float32),
        lax.psum_scatter(
            partial_sums[1].astype(jnp.bfloat16), "batch", scatter_dimension=1, tiled=True
        ).astype(jnp.float32),
        lax.psum_scatter(
            partial_sums[2].astype(jnp.bfloat16), "batch", scatter_dimension=1, tiled=True
        ).astype(jnp.float32),
        lax.psum_scatter(
            partial_sums[3].astype(jnp.bfloat16), "batch", scatter_dimension=1, tiled=True
        ).astype(jnp.float32),
        lax.psum_scatter(
            partial_sums[4].astype(jnp.bfloat16), "batch", scatter_dimension=1, tiled=True
        ).astype(jnp.float32),
        lax.psum_scatter(
            partial_sums[5].astype(jnp.bfloat16), "batch", scatter_dimension=1, tiled=True
        ).astype(jnp.float32),
        lax.psum_scatter(
            partial_sums[6].astype(jnp.bfloat16), "batch", scatter_dimension=1, tiled=True
        ).astype(jnp.float32),
        lax.psum_scatter(
            partial_sums[7].astype(jnp.bfloat16), "batch", scatter_dimension=1, tiled=True
        ).astype(jnp.float32),
    )
    return (
        likely,
        grad_input,
        finished[0],
        finished[1],
        finished[2],
        finished[3],
        finished[4],
        finished[5],
        finished[6],
        finished[7],
        gain_a_sum,
        shift_a_sum,
        gain_b_sum,
        shift_b_sum,
        head_sums[1],
        head_sums[0],
        head_sums[2],
        head_sums[3],
        head_sums[4],
    )


def solution(mesh):
    return jax.shard_map(
        on_device,
        mesh=mesh,
        in_specs=(
            P("batch", "rows", None, None),
            P("rows", None),
            P("rows", None),
            P("rows", None),
            P("rows", None),
            P("rows", None),
            P("rows", None),
            P("rows", None),
            P("rows", None),
            P(),
            P(),
            P(),
            P(),
            P(),
            P(),
            P(),
            P(),
            P(),
            P(("batch", "rows"), None),
            P(("batch", "rows"), None),
            P(("batch", "rows"), None),
            P(("batch", "rows")),
            P(("batch", "rows"), None),
            P(("batch", "rows"), None),
            P(("batch", "rows")),
            P(("batch", "rows")),
            P(("batch", "rows"), None),
        ),
        out_specs=(
            P(("batch", "rows"), None),
            P("batch", "rows", None, None),
            P("rows", "batch"),
            P("rows", "batch"),
            P("rows", "batch"),
            P("rows", "batch"),
            P("rows", "batch"),
            P("rows", "batch"),
            P("rows", "batch"),
            P("rows", "batch"),
            P(),
            P(),
            P(),
            P(),
            P(),
            P(),
            P(),
            P(),
            P(),
        ),
        check_vma=False,
    )
```

```python
import jax
import jax.numpy as jnp
from jax import lax
from jax.experimental import pallas as pl
from jax.experimental.pallas import tpu as pltpu
from jax.sharding import PartitionSpec as P


def padded(cells, sides, width):
    for axis, dim in sides:
        count = lax.axis_size(axis)
        ends = count - 1
        head = lax.slice_in_dim(cells, 0, width, axis=dim)
        tail = lax.slice_in_dim(cells, cells.shape[dim] - width, cells.shape[dim], axis=dim)
        cells = jnp.concatenate(
            [
                lax.ppermute(tail, axis, [(i, (i + 1) % count) for i in range(ends)]),
                cells,
                lax.ppermute(head, axis, [((i + 1) % count, i) for i in range(ends)]),
            ],
            axis=dim,
        )
    return cells


def split_up(value, dim, peers):
    shape = value.shape
    parts = value.reshape(*shape[:dim], peers, shape[dim] // peers, *shape[dim + 1 :])
    return jnp.moveaxis(parts, dim, 0)


def sum_at_owner(value, axis, dim):
    peers = lax.axis_size(axis)
    parts = lax.all_to_all(split_up(value, dim, peers), axis, 0, 0, tiled=True)
    return jnp.sum(parts.astype(jnp.float32), axis=0)


def side_by_side(arrays, axis, dim, along):
    ends, at = ([], 0)
    for a in arrays[:-1]:
        at += a.shape[along]
        ends.append(at)
    both = jnp.concatenate(arrays, axis=along)
    return tuple(jnp.split(sum_at_owner(both, axis, dim), ends, axis=along))


def tdot(left, right):
    return lax.dot_general(
        left, right, (((0,), (0,)), ((), ())), preferred_element_type=jnp.float32
    )


def ndot(left, right):
    return lax.dot_general(
        left, right, (((1,), (1,)), ((), ())), preferred_element_type=jnp.float32
    )


def silu_slope(value):
    sig = jax.nn.sigmoid(value)
    return sig * (1.0 + value * (1.0 - sig))


def norm_back(grad, normed, inverse, gain, shift_sum, gain_total_grad, total_count):
    return (
        gain * inverse * (grad - shift_sum / total_count - normed * gain_total_grad / total_count)
    )


MESH = pl.DeviceIdType.MESH
LOW = jnp.bfloat16
F32 = jnp.float32


class Wires:
    def __init__(self, send, recv):
        self.send, self.recv, self.at, self.open = send, recv, 0, []

    def push(self, source, target, peer):
        copy = pltpu.make_async_remote_copy(
            src_ref=source,
            dst_ref=target,
            send_sem=self.send.at[self.at],
            recv_sem=self.recv.at[self.at],
            device_id=peer,
            device_id_type=MESH,
        )
        self.at += 1
        copy.start()
        self.open.append(copy)
        return copy

    def close(self):
        for copy in self.open:
            copy.wait_send()


def greet(peers):
    barrier = pltpu.get_barrier_semaphore()
    for peer in peers:
        pl.semaphore_signal(barrier, inc=1, device_id=peer, device_id_type=MESH)
    pl.semaphore_wait(barrier, len(peers))


class Place:
    def __init__(self):
        self.groups, self.ranks = lax.axis_size("batch"), lax.axis_size("rows")
        self.g, self.s = lax.axis_index("batch"), lax.axis_index("rows")
        self.chips = self.ranks // 2
        self.z, self.core = self.s // 2, lax.rem(self.s, 2)
        self.other = 1 - self.core

    def row_peers(self):
        return [(self.g, lax.rem(self.s + k, self.ranks)) for k in range(1, self.ranks)]

    def batch_peers(self):
        return [(lax.rem(self.g + k, self.groups), self.s) for k in range(1, self.groups)]

    def line_peers(self):
        return [
            (self.g, lax.rem(self.z + k, self.chips) * 2 + self.core) for k in range(1, self.chips)
        ]

    def twin(self):
        return (self.g, self.z * 2 + self.other)


def rows_of(ref, index, size):
    return ref.at[pl.ds(pl.multiple_of(index * size, size), size)]


def total_start(net, place, held, from_rows):
    return [net.push(held, from_rows.at[k], peer) for k, peer in enumerate(place.row_peers())]


def total_finish(net, place, copies, held, from_rows, second, from_batch):
    for copy in copies:
        copy.wait_recv()
    total = held[...]
    for k in range(len(copies)):
        total = total + from_rows[k]
    second[...] = total
    more = [net.push(second, from_batch.at[k], peer) for k, peer in enumerate(place.batch_peers())]
    for copy in more:
        copy.wait_recv()
    for k in range(len(more)):
        total = total + from_batch[k]
    return total


def spread(ref, values):
    quarter = values[0].shape[1] // 4
    for n, value in enumerate(values):
        for k in range(4):
            ref[4 * n + k : 4 * n + k + 1, 0:quarter] = value[:, k * quarter : (k + 1) * quarter]


def gathered(block, n, quarter, at=0):
    return jnp.concatenate(
        [block[4 * n + k : 4 * n + k + 1, at : at + quarter] for k in range(4)], axis=1
    )


class Scatter:
    def __init__(self, net, place, shard, part, from_twin, from_batch, partial, from_line, result):
        self.net, self.place, self.shard, self.part = net, place, shard, part
        self.from_twin, self.from_batch, self.partial = from_twin, from_batch, partial
        self.from_line, self.result = from_line, result

    def pair(self):
        place = self.place
        self.first = [
            self.net.push(self.shard(2 * z + place.other), self.from_twin.at[z], place.twin())
            for z in range(place.chips)
        ]

    def batch(self):
        place = self.place
        self.second = []
        for z in range(place.chips):
            self.first[z].wait_recv()
            mine = self.shard(2 * z + place.core)
            rows = mine.shape[0]
            step = next(n for n in (64, 32, 16) if rows % n == 0)

            @pl.loop(0, rows // step)
            def _(n):
                at = pl.ds(pl.multiple_of(n * step, step), step)
                mine[at, :] = (
                    mine[at, :].astype(F32) + self.from_twin[z, at, :].astype(F32)
                ).astype(LOW)

            for k, peer in enumerate(place.batch_peers()):
                self.second.append(
                    self.net.push(self.part(mine, peer[0]), self.from_batch.at[k, z], peer)
                )

    def line(self):
        place = self.place
        peers = place.groups - 1
        self.third = []
        for copy in self.second:
            copy.wait_recv()
        for z in range(place.chips):
            mine = self.part(self.shard(2 * z + place.core), place.g)
            total = mine[...].astype(F32)
            for k in range(peers):
                total = total + self.from_batch[k, z].astype(F32)
            self.partial[z] = total.astype(LOW)
        for k, peer in enumerate(place.line_peers()):
            self.third.append(
                self.net.push(self.partial.at[peer[1] // 2], self.from_line.at[k], peer)
            )

    def finish(self):
        for copy in self.third:
            copy.wait_recv()
        total = self.partial[self.place.z].astype(F32)
        for k in range(self.place.chips - 1):
            total = total + self.from_line[k].astype(F32)
        self.result[...] = total


def slope_of(value):
    sig = 0.5 * jnp.tanh(0.5 * value) + 0.5
    return sig * (1.0 + value * (1.0 - sig))


def column_of(shape, columns):
    return lax.rem(lax.broadcasted_iota(jnp.int32, shape, 0), columns)


def from_left(value, columns):
    return jnp.where(
        column_of(value.shape, columns) == 0, 0.0, pltpu.roll(value, 1, 0)
    )


def from_right(value, columns):
    return jnp.where(
        column_of(value.shape, columns) == columns - 1,
        0.0,
        pltpu.roll(value, value.shape[0] - 1, 0),
    )


def folded(value):
    rows, width = value.shape
    return jnp.sum(value.reshape(rows // 8, 8, width), axis=0)


def backward_kernel(geometry, r):
    cells, d_in, d_mid, columns, total_count, capacity, entries, samples = geometry
    place = Place()
    net = Wires(r.send, r.recv)
    ranks, groups, chips = place.ranks, place.groups, place.chips
    half = d_in // 2
    greet(place.row_peers() + place.batch_peers())
    local = r.local
    loads = {}
    for n, (key, source, target) in enumerate(
        (
            (0, r.in_hat_c, r.hat_c),
            (1, r.in_slope, r.slope),
            (2, r.in_w_c, r.w_c),
            (3, r.in_hat_b, r.hat_b),
            (4, r.in_low_bt, r.low_bt),
            ("q", r.in_g_q, r.g_q),
            ("o", r.in_g_o, r.g_o),
            ("h", r.in_g_h, r.g_h),
            (5, r.in_low_t, r.low_t),
            (6, r.in_w_b, r.w_b),
        )
    ):
        loads[key] = pltpu.make_async_copy(source, target, local.at[n])
        loads[key].start()

    back = r.back
    dkv, dkv_in, dkv_own, dkv_all = r.dkv, r.dkv_in, r.dkv_own, r.dkv_all
    bank_cols = r.bank_cols
    depth = d_in // ranks
    entry = bank_cols.shape[0] // ranks
    kv = [
        net.push(dkv.at[:, pl.ds(pl.multiple_of(peer[1] * entry, entry), entry)], dkv_in.at[k], peer)
        for k, peer in enumerate(place.row_peers())
    ]

    def block_rows(ref, count):
        return lambda s: rows_of(ref, s, ref.shape[0] // count)

    def by_columns(width):
        return lambda view, g: view.at[:, pl.ds(pl.multiple_of(g * width, width), width)]

    def by_rows(height):
        return lambda view, g: view.at[pl.ds(pl.multiple_of(g * height, height), height)]

    def scatter(key, shard, part):
        return Scatter(
            net, place, shard, part, *(getattr(r, n + key) for n in ("tw_", "ba_", "pa_", "li_", "out_"))
        )

    per = cells // depth

    def shard_a(s):
        at = pl.ds(pl.multiple_of(lax.rem(s, per) * depth, depth), depth)
        return r.low_t.at[s // per, :, at]

    sc = {
        "q": scatter("q", block_rows(r.g_q, ranks), by_columns(d_mid // groups)),
        "o": scatter("o", block_rows(r.g_o, ranks), by_columns(d_in // groups)),
        "h": scatter("h", lambda s: r.g_h.at[s], by_rows(r.g_h.shape[1] // groups)),
        "c": scatter("c", block_rows(r.g_c, ranks), by_columns(d_in // groups)),
        "b": scatter("b", block_rows(r.g_b, ranks), by_columns(d_mid // groups)),
        "a": scatter("a", shard_a, by_rows(d_mid // groups)),
    }
    for key in "qoh":
        loads[key].wait()
        sc[key].pair()

    for key in (0, 1):
        loads[key].wait()
    hat_c, slope, d_pre, d_c = r.hat_c, r.slope, r.d_pre, r.slope
    acc = r.acc
    acc[...] = jnp.zeros_like(acc)
    tile = 128

    @pl.loop(0, cells // tile)
    def _(t):
        at = pl.ds(pl.multiple_of(t * tile, tile), tile)
        for h in range(2):
            on = slice(h * half, (h + 1) * half)
            grad = jnp.dot(
                r.et[h, at, :], back[...], preferred_element_type=F32
            ) * slope[at, on].astype(F32)
            d_pre[at, on] = grad.astype(LOW)
            acc[0, :, on] += folded(grad)
            acc[1, :, on] += folded(grad * hat_c[at, on].astype(F32))

    own1 = r.own1
    own1[...] = r.head_part[...]
    spread(own1, [jnp.sum(acc[n], axis=0, keepdims=True) for n in range(2)])
    started = total_start(net, place, own1, r.rows1)
    for key in "qoh":
        sc[key].batch()
    total = total_finish(net, place, started, own1, r.rows1, r.mid1, r.batch1)
    r.out_head[...] = total
    shift_c = gathered(total, 0, d_in // 4) / total_count
    gain_c = gathered(total, 1, d_in // 4) / total_count
    scale_c = r.scale_c[...]

    for key in (2, 3):
        loads[key].wait()
    w_c, hat_b, d_act = r.w_c, r.hat_b, r.d_act
    acc[...] = jnp.zeros_like(acc)
    norm_b, norm_a = r.norm_b, r.norm_a

    @pl.loop(0, cells // tile)
    def _(t):
        at = pl.ds(pl.multiple_of(t * tile, tile), tile)
        grad = scale_c * (
            d_pre[at, :].astype(F32) - shift_c - hat_c[at, :].astype(F32) * gain_c
        )
        low = grad.astype(LOW)
        d_c[at, :] = low
        hat = hat_b[at, :].astype(F32)
        back_b = ndot(low, w_c[...]) * slope_of(norm_b[0:1, :] * hat + norm_b[1:2, :])
        d_act[at, :] = back_b
        acc[0, :, 0:d_mid] += folded(back_b)
        acc[1, :, 0:d_mid] += folded(back_b * hat)

    reload = pltpu.make_async_copy(r.in_x, r.hat_c, local.at[20])
    reload.start()
    own2 = r.own2
    spread(own2, [jnp.sum(acc[n, :, 0:d_mid], axis=0, keepdims=True) for n in range(2)])
    started = total_start(net, place, own2, r.rows2)
    loads[4].wait()
    wide = 256

    @pl.loop(0, d_in // wide)
    def _(t):
        at = pl.ds(pl.multiple_of(t * wide, wide), wide)
        r.g_c[:, at] = jnp.dot(
            r.low_bt[...], d_c[:, at], preferred_element_type=F32
        ).astype(LOW)

    sc["c"].pair()
    total = total_finish(net, place, started, own2, r.rows2, r.mid2, r.batch2)
    r.out_b_sums[...] = total
    shift_b = gathered(total, 0, d_mid // 4) / total_count
    gain_b = gathered(total, 1, d_mid // 4) / total_count

    d_b, d_up, d_down = r.d_b, r.d_up, r.d_down
    big = 256
    tiles = cells // big
    first, last = place.s == 0, place.s == ranks - 1
    halo_send, halo_recv = r.halo_send, r.halo_recv

    def halo(t, way):
        at = pl.ds(pl.multiple_of(t * big, big), big)
        return pltpu.make_async_remote_copy(
            src_ref=d_b.at[1, at],
            dst_ref=(d_up if way == 0 else d_down).at[at],
            send_sem=halo_send.at[way, t],
            recv_sem=halo_recv.at[way, t],
            device_id=(place.g, place.s + 1 if way == 0 else place.s - 1),
            device_id_type=MESH,
        )

    @pl.when(first)
    def _():
        d_up[...] = jnp.zeros_like(d_up)

    @pl.when(last)
    def _():
        d_down[...] = jnp.zeros_like(d_down)

    @pl.loop(0, tiles)
    def _(t):
        at = pl.ds(pl.multiple_of(t * big, big), big)
        grad = norm_b[2:3, :] * (
            d_act[at, :] - shift_b - hat_b[at, :].astype(F32) * gain_b
        )
        d_b[1, at, :] = grad.astype(LOW)

        @pl.when(jnp.logical_not(last))
        def _():
            halo(t, 0).start()

        @pl.when(jnp.logical_not(first))
        def _():
            halo(t, 1).start()

        d_b[0, at, :] = from_right(grad, columns).astype(LOW)
        d_b[2, at, :] = from_left(grad, columns).astype(LOW)

    loads[5].wait()

    @pl.loop(0, 9)
    def _(t):
        i, j = t // 3, lax.rem(t, 3)
        r.g_b[pl.ds(pl.multiple_of(t * d_mid, d_mid), d_mid), :] = jnp.dot(
            r.low_t[i], d_b[j], preferred_element_type=F32
        ).astype(LOW)

    more = pltpu.make_async_copy(r.in_hat_a, hat_b, local.at[18])
    more.start()
    sc["b"].pair()
    for key in "qoh":
        sc[key].line()
    sc["c"].batch()

    loads[6].wait()
    more.wait()
    w_b, hat_a = r.w_b, hat_b
    acc[...] = jnp.zeros_like(acc)

    @pl.loop(0, tiles)
    def _(t):
        at = pl.ds(pl.multiple_of(t * big, big), big)

        @pl.when(jnp.logical_not(first))
        def _():
            halo(t, 0).wait_recv()

        @pl.when(jnp.logical_not(last))
        def _():
            halo(t, 1).wait_recv()

        parts = []
        for j in range(3):
            taps = [w_b[(3 * i + j) * d_mid : (3 * i + j + 1) * d_mid, :] for i in range(3)]
            parts.append(
                ndot(d_down[at, :], taps[0]) + ndot(d_b[1, at, :], taps[1]) + ndot(d_up[at, :], taps[2])
            )
        grad = from_right(parts[0], columns) + parts[1] + from_left(parts[2], columns)
        hat = hat_a[at, :].astype(F32)
        grad = grad * slope_of(norm_a[0:1, :] * hat + norm_a[1:2, :])
        d_act[at, :] = grad
        acc[0, :, 0:d_mid] += folded(grad)
        acc[1, :, 0:d_mid] += folded(grad * hat)

    again = pltpu.make_async_copy(r.in_w_a, w_b.at[0:d_in], local.at[19])
    again.start()
    own3 = r.own3
    spread(own3, [jnp.sum(acc[n, :, 0:d_mid], axis=0, keepdims=True) for n in range(2)])
    started = total_start(net, place, own3, r.rows3)
    sc["b"].batch()
    total = total_finish(net, place, started, own3, r.rows3, r.mid3, r.batch3)
    r.out_a_sums[...] = total
    shift_a = gathered(total, 0, d_mid // 4) / total_count
    gain_a = gathered(total, 1, d_mid // 4) / total_count
    d_a, d_at = d_b.at[0], r.low_bt

    @pl.loop(0, tiles)
    def _(t):
        at = pl.ds(pl.multiple_of(t * big, big), big)
        grad = norm_a[2:3, :] * (
            d_act[at, :] - shift_a - hat_a[at, :].astype(F32) * gain_a
        )
        d_a[at, :] = grad.astype(LOW)
        d_at[:, at] = jnp.transpose(grad).astype(LOW)

    reload.wait()
    x = r.hat_c

    @pl.loop(0, ranks)
    def _(s):
        shard_a(s)[...] = jnp.dot(
            d_at[...],
            x[:, pl.ds(pl.multiple_of(s * depth, depth), depth)],
            preferred_element_type=F32,
        ).astype(LOW)

    sc["a"].pair()
    sc["c"].line()
    sc["b"].line()

    for copy in kv:
        copy.wait_recv()
    own = pl.ds(pl.multiple_of(place.s * entry, entry), entry)
    for n in range(2):
        total = dkv[n, own, :].astype(F32)
        for k in range(ranks - 1):
            total = total + dkv_in[k, n].astype(F32)
        dkv_own[n] = total.astype(LOW)
        dkv_all[n, own, :] = total.astype(LOW)
    every = [
        net.push(dkv_own, dkv_all.at[:, own], peer)
        for peer in place.row_peers()
    ]
    sc["a"].batch()
    for copy in every:
        copy.wait_recv()
    kv_out, kv_in = r.kv_out, r.kv_in
    for n in range(2):
        kv_out[n] = tdot(bank_cols[...], dkv_all[n]).astype(LOW)
    share = d_mid // groups
    crossing = [
        net.push(
            kv_out.at[:, :, pl.ds(pl.multiple_of(peer[0] * share, share), share)], kv_in.at[k], peer
        )
        for k, peer in enumerate(place.batch_peers())
    ]

    again.wait()
    out_x = r.out_x

    def leave(t):
        at = pl.ds(pl.multiple_of(t * tile, tile), tile)
        return pltpu.make_async_copy(d_pre.at[at], out_x.at[at], local.at[21 + t])

    @pl.loop(0, cells // tile)
    def _(t):
        at = pl.ds(pl.multiple_of(t * tile, tile), tile)
        d_pre[at, :] = (
            ndot(d_a[at, :], w_b[0:d_in, :]) + d_pre[at, :].astype(F32)
        ).astype(LOW)
        leave(t).start()

    sc["a"].line()
    for key in "qohcb":
        sc[key].finish()
    for copy in crossing:
        copy.wait_recv()
    for n, key in enumerate((r.out_k, r.out_v)):
        total = kv_out[n, :, pl.ds(pl.multiple_of(place.g * share, share), share)].astype(F32)
        for k in range(groups - 1):
            total = total + kv_in[k, n].astype(F32)
        key[...] = total
    sc["a"].finish()

    @pl.loop(0, cells // tile)
    def _(t):
        leave(t).wait()

    @pl.loop(0, tiles)
    def _(t):
        @pl.when(jnp.logical_not(last))
        def _():
            halo(t, 0).wait_send()

        @pl.when(jnp.logical_not(first))
        def _():
            halo(t, 1).wait_send()

    net.close()


class Gather:
    def __init__(self, net, place, shard, whole, local):
        self.net, self.place, self.shard, self.whole = net, place, shard, whole
        self.rows = whole.shape[0] // place.ranks
        self.own = pltpu.make_async_copy(shard, self.block(place.s), local)

    def block(self, s):
        return rows_of(self.whole, s, self.rows)

    def quarter(self, s, g):
        part = self.rows // self.place.groups
        return self.whole.at[pl.ds(pl.multiple_of(s * self.rows + g * part, part), part)]

    def line(self):
        place = self.place
        part = self.rows // place.groups
        source = self.shard.at[pl.ds(pl.multiple_of(place.g * part, part), part)]
        self.first = [
            self.net.push(source, self.quarter(place.s, place.g), peer)
            for peer in place.line_peers()
        ]
        self.own.start()
        self.third = [self.net.push(self.shard, self.block(place.s), place.twin())]

    def batch(self):
        place = self.place
        self.blocks = [
            lax.rem(place.z + place.chips - k, place.chips) * 2 + place.core
            for k in range(1, place.chips)
        ]
        self.second = []
        for copy, s in zip(self.first, self.blocks):
            copy.wait_recv()
            view = self.quarter(s, place.g)
            self.second.append(
                [self.net.push(view, view, peer) for peer in place.batch_peers()]
            )

    def pair(self):
        for copies, s in zip(self.second, self.blocks):
            for copy in copies:
                copy.wait_recv()
            self.third.append(self.net.push(self.block(s), self.block(s), self.place.twin()))

    def ready(self):
        self.own.wait()
        for copy in self.third:
            copy.wait_recv()


def moments(total, width, total_count):
    centre = gathered(total, 0, width // 4) / total_count
    square = gathered(total, 1, width // 4) / total_count
    return centre, lax.rsqrt(square - centre * centre + 1e-05)


def sigma(value):
    return 0.5 * jnp.tanh(0.5 * value) + 0.5


def forward_kernel(geometry, r):
    cells, d_in, d_mid, columns, total_count, capacity, entries, samples = geometry
    place = Place()
    net = Wires(r.send, r.recv)
    ranks, groups = place.ranks, place.groups
    half, size = d_in // 2, 2 * capacity
    depth = d_in // ranks
    entry = r.bank16.shape[0]
    local = r.local
    load_x = pltpu.make_async_copy(r.features, r.x, local.at[0])
    load_x.start()
    greet(place.row_peers() + place.batch_peers())
    a, b, c, q, o, h = (
        Gather(net, place, shard, whole, local.at[n + 1])
        for n, (shard, whole) in enumerate(
            (
                (r.w_reduce, r.w_a),
                (r.w_spatial, r.w_b),
                (r.w_expand, r.w_c),
                (r.w_query, r.w_q),
                (r.w_out, r.w_o),
                (r.w_head, r.w_h),
            )
        )
    )
    a.line()

    def at_block(s):
        return pl.ds(pl.multiple_of(s * entry, entry), entry)

    def at_depth(s):
        return pl.ds(pl.multiple_of(s * depth, depth), depth)

    asked = [
        net.push(r.bank16.at[:, at_depth(peer[1])], rows_of(r.bank_cols, place.s, entry), peer)
        for peer in place.row_peers()
    ]
    named = [
        net.push(rows_of(r.box16, peer[1], size), rows_of(r.box_in, place.s, size), peer)
        for peer in place.row_peers()
    ]
    r.bank_cols[at_block(place.s), :] = r.bank16[:, at_depth(place.s)]
    mine = pl.ds(pl.multiple_of(place.s * size, size), size)
    r.box_in[mine, :] = r.box16[mine, :]

    strip = 64
    lane = lax.rem(lax.broadcasted_iota(jnp.int32, (strip, ranks * size), 1), size)

    @pl.loop(0, cells // strip)
    def _(t):
        at = pl.ds(pl.multiple_of(t * strip, strip), strip)
        cell = lax.broadcasted_iota(jnp.int32, (strip, ranks * size), 0) + t * strip
        total = jnp.zeros((strip, ranks * size), F32)
        for j in range(samples):
            total = total + jnp.where(
                cell == r.slot_cells[j : j + 1, :], r.slot_weights[j : j + 1, :], 0.0
            )
        r.et[0, at, :] = jnp.where(lane < capacity, total, 0.0).astype(LOW)
        r.et[1, at, :] = jnp.where(lane < capacity, 0.0, total).astype(LOW)

    a.batch()
    b.line()
    for copy in asked:
        copy.wait_recv()
    for n, weight in enumerate((r.w_key, r.w_value)):
        r.kv_part[n] = jnp.dot(r.bank_cols[...], weight[...], preferred_element_type=F32)
    kv = [
        net.push(r.kv_part.at[:, at_block(peer[1])], r.kv_in.at[k], peer)
        for k, peer in enumerate(place.row_peers())
    ]
    a.pair()
    b.batch()
    c.line()
    load_x.wait()
    a.ready()

    acc = r.acc
    acc[...] = jnp.zeros_like(acc)
    big = 256
    tiles = cells // big

    @pl.loop(0, tiles)
    def _(t):
        at = pl.ds(pl.multiple_of(t * big, big), big)
        value = jnp.dot(r.x[at, :], r.w_a[...], preferred_element_type=F32)
        r.pre_a[at, :] = value
        acc[0, :, 0:d_mid] += folded(value)
        acc[1, :, 0:d_mid] += folded(value * value)

    spread(r.own1, [jnp.sum(acc[n, :, 0:d_mid], axis=0, keepdims=True) for n in range(2)])
    started = total_start(net, place, r.own1, r.rows1)
    keep_a = pltpu.make_async_copy(r.w_a, r.out_w_a, local.at[8])
    keep_a.start()
    total = total_finish(net, place, started, r.own1, r.rows1, r.mid1, r.batch1)
    centre, inverse = moments(total, d_mid, total_count)
    gain, bias = r.norm_a[0:1, :], r.norm_a[1:2, :]
    r.out_norm_a[...] = r.norm_a[...]
    r.out_norm_a[2:3, :] = gain * inverse

    first, last = place.s == 0, place.s == ranks - 1
    low_a, low_up, low_down = r.low_a, r.low_up, r.low_down

    def halo(t, way):
        at = pl.ds(pl.multiple_of(t * big, big), big)
        return pltpu.make_async_remote_copy(
            src_ref=low_a.at[at],
            dst_ref=(low_up if way == 0 else low_down).at[at],
            send_sem=r.halo_send.at[way, t],
            recv_sem=r.halo_recv.at[way, t],
            device_id=(place.g, place.s + 1 if way == 0 else place.s - 1),
            device_id_type=MESH,
        )

    @pl.when(first)
    def _():
        low_up[...] = jnp.zeros_like(low_up)

    @pl.when(last)
    def _():
        low_down[...] = jnp.zeros_like(low_down)

    @pl.loop(0, tiles)
    def _(t):
        at = pl.ds(pl.multiple_of(t * big, big), big)
        hat = (r.pre_a[at, :] - centre) * inverse
        r.hat_a[at, :] = hat.astype(LOW)
        act = gain * hat + bias
        low_a[at, :] = (act * sigma(act)).astype(LOW)

        @pl.when(jnp.logical_not(last))
        def _():
            halo(t, 0).start()

        @pl.when(jnp.logical_not(first))
        def _():
            halo(t, 1).start()

    keep_hat_a = pltpu.make_async_copy(r.hat_a, r.out_hat_a, local.at[9])
    keep_hat_a.start()
    b.pair()
    c.batch()
    q.line()

    @pl.loop(0, tiles)
    def _(t):
        at = pl.ds(pl.multiple_of(t * big, big), big)
        r.low_t[1, :, at] = jnp.transpose(low_a[at, :].astype(F32)).astype(LOW)

    b.ready()
    acc[...] = jnp.zeros_like(acc)

    @pl.loop(0, tiles)
    def _(t):
        at = pl.ds(pl.multiple_of(t * big, big), big)

        @pl.when(jnp.logical_not(first))
        def _():
            halo(t, 0).wait_recv()

        @pl.when(jnp.logical_not(last))
        def _():
            halo(t, 1).wait_recv()

        parts = []
        for j in range(3):
            taps = [r.w_b[(3 * i + j) * d_mid : (3 * i + j + 1) * d_mid, :] for i in range(3)]
            parts.append(
                jnp.dot(low_up[at, :], taps[0], preferred_element_type=F32)
                + jnp.dot(low_a[at, :], taps[1], preferred_element_type=F32)
                + jnp.dot(low_down[at, :], taps[2], preferred_element_type=F32)
            )
        value = from_left(parts[0], columns) + parts[1] + from_right(parts[2], columns)
        r.pre_b[at, :] = value
        acc[0, :, 0:d_mid] += folded(value)
        acc[1, :, 0:d_mid] += folded(value * value)

    spread(r.own2, [jnp.sum(acc[n, :, 0:d_mid], axis=0, keepdims=True) for n in range(2)])
    started = total_start(net, place, r.own2, r.rows2)
    keep_b = pltpu.make_async_copy(r.w_b, r.out_w_b, local.at[10])
    keep_b.start()

    @pl.loop(0, tiles)
    def _(t):
        at = pl.ds(pl.multiple_of(t * big, big), big)
        r.low_t[0, :, at] = jnp.transpose(low_up[at, :].astype(F32)).astype(LOW)
        r.low_t[2, :, at] = jnp.transpose(low_down[at, :].astype(F32)).astype(LOW)

    keep_low_t = pltpu.make_async_copy(r.low_t, r.out_low_t, local.at[11])
    keep_low_t.start()
    total = total_finish(net, place, started, r.own2, r.rows2, r.mid2, r.batch2)
    centre, inverse = moments(total, d_mid, total_count)
    gain, bias = r.norm_b[0:1, :], r.norm_b[1:2, :]
    r.out_norm_b[...] = r.norm_b[...]
    r.out_norm_b[2:3, :] = gain * inverse
    c.pair()
    q.batch()
    o.line()
    h.line()
    c.ready()
    acc[...] = jnp.zeros_like(acc)

    @pl.loop(0, tiles)
    def _(t):
        at = pl.ds(pl.multiple_of(t * big, big), big)
        hat = (r.pre_b[at, :] - centre) * inverse
        r.hat_b[at, :] = hat.astype(LOW)
        act = gain * hat + bias
        low = (act * sigma(act)).astype(LOW)
        r.low_b[at, :] = low
        for k in range(4):
            on = slice(k * (d_in // 4), (k + 1) * (d_in // 4))
            value = jnp.dot(low, r.w_c[:, on], preferred_element_type=F32)
            r.pre_c[at, on] = value
            acc[0, :, on] += folded(value)
            acc[1, :, on] += folded(value * value)

    keep_c = pltpu.make_async_copy(r.w_c, r.out_w_c, local.at[12])
    keep_c.start()
    keep_hat_b = pltpu.make_async_copy(r.hat_b, r.out_hat_b, local.at[13])
    keep_hat_b.start()
    spread(r.own3, [jnp.sum(acc[n], axis=0, keepdims=True) for n in range(2)])
    started = total_start(net, place, r.own3, r.rows3)

    for copy in kv:
        copy.wait_recv()
    for n in range(2):
        total = r.kv_part[n, at_block(place.s), :]
        for k in range(ranks - 1):
            total = total + r.kv_in[k, n]
        r.kv_own[n] = total.astype(LOW)
        r.kv_all[n, at_block(place.s), :] = total.astype(LOW)
    every = [
        net.push(r.kv_own, r.kv_all.at[:, at_block(place.s)], peer) for peer in place.row_peers()
    ]

    @pl.loop(0, tiles)
    def _(t):
        at = pl.ds(pl.multiple_of(t * big, big), big)
        r.low_bt[:, at] = jnp.transpose(r.low_b[at, :].astype(F32)).astype(LOW)

    keep_low_bt = pltpu.make_async_copy(r.low_bt, r.out_low_bt, local.at[14])
    keep_low_bt.start()
    total = total_finish(net, place, started, r.own3, r.rows3, r.mid3, r.batch3)
    centre, inverse = moments(total, d_in, total_count)
    r.scale_c[...] = r.norm_c[0:1, :] * inverse
    r.centre_c[0:1, :] = centre
    r.centre_c[1:2, :] = inverse
    q.pair()
    o.batch()
    h.batch()
    r.pieces[...] = jnp.zeros_like(r.pieces)
    tile = 128

    @pl.loop(0, cells // tile)
    def _(t):
        at = pl.ds(pl.multiple_of(t * tile, tile), tile)
        for k in range(4):
            on = slice(k * (d_in // 4), (k + 1) * (d_in // 4))
            into = slice((k % 2) * (d_in // 4), (k % 2 + 1) * (d_in // 4))
            hat = (r.pre_c[at, on] - r.centre_c[0:1, on]) * r.centre_c[1:2, on]
            r.hat_c[at, on] = hat.astype(LOW)
            value = r.norm_c[0:1, on] * hat + r.norm_c[1:2, on] + r.x[at, on].astype(F32)
            sig = sigma(value)
            fmap = value * sig
            r.x[at, on] = (sig + fmap * (1.0 - sig)).astype(LOW)
            r.pieces[:, into] += tdot(r.et[k // 2, at, :], fmap.astype(LOW))

    keep_hat_c = pltpu.make_async_copy(r.hat_c, r.out_hat_c, local.at[15])
    keep_hat_c.start()
    keep_slope = pltpu.make_async_copy(r.x, r.out_slope, local.at[16])
    keep_slope.start()
    r.blocks[...] = r.pieces[...].astype(LOW)
    pushed = [
        net.push(rows_of(r.blocks, peer[1], size), rows_of(r.arrived, place.s, size), peer)
        for peer in place.row_peers()
    ]
    r.arrived[mine, :] = r.blocks[mine, :]
    o.pair()
    h.pair()
    for copy in named + every + pushed:
        copy.wait_recv()

    boxes = r.windows.shape[0]
    slot = lax.rem(lax.broadcasted_iota(jnp.int32, (ranks * size, boxes), 0), size)
    hit = r.box_in[...] == lax.broadcasted_iota(jnp.int32, (ranks * size, boxes), 1)
    picks = [
        jnp.where(hit & (slot < capacity), 1.0, 0.0).astype(LOW),
        jnp.where(hit & (slot >= capacity), 1.0, 0.0).astype(LOW),
    ]
    for k in range(2):
        r.pooled[:, k * half : (k + 1) * half] = tdot(picks[k], r.arrived[...])
    r.joined[:, 0:d_in] = r.pooled[...].astype(LOW)
    pooled_low = r.joined.at[:, 0:d_in]
    keys, vals = r.kv_all.at[0], r.kv_all.at[1]
    scale = d_mid ** (-0.5)
    q.ready()
    queries = jnp.dot(pooled_low[...], r.w_q[...], preferred_element_type=F32).astype(LOW)
    scores = jnp.where(r.windows[...] > 0, ndot(queries, keys[...]) * scale, -1e30)
    raised = jnp.exp(scores - jnp.max(scores, axis=1, keepdims=True))
    attend = raised / jnp.sum(raised, axis=1, keepdims=True)
    attend_low = attend.astype(LOW)
    mixture = jnp.dot(attend_low, vals[...], preferred_element_type=F32)
    centred = mixture - jnp.mean(mixture, axis=1, keepdims=True)
    inverse_z = lax.rsqrt(jnp.mean(centred * centred, axis=1, keepdims=True) + 1e-05)
    hat_z = centred * inverse_z
    pre_ln = r.norm_z[0:1, :] * hat_z + r.norm_z[1:2, :]
    sig_z = sigma(pre_ln)
    low_r = (pre_ln * sig_z).astype(LOW)
    slope_z = sig_z * (1.0 + pre_ln * (1.0 - sig_z))
    o.ready()
    for k in range(4):
        on = slice(k * (d_in // 4), (k + 1) * (d_in // 4))
        into = slice(d_in + k * (d_in // 4), d_in + (k + 1) * (d_in // 4))
        r.joined[:, into] = (
            r.pooled[:, on] + jnp.dot(low_r, r.w_o[:, on], preferred_element_type=F32)
        ).astype(LOW)
    h.ready()
    logits = (
        jnp.dot(r.joined[...], r.w_h[...], preferred_element_type=F32) + r.head_bias[...]
    )
    likely = jax.nn.sigmoid(logits)
    r.out_probs[...] = likely
    d_logit = (r.cotangent[...] * (likely * (1.0 - likely))).astype(LOW)
    for k in range(4):
        on = slice(k * (d_in // 4), (k + 1) * (d_in // 4))
        below = slice(d_in + k * (d_in // 4), d_in + (k + 1) * (d_in // 4))
        upper = ndot(d_logit, r.w_h[below, :])
        r.d_branch[:, on] = upper.astype(LOW)
        r.pooled[:, on] = ndot(d_logit, r.w_h[on, :]) + upper
    d_ln = ndot(r.d_branch[...], r.w_o[...]) * slope_z
    d_hat = d_ln * r.norm_z[0:1, :]
    d_mixture = (
        inverse_z
        * (
            d_hat
            - jnp.mean(d_hat, axis=1, keepdims=True)
            - hat_z * jnp.mean(d_hat * hat_z, axis=1, keepdims=True)
        )
    ).astype(LOW)
    d_attend = ndot(d_mixture, vals[...])
    d_scores = (attend * (d_attend - jnp.sum(d_attend * attend, axis=1, keepdims=True))).astype(LOW)
    d_queries = (jnp.dot(d_scores, keys[...], preferred_element_type=F32) * scale).astype(LOW)
    for k in range(4):
        on = slice(k * (d_in // 4), (k + 1) * (d_in // 4))
        r.d_pooled[:, on] = (r.pooled[:, on] + ndot(d_queries, r.w_q[on, :])).astype(LOW)
    r.blocks_out[...] = (
        jnp.dot(picks[0], r.d_pooled[:, 0:half], preferred_element_type=F32)
        + jnp.dot(picks[1], r.d_pooled[:, half:d_in], preferred_element_type=F32)
    ).astype(LOW)
    returned = [
        net.push(rows_of(r.blocks_out, peer[1], size), rows_of(r.back_in, place.s, size), peer)
        for peer in place.row_peers()
    ]
    r.back_in[mine, :] = r.blocks_out[mine, :]

    r.out_dkv[0] = (tdot(d_scores, queries) * scale).astype(LOW)
    r.out_dkv[1] = tdot(attend_low, d_mixture).astype(LOW)
    for k in range(4):
        on = slice(k * (d_in // 4), (k + 1) * (d_in // 4))
        r.g_q[on, :] = tdot(r.joined[:, on], d_queries).astype(LOW)
        r.g_o[:, on] = tdot(low_r, r.d_branch[:, on]).astype(LOW)
    width = 2 * depth
    for s in range(ranks):
        r.g_h[s] = tdot(d_logit, r.joined[:, s * width : (s + 1) * width]).astype(LOW)
    keeps = []
    for n, (source, target) in enumerate(((r.g_q, r.out_g_q), (r.g_o, r.out_g_o), (r.g_h, r.out_g_h))):
        keeps.append(pltpu.make_async_copy(source, target, local.at[17 + n]))
        keeps[-1].start()
    quarter = d_mid // 4
    r.out_head_part[...] = jnp.zeros_like(r.out_head_part)
    for n, value in enumerate(
        (jnp.sum(d_ln * hat_z, axis=0, keepdims=True), jnp.sum(d_ln, axis=0, keepdims=True))
    ):
        for k in range(4):
            r.out_head_part[4 * n + k : 4 * n + k + 1, d_in // 4 : d_in // 4 + quarter] = value[
                :, k * quarter : (k + 1) * quarter
            ]
    classes = d_logit.shape[1]
    r.out_head_part[0:1, d_in // 4 + quarter : d_in // 4 + quarter + classes] = jnp.sum(
        d_logit.astype(F32), axis=0, keepdims=True
    )
    for copy in keeps + [
        keep_a, keep_hat_a, keep_b, keep_low_t, keep_c, keep_hat_b, keep_low_bt, keep_hat_c, keep_slope
    ]:
        copy.wait()
    for copy in returned:
        copy.wait_recv()
    r.out_back[...] = r.back_in[...]
    r.bank_cols_out[...] = r.bank_cols[...]

    @pl.loop(0, tiles)
    def _(t):
        @pl.when(jnp.logical_not(last))
        def _():
            halo(t, 0).wait_send()

        @pl.when(jnp.logical_not(first))
        def _():
            halo(t, 1).wait_send()

    net.close()


class Refs:
    def __init__(self, names, refs):
        self.__dict__.update(zip(names, refs))


def run_kernel(body, geometry, channel, held, far, outs, far_outs, scratch):
    anywhere = pl.BlockSpec(memory_space=pl.ANY)
    inside = pl.BlockSpec(memory_space=pltpu.VMEM)
    names = [*held, *far, *outs, *far_outs, *scratch]
    results = pl.pallas_call(
        lambda *refs: body(geometry, Refs(names, refs)),
        out_shape=(*outs.values(), *far_outs.values()),
        in_specs=[inside] * len(held) + [anywhere] * len(far),
        out_specs=(inside,) * len(outs) + (anywhere,) * len(far_outs),
        scratch_shapes=[*scratch.values()],
        compiler_params=pltpu.CompilerParams(
            collective_id=channel, has_side_effects=True, vmem_limit_bytes=64 << 20
        ),
    )(*held.values(), *far.values())
    return Refs([*outs, *far_outs], results)


def shape(kind, *sizes):
    return jax.ShapeDtypeStruct(sizes, kind)


def room(kind, *sizes):
    return pltpu.VMEM(sizes, kind)


def sums_room(scratch, ranks, groups, widths):
    for n, width in widths:
        scratch["own%d" % n] = room(F32, 8, width)
        scratch["mid%d" % n] = room(F32, 8, width)
        scratch["rows%d" % n] = room(F32, ranks - 1, 8, width)
        scratch["batch%d" % n] = room(F32, groups - 1, 8, width)
    return scratch


def wires_room(cells):
    dma = pltpu.SemaphoreType.DMA
    return dict(
        halo_send=dma((2, cells // 256)),
        halo_recv=dma((2, cells // 256)),
        local=dma((32,)),
        send=dma((256,)),
        recv=dma((256,)),
    )


def run_forward(geometry, held, far):
    cells, d_in, d_mid, columns, total_count, capacity, entries, samples = geometry
    groups, ranks = lax.axis_size("batch"), lax.axis_size("rows")
    slots = ranks * 2 * capacity
    entry = held["bank16"].shape[0]
    bank = ranks * entry
    boxes = held["windows"].shape[0]
    classes = held["head_bias"].shape[1]
    spatial = far["w_spatial"].shape[0] * ranks
    half = d_in // 2
    outs = dict(
        out_norm_a=shape(F32, 8, d_mid),
        out_norm_b=shape(F32, 8, d_mid),
        scale_c=shape(F32, 1, d_in),
        out_probs=shape(F32, boxes, classes),
        out_dkv=shape(LOW, 2, bank, d_mid),
        out_back=shape(LOW, slots, half),
        out_head_part=shape(F32, 8, d_in // 4 + d_mid // 4 + classes),
        et=shape(LOW, 2, cells, slots),
        bank_cols_out=shape(LOW, bank, d_in // ranks),
    )
    far_outs = dict(
        out_w_a=shape(LOW, d_in, d_mid),
        out_w_b=shape(LOW, spatial, d_mid),
        out_w_c=shape(LOW, d_mid, d_in),
        out_hat_a=shape(LOW, cells, d_mid),
        out_hat_b=shape(LOW, cells, d_mid),
        out_hat_c=shape(LOW, cells, d_in),
        out_slope=shape(LOW, cells, d_in),
        out_low_t=shape(LOW, 3, d_mid, cells),
        out_low_bt=shape(LOW, d_mid, cells),
        out_g_q=shape(LOW, d_in, d_mid),
        out_g_o=shape(LOW, d_mid, d_in),
        out_g_h=shape(LOW, ranks, classes, 2 * d_in // ranks),
    )
    scratch = dict(
        x=room(LOW, cells, d_in),
        w_a=room(LOW, d_in, d_mid),
        w_b=room(LOW, spatial, d_mid),
        w_c=room(LOW, d_mid, d_in),
        w_q=room(LOW, d_in, d_mid),
        w_o=room(LOW, d_mid, d_in),
        w_h=room(LOW, 2 * d_in, classes),
        bank_cols=room(LOW, bank, d_in // ranks),
        box_in=room(jnp.int32, slots, boxes),
        kv_part=room(F32, 2, bank, d_mid),
        kv_in=room(F32, ranks - 1, 2, entry, d_mid),
        kv_own=room(LOW, 2, entry, d_mid),
        kv_all=room(LOW, 2, bank, d_mid),
        acc=room(F32, 2, 8, d_in),
        pre_a=room(F32, cells, d_mid),
        hat_a=room(LOW, cells, d_mid),
        low_a=room(LOW, cells, d_mid),
        low_up=room(LOW, cells, d_mid),
        low_down=room(LOW, cells, d_mid),
        low_t=room(LOW, 3, d_mid, cells),
        pre_b=room(F32, cells, d_mid),
        hat_b=room(LOW, cells, d_mid),
        low_b=room(LOW, cells, d_mid),
        low_bt=room(LOW, d_mid, cells),
        pre_c=room(F32, cells, d_in),
        hat_c=room(LOW, cells, d_in),
        centre_c=room(F32, 8, d_in),
        pieces=room(F32, slots, half),
        blocks=room(LOW, slots, half),
        arrived=room(LOW, slots, half),
        pooled=room(F32, boxes, d_in),
        joined=room(LOW, boxes, 2 * d_in),
        d_branch=room(LOW, boxes, d_in),
        d_pooled=room(LOW, boxes, d_in),
        blocks_out=room(LOW, slots, half),
        back_in=room(LOW, slots, half),
        g_q=room(LOW, d_in, d_mid),
        g_o=room(LOW, d_mid, d_in),
        g_h=room(LOW, ranks, classes, 2 * d_in // ranks),
        **wires_room(cells),
    )
    sums_room(scratch, ranks, groups, ((1, d_mid // 4), (2, d_mid // 4), (3, d_in // 4)))
    return run_kernel(forward_kernel, geometry, 11, held, far, outs, far_outs, scratch)


def run_backward(geometry, held, far):
    cells, d_in, d_mid, columns, total_count, capacity, entries, samples = geometry
    groups, ranks = lax.axis_size("batch"), lax.axis_size("rows")
    chips = ranks // 2
    slots = ranks * 2 * capacity
    depth = d_in // ranks
    entry = held["bank_cols"].shape[0] // ranks
    spatial = far["in_w_b"].shape[0]
    classes = far["in_g_h"].shape[1]
    share = dict(
        q=(d_in // ranks, d_mid // groups),
        o=(d_mid // ranks, d_in // groups),
        h=(classes // groups, 2 * d_in // ranks),
        c=(d_mid // ranks, d_in // groups),
        b=(spatial // ranks, d_mid // groups),
        a=(d_mid // groups, d_in // ranks),
    )
    block = dict(
        q=(d_in // ranks, d_mid),
        o=(d_mid // ranks, d_in),
        h=(classes, 2 * d_in // ranks),
        c=(d_mid // ranks, d_in),
        b=(spatial // ranks, d_mid),
        a=(d_mid, d_in // ranks),
    )
    head = held["head_part"].shape[1]
    outs = dict(
        out_head=shape(F32, 8, head),
        out_b_sums=shape(F32, 8, d_mid // 4),
        out_a_sums=shape(F32, 8, d_mid // 4),
        out_k=shape(F32, depth, d_mid // groups),
        out_v=shape(F32, depth, d_mid // groups),
    )
    scratch = dict(
        hat_c=room(LOW, cells, d_in),
        slope=room(LOW, cells, d_in),
        d_pre=room(LOW, cells, d_in),
        w_c=room(LOW, d_mid, d_in),
        hat_b=room(LOW, cells, d_mid),
        low_bt=room(LOW, d_mid, cells),
        low_t=room(LOW, 3, d_mid, cells),
        w_b=room(LOW, spatial, d_mid),
        g_q=room(LOW, d_in, d_mid),
        g_o=room(LOW, d_mid, d_in),
        g_h=room(LOW, ranks, classes, 2 * d_in // ranks),
        g_c=room(LOW, d_mid, d_in),
        g_b=room(LOW, spatial, d_mid),
        d_act=room(F32, cells, d_mid),
        d_b=room(LOW, 3, cells, d_mid),
        d_up=room(LOW, cells, d_mid),
        d_down=room(LOW, cells, d_mid),
        acc=room(F32, 2, 8, d_in),
        dkv_in=room(LOW, ranks - 1, 2, entry, d_mid),
        dkv_own=room(LOW, 2, entry, d_mid),
        dkv_all=room(LOW, 2, ranks * entry, d_mid),
        kv_out=room(LOW, 2, depth, d_mid),
        kv_in=room(LOW, groups - 1, 2, depth, d_mid // groups),
        **wires_room(cells),
    )
    sums_room(scratch, ranks, groups, ((1, head), (2, d_mid // 4), (3, d_mid // 4)))
    for key in share:
        outs["out_" + key] = shape(F32, *share[key])
        scratch["tw_" + key] = room(LOW, chips, *block[key])
        scratch["ba_" + key] = room(LOW, groups - 1, chips, *share[key])
        scratch["pa_" + key] = room(LOW, chips, *share[key])
        scratch["li_" + key] = room(LOW, chips - 1, *share[key])
    far_outs = dict(out_x=shape(LOW, cells, d_in))
    return run_kernel(backward_kernel, geometry, 12, held, far, outs, far_outs, scratch)


def fused_device(
    features,
    w_reduce,
    w_spatial,
    w_expand,
    query_weight,
    w_key,
    w_value,
    w_out,
    w_head,
    gain_a,
    bias_a,
    gain_b,
    bias_b,
    gain_c,
    bias_c,
    ln_gain,
    ln_bias,
    head_bias,
    bank,
    piece_box,
    piece_clip,
    send_count,
    sample_pos,
    sample_weight,
    win_start,
    win_len,
    prob_cotangent,
):
    groups, ranks = lax.axis_size("batch"), lax.axis_size("rows")
    clip_dev, row_dev, columns, d_in = features.shape
    d_mid = w_reduce.shape[1]
    cells = clip_dev * row_dev * columns
    total_count = cells * ranks * groups
    capacity = piece_box.shape[1]
    samples = sample_pos.shape[1] // capacity
    entries = bank.shape[0]
    entry = -(-entries // 16) * 16
    classes = head_bias.shape[0]
    class_share = classes // groups
    geometry = (cells, d_in, d_mid, columns, total_count, capacity, entries, samples)
    twice = lambda v: jnp.concatenate([v, v], axis=-1)

    def by_class(value):
        rows = value.reshape(-1, groups, class_share)
        return jnp.pad(rows, ((0, 0), (0, 0), (0, 32 - class_share))).reshape(-1, groups * 32)

    def from_class(value):
        rows = value.reshape(-1, groups, 32)[:, :, :class_share]
        return rows.reshape(-1, classes)

    def stacked(*rows):
        return jnp.pad(jnp.stack(rows), ((0, 8 - len(rows)), (0, 0)))

    def by_slot(value):
        rows = value.reshape(ranks, capacity, samples).transpose(2, 0, 1)
        rows = twice(rows).reshape(samples, ranks * 2 * capacity)
        return jnp.pad(rows, ((0, -samples % 8), (0, 0)))

    at_clip = jnp.repeat(piece_clip * (row_dev * columns), samples, axis=1)
    is_live = (jnp.arange(capacity)[None, :] < send_count[:, None]).astype(F32)
    live = jnp.repeat(is_live, samples, axis=1)
    boxes = win_start.shape[0]
    box16 = jnp.broadcast_to(
        twice(piece_box).reshape(ranks * 2 * capacity, 1), (ranks * 2 * capacity, boxes)
    )
    spot = jnp.arange(ranks * entry)
    position = spot // entry * entries + spot % entry
    windows = (
        (spot % entry < entries)
        & (position >= win_start[:, None])
        & (position < (win_start + win_len)[:, None])
    ).astype(jnp.int32)
    held = dict(
        bank16=jnp.pad(bank, ((0, entry - entries), (0, 0))),
        box16=box16,
        slot_cells=by_slot(at_clip + sample_pos),
        slot_weights=by_slot(sample_weight * live),
        w_key=w_key,
        w_value=w_value,
        norm_a=stacked(gain_a, bias_a),
        norm_b=stacked(gain_b, bias_b),
        norm_c=stacked(gain_c, bias_c),
        norm_z=stacked(ln_gain, ln_bias),
        windows=windows,
        head_bias=by_class(head_bias),
        cotangent=by_class(prob_cotangent),
    )
    far = dict(
        features=features.reshape(cells, d_in),
        w_reduce=w_reduce,
        w_spatial=w_spatial,
        w_expand=w_expand,
        w_query=query_weight,
        w_out=w_out,
        w_head=by_class(w_head),
    )
    one = run_forward(geometry, held, far)
    back_held = dict(
        back=one.out_back,
        et=one.et,
        dkv=one.out_dkv,
        bank_cols=one.bank_cols_out,
        head_part=one.out_head_part,
        scale_c=one.scale_c,
        norm_b=one.out_norm_b,
        norm_a=one.out_norm_a,
    )
    back_far = dict(
        in_hat_c=one.out_hat_c,
        in_slope=one.out_slope,
        in_w_c=one.out_w_c,
        in_hat_b=one.out_hat_b,
        in_low_bt=one.out_low_bt,
        in_low_t=one.out_low_t,
        in_w_b=one.out_w_b,
        in_hat_a=one.out_hat_a,
        in_w_a=one.out_w_a,
        in_x=far["features"],
        in_g_q=one.out_g_q,
        in_g_o=one.out_g_o,
        in_g_h=one.out_g_h,
    )
    two = run_backward(geometry, back_held, back_far)
    head, wide, quarter = two.out_head, d_in // 4, d_mid // 4
    b_sums, a_sums = two.out_b_sums.reshape(2, d_mid), two.out_a_sums.reshape(2, d_mid)
    return (
        from_class(one.out_probs),
        two.out_x.reshape(features.shape),
        two.out_a.T,
        two.out_b,
        two.out_c,
        two.out_q,
        two.out_k,
        two.out_v,
        two.out_o,
        two.out_h[:class_share].T,
        a_sums[1],
        a_sums[0],
        b_sums[1],
        b_sums[0],
        head[4:8, :wide].reshape(d_in),
        head[0:4, :wide].reshape(d_in),
        head[0:4, wide : wide + quarter].reshape(d_mid),
        head[4:8, wide : wide + quarter].reshape(d_mid),
        from_class(head[0:1, wide + quarter :]).reshape(classes),
    )


def plain_normalize(field, total_count):
    sums, squares = lax.psum((jnp.sum(field, 0), jnp.sum(field * field, 0)), ("batch", "rows"))
    centre_value = sums / total_count
    inverse = lax.rsqrt(squares / total_count - centre_value * centre_value + 1e-05)
    return ((field - centre_value) * inverse, inverse)


def plain_totals(grad, normed):
    return lax.psum((jnp.sum(grad, 0), jnp.sum(grad * normed, 0)), ("batch", "rows"))


def plain_device(
    features,
    w_reduce,
    w_spatial,
    w_expand,
    query_weight,
    w_key,
    w_value,
    w_out,
    w_head,
    gain_a,
    bias_a,
    gain_b,
    bias_b,
    gain_c,
    bias_c,
    ln_gain,
    ln_bias,
    head_bias,
    bank,
    piece_box,
    piece_clip,
    send_count,
    sample_pos,
    sample_weight,
    win_start,
    win_len,
    prob_cotangent,
):
    owners = lax.axis_size("rows")
    clip_dev, row_dev, col_count, d_in = features.shape
    cell_count = clip_dev * row_dev * col_count
    total_count = cell_count * owners * lax.axis_size("batch")
    w_a, w_b, w_c, w_q, w_k, w_v, w_o, w_h = (
        lax.all_gather(w_reduce, "rows", axis=0, tiled=True),
        lax.all_gather(w_spatial, "rows", axis=0, tiled=True),
        lax.all_gather(w_expand, "rows", axis=0, tiled=True),
        lax.all_gather(query_weight, "rows", axis=0, tiled=True),
        lax.all_gather(w_key, "rows", axis=0, tiled=True),
        lax.all_gather(w_value, "rows", axis=0, tiled=True),
        lax.all_gather(w_out, "rows", axis=0, tiled=True),
        lax.all_gather(w_head, "rows", axis=0, tiled=True),
    )
    d_mid = w_a.shape[1]
    flat_x = features.reshape(cell_count, d_in)
    pre_a = jnp.dot(flat_x, w_a, preferred_element_type=jnp.float32)
    hat_a, inverse_a = plain_normalize(pre_a, total_count)
    act_a = gain_a * hat_a + bias_a
    low_a = jax.nn.silu(act_a).astype(jnp.bfloat16)
    halo_a = padded(low_a.reshape(clip_dev, row_dev, col_count, d_mid), (("rows", 1),), 1)
    halo_a = jnp.pad(halo_a, ((0, 0), (0, 0), (1, 1), (0, 0)))
    window_a = jnp.concatenate(
        [
            halo_a[:, row_step : row_step + row_dev, col_step : col_step + col_count]
            for row_step in range(3)
            for col_step in range(3)
        ],
        axis=3,
    ).reshape(cell_count, 9 * d_mid)
    pre_b = jnp.dot(window_a, w_b, preferred_element_type=jnp.float32)
    hat_b, inverse_b = plain_normalize(pre_b, total_count)
    act_b = gain_b * hat_b + bias_b
    low_b = jax.nn.silu(act_b).astype(jnp.bfloat16)
    pre_c = jnp.dot(low_b, w_c, preferred_element_type=jnp.float32)
    hat_c, inverse_c = plain_normalize(pre_c, total_count)
    pre_out = gain_c * hat_c + bias_c + flat_x.astype(jnp.float32)
    fmap = jax.nn.silu(pre_out).astype(jnp.bfloat16)
    capacity = piece_box.shape[1]
    samples = sample_pos.shape[1] // capacity
    slot_count = owners * capacity
    sample_cells = (
        piece_clip[:, :, None] * (row_dev * col_count)
        + sample_pos.reshape(owners, capacity, samples)
    ).reshape(slot_count, samples)
    is_live = (jnp.arange(capacity)[None, :] < send_count[:, None]).reshape(slot_count)
    slot_weights = sample_weight.reshape(slot_count, samples) * is_live[:, None].astype(jnp.float32)
    cell_ids = jnp.arange(cell_count)[None, :]
    interp_sum = jnp.zeros((slot_count, cell_count), jnp.float32)
    for sample_index in range(samples):
        interp_sum = interp_sum + jnp.where(
            sample_cells[:, sample_index, None] == cell_ids,
            slot_weights[:, sample_index, None],
            0.0,
        )
    interpolated_value = interp_sum.astype(jnp.bfloat16)
    region_parts = (
        jnp.dot(interpolated_value, fmap, preferred_element_type=jnp.float32)
        .astype(jnp.bfloat16)
        .reshape(owners, capacity, d_in)
    )
    arrived, arrived_box = (
        lax.all_to_all(region_parts, "rows", split_axis=0, concat_axis=0, tiled=True),
        lax.all_to_all(piece_box, "rows", split_axis=0, concat_axis=0, tiled=True),
    )
    box_dev = win_start.shape[0]
    flat_box = arrived_box.reshape(slot_count)
    owner_hits = (flat_box[None, :] == jnp.arange(box_dev)[:, None]).astype(jnp.bfloat16)
    pooled = jnp.dot(
        owner_hits, arrived.reshape(slot_count, d_in), preferred_element_type=jnp.float32
    )
    pooled_low = pooled.astype(jnp.bfloat16)
    keys_own = jnp.dot(bank, w_k, preferred_element_type=jnp.float32).astype(jnp.bfloat16)
    values_own = jnp.dot(bank, w_v, preferred_element_type=jnp.float32).astype(jnp.bfloat16)
    key_rows, value_rows = (
        lax.all_gather(keys_own, "rows", axis=0, tiled=True),
        lax.all_gather(values_own, "rows", axis=0, tiled=True),
    )
    bank_length = key_rows.shape[0]
    queries = jnp.dot(pooled_low, w_q, preferred_element_type=jnp.float32).astype(jnp.bfloat16)
    score_scale = d_mid ** (-0.5)
    scores = ndot(queries, key_rows) * score_scale
    positions = jnp.arange(bank_length)[None, :]
    window_mask = (positions >= win_start[:, None]) & (positions < (win_start + win_len)[:, None])
    attend = jax.nn.softmax(jnp.where(window_mask, scores, -1e30), axis=-1)
    attend_low = attend.astype(jnp.bfloat16)
    mixture = jnp.dot(attend_low, value_rows, preferred_element_type=jnp.float32)
    centred = mixture - jnp.mean(mixture, axis=-1, keepdims=True)
    inverse_z = lax.rsqrt(jnp.mean(centred * centred, axis=-1, keepdims=True) + 1e-05)
    hat_z = centred * inverse_z
    pre_ln = ln_gain * hat_z + ln_bias
    low_r = jax.nn.silu(pre_ln).astype(jnp.bfloat16)
    branch = jnp.dot(low_r, w_o, preferred_element_type=jnp.float32)
    joined = jnp.concatenate([pooled, pooled + branch], axis=1).astype(jnp.bfloat16)
    logits = jnp.dot(joined, w_h, preferred_element_type=jnp.float32) + head_bias
    likely = jax.nn.sigmoid(logits)
    d_logit = (prob_cotangent * (likely * (1.0 - likely))).astype(jnp.bfloat16)
    grad_head_bias = jnp.sum(d_logit.astype(jnp.float32), 0)
    grad_wh = tdot(joined, d_logit)
    d_joined = ndot(d_logit, w_h)
    d_pooled = d_joined[:, :d_in] + d_joined[:, d_in:]
    d_branch = d_joined[:, d_in:].astype(jnp.bfloat16)
    grad_wo = tdot(low_r, d_branch)
    d_ln = ndot(d_branch, w_o) * silu_slope(pre_ln)
    grad_ln_gain = jnp.sum(d_ln * hat_z, 0)
    grad_ln_bias = jnp.sum(d_ln, 0)
    d_hat = d_ln * ln_gain
    d_mixture = (
        inverse_z
        * (
            d_hat
            - jnp.mean(d_hat, axis=-1, keepdims=True)
            - hat_z * jnp.mean(d_hat * hat_z, axis=-1, keepdims=True)
        )
    ).astype(jnp.bfloat16)
    d_attend = ndot(d_mixture, value_rows)
    d_values = tdot(attend_low, d_mixture)
    d_scores = (attend * (d_attend - jnp.sum(d_attend * attend, axis=-1, keepdims=True))).astype(
        jnp.bfloat16
    )
    d_queries = (
        jnp.dot(d_scores, key_rows, preferred_element_type=jnp.float32) * score_scale
    ).astype(jnp.bfloat16)
    d_keys = tdot(d_scores, queries) * score_scale
    grad_wq = tdot(pooled_low, d_queries)
    d_pooled = d_pooled + ndot(d_queries, w_q)
    key_sum, value_sum = side_by_side(
        (d_keys.astype(jnp.bfloat16), d_values.astype(jnp.bfloat16)), "rows", 0, 1
    )
    grad_wk = tdot(bank, key_sum.astype(jnp.bfloat16))
    grad_wv = tdot(bank, value_sum.astype(jnp.bfloat16))
    back_pieces = jnp.take(d_pooled.astype(jnp.bfloat16), flat_box, axis=0).reshape(
        owners, capacity, d_in
    )
    returned = lax.all_to_all(back_pieces, "rows", split_axis=0, concat_axis=0, tiled=True)
    d_fmap = tdot(interpolated_value, returned.reshape(slot_count, d_in))
    d_pre = d_fmap * silu_slope(pre_out)
    head_sums = lax.psum(
        (jnp.sum(d_pre, 0), jnp.sum(d_pre * hat_c, 0), grad_ln_gain, grad_ln_bias, grad_head_bias),
        ("batch", "rows"),
    )
    d_c = norm_back(
        d_pre, hat_c, inverse_c, gain_c, head_sums[0], head_sums[1], total_count
    ).astype(jnp.bfloat16)
    grad_wc = tdot(low_b, d_c)
    d_act_b = ndot(d_c, w_c) * silu_slope(act_b)
    shift_b_sum, gain_b_sum = plain_totals(d_act_b, hat_b)
    d_b = norm_back(d_act_b, hat_b, inverse_b, gain_b, shift_b_sum, gain_b_sum, total_count).astype(
        jnp.bfloat16
    )
    grad_wb = tdot(window_a, d_b)
    halo_d = padded(d_b.reshape(clip_dev, row_dev, col_count, d_mid), (("rows", 1),), 1)
    halo_d = jnp.pad(halo_d, ((0, 0), (0, 0), (1, 1), (0, 0)))
    window_d = jnp.concatenate(
        [
            halo_d[
                :, 2 - row_step : 2 - row_step + row_dev, 2 - col_step : 2 - col_step + col_count
            ]
            for row_step in range(3)
            for col_step in range(3)
        ],
        axis=3,
    ).reshape(cell_count, 9 * d_mid)
    flipped = w_b.reshape(9, d_mid, d_mid).transpose(0, 2, 1).reshape(9 * d_mid, d_mid)
    d_act_a = jnp.dot(window_d, flipped, preferred_element_type=jnp.float32) * silu_slope(act_a)
    shift_a_sum, gain_a_sum = plain_totals(d_act_a, hat_a)
    d_a = norm_back(d_act_a, hat_a, inverse_a, gain_a, shift_a_sum, gain_a_sum, total_count).astype(
        jnp.bfloat16
    )
    grad_wa = tdot(flat_x, d_a)
    grad_input = (ndot(d_a, w_a) + d_pre).astype(jnp.bfloat16).reshape(features.shape)
    partial_sums = (
        lax.psum_scatter(grad_wa, "rows", scatter_dimension=0, tiled=True),
        lax.psum_scatter(grad_wb, "rows", scatter_dimension=0, tiled=True),
        lax.psum_scatter(grad_wc, "rows", scatter_dimension=0, tiled=True),
        lax.psum_scatter(grad_wq, "rows", scatter_dimension=0, tiled=True),
        lax.psum_scatter(grad_wk, "rows", scatter_dimension=0, tiled=True),
        lax.psum_scatter(grad_wv, "rows", scatter_dimension=0, tiled=True),
        lax.psum_scatter(grad_wo, "rows", scatter_dimension=0, tiled=True),
        lax.psum_scatter(grad_wh, "rows", scatter_dimension=0, tiled=True),
    )
    finished = (
        lax.psum_scatter(
            partial_sums[0].astype(jnp.bfloat16), "batch", scatter_dimension=1, tiled=True
        ).astype(jnp.float32),
        lax.psum_scatter(
            partial_sums[1].astype(jnp.bfloat16), "batch", scatter_dimension=1, tiled=True
        ).astype(jnp.float32),
        lax.psum_scatter(
            partial_sums[2].astype(jnp.bfloat16), "batch", scatter_dimension=1, tiled=True
        ).astype(jnp.float32),
        lax.psum_scatter(
            partial_sums[3].astype(jnp.bfloat16), "batch", scatter_dimension=1, tiled=True
        ).astype(jnp.float32),
        lax.psum_scatter(
            partial_sums[4].astype(jnp.bfloat16), "batch", scatter_dimension=1, tiled=True
        ).astype(jnp.float32),
        lax.psum_scatter(
            partial_sums[5].astype(jnp.bfloat16), "batch", scatter_dimension=1, tiled=True
        ).astype(jnp.float32),
        lax.psum_scatter(
            partial_sums[6].astype(jnp.bfloat16), "batch", scatter_dimension=1, tiled=True
        ).astype(jnp.float32),
        lax.psum_scatter(
            partial_sums[7].astype(jnp.bfloat16), "batch", scatter_dimension=1, tiled=True
        ).astype(jnp.float32),
    )
    return (
        likely,
        grad_input,
        finished[0],
        finished[1],
        finished[2],
        finished[3],
        finished[4],
        finished[5],
        finished[6],
        finished[7],
        gain_a_sum,
        shift_a_sum,
        gain_b_sum,
        shift_b_sum,
        head_sums[1],
        head_sums[0],
        head_sums[2],
        head_sums[3],
        head_sums[4],
    )


def on_device(*args):
    fits = all(a.shape[0] % 64 == 0 for a in args[1:9]) and lax.axis_size("rows") % 2 == 0
    return (fused_device if fits else plain_device)(*args)


def solution(mesh):
    return jax.shard_map(
        on_device,
        mesh=mesh,
        in_specs=(
            P("batch", "rows", None, None),
            P("rows", None),
            P("rows", None),
            P("rows", None),
            P("rows", None),
            P("rows", None),
            P("rows", None),
            P("rows", None),
            P("rows", None),
            P(),
            P(),
            P(),
            P(),
            P(),
            P(),
            P(),
            P(),
            P(),
            P(("batch", "rows"), None),
            P(("batch", "rows"), None),
            P(("batch", "rows"), None),
            P(("batch", "rows")),
            P(("batch", "rows"), None),
            P(("batch", "rows"), None),
            P(("batch", "rows")),
            P(("batch", "rows")),
            P(("batch", "rows"), None),
        ),
        out_specs=(
            P(("batch", "rows"), None),
            P("batch", "rows", None, None),
            P("rows", "batch"),
            P("rows", "batch"),
            P("rows", "batch"),
            P("rows", "batch"),
            P("rows", "batch"),
            P("rows", "batch"),
            P("rows", "batch"),
            P("rows", "batch"),
            P(),
            P(),
            P(),
            P(),
            P(),
            P(),
            P(),
            P(),
            P(),
        ),
        check_vma=False,
    )
```

```python
import jax
import jax.numpy as jnp
from jax import lax
from jax.experimental import pallas as pl
from jax.experimental.pallas import tpu as pltpu
from jax.sharding import PartitionSpec as P


def padded(cells, sides, width):
    for axis, dim in sides:
        count = lax.axis_size(axis)
        ends = count - 1
        head = lax.slice_in_dim(cells, 0, width, axis=dim)
        tail = lax.slice_in_dim(cells, cells.shape[dim] - width, cells.shape[dim], axis=dim)
        cells = jnp.concatenate(
            [
                lax.ppermute(tail, axis, [(i, (i + 1) % count) for i in range(ends)]),
                cells,
                lax.ppermute(head, axis, [((i + 1) % count, i) for i in range(ends)]),
            ],
            axis=dim,
        )
    return cells


def split_up(value, dim, peers):
    shape = value.shape
    parts = value.reshape(*shape[:dim], peers, shape[dim] // peers, *shape[dim + 1 :])
    return jnp.moveaxis(parts, dim, 0)


def sum_at_owner(value, axis, dim):
    peers = lax.axis_size(axis)
    parts = lax.all_to_all(split_up(value, dim, peers), axis, 0, 0, tiled=True)
    return jnp.sum(parts.astype(jnp.float32), axis=0)


def side_by_side(arrays, axis, dim, along):
    ends, at = ([], 0)
    for a in arrays[:-1]:
        at += a.shape[along]
        ends.append(at)
    both = jnp.concatenate(arrays, axis=along)
    return tuple(jnp.split(sum_at_owner(both, axis, dim), ends, axis=along))


def tdot(left, right):
    return lax.dot_general(
        left, right, (((0,), (0,)), ((), ())), preferred_element_type=jnp.float32
    )


def ndot(left, right):
    return lax.dot_general(
        left, right, (((1,), (1,)), ((), ())), preferred_element_type=jnp.float32
    )


def silu_slope(value):
    sig = jax.nn.sigmoid(value)
    return sig * (1.0 + value * (1.0 - sig))


def norm_back(grad, normed, inverse, gain, shift_sum, gain_total_grad, total_count):
    return (
        gain * inverse * (grad - shift_sum / total_count - normed * gain_total_grad / total_count)
    )


MESH = pl.DeviceIdType.MESH
LOW = jnp.bfloat16
F32 = jnp.float32


class Wires:
    def __init__(self, send, recv):
        self.send, self.recv, self.at, self.open = send, recv, 0, []

    def push(self, source, target, peer):
        copy = pltpu.make_async_remote_copy(
            src_ref=source,
            dst_ref=target,
            send_sem=self.send.at[self.at],
            recv_sem=self.recv.at[self.at],
            device_id=peer,
            device_id_type=MESH,
        )
        self.at += 1
        copy.start()
        self.open.append(copy)
        return copy

    def close(self):
        for copy in self.open:
            copy.wait_send()


def greet(peers):
    barrier = pltpu.get_barrier_semaphore()
    for peer in peers:
        pl.semaphore_signal(barrier, inc=1, device_id=peer, device_id_type=MESH)
    pl.semaphore_wait(barrier, len(peers))


class Place:
    def __init__(self):
        self.groups, self.ranks = lax.axis_size("batch"), lax.axis_size("rows")
        self.g, self.s = lax.axis_index("batch"), lax.axis_index("rows")
        self.chips = self.ranks // 2
        self.z, self.core = self.s // 2, lax.rem(self.s, 2)
        self.other = 1 - self.core

    def row_peers(self):
        return [(self.g, lax.rem(self.s + k, self.ranks)) for k in range(1, self.ranks)]

    def batch_peers(self):
        return [(lax.rem(self.g + k, self.groups), self.s) for k in range(1, self.groups)]

    def line_peers(self):
        return [
            (self.g, lax.rem(self.z + k, self.chips) * 2 + self.core) for k in range(1, self.chips)
        ]

    def twin(self):
        return (self.g, self.z * 2 + self.other)


def rows_of(ref, index, size):
    return ref.at[pl.ds(pl.multiple_of(index * size, size), size)]


def total_start(net, place, held, from_rows):
    return [net.push(held, from_rows.at[k], peer) for k, peer in enumerate(place.row_peers())]


def total_finish(net, place, copies, held, from_rows, second, from_batch, behind=None):
    for copy in copies:
        copy.wait_recv()
    total = held[...]
    for k in range(len(copies)):
        total = total + from_rows[k]
    second[...] = total
    more = [net.push(second, from_batch.at[k], peer) for k, peer in enumerate(place.batch_peers())]
    if behind is not None:
        behind()
    for copy in more:
        copy.wait_recv()
    for k in range(len(more)):
        total = total + from_batch[k]
    return total


def spread(ref, values):
    quarter = values[0].shape[1] // 4
    for n, value in enumerate(values):
        for k in range(4):
            ref[4 * n + k : 4 * n + k + 1, 0:quarter] = value[:, k * quarter : (k + 1) * quarter]


def gathered(block, n, quarter, at=0):
    return jnp.concatenate(
        [block[4 * n + k : 4 * n + k + 1, at : at + quarter] for k in range(4)], axis=1
    )


class Scatter:
    def __init__(self, net, place, shard, part, from_twin, from_batch, partial, from_line, result):
        self.net, self.place, self.shard, self.part = net, place, shard, part
        self.from_twin, self.from_batch, self.partial = from_twin, from_batch, partial
        self.from_line, self.result = from_line, result

    def pair(self):
        place = self.place
        self.second = []
        self.first = [
            self.net.push(self.shard(2 * z + place.other), self.from_twin.at[z], place.twin())
            for z in range(place.chips)
        ]

    def batch(self, turns=None):
        place = self.place
        for z in range(place.chips) if turns is None else turns:
            self.first[z].wait_recv()
            mine = self.shard(2 * z + place.core)
            rows = mine.shape[0]
            step = next(n for n in (64, 32, 16) if rows % n == 0)

            @pl.loop(0, rows // step)
            def _(n):
                at = pl.ds(pl.multiple_of(n * step, step), step)
                mine[at, :] = (
                    mine[at, :].astype(F32) + self.from_twin[z, at, :].astype(F32)
                ).astype(LOW)

            for k, peer in enumerate(place.batch_peers()):
                self.second.append(
                    self.net.push(self.part(mine, peer[0]), self.from_batch.at[k, z], peer)
                )

    def line(self):
        place = self.place
        peers = place.groups - 1
        self.third = []
        for copy in self.second:
            copy.wait_recv()
        for z in range(place.chips):
            mine = self.part(self.shard(2 * z + place.core), place.g)
            total = mine[...].astype(F32)
            for k in range(peers):
                total = total + self.from_batch[k, z].astype(F32)
            self.partial[z] = total.astype(LOW)
        for k, peer in enumerate(place.line_peers()):
            self.third.append(
                self.net.push(self.partial.at[peer[1] // 2], self.from_line.at[k], peer)
            )

    def finish(self):
        for copy in self.third:
            copy.wait_recv()
        total = self.partial[self.place.z].astype(F32)
        for k in range(self.place.chips - 1):
            total = total + self.from_line[k].astype(F32)
        self.result[...] = total


def slope_of(value):
    sig = 0.5 * jnp.tanh(0.5 * value) + 0.5
    return sig * (1.0 + value * (1.0 - sig))


def column_of(shape, columns):
    return lax.rem(lax.broadcasted_iota(jnp.int32, shape, 0), columns)


def from_left(value, columns):
    return jnp.where(
        column_of(value.shape, columns) == 0, 0.0, pltpu.roll(value, 1, 0)
    )


def from_right(value, columns):
    return jnp.where(
        column_of(value.shape, columns) == columns - 1,
        0.0,
        pltpu.roll(value, value.shape[0] - 1, 0),
    )


def folded(value):
    rows, width = value.shape
    return jnp.sum(value.reshape(rows // 8, 8, width), axis=0)


def backward_kernel(geometry, r):
    cells, d_in, d_mid, columns, total_count, capacity, entries, samples, clips = geometry
    place = Place()
    net = Wires(r.send, r.recv)
    ranks, groups, chips = place.ranks, place.groups, place.chips
    half = d_in // 2
    greet(place.row_peers() + place.batch_peers())
    local = r.local
    loads = {}
    for n, (key, source, target) in enumerate(
        (
            (0, r.in_hat_c, r.hat_c),
            (1, r.in_slope, r.slope),
            (2, r.in_w_c, r.w_c),
            (3, r.in_hat_b, r.hat_b),
            (4, r.in_low_bt, r.low_bt),
            ("q", r.in_g_q, r.g_q),
            ("o", r.in_g_o, r.g_o),
            ("h", r.in_g_h, r.g_h),
            (5, r.in_low_t, r.low_t),
            (6, r.in_w_b, r.w_b),
        )
    ):
        loads[key] = pltpu.make_async_copy(source, target, local.at[n])
        loads[key].start()

    back = r.back
    dkv, dkv_in, dkv_own, dkv_all = r.dkv, r.dkv_in, r.dkv_own, r.dkv_all
    bank_cols = r.bank_cols
    depth = d_in // ranks
    entry = bank_cols.shape[0] // ranks
    kv = [
        net.push(dkv.at[:, pl.ds(pl.multiple_of(peer[1] * entry, entry), entry)], dkv_in.at[k], peer)
        for k, peer in enumerate(place.row_peers())
    ]

    def block_rows(ref, count):
        return lambda s: rows_of(ref, s, ref.shape[0] // count)

    def by_columns(width):
        return lambda view, g: view.at[:, pl.ds(pl.multiple_of(g * width, width), width)]

    def by_rows(height):
        return lambda view, g: view.at[pl.ds(pl.multiple_of(g * height, height), height)]

    def scatter(key, shard, part):
        return Scatter(
            net, place, shard, part, *(getattr(r, n + key) for n in ("tw_", "ba_", "pa_", "li_", "out_"))
        )

    per = cells // depth

    def shard_a(s):
        at = pl.ds(pl.multiple_of(lax.rem(s, per) * depth, depth), depth)
        return r.low_t.at[s // per, :, at]

    sc = {
        "q": scatter("q", block_rows(r.g_q, ranks), by_columns(d_mid // groups)),
        "o": scatter("o", block_rows(r.g_o, ranks), by_columns(d_in // groups)),
        "h": scatter("h", lambda s: r.g_h.at[s], by_rows(r.g_h.shape[1] // groups)),
        "c": scatter("c", block_rows(r.g_c, ranks), by_columns(d_in // groups)),
        "b": scatter("b", block_rows(r.g_b, ranks), by_columns(d_mid // groups)),
        "a": scatter("a", shard_a, by_rows(d_mid // groups)),
    }
    for key in "qoh":
        loads[key].wait()
        sc[key].pair()
    sc["h"].batch()

    for key in (0, 1):
        loads[key].wait()
    hat_c, slope, d_pre, d_c = r.hat_c, r.slope, r.d_pre, r.slope
    acc = r.acc
    acc[...] = jnp.zeros_like(acc)
    tile = 128

    @pl.loop(0, cells // tile)
    def _(t):
        at = pl.ds(pl.multiple_of(t * tile, tile), tile)
        for h in range(2):
            on = slice(h * half, (h + 1) * half)
            grad = jnp.dot(
                r.et[h, at, :], back[...], preferred_element_type=F32
            ) * slope[at, on].astype(F32)
            d_pre[at, on] = grad.astype(LOW)
            acc[0, :, on] += folded(grad)
            acc[1, :, on] += folded(grad * hat_c[at, on].astype(F32))

    own1 = r.own1
    own1[...] = r.head_part[...]
    spread(own1, [jnp.sum(acc[n], axis=0, keepdims=True) for n in range(2)])
    started = total_start(net, place, own1, r.rows1)
    total = total_finish(
        net, place, started, own1, r.rows1, r.mid1, r.batch1, sc["q"].batch
    )
    r.out_head[...] = total
    shift_c = gathered(total, 0, d_in // 4) / total_count
    gain_c = gathered(total, 1, d_in // 4) / total_count
    scale_c = r.scale_c[...]

    for key in (2, 3):
        loads[key].wait()
    w_c, hat_b, d_act = r.w_c, r.hat_b, r.d_act
    acc[...] = jnp.zeros_like(acc)
    norm_b, norm_a = r.norm_b, r.norm_a

    @pl.loop(0, cells // tile)
    def _(t):
        at = pl.ds(pl.multiple_of(t * tile, tile), tile)
        grad = scale_c * (
            d_pre[at, :].astype(F32) - shift_c - hat_c[at, :].astype(F32) * gain_c
        )
        low = grad.astype(LOW)
        d_c[at, :] = low
        hat = hat_b[at, :].astype(F32)
        back_b = ndot(low, w_c[...]) * slope_of(norm_b[0:1, :] * hat + norm_b[1:2, :])
        d_act[at, :] = back_b
        acc[0, :, 0:d_mid] += folded(back_b)
        acc[1, :, 0:d_mid] += folded(back_b * hat)

    reload = pltpu.make_async_copy(r.in_x, r.hat_c, local.at[20])
    reload.start()
    own2 = r.own2
    spread(own2, [jnp.sum(acc[n, :, 0:d_mid], axis=0, keepdims=True) for n in range(2)])
    started = total_start(net, place, own2, r.rows2)
    loads[4].wait()
    wide = 256

    @pl.loop(0, d_in // wide)
    def _(t):
        at = pl.ds(pl.multiple_of(t * wide, wide), wide)
        r.g_c[:, at] = jnp.dot(
            r.low_bt[...], d_c[:, at], preferred_element_type=F32
        ).astype(LOW)

    sc["c"].pair()

    def middle():
        sc["o"].batch()
        sc["c"].batch()

    total = total_finish(net, place, started, own2, r.rows2, r.mid2, r.batch2, middle)
    r.out_b_sums[...] = total
    shift_b = gathered(total, 0, d_mid // 4) / total_count
    gain_b = gathered(total, 1, d_mid // 4) / total_count

    d_b, d_up, d_down = r.d_b, r.d_up, r.d_down
    big = 256
    tiles = cells // big
    first, last = place.s == 0, place.s == ranks - 1
    halo_send, halo_recv = r.halo_send, r.halo_recv

    def halo(t, way):
        at = pl.ds(pl.multiple_of(t * big, big), big)
        return pltpu.make_async_remote_copy(
            src_ref=d_b.at[1, at],
            dst_ref=(d_up if way == 0 else d_down).at[at],
            send_sem=halo_send.at[way, t],
            recv_sem=halo_recv.at[way, t],
            device_id=(place.g, place.s + 1 if way == 0 else place.s - 1),
            device_id_type=MESH,
        )

    @pl.when(first)
    def _():
        d_up[...] = jnp.zeros_like(d_up)

    @pl.when(last)
    def _():
        d_down[...] = jnp.zeros_like(d_down)

    @pl.loop(0, tiles)
    def _(t):
        at = pl.ds(pl.multiple_of(t * big, big), big)
        grad = norm_b[2:3, :] * (
            d_act[at, :] - shift_b - hat_b[at, :].astype(F32) * gain_b
        )
        d_b[1, at, :] = grad.astype(LOW)

        @pl.when(jnp.logical_not(last))
        def _():
            halo(t, 0).start()

        @pl.when(jnp.logical_not(first))
        def _():
            halo(t, 1).start()

        d_b[0, at, :] = from_right(grad, columns).astype(LOW)
        d_b[2, at, :] = from_left(grad, columns).astype(LOW)

    loads[5].wait()

    @pl.loop(0, 9)
    def _(t):
        i, j = t // 3, lax.rem(t, 3)
        r.g_b[pl.ds(pl.multiple_of(t * d_mid, d_mid), d_mid), :] = jnp.dot(
            r.low_t[i], d_b[j], preferred_element_type=F32
        ).astype(LOW)

    more = pltpu.make_async_copy(r.in_hat_a, hat_b, local.at[18])
    more.start()
    sc["b"].pair()
    sc["h"].line()
    sc["q"].line()

    loads[6].wait()
    more.wait()
    w_b, hat_a = r.w_b, hat_b
    acc[...] = jnp.zeros_like(acc)

    @pl.loop(0, tiles)
    def _(t):
        at = pl.ds(pl.multiple_of(t * big, big), big)

        @pl.when(jnp.logical_not(first))
        def _():
            halo(t, 0).wait_recv()

        @pl.when(jnp.logical_not(last))
        def _():
            halo(t, 1).wait_recv()

        parts = []
        for j in range(3):
            taps = [w_b[(3 * i + j) * d_mid : (3 * i + j + 1) * d_mid, :] for i in range(3)]
            parts.append(
                ndot(d_down[at, :], taps[0]) + ndot(d_b[1, at, :], taps[1]) + ndot(d_up[at, :], taps[2])
            )
        grad = from_right(parts[0], columns) + parts[1] + from_left(parts[2], columns)
        hat = hat_a[at, :].astype(F32)
        grad = grad * slope_of(norm_a[0:1, :] * hat + norm_a[1:2, :])
        d_act[at, :] = grad
        acc[0, :, 0:d_mid] += folded(grad)
        acc[1, :, 0:d_mid] += folded(grad * hat)

    sc["b"].batch((0, 1))
    again = pltpu.make_async_copy(r.in_w_a, w_b.at[0:d_in], local.at[19])
    again.start()
    own3 = r.own3
    spread(own3, [jnp.sum(acc[n, :, 0:d_mid], axis=0, keepdims=True) for n in range(2)])
    started = total_start(net, place, own3, r.rows3)
    total = total_finish(
        net, place, started, own3, r.rows3, r.mid3, r.batch3, lambda: sc["b"].batch((2, 3))
    )
    r.out_a_sums[...] = total
    shift_a = gathered(total, 0, d_mid // 4) / total_count
    gain_a = gathered(total, 1, d_mid // 4) / total_count
    d_a, d_at = d_b.at[0], r.low_bt

    @pl.loop(0, tiles)
    def _(t):
        at = pl.ds(pl.multiple_of(t * big, big), big)
        grad = norm_a[2:3, :] * (
            d_act[at, :] - shift_a - hat_a[at, :].astype(F32) * gain_a
        )
        d_a[at, :] = grad.astype(LOW)
        d_at[:, at] = jnp.transpose(grad).astype(LOW)

    reload.wait()
    x = r.hat_c

    @pl.loop(0, ranks)
    def _(s):
        shard_a(s)[...] = jnp.dot(
            d_at[...],
            x[:, pl.ds(pl.multiple_of(s * depth, depth), depth)],
            preferred_element_type=F32,
        ).astype(LOW)

    sc["a"].pair()
    sc["o"].line()
    sc["c"].line()

    for copy in kv:
        copy.wait_recv()
    own = pl.ds(pl.multiple_of(place.s * entry, entry), entry)
    for n in range(2):
        total = dkv[n, own, :].astype(F32)
        for k in range(ranks - 1):
            total = total + dkv_in[k, n].astype(F32)
        dkv_own[n] = total.astype(LOW)
        dkv_all[n, own, :] = total.astype(LOW)
    every = [
        net.push(dkv_own, dkv_all.at[:, own], peer)
        for peer in place.row_peers()
    ]
    sc["a"].batch()
    sc["b"].line()
    for copy in every:
        copy.wait_recv()
    kv_out, kv_in = r.kv_out, r.kv_in
    for n in range(2):
        kv_out[n] = tdot(bank_cols[...], dkv_all[n]).astype(LOW)
    share = d_mid // groups
    crossing = [
        net.push(
            kv_out.at[:, :, pl.ds(pl.multiple_of(peer[0] * share, share), share)], kv_in.at[k], peer
        )
        for k, peer in enumerate(place.batch_peers())
    ]

    again.wait()
    out_x = r.out_x

    def leave(t):
        at = pl.ds(pl.multiple_of(t * tile, tile), tile)
        return pltpu.make_async_copy(d_pre.at[at], out_x.at[at], local.at[21 + t])

    @pl.loop(0, cells // tile)
    def _(t):
        at = pl.ds(pl.multiple_of(t * tile, tile), tile)
        d_pre[at, :] = (
            ndot(d_a[at, :], w_b[0:d_in, :]) + d_pre[at, :].astype(F32)
        ).astype(LOW)
        leave(t).start()

    sc["a"].line()
    for key in "qohcb":
        sc[key].finish()
    for copy in crossing:
        copy.wait_recv()
    for n, key in enumerate((r.out_k, r.out_v)):
        total = kv_out[n, :, pl.ds(pl.multiple_of(place.g * share, share), share)].astype(F32)
        for k in range(groups - 1):
            total = total + kv_in[k, n].astype(F32)
        key[...] = total
    sc["a"].finish()

    @pl.loop(0, cells // tile)
    def _(t):
        leave(t).wait()

    @pl.loop(0, tiles)
    def _(t):
        @pl.when(jnp.logical_not(last))
        def _():
            halo(t, 0).wait_send()

        @pl.when(jnp.logical_not(first))
        def _():
            halo(t, 1).wait_send()

    net.close()


class Gather:
    def __init__(self, net, place, shard, whole, local, dim=0):
        self.net, self.place, self.shard, self.whole = net, place, shard, whole
        self.dim, self.rows = dim, whole.shape[dim] // place.ranks
        self.own = pltpu.make_async_copy(shard, self.block(place.s), local)

    def cut(self, ref, start, size):
        at = pl.ds(pl.multiple_of(start, size), size)
        return ref.at[at] if self.dim == 0 else ref.at[:, at]

    def block(self, s):
        return self.cut(self.whole, s * self.rows, self.rows)

    def quarter(self, s, g):
        part = self.rows // self.place.groups
        return self.cut(self.whole, s * self.rows + g * part, part)

    def line(self):
        place = self.place
        part = self.rows // place.groups
        source = self.cut(self.shard, place.g * part, part)
        self.first = [
            self.net.push(source, self.quarter(place.s, place.g), peer)
            for peer in place.line_peers()
        ]
        self.own.start()
        self.second = []
        self.blocks = [
            lax.rem(place.z + place.chips - k, place.chips) * 2 + place.core
            for k in range(1, place.chips)
        ]
        self.third = [self.net.push(self.shard, self.block(place.s), place.twin())]

    def batch(self, turns=None):
        place = self.place
        for k in range(len(self.first)) if turns is None else turns:
            self.first[k].wait_recv()
            view = self.quarter(self.blocks[k], place.g)
            self.second.append(
                [self.net.push(view, view, peer) for peer in place.batch_peers()]
            )

    def pair(self):
        for copies, s in zip(self.second, self.blocks):
            for copy in copies:
                copy.wait_recv()
            self.third.append(self.net.push(self.block(s), self.block(s), self.place.twin()))

    def ready(self):
        self.own.wait()
        for copy in self.third:
            copy.wait_recv()


def moments(total, width, total_count):
    centre = gathered(total, 0, width // 4) / total_count
    square = gathered(total, 1, width // 4) / total_count
    return centre, lax.rsqrt(square - centre * centre + 1e-05)


def sigma(value):
    return 0.5 * jnp.tanh(0.5 * value) + 0.5


def forward_kernel(geometry, r):
    cells, d_in, d_mid, columns, total_count, capacity, entries, samples, clips = geometry
    place = Place()
    net = Wires(r.send, r.recv)
    ranks, groups = place.ranks, place.groups
    half, size = d_in // 2, 2 * capacity
    depth = d_in // ranks
    entry = r.bank16.shape[0]
    local = r.local
    load_x = pltpu.make_async_copy(r.features, r.x, local.at[0])
    load_x.start()
    greet(place.row_peers() + place.batch_peers())
    a, b, c, q, o, h = (
        Gather(net, place, shard, whole, local.at[n + 1], n // 5)
        for n, (shard, whole) in enumerate(
            (
                (r.w_reduce, r.w_a),
                (r.w_spatial, r.w_b),
                (r.w_expand, r.w_c),
                (r.w_query, r.w_q),
                (r.w_out, r.w_o),
                (r.w_head, r.w_h),
            )
        )
    )
    a.line()
    b.line()

    def at_block(s):
        return pl.ds(pl.multiple_of(s * entry, entry), entry)

    def at_depth(s):
        return pl.ds(pl.multiple_of(s * depth, depth), depth)

    r.bank16[...] = jnp.zeros_like(r.bank16)
    r.bank16[0:entries, :] = r.bank[...]
    for n in range(ranks):
        r.box16[n, 0:1, 0:capacity] = r.piece_box[n : n + 1, :]
    owner = lax.broadcasted_iota(jnp.int32, (ranks, 1), 0)
    count = jnp.zeros((ranks, 1), jnp.int32)
    for n in range(ranks):
        count = jnp.where(owner == n, r.send_count[n], count)
    for k in range(capacity):
        on = slice(k * samples, (k + 1) * samples)
        r.slot_cells[k] = r.sample_pos[:, on] + r.piece_clip[:, k : k + 1] * (cells // clips)
        r.slot_weights[k] = jnp.where(k < count, r.sample_weight[:, on], 0.0)
    asked = [
        net.push(r.bank16.at[:, at_depth(peer[1])], rows_of(r.bank_cols, place.s, entry), peer)
        for peer in place.row_peers()
    ]
    named = [
        net.push(r.box16.at[peer[1]], r.box_in.at[place.s], peer) for peer in place.row_peers()
    ]
    r.bank_cols[at_block(place.s), :] = r.bank16[:, at_depth(place.s)]
    mine = pl.ds(pl.multiple_of(place.s * size, size), size)
    r.box_in[place.s] = r.box16[place.s]

    by_rank = (capacity * ranks, ranks * size)
    row, slot = (lax.broadcasted_iota(jnp.int32, by_rank, n) for n in range(2))
    goal = lax.rem(row, ranks) * size + row // ranks
    perms = [jnp.where(slot == goal + n * capacity, 1.0, 0.0).astype(LOW) for n in range(2)]

    @pl.loop(0, capacity)
    def _(k):
        cell = lax.broadcasted_iota(jnp.int32, (ranks, cells), 1)
        spots, weights = r.slot_cells[k], r.slot_weights[k]
        total = jnp.zeros((ranks, cells), F32)
        for j in range(samples):
            total = total + jnp.where(cell == spots[:, j : j + 1], weights[:, j : j + 1], 0.0)
        r.by_slot[pl.ds(pl.multiple_of(k * ranks, ranks), ranks), :] = total

    for n in range(2):
        r.et[n] = tdot(r.by_slot[...].astype(LOW), perms[n]).astype(LOW)

    a.batch()
    a.pair()
    b.batch((0,))
    load_x.wait()
    a.ready()

    acc = r.acc
    acc[...] = jnp.zeros_like(acc)
    big = 256
    tiles = cells // big

    @pl.loop(0, tiles)
    def _(t):
        at = pl.ds(pl.multiple_of(t * big, big), big)
        value = jnp.dot(r.x[at, :], r.w_a[...], preferred_element_type=F32)
        r.pre_a[at, :] = value
        acc[0, :, 0:d_mid] += folded(value)
        acc[1, :, 0:d_mid] += folded(value * value)

    spread(r.own1, [jnp.sum(acc[n, :, 0:d_mid], axis=0, keepdims=True) for n in range(2)])
    started = total_start(net, place, r.own1, r.rows1)
    c.line()
    for copy in asked:
        copy.wait_recv()
    for n, weight in enumerate((r.w_key, r.w_value)):
        r.kv_part[n] = jnp.dot(
            r.bank_cols[...], weight[...], preferred_element_type=F32
        ).astype(LOW)
    kv = [
        net.push(r.kv_part.at[:, at_block(peer[1])], r.kv_in.at[k], peer)
        for k, peer in enumerate(place.row_peers())
    ]
    keep_a = pltpu.make_async_copy(r.w_a, r.out_w_a, local.at[8])
    keep_a.start()
    total = total_finish(
        net, place, started, r.own1, r.rows1, r.mid1, r.batch1, lambda: b.batch((1, 2))
    )
    centre, inverse = moments(total, d_mid, total_count)
    gain, bias = r.gain_a[...], r.bias_a[...]
    for n, value in enumerate((gain, bias, gain * inverse)):
        r.out_norm_a[n : n + 1, :] = value

    first, last = place.s == 0, place.s == ranks - 1
    low_a, low_up, low_down = r.low_a, r.low_up, r.low_down

    def halo(t, way):
        at = pl.ds(pl.multiple_of(t * big, big), big)
        return pltpu.make_async_remote_copy(
            src_ref=low_a.at[at],
            dst_ref=(low_up if way == 0 else low_down).at[at],
            send_sem=r.halo_send.at[way, t],
            recv_sem=r.halo_recv.at[way, t],
            device_id=(place.g, place.s + 1 if way == 0 else place.s - 1),
            device_id_type=MESH,
        )

    @pl.when(first)
    def _():
        low_up[...] = jnp.zeros_like(low_up)

    @pl.when(last)
    def _():
        low_down[...] = jnp.zeros_like(low_down)

    @pl.loop(0, tiles)
    def _(t):
        at = pl.ds(pl.multiple_of(t * big, big), big)
        hat = (r.pre_a[at, :] - centre) * inverse
        r.hat_a[at, :] = hat.astype(LOW)
        act = gain * hat + bias
        low_a[at, :] = (act * sigma(act)).astype(LOW)

        @pl.when(jnp.logical_not(last))
        def _():
            halo(t, 0).start()

        @pl.when(jnp.logical_not(first))
        def _():
            halo(t, 1).start()

    keep_hat_a = pltpu.make_async_copy(r.hat_a, r.out_hat_a, local.at[9])
    keep_hat_a.start()
    q.line()

    @pl.loop(0, tiles)
    def _(t):
        at = pl.ds(pl.multiple_of(t * big, big), big)
        r.low_t[1, :, at] = jnp.transpose(low_a[at, :].astype(F32)).astype(LOW)

    b.pair()
    c.batch()
    b.ready()
    acc[...] = jnp.zeros_like(acc)

    @pl.loop(0, tiles)
    def _(t):
        at = pl.ds(pl.multiple_of(t * big, big), big)

        @pl.when(jnp.logical_not(first))
        def _():
            halo(t, 0).wait_recv()

        @pl.when(jnp.logical_not(last))
        def _():
            halo(t, 1).wait_recv()

        parts = []
        for j in range(3):
            taps = [r.w_b[(3 * i + j) * d_mid : (3 * i + j + 1) * d_mid, :] for i in range(3)]
            parts.append(
                jnp.dot(low_up[at, :], taps[0], preferred_element_type=F32)
                + jnp.dot(low_a[at, :], taps[1], preferred_element_type=F32)
                + jnp.dot(low_down[at, :], taps[2], preferred_element_type=F32)
            )
        value = from_left(parts[0], columns) + parts[1] + from_right(parts[2], columns)
        r.pre_b[at, :] = value
        acc[0, :, 0:d_mid] += folded(value)
        acc[1, :, 0:d_mid] += folded(value * value)

    spread(r.own2, [jnp.sum(acc[n, :, 0:d_mid], axis=0, keepdims=True) for n in range(2)])
    started = total_start(net, place, r.own2, r.rows2)
    o.line()
    h.line()
    keep_b = pltpu.make_async_copy(r.w_b, r.out_w_b, local.at[10])
    keep_b.start()

    @pl.loop(0, tiles)
    def _(t):
        at = pl.ds(pl.multiple_of(t * big, big), big)
        r.low_t[0, :, at] = jnp.transpose(low_up[at, :].astype(F32)).astype(LOW)
        r.low_t[2, :, at] = jnp.transpose(low_down[at, :].astype(F32)).astype(LOW)

    keep_low_t = pltpu.make_async_copy(r.low_t, r.out_low_t, local.at[11])
    keep_low_t.start()
    total = total_finish(net, place, started, r.own2, r.rows2, r.mid2, r.batch2, q.batch)
    centre, inverse = moments(total, d_mid, total_count)
    gain, bias = r.gain_b[...], r.bias_b[...]
    for n, value in enumerate((gain, bias, gain * inverse)):
        r.out_norm_b[n : n + 1, :] = value
    c.pair()
    c.ready()
    acc[...] = jnp.zeros_like(acc)

    @pl.loop(0, tiles)
    def _(t):
        at = pl.ds(pl.multiple_of(t * big, big), big)
        hat = (r.pre_b[at, :] - centre) * inverse
        r.hat_b[at, :] = hat.astype(LOW)
        act = gain * hat + bias
        low = (act * sigma(act)).astype(LOW)
        r.low_b[at, :] = low
        for k in range(4):
            on = slice(k * (d_in // 4), (k + 1) * (d_in // 4))
            value = jnp.dot(low, r.w_c[:, on], preferred_element_type=F32)
            r.pre_c[at, on] = value
            acc[0, :, on] += folded(value)
            acc[1, :, on] += folded(value * value)

    keep_c = pltpu.make_async_copy(r.w_c, r.out_w_c, local.at[12])
    keep_c.start()
    keep_hat_b = pltpu.make_async_copy(r.hat_b, r.out_hat_b, local.at[13])
    keep_hat_b.start()
    spread(r.own3, [jnp.sum(acc[n], axis=0, keepdims=True) for n in range(2)])
    started = total_start(net, place, r.own3, r.rows3)

    for copy in kv:
        copy.wait_recv()
    for n in range(2):
        total = r.kv_part[n, at_block(place.s), :].astype(F32)
        for k in range(ranks - 1):
            total = total + r.kv_in[k, n].astype(F32)
        r.kv_own[n] = total.astype(LOW)
        r.kv_all[n, at_block(place.s), :] = total.astype(LOW)
    every = [
        net.push(r.kv_own, r.kv_all.at[:, at_block(place.s)], peer) for peer in place.row_peers()
    ]

    @pl.loop(0, tiles)
    def _(t):
        at = pl.ds(pl.multiple_of(t * big, big), big)
        r.low_bt[:, at] = jnp.transpose(r.low_b[at, :].astype(F32)).astype(LOW)

    keep_low_bt = pltpu.make_async_copy(r.low_bt, r.out_low_bt, local.at[14])
    keep_low_bt.start()

    def rest():
        o.batch()
        h.batch()

    total = total_finish(net, place, started, r.own3, r.rows3, r.mid3, r.batch3, rest)
    centre, inverse = moments(total, d_in, total_count)
    r.scale_c[...] = r.gain_c[...] * inverse
    r.centre_c[0:1, :] = centre
    r.centre_c[1:2, :] = inverse
    q.pair()
    r.pieces[...] = jnp.zeros_like(r.pieces)
    tile = 128

    @pl.loop(0, cells // tile)
    def _(t):
        at = pl.ds(pl.multiple_of(t * tile, tile), tile)
        for k in range(4):
            on = slice(k * (d_in // 4), (k + 1) * (d_in // 4))
            into = slice((k % 2) * (d_in // 4), (k % 2 + 1) * (d_in // 4))
            hat = (r.pre_c[at, on] - r.centre_c[0:1, on]) * r.centre_c[1:2, on]
            r.hat_c[at, on] = hat.astype(LOW)
            value = r.gain_c[:, on] * hat + r.bias_c[:, on] + r.x[at, on].astype(F32)
            sig = sigma(value)
            fmap = value * sig
            r.x[at, on] = (sig + fmap * (1.0 - sig)).astype(LOW)
            r.pieces[:, into] += tdot(r.et[k // 2, at, :], fmap.astype(LOW))

    keep_hat_c = pltpu.make_async_copy(r.hat_c, r.out_hat_c, local.at[15])
    keep_hat_c.start()
    keep_slope = pltpu.make_async_copy(r.x, r.out_slope, local.at[16])
    keep_slope.start()
    r.blocks[...] = r.pieces[...].astype(LOW)
    pushed = [
        net.push(rows_of(r.blocks, peer[1], size), rows_of(r.arrived, place.s, size), peer)
        for peer in place.row_peers()
    ]
    r.arrived[mine, :] = r.blocks[mine, :]
    o.pair()
    h.pair()
    for copy in named + every + pushed:
        copy.wait_recv()

    boxes = r.cotangent.shape[1]
    number = jnp.concatenate([r.box_in[n, 0:1, :] for n in range(ranks)], axis=0)
    box = lax.broadcasted_iota(jnp.int32, (ranks, boxes), 1)
    hits = jnp.concatenate(
        [jnp.where(number[:, k : k + 1] == box, 1.0, 0.0) for k in range(capacity)], axis=0
    ).astype(LOW)
    picks = [tdot(perm, hits).astype(LOW) for perm in perms]
    across = lax.broadcasted_iota(jnp.int32, (boxes, boxes), 0) == lax.broadcasted_iota(
        jnp.int32, (boxes, boxes), 1
    )

    def upright(value):
        wide = jnp.broadcast_to(value.astype(F32), (boxes, boxes))
        return jnp.sum(jnp.where(across, wide, 0.0), axis=1, keepdims=True)

    bank_row = lax.broadcasted_iota(jnp.int32, (boxes, ranks * entry), 1)
    inner = lax.rem(bank_row, entry)
    spot = (bank_row // entry * entries + inner).astype(F32)
    start, length = upright(r.win_start[...]), upright(r.win_len[...])
    window = (inner < entries) & (spot >= start) & (spot < start + length)
    for k in range(2):
        r.pooled[:, k * half : (k + 1) * half] = tdot(picks[k], r.arrived[...])
    r.joined[:, 0:d_in] = r.pooled[...].astype(LOW)
    pooled_low = r.joined.at[:, 0:d_in]
    keys, vals = r.kv_all.at[0], r.kv_all.at[1]
    scale = d_mid ** (-0.5)
    q.ready()
    queries = jnp.dot(pooled_low[...], r.w_q[...], preferred_element_type=F32).astype(LOW)
    scores = jnp.where(window, ndot(queries, keys[...]) * scale, -1e30)
    raised = jnp.exp(scores - jnp.max(scores, axis=1, keepdims=True))
    attend = raised / jnp.sum(raised, axis=1, keepdims=True)
    attend_low = attend.astype(LOW)
    mixture = jnp.dot(attend_low, vals[...], preferred_element_type=F32)
    centred = mixture - jnp.mean(mixture, axis=1, keepdims=True)
    inverse_z = lax.rsqrt(jnp.mean(centred * centred, axis=1, keepdims=True) + 1e-05)
    hat_z = centred * inverse_z
    pre_ln = r.ln_gain[...] * hat_z + r.ln_bias[...]
    sig_z = sigma(pre_ln)
    low_r = (pre_ln * sig_z).astype(LOW)
    slope_z = sig_z * (1.0 + pre_ln * (1.0 - sig_z))
    o.ready()
    for k in range(4):
        on = slice(k * (d_in // 4), (k + 1) * (d_in // 4))
        into = slice(d_in + k * (d_in // 4), d_in + (k + 1) * (d_in // 4))
        r.joined[:, into] = (
            r.pooled[:, on] + jnp.dot(low_r, r.w_o[:, on], preferred_element_type=F32)
        ).astype(LOW)
    h.ready()
    logits = (
        ndot(r.joined[...], r.w_h[...]) + r.head_bias[...]
    )
    likely = jax.nn.sigmoid(logits)
    r.out_probs[...] = likely
    d_logit = (jnp.transpose(r.cotangent[...]) * (likely * (1.0 - likely))).astype(LOW)
    for k in range(4):
        on = slice(k * (d_in // 4), (k + 1) * (d_in // 4))
        below = slice(d_in + k * (d_in // 4), d_in + (k + 1) * (d_in // 4))
        upper = jnp.dot(d_logit, r.w_h[:, below], preferred_element_type=F32)
        r.d_branch[:, on] = upper.astype(LOW)
        r.pooled[:, on] = (
            jnp.dot(d_logit, r.w_h[:, on], preferred_element_type=F32) + upper
        )
    d_ln = ndot(r.d_branch[...], r.w_o[...]) * slope_z
    d_hat = d_ln * r.ln_gain[...]
    d_mixture = (
        inverse_z
        * (
            d_hat
            - jnp.mean(d_hat, axis=1, keepdims=True)
            - hat_z * jnp.mean(d_hat * hat_z, axis=1, keepdims=True)
        )
    ).astype(LOW)
    d_attend = ndot(d_mixture, vals[...])
    d_scores = (attend * (d_attend - jnp.sum(d_attend * attend, axis=1, keepdims=True))).astype(LOW)
    d_queries = (jnp.dot(d_scores, keys[...], preferred_element_type=F32) * scale).astype(LOW)
    for k in range(4):
        on = slice(k * (d_in // 4), (k + 1) * (d_in // 4))
        r.d_pooled[:, on] = (r.pooled[:, on] + ndot(d_queries, r.w_q[on, :])).astype(LOW)
    r.blocks_out[...] = (
        jnp.dot(picks[0], r.d_pooled[:, 0:half], preferred_element_type=F32)
        + jnp.dot(picks[1], r.d_pooled[:, half:d_in], preferred_element_type=F32)
    ).astype(LOW)
    returned = [
        net.push(rows_of(r.blocks_out, peer[1], size), rows_of(r.back_in, place.s, size), peer)
        for peer in place.row_peers()
    ]
    r.back_in[mine, :] = r.blocks_out[mine, :]

    r.out_dkv[0] = (tdot(d_scores, queries) * scale).astype(LOW)
    r.out_dkv[1] = tdot(attend_low, d_mixture).astype(LOW)
    for k in range(4):
        on = slice(k * (d_in // 4), (k + 1) * (d_in // 4))
        r.g_q[on, :] = tdot(r.joined[:, on], d_queries).astype(LOW)
        r.g_o[:, on] = tdot(low_r, r.d_branch[:, on]).astype(LOW)
    width = 2 * depth
    classes = d_logit.shape[1]
    share = classes // groups
    held, kind = (
        lax.broadcasted_iota(jnp.int32, (classes, r.g_h.shape[1]), n) for n in range(2)
    )
    padded_class = held // share * (r.g_h.shape[1] // groups) + lax.rem(held, share)
    spaced = jnp.where(kind == padded_class, 1.0, 0.0).astype(LOW)
    d_spaced = jnp.dot(d_logit, spaced, preferred_element_type=F32).astype(LOW)
    for s in range(ranks):
        r.g_h[s] = tdot(d_spaced, r.joined[:, s * width : (s + 1) * width]).astype(LOW)
    keeps = []
    for n, (source, target) in enumerate(((r.g_q, r.out_g_q), (r.g_o, r.out_g_o), (r.g_h, r.out_g_h))):
        keeps.append(pltpu.make_async_copy(source, target, local.at[17 + n]))
        keeps[-1].start()
    quarter = d_mid // 4
    r.out_head_part[...] = jnp.zeros_like(r.out_head_part)
    for n, value in enumerate(
        (jnp.sum(d_ln * hat_z, axis=0, keepdims=True), jnp.sum(d_ln, axis=0, keepdims=True))
    ):
        for k in range(4):
            r.out_head_part[4 * n + k : 4 * n + k + 1, d_in // 4 : d_in // 4 + quarter] = value[
                :, k * quarter : (k + 1) * quarter
            ]
    r.out_head_part[0:1, d_in // 4 + quarter : d_in // 4 + quarter + classes] = jnp.sum(
        d_logit.astype(F32), axis=0, keepdims=True
    )
    for copy in keeps + [
        keep_a, keep_hat_a, keep_b, keep_low_t, keep_c, keep_hat_b, keep_low_bt, keep_hat_c, keep_slope
    ]:
        copy.wait()
    for copy in returned:
        copy.wait_recv()
    r.out_back[...] = r.back_in[...]
    r.bank_cols_out[...] = r.bank_cols[...]

    @pl.loop(0, tiles)
    def _(t):
        @pl.when(jnp.logical_not(last))
        def _():
            halo(t, 0).wait_send()

        @pl.when(jnp.logical_not(first))
        def _():
            halo(t, 1).wait_send()

    net.close()


class Refs:
    def __init__(self, names, refs, **more):
        self.__dict__.update(zip(names, refs), **more)


def run_kernel(body, geometry, channel, held, far, outs, far_outs, scratch):
    anywhere = pl.BlockSpec(memory_space=pl.ANY)
    inside = pl.BlockSpec(memory_space=pltpu.VMEM)
    names = [*held, *far, *outs, *far_outs, *scratch]
    scalars = pl.BlockSpec(memory_space=pltpu.SMEM)
    results = pl.pallas_call(
        lambda *refs: body(geometry, Refs(names, refs)),
        out_shape=(*outs.values(), *far_outs.values()),
        in_specs=[scalars if v.ndim == 1 else inside for v in held.values()] + [anywhere] * len(far),
        out_specs=(inside,) * len(outs) + (anywhere,) * len(far_outs),
        scratch_shapes=[*scratch.values()],
        compiler_params=pltpu.CompilerParams(
            collective_id=channel, has_side_effects=True, vmem_limit_bytes=64 << 20
        ),
    )(*held.values(), *far.values())
    return Refs([*outs, *far_outs], results)


def shape(kind, *sizes):
    return jax.ShapeDtypeStruct(sizes, kind)


def room(kind, *sizes):
    return pltpu.VMEM(sizes, kind)


def sums_room(scratch, ranks, groups, widths):
    for n, width in widths:
        scratch["own%d" % n] = room(F32, 8, width)
        scratch["mid%d" % n] = room(F32, 8, width)
        scratch["rows%d" % n] = room(F32, ranks - 1, 8, width)
        scratch["batch%d" % n] = room(F32, groups - 1, 8, width)
    return scratch


def wires_room(cells):
    dma = pltpu.SemaphoreType.DMA
    return dict(
        halo_send=dma((2, cells // 256)),
        halo_recv=dma((2, cells // 256)),
        local=dma((32,)),
        send=dma((256,)),
        recv=dma((256,)),
    )


def run_forward(geometry, held, far):
    cells, d_in, d_mid, columns, total_count, capacity, entries, samples, clips = geometry
    groups, ranks = lax.axis_size("batch"), lax.axis_size("rows")
    slots = ranks * 2 * capacity
    entry = -(-entries // 16) * 16
    bank = ranks * entry
    classes, boxes = held["cotangent"].shape
    spaced = groups * (-(-classes // groups // 16) * 16)
    spatial = far["w_spatial"].shape[0] * ranks
    half = d_in // 2
    outs = dict(
        out_norm_a=shape(F32, 8, d_mid),
        out_norm_b=shape(F32, 8, d_mid),
        scale_c=shape(F32, 1, d_in),
        out_probs=shape(F32, boxes, classes),
        out_dkv=shape(LOW, 2, bank, d_mid),
        out_back=shape(LOW, slots, half),
        out_head_part=shape(F32, 8, d_in // 4 + d_mid // 4 + spaced),
        et=shape(LOW, 2, cells, slots),
        bank_cols_out=shape(LOW, bank, d_in // ranks),
    )
    far_outs = dict(
        out_w_a=shape(LOW, d_in, d_mid),
        out_w_b=shape(LOW, spatial, d_mid),
        out_w_c=shape(LOW, d_mid, d_in),
        out_hat_a=shape(LOW, cells, d_mid),
        out_hat_b=shape(LOW, cells, d_mid),
        out_hat_c=shape(LOW, cells, d_in),
        out_slope=shape(LOW, cells, d_in),
        out_low_t=shape(LOW, 3, d_mid, cells),
        out_low_bt=shape(LOW, d_mid, cells),
        out_g_q=shape(LOW, d_in, d_mid),
        out_g_o=shape(LOW, d_mid, d_in),
        out_g_h=shape(LOW, ranks, spaced, 2 * d_in // ranks),
    )
    scratch = dict(
        x=room(LOW, cells, d_in),
        w_a=room(LOW, d_in, d_mid),
        w_b=room(LOW, spatial, d_mid),
        w_c=room(LOW, d_mid, d_in),
        w_q=room(LOW, d_in, d_mid),
        w_o=room(LOW, d_mid, d_in),
        w_h=room(LOW, classes, 2 * d_in),
        bank_cols=room(LOW, bank, d_in // ranks),
        bank16=room(LOW, entry, d_in),
        box16=room(jnp.int32, ranks, 8, 128),
        box_in=room(jnp.int32, ranks, 8, 128),
        slot_cells=room(jnp.int32, capacity, ranks, samples),
        slot_weights=room(F32, capacity, ranks, samples),
        by_slot=room(F32, capacity * ranks, cells),
        kv_part=room(LOW, 2, bank, d_mid),
        kv_in=room(LOW, ranks - 1, 2, entry, d_mid),
        kv_own=room(LOW, 2, entry, d_mid),
        kv_all=room(LOW, 2, bank, d_mid),
        acc=room(F32, 2, 8, d_in),
        pre_a=room(F32, cells, d_mid),
        hat_a=room(LOW, cells, d_mid),
        low_a=room(LOW, cells, d_mid),
        low_up=room(LOW, cells, d_mid),
        low_down=room(LOW, cells, d_mid),
        low_t=room(LOW, 3, d_mid, cells),
        pre_b=room(F32, cells, d_mid),
        hat_b=room(LOW, cells, d_mid),
        low_b=room(LOW, cells, d_mid),
        low_bt=room(LOW, d_mid, cells),
        pre_c=room(F32, cells, d_in),
        hat_c=room(LOW, cells, d_in),
        centre_c=room(F32, 8, d_in),
        pieces=room(F32, slots, half),
        blocks=room(LOW, slots, half),
        arrived=room(LOW, slots, half),
        pooled=room(F32, boxes, d_in),
        joined=room(LOW, boxes, 2 * d_in),
        d_branch=room(LOW, boxes, d_in),
        d_pooled=room(LOW, boxes, d_in),
        blocks_out=room(LOW, slots, half),
        back_in=room(LOW, slots, half),
        g_q=room(LOW, d_in, d_mid),
        g_o=room(LOW, d_mid, d_in),
        g_h=room(LOW, ranks, spaced, 2 * d_in // ranks),
        **wires_room(cells),
    )
    sums_room(scratch, ranks, groups, ((1, d_mid // 4), (2, d_mid // 4), (3, d_in // 4)))
    return run_kernel(forward_kernel, geometry, 11, held, far, outs, far_outs, scratch)


def run_backward(geometry, held, far):
    cells, d_in, d_mid, columns, total_count, capacity, entries, samples, clips = geometry
    groups, ranks = lax.axis_size("batch"), lax.axis_size("rows")
    chips = ranks // 2
    slots = ranks * 2 * capacity
    depth = d_in // ranks
    entry = held["bank_cols"].shape[0] // ranks
    spatial = far["in_w_b"].shape[0]
    classes = far["in_g_h"].shape[1]
    share = dict(
        q=(d_in // ranks, d_mid // groups),
        o=(d_mid // ranks, d_in // groups),
        h=(classes // groups, 2 * d_in // ranks),
        c=(d_mid // ranks, d_in // groups),
        b=(spatial // ranks, d_mid // groups),
        a=(d_mid // groups, d_in // ranks),
    )
    block = dict(
        q=(d_in // ranks, d_mid),
        o=(d_mid // ranks, d_in),
        h=(classes, 2 * d_in // ranks),
        c=(d_mid // ranks, d_in),
        b=(spatial // ranks, d_mid),
        a=(d_mid, d_in // ranks),
    )
    head = held["head_part"].shape[1]
    outs = dict(
        out_head=shape(F32, 8, head),
        out_b_sums=shape(F32, 8, d_mid // 4),
        out_a_sums=shape(F32, 8, d_mid // 4),
        out_k=shape(F32, depth, d_mid // groups),
        out_v=shape(F32, depth, d_mid // groups),
    )
    scratch = dict(
        hat_c=room(LOW, cells, d_in),
        slope=room(LOW, cells, d_in),
        d_pre=room(LOW, cells, d_in),
        w_c=room(LOW, d_mid, d_in),
        hat_b=room(LOW, cells, d_mid),
        low_bt=room(LOW, d_mid, cells),
        low_t=room(LOW, 3, d_mid, cells),
        w_b=room(LOW, spatial, d_mid),
        g_q=room(LOW, d_in, d_mid),
        g_o=room(LOW, d_mid, d_in),
        g_h=room(LOW, ranks, classes, 2 * d_in // ranks),
        g_c=room(LOW, d_mid, d_in),
        g_b=room(LOW, spatial, d_mid),
        d_act=room(F32, cells, d_mid),
        d_b=room(LOW, 3, cells, d_mid),
        d_up=room(LOW, cells, d_mid),
        d_down=room(LOW, cells, d_mid),
        acc=room(F32, 2, 8, d_in),
        dkv_in=room(LOW, ranks - 1, 2, entry, d_mid),
        dkv_own=room(LOW, 2, entry, d_mid),
        dkv_all=room(LOW, 2, ranks * entry, d_mid),
        kv_out=room(LOW, 2, depth, d_mid),
        kv_in=room(LOW, groups - 1, 2, depth, d_mid // groups),
        **wires_room(cells),
    )
    sums_room(scratch, ranks, groups, ((1, head), (2, d_mid // 4), (3, d_mid // 4)))
    for key in share:
        outs["out_" + key] = shape(F32, *share[key])
        scratch["tw_" + key] = room(LOW, chips, *block[key])
        scratch["ba_" + key] = room(LOW, groups - 1, chips, *share[key])
        scratch["pa_" + key] = room(LOW, chips, *share[key])
        scratch["li_" + key] = room(LOW, chips - 1, *share[key])
    far_outs = dict(out_x=shape(LOW, cells, d_in))
    return run_kernel(backward_kernel, geometry, 12, held, far, outs, far_outs, scratch)


def finish_kernel(r):
    chunk = r.in_x.shape[0] // 8

    def across(n, leave):
        at = pl.ds(n * chunk, chunk)
        source, target = (r.stage, r.x) if leave else (r.in_x, r.stage)
        return pltpu.make_async_copy(source.at[at], target.at[at], r.local.at[leave, n])

    for n in range(8):
        across(n, 0).start()
    for n in range(8):
        across(n, 0).wait()
        across(n, 1).start()
    r.probs[...] = jnp.transpose(r.in_probs[...])
    r.a[...] = jnp.transpose(r.in_a[...])
    r.b[...] = r.in_b[...]
    r.c[...] = r.in_c[...]
    r.q[...] = r.in_q[...]
    r.k[...] = r.in_k[...]
    r.v[...] = r.in_v[...]
    r.o[...] = r.in_o[...]
    r.h[...] = r.in_h[0 : r.h.shape[0], :]
    r.bias_a[...], r.gain_a[...] = r.in_a_sums[0:4, :], r.in_a_sums[4:8, :]
    r.bias_b[...], r.gain_b[...] = r.in_b_sums[0:4, :], r.in_b_sums[4:8, :]
    lanes = r.ln_gain.shape[1]
    per = r.gain_c.shape[0] // 4
    for n in range(4):
        for k in range(per):
            on = slice(k * lanes, (k + 1) * lanes)
            r.bias_c[per * n + k : per * n + k + 1, :] = r.in_head[n : n + 1, on]
            r.gain_c[per * n + k : per * n + k + 1, :] = r.in_head[4 + n : 5 + n, on]
    on = slice(per * lanes, (per + 1) * lanes)
    r.ln_gain[...], r.ln_bias[...] = r.in_head[0:4, on], r.in_head[4:8, on]
    at = (per + 1) * lanes
    r.head_bias[...] = r.in_head[0:1, at : at + r.head_bias.shape[1]]
    for n in range(8):
        across(n, 1).wait()


def run_finish(probs, two, groups, d_mid, classes):
    held = dict(
        in_probs=probs,
        in_a=two.out_a,
        in_b=two.out_b,
        in_c=two.out_c,
        in_q=two.out_q,
        in_k=two.out_k,
        in_v=two.out_v,
        in_o=two.out_o,
        in_h=two.out_h,
        in_a_sums=two.out_a_sums,
        in_b_sums=two.out_b_sums,
        in_head=two.out_head,
    )
    like = lambda v: shape(F32, *v.shape)
    lanes = two.out_a_sums.shape[1]
    row = shape(F32, 4, lanes)
    wide = shape(F32, 4 * (two.out_x.shape[1] // 4 // lanes), lanes)
    outs = dict(
        probs=shape(F32, *probs.shape[::-1]),
        a=shape(F32, *two.out_a.shape[::-1]),
        b=like(two.out_b),
        c=like(two.out_c),
        q=like(two.out_q),
        k=like(two.out_k),
        v=like(two.out_v),
        o=like(two.out_o),
        h=shape(F32, classes // groups, two.out_h.shape[1]),
        gain_a=row,
        bias_a=row,
        gain_b=row,
        bias_b=row,
        gain_c=wide,
        bias_c=wide,
        ln_gain=row,
        ln_bias=row,
        head_bias=shape(F32, 1, classes),
    )
    far_outs = dict(x=shape(LOW, *two.out_x.shape))
    anywhere = pl.BlockSpec(memory_space=pl.ANY)
    inside = pl.BlockSpec(memory_space=pltpu.VMEM)
    names = [*held, "in_x", *outs, *far_outs, "stage", "local"]
    results = pl.pallas_call(
        lambda *refs: finish_kernel(Refs(names, refs)),
        out_shape=(*outs.values(), *far_outs.values()),
        in_specs=[inside] * len(held) + [anywhere],
        out_specs=(inside,) * len(outs) + (anywhere,),
        scratch_shapes=[room(LOW, *two.out_x.shape), pltpu.SemaphoreType.DMA((2, 8))],
        compiler_params=pltpu.CompilerParams(vmem_limit_bytes=64 << 20),
    )(*held.values(), two.out_x)
    return Refs([*outs, *far_outs], results)


def fused_device(
    features,
    w_reduce,
    w_spatial,
    w_expand,
    query_weight,
    w_key,
    w_value,
    w_out,
    w_head,
    gain_a,
    bias_a,
    gain_b,
    bias_b,
    gain_c,
    bias_c,
    ln_gain,
    ln_bias,
    head_bias,
    bank,
    piece_box,
    piece_clip,
    send_count,
    sample_pos,
    sample_weight,
    win_start,
    win_len,
    prob_cotangent,
):
    groups, ranks = lax.axis_size("batch"), lax.axis_size("rows")
    clip_dev, row_dev, columns, d_in = features.shape
    d_mid = w_reduce.shape[1]
    cells = clip_dev * row_dev * columns
    total_count = cells * ranks * groups
    capacity = piece_box.shape[1]
    samples = sample_pos.shape[1] // capacity
    entries = bank.shape[0]
    geometry = (cells, d_in, d_mid, columns, total_count, capacity, entries, samples, clip_dev)
    line = lambda v: v.reshape(1, -1)
    held = dict(
        bank=bank,
        piece_box=piece_box,
        piece_clip=piece_clip,
        send_count=send_count,
        sample_pos=sample_pos,
        sample_weight=sample_weight,
        w_key=w_key,
        w_value=w_value,
        gain_a=line(gain_a),
        bias_a=line(bias_a),
        gain_b=line(gain_b),
        bias_b=line(bias_b),
        gain_c=line(gain_c),
        bias_c=line(bias_c),
        ln_gain=line(ln_gain),
        ln_bias=line(ln_bias),
        win_start=line(win_start),
        win_len=line(win_len),
        head_bias=line(head_bias),
        cotangent=prob_cotangent.T,
    )
    far = dict(
        features=features.reshape(cells, d_in),
        w_reduce=w_reduce,
        w_spatial=w_spatial,
        w_expand=w_expand,
        w_query=query_weight,
        w_out=w_out,
        w_head=w_head.T,
    )
    one = run_forward(geometry, held, far)
    back_held = dict(
        back=one.out_back,
        et=one.et,
        dkv=one.out_dkv,
        bank_cols=one.bank_cols_out,
        head_part=one.out_head_part,
        scale_c=one.scale_c,
        norm_b=one.out_norm_b,
        norm_a=one.out_norm_a,
    )
    back_far = dict(
        in_hat_c=one.out_hat_c,
        in_slope=one.out_slope,
        in_w_c=one.out_w_c,
        in_hat_b=one.out_hat_b,
        in_low_bt=one.out_low_bt,
        in_low_t=one.out_low_t,
        in_w_b=one.out_w_b,
        in_hat_a=one.out_hat_a,
        in_w_a=one.out_w_a,
        in_x=far["features"],
        in_g_q=one.out_g_q,
        in_g_o=one.out_g_o,
        in_g_h=one.out_g_h,
    )
    two = run_backward(geometry, back_held, back_far)
    last = run_finish(one.out_probs, two, groups, d_mid, prob_cotangent.shape[1])
    flat = lambda v: v.reshape(-1)
    return (
        last.probs.T,
        last.x.reshape(features.shape),
        last.a,
        last.b,
        last.c,
        last.q,
        last.k,
        last.v,
        last.o,
        last.h.T,
        flat(last.gain_a),
        flat(last.bias_a),
        flat(last.gain_b),
        flat(last.bias_b),
        flat(last.gain_c),
        flat(last.bias_c),
        flat(last.ln_gain),
        flat(last.ln_bias),
        flat(last.head_bias),
    )


def plain_normalize(field, total_count):
    sums, squares = lax.psum((jnp.sum(field, 0), jnp.sum(field * field, 0)), ("batch", "rows"))
    centre_value = sums / total_count
    inverse = lax.rsqrt(squares / total_count - centre_value * centre_value + 1e-05)
    return ((field - centre_value) * inverse, inverse)


def plain_totals(grad, normed):
    return lax.psum((jnp.sum(grad, 0), jnp.sum(grad * normed, 0)), ("batch", "rows"))


def plain_device(
    features,
    w_reduce,
    w_spatial,
    w_expand,
    query_weight,
    w_key,
    w_value,
    w_out,
    w_head,
    gain_a,
    bias_a,
    gain_b,
    bias_b,
    gain_c,
    bias_c,
    ln_gain,
    ln_bias,
    head_bias,
    bank,
    piece_box,
    piece_clip,
    send_count,
    sample_pos,
    sample_weight,
    win_start,
    win_len,
    prob_cotangent,
):
    owners = lax.axis_size("rows")
    clip_dev, row_dev, col_count, d_in = features.shape
    cell_count = clip_dev * row_dev * col_count
    total_count = cell_count * owners * lax.axis_size("batch")
    w_a, w_b, w_c, w_q, w_k, w_v, w_o, w_h = (
        lax.all_gather(w_reduce, "rows", axis=0, tiled=True),
        lax.all_gather(w_spatial, "rows", axis=0, tiled=True),
        lax.all_gather(w_expand, "rows", axis=0, tiled=True),
        lax.all_gather(query_weight, "rows", axis=0, tiled=True),
        lax.all_gather(w_key, "rows", axis=0, tiled=True),
        lax.all_gather(w_value, "rows", axis=0, tiled=True),
        lax.all_gather(w_out, "rows", axis=0, tiled=True),
        lax.all_gather(w_head, "rows", axis=0, tiled=True),
    )
    d_mid = w_a.shape[1]
    flat_x = features.reshape(cell_count, d_in)
    pre_a = jnp.dot(flat_x, w_a, preferred_element_type=jnp.float32)
    hat_a, inverse_a = plain_normalize(pre_a, total_count)
    act_a = gain_a * hat_a + bias_a
    low_a = jax.nn.silu(act_a).astype(jnp.bfloat16)
    halo_a = padded(low_a.reshape(clip_dev, row_dev, col_count, d_mid), (("rows", 1),), 1)
    halo_a = jnp.pad(halo_a, ((0, 0), (0, 0), (1, 1), (0, 0)))
    window_a = jnp.concatenate(
        [
            halo_a[:, row_step : row_step + row_dev, col_step : col_step + col_count]
            for row_step in range(3)
            for col_step in range(3)
        ],
        axis=3,
    ).reshape(cell_count, 9 * d_mid)
    pre_b = jnp.dot(window_a, w_b, preferred_element_type=jnp.float32)
    hat_b, inverse_b = plain_normalize(pre_b, total_count)
    act_b = gain_b * hat_b + bias_b
    low_b = jax.nn.silu(act_b).astype(jnp.bfloat16)
    pre_c = jnp.dot(low_b, w_c, preferred_element_type=jnp.float32)
    hat_c, inverse_c = plain_normalize(pre_c, total_count)
    pre_out = gain_c * hat_c + bias_c + flat_x.astype(jnp.float32)
    fmap = jax.nn.silu(pre_out).astype(jnp.bfloat16)
    capacity = piece_box.shape[1]
    samples = sample_pos.shape[1] // capacity
    slot_count = owners * capacity
    sample_cells = (
        piece_clip[:, :, None] * (row_dev * col_count)
        + sample_pos.reshape(owners, capacity, samples)
    ).reshape(slot_count, samples)
    is_live = (jnp.arange(capacity)[None, :] < send_count[:, None]).reshape(slot_count)
    slot_weights = sample_weight.reshape(slot_count, samples) * is_live[:, None].astype(jnp.float32)
    cell_ids = jnp.arange(cell_count)[None, :]
    interp_sum = jnp.zeros((slot_count, cell_count), jnp.float32)
    for sample_index in range(samples):
        interp_sum = interp_sum + jnp.where(
            sample_cells[:, sample_index, None] == cell_ids,
            slot_weights[:, sample_index, None],
            0.0,
        )
    interpolated_value = interp_sum.astype(jnp.bfloat16)
    region_parts = (
        jnp.dot(interpolated_value, fmap, preferred_element_type=jnp.float32)
        .astype(jnp.bfloat16)
        .reshape(owners, capacity, d_in)
    )
    arrived, arrived_box = (
        lax.all_to_all(region_parts, "rows", split_axis=0, concat_axis=0, tiled=True),
        lax.all_to_all(piece_box, "rows", split_axis=0, concat_axis=0, tiled=True),
    )
    box_dev = win_start.shape[0]
    flat_box = arrived_box.reshape(slot_count)
    owner_hits = (flat_box[None, :] == jnp.arange(box_dev)[:, None]).astype(jnp.bfloat16)
    pooled = jnp.dot(
        owner_hits, arrived.reshape(slot_count, d_in), preferred_element_type=jnp.float32
    )
    pooled_low = pooled.astype(jnp.bfloat16)
    keys_own = jnp.dot(bank, w_k, preferred_element_type=jnp.float32).astype(jnp.bfloat16)
    values_own = jnp.dot(bank, w_v, preferred_element_type=jnp.float32).astype(jnp.bfloat16)
    key_rows, value_rows = (
        lax.all_gather(keys_own, "rows", axis=0, tiled=True),
        lax.all_gather(values_own, "rows", axis=0, tiled=True),
    )
    bank_length = key_rows.shape[0]
    queries = jnp.dot(pooled_low, w_q, preferred_element_type=jnp.float32).astype(jnp.bfloat16)
    score_scale = d_mid ** (-0.5)
    scores = ndot(queries, key_rows) * score_scale
    positions = jnp.arange(bank_length)[None, :]
    window_mask = (positions >= win_start[:, None]) & (positions < (win_start + win_len)[:, None])
    attend = jax.nn.softmax(jnp.where(window_mask, scores, -1e30), axis=-1)
    attend_low = attend.astype(jnp.bfloat16)
    mixture = jnp.dot(attend_low, value_rows, preferred_element_type=jnp.float32)
    centred = mixture - jnp.mean(mixture, axis=-1, keepdims=True)
    inverse_z = lax.rsqrt(jnp.mean(centred * centred, axis=-1, keepdims=True) + 1e-05)
    hat_z = centred * inverse_z
    pre_ln = ln_gain * hat_z + ln_bias
    low_r = jax.nn.silu(pre_ln).astype(jnp.bfloat16)
    branch = jnp.dot(low_r, w_o, preferred_element_type=jnp.float32)
    joined = jnp.concatenate([pooled, pooled + branch], axis=1).astype(jnp.bfloat16)
    logits = jnp.dot(joined, w_h, preferred_element_type=jnp.float32) + head_bias
    likely = jax.nn.sigmoid(logits)
    d_logit = (prob_cotangent * (likely * (1.0 - likely))).astype(jnp.bfloat16)
    grad_head_bias = jnp.sum(d_logit.astype(jnp.float32), 0)
    grad_wh = tdot(joined, d_logit)
    d_joined = ndot(d_logit, w_h)
    d_pooled = d_joined[:, :d_in] + d_joined[:, d_in:]
    d_branch = d_joined[:, d_in:].astype(jnp.bfloat16)
    grad_wo = tdot(low_r, d_branch)
    d_ln = ndot(d_branch, w_o) * silu_slope(pre_ln)
    grad_ln_gain = jnp.sum(d_ln * hat_z, 0)
    grad_ln_bias = jnp.sum(d_ln, 0)
    d_hat = d_ln * ln_gain
    d_mixture = (
        inverse_z
        * (
            d_hat
            - jnp.mean(d_hat, axis=-1, keepdims=True)
            - hat_z * jnp.mean(d_hat * hat_z, axis=-1, keepdims=True)
        )
    ).astype(jnp.bfloat16)
    d_attend = ndot(d_mixture, value_rows)
    d_values = tdot(attend_low, d_mixture)
    d_scores = (attend * (d_attend - jnp.sum(d_attend * attend, axis=-1, keepdims=True))).astype(
        jnp.bfloat16
    )
    d_queries = (
        jnp.dot(d_scores, key_rows, preferred_element_type=jnp.float32) * score_scale
    ).astype(jnp.bfloat16)
    d_keys = tdot(d_scores, queries) * score_scale
    grad_wq = tdot(pooled_low, d_queries)
    d_pooled = d_pooled + ndot(d_queries, w_q)
    key_sum, value_sum = side_by_side(
        (d_keys.astype(jnp.bfloat16), d_values.astype(jnp.bfloat16)), "rows", 0, 1
    )
    grad_wk = tdot(bank, key_sum.astype(jnp.bfloat16))
    grad_wv = tdot(bank, value_sum.astype(jnp.bfloat16))
    back_pieces = jnp.take(d_pooled.astype(jnp.bfloat16), flat_box, axis=0).reshape(
        owners, capacity, d_in
    )
    returned = lax.all_to_all(back_pieces, "rows", split_axis=0, concat_axis=0, tiled=True)
    d_fmap = tdot(interpolated_value, returned.reshape(slot_count, d_in))
    d_pre = d_fmap * silu_slope(pre_out)
    head_sums = lax.psum(
        (jnp.sum(d_pre, 0), jnp.sum(d_pre * hat_c, 0), grad_ln_gain, grad_ln_bias, grad_head_bias),
        ("batch", "rows"),
    )
    d_c = norm_back(
        d_pre, hat_c, inverse_c, gain_c, head_sums[0], head_sums[1], total_count
    ).astype(jnp.bfloat16)
    grad_wc = tdot(low_b, d_c)
    d_act_b = ndot(d_c, w_c) * silu_slope(act_b)
    shift_b_sum, gain_b_sum = plain_totals(d_act_b, hat_b)
    d_b = norm_back(d_act_b, hat_b, inverse_b, gain_b, shift_b_sum, gain_b_sum, total_count).astype(
        jnp.bfloat16
    )
    grad_wb = tdot(window_a, d_b)
    halo_d = padded(d_b.reshape(clip_dev, row_dev, col_count, d_mid), (("rows", 1),), 1)
    halo_d = jnp.pad(halo_d, ((0, 0), (0, 0), (1, 1), (0, 0)))
    window_d = jnp.concatenate(
        [
            halo_d[
                :, 2 - row_step : 2 - row_step + row_dev, 2 - col_step : 2 - col_step + col_count
            ]
            for row_step in range(3)
            for col_step in range(3)
        ],
        axis=3,
    ).reshape(cell_count, 9 * d_mid)
    flipped = w_b.reshape(9, d_mid, d_mid).transpose(0, 2, 1).reshape(9 * d_mid, d_mid)
    d_act_a = jnp.dot(window_d, flipped, preferred_element_type=jnp.float32) * silu_slope(act_a)
    shift_a_sum, gain_a_sum = plain_totals(d_act_a, hat_a)
    d_a = norm_back(d_act_a, hat_a, inverse_a, gain_a, shift_a_sum, gain_a_sum, total_count).astype(
        jnp.bfloat16
    )
    grad_wa = tdot(flat_x, d_a)
    grad_input = (ndot(d_a, w_a) + d_pre).astype(jnp.bfloat16).reshape(features.shape)
    partial_sums = (
        lax.psum_scatter(grad_wa, "rows", scatter_dimension=0, tiled=True),
        lax.psum_scatter(grad_wb, "rows", scatter_dimension=0, tiled=True),
        lax.psum_scatter(grad_wc, "rows", scatter_dimension=0, tiled=True),
        lax.psum_scatter(grad_wq, "rows", scatter_dimension=0, tiled=True),
        lax.psum_scatter(grad_wk, "rows", scatter_dimension=0, tiled=True),
        lax.psum_scatter(grad_wv, "rows", scatter_dimension=0, tiled=True),
        lax.psum_scatter(grad_wo, "rows", scatter_dimension=0, tiled=True),
        lax.psum_scatter(grad_wh, "rows", scatter_dimension=0, tiled=True),
    )
    finished = (
        lax.psum_scatter(
            partial_sums[0].astype(jnp.bfloat16), "batch", scatter_dimension=1, tiled=True
        ).astype(jnp.float32),
        lax.psum_scatter(
            partial_sums[1].astype(jnp.bfloat16), "batch", scatter_dimension=1, tiled=True
        ).astype(jnp.float32),
        lax.psum_scatter(
            partial_sums[2].astype(jnp.bfloat16), "batch", scatter_dimension=1, tiled=True
        ).astype(jnp.float32),
        lax.psum_scatter(
            partial_sums[3].astype(jnp.bfloat16), "batch", scatter_dimension=1, tiled=True
        ).astype(jnp.float32),
        lax.psum_scatter(
            partial_sums[4].astype(jnp.bfloat16), "batch", scatter_dimension=1, tiled=True
        ).astype(jnp.float32),
        lax.psum_scatter(
            partial_sums[5].astype(jnp.bfloat16), "batch", scatter_dimension=1, tiled=True
        ).astype(jnp.float32),
        lax.psum_scatter(
            partial_sums[6].astype(jnp.bfloat16), "batch", scatter_dimension=1, tiled=True
        ).astype(jnp.float32),
        lax.psum_scatter(
            partial_sums[7].astype(jnp.bfloat16), "batch", scatter_dimension=1, tiled=True
        ).astype(jnp.float32),
    )
    return (
        likely,
        grad_input,
        finished[0],
        finished[1],
        finished[2],
        finished[3],
        finished[4],
        finished[5],
        finished[6],
        finished[7],
        gain_a_sum,
        shift_a_sum,
        gain_b_sum,
        shift_b_sum,
        head_sums[1],
        head_sums[0],
        head_sums[2],
        head_sums[3],
        head_sums[4],
    )


def on_device(*args):
    fits = all(a.shape[0] % 64 == 0 for a in args[1:9]) and lax.axis_size("rows") % 2 == 0
    return (fused_device if fits else plain_device)(*args)


def solution(mesh):
    return jax.shard_map(
        on_device,
        mesh=mesh,
        in_specs=(
            P("batch", "rows", None, None),
            P("rows", None),
            P("rows", None),
            P("rows", None),
            P("rows", None),
            P("rows", None),
            P("rows", None),
            P("rows", None),
            P("rows", None),
            P(),
            P(),
            P(),
            P(),
            P(),
            P(),
            P(),
            P(),
            P(),
            P(("batch", "rows"), None),
            P(("batch", "rows"), None),
            P(("batch", "rows"), None),
            P(("batch", "rows")),
            P(("batch", "rows"), None),
            P(("batch", "rows"), None),
            P(("batch", "rows")),
            P(("batch", "rows")),
            P(("batch", "rows"), None),
        ),
        out_specs=(
            P(("batch", "rows"), None),
            P("batch", "rows", None, None),
            P("rows", "batch"),
            P("rows", "batch"),
            P("rows", "batch"),
            P("rows", "batch"),
            P("rows", "batch"),
            P("rows", "batch"),
            P("rows", "batch"),
            P("rows", "batch"),
            P(),
            P(),
            P(),
            P(),
            P(),
            P(),
            P(),
            P(),
            P(),
        ),
        check_vma=False,
    )
```

```python
import jax
import jax.numpy as jnp
from jax import lax
from jax.experimental import pallas as pl
from jax.experimental.pallas import tpu as pltpu
from jax.sharding import PartitionSpec as P


def padded(cells, sides, width):
    for axis, dim in sides:
        count = lax.axis_size(axis)
        ends = count - 1
        head = lax.slice_in_dim(cells, 0, width, axis=dim)
        tail = lax.slice_in_dim(cells, cells.shape[dim] - width, cells.shape[dim], axis=dim)
        cells = jnp.concatenate(
            [
                lax.ppermute(tail, axis, [(i, (i + 1) % count) for i in range(ends)]),
                cells,
                lax.ppermute(head, axis, [((i + 1) % count, i) for i in range(ends)]),
            ],
            axis=dim,
        )
    return cells


def split_up(value, dim, peers):
    shape = value.shape
    parts = value.reshape(*shape[:dim], peers, shape[dim] // peers, *shape[dim + 1 :])
    return jnp.moveaxis(parts, dim, 0)


def sum_at_owner(value, axis, dim):
    peers = lax.axis_size(axis)
    parts = lax.all_to_all(split_up(value, dim, peers), axis, 0, 0, tiled=True)
    return jnp.sum(parts.astype(jnp.float32), axis=0)


def side_by_side(arrays, axis, dim, along):
    ends, at = ([], 0)
    for a in arrays[:-1]:
        at += a.shape[along]
        ends.append(at)
    both = jnp.concatenate(arrays, axis=along)
    return tuple(jnp.split(sum_at_owner(both, axis, dim), ends, axis=along))


def tdot(left, right):
    return lax.dot_general(
        left, right, (((0,), (0,)), ((), ())), preferred_element_type=jnp.float32
    )


def ndot(left, right):
    return lax.dot_general(
        left, right, (((1,), (1,)), ((), ())), preferred_element_type=jnp.float32
    )


def silu_slope(value):
    sig = jax.nn.sigmoid(value)
    return sig * (1.0 + value * (1.0 - sig))


def norm_back(grad, normed, inverse, gain, shift_sum, gain_total_grad, total_count):
    return (
        gain * inverse * (grad - shift_sum / total_count - normed * gain_total_grad / total_count)
    )


MESH = pl.DeviceIdType.MESH
LOW = jnp.bfloat16
F32 = jnp.float32


class Wires:
    def __init__(self, send, recv):
        self.send, self.recv, self.at, self.open = send, recv, 0, []

    def plan(self, source, target, peer):
        copy = pltpu.make_async_remote_copy(
            src_ref=source,
            dst_ref=target,
            send_sem=self.send.at[self.at],
            recv_sem=self.recv.at[self.at],
            device_id=peer,
            device_id_type=MESH,
        )
        self.at += 1
        self.open.append(copy)
        return copy

    def push(self, source, target, peer):
        return start(self.plan(source, target, peer))

    def settle(self, copies):
        for copy in copies:
            copy.wait_send()
        done = {id(copy) for copy in copies}
        self.open = [copy for copy in self.open if id(copy) not in done]

    def close(self):
        for copy in self.open:
            copy.wait_send()


def start(copy):
    copy.start()
    return copy


def greet(peers):
    barrier = pltpu.get_barrier_semaphore()
    for peer in peers:
        pl.semaphore_signal(barrier, inc=1, device_id=peer, device_id_type=MESH)
    pl.semaphore_wait(barrier, len(peers))


class Place:
    def __init__(self):
        self.groups, self.ranks = lax.axis_size("batch"), lax.axis_size("rows")
        self.g, self.s = lax.axis_index("batch"), lax.axis_index("rows")
        self.chips = self.ranks // 2
        self.z, self.core = self.s // 2, lax.rem(self.s, 2)
        self.other = 1 - self.core
        self.row_peers = [(self.g, lax.rem(self.s + k, self.ranks)) for k in range(1, self.ranks)]
        self.batch_peers = [
            (lax.rem(self.g + k, self.groups), self.s) for k in range(1, self.groups)
        ]
        self.line = [lax.rem(self.z + k, self.chips) for k in range(self.chips)]
        self.line_peers = [(self.g, z * 2 + self.core) for z in self.line[1:]]
        self.twin = (self.g, self.z * 2 + self.other)
        low, high = lax.rem(self.g, 2), self.g // 2
        beside, above = high * 2 + 1 - low, (1 - high) * 2 + low
        self.near = beside + self.core * (above - beside)
        self.far, self.across = beside + above - self.near, 3 - self.g


def rows_of(ref, index, size):
    return ref.at[pl.ds(pl.multiple_of(index * size, size), size)]


class Total:
    def __init__(self, net, place, held, from_rows, second, from_batch):
        self.held, self.from_rows, self.second, self.from_batch = (
            held,
            from_rows,
            second,
            from_batch,
        )
        self.rows = [
            net.plan(held, from_rows.at[k], peer) for k, peer in enumerate(place.row_peers)
        ]
        self.batch = [
            net.plan(second, from_batch.at[k], peer) for k, peer in enumerate(place.batch_peers)
        ]

    def start(self):
        for copy in self.rows:
            copy.start()

    def finish(self, behind=None):
        for copy in self.rows:
            copy.wait_recv()
        total = self.held[...]
        for k in range(len(self.rows)):
            total = total + self.from_rows[k]
        self.second[...] = total
        for copy in self.batch:
            copy.start()
        if behind is not None:
            behind()
        for copy in self.batch:
            copy.wait_recv()
        for k in range(len(self.batch)):
            total = total + self.from_batch[k]
        return total


def spread(ref, values):
    quarter = values[0].shape[1] // 4
    for n, value in enumerate(values):
        for k in range(4):
            ref[4 * n + k : 4 * n + k + 1, 0:quarter] = value[:, k * quarter : (k + 1) * quarter]


def gathered(block, n, quarter, at=0):
    return jnp.concatenate(
        [block[4 * n + k : 4 * n + k + 1, at : at + quarter] for k in range(4)], axis=1
    )


class Corner:
    def __init__(self, ref, height, width):
        self.ref, self.height, self.width = ref, height, width

    def __getitem__(self, z):
        beside = self.ref.shape[1] // self.width
        down, along = z // beside * self.height, z % beside * self.width
        return self.ref.at[down : down + self.height, along : along + self.width]


class Scatter:
    def __init__(self, net, place, shard, part, from_twin, from_batch, partial, from_line, result):
        self.place, self.shard, self.part = place, shard, part
        self.from_twin, self.from_batch, self.partial = from_twin, from_batch, partial
        self.from_line, self.result = from_line, result
        self.first, self.second, self.last = [], [], []
        for z in range(place.chips):
            self.first.append(net.plan(shard(2 * z + place.other), from_twin[z], place.twin))
            mine = shard(2 * z + place.core)
            self.second.append(
                [
                    net.plan(part(mine, g), from_batch.at[k, z], (near, place.s))
                    for k, (g, near) in enumerate(
                        (
                            (place.near, place.near),
                            (place.across, place.near),
                            (place.far, place.far),
                        )
                    )
                ]
            )
        self.third = [
            net.plan(partial.at[k + 1], from_line.at[k], peer)
            for k, peer in enumerate(place.line_peers)
        ]

    def pair(self):
        for copy in self.first:
            copy.start()

    def batch(self, *turns):
        place = self.place
        for z in turns or range(place.chips):
            self.first[z].wait_recv()
            mine = self.shard(2 * z + place.core)
            rows = mine.shape[0]
            step = next(n for n in (64, 32, 16) if rows % n == 0)

            @pl.loop(0, rows // step)
            def _(n):
                at = pl.ds(pl.multiple_of(n * step, step), step)
                mine[at, :] = (
                    mine[at, :].astype(F32) + self.from_twin[z][at, :].astype(F32)
                ).astype(LOW)

            for copy in self.second[z][:2]:
                copy.start()

    def forward(self, *turns):
        place = self.place
        for z in turns or range(place.chips):
            for copy in self.second[z][:2]:
                copy.wait_recv()
            theirs = self.part(self.shard(2 * z + place.core), place.far)
            theirs[...] = (
                theirs[...].astype(F32) + self.from_batch[1, z].astype(F32)
            ).astype(LOW)
            self.second[z][2].start()

    def line(self):
        place = self.place
        for copies in self.second:
            copies[2].wait_recv()
        for k, z in enumerate(place.line):
            mine = self.part(self.shard(2 * z + place.core), place.g)
            total = mine[...].astype(F32)
            for n in (0, 2):
                total = total + self.from_batch[n, z].astype(F32)
            self.partial[k] = total.astype(LOW)
            if k:
                self.third[k - 1].start()

    def finish(self):
        for copy in self.third:
            copy.wait_recv()
        total = self.partial[0].astype(F32)
        for k in range(self.place.chips - 1):
            total = total + self.from_line[k].astype(F32)
        self.result[...] = total


def slope_of(value):
    sig = 0.5 * jnp.tanh(0.5 * value) + 0.5
    return sig * (1.0 + value * (1.0 - sig))


def column_of(shape, columns):
    return lax.rem(lax.broadcasted_iota(jnp.int32, shape, 0), columns)


def from_left(value, columns):
    return jnp.where(
        column_of(value.shape, columns) == 0, 0.0, pltpu.roll(value, 1, 0)
    )


def from_right(value, columns):
    return jnp.where(
        column_of(value.shape, columns) == columns - 1,
        0.0,
        pltpu.roll(value, value.shape[0] - 1, 0),
    )


def folded(value):
    rows, width = value.shape
    return jnp.sum(value.reshape(rows // 8, 8, width), axis=0)


class Gather:
    def __init__(self, net, place, shard, whole, local, dim=0):
        self.net, self.place, self.shard, self.whole = net, place, shard, whole
        self.dim, self.rows = dim, whole.shape[dim] // place.ranks
        self.own = pltpu.make_async_copy(shard, self.block(place.s), local)
        part = self.rows // place.groups
        source = self.cut(shard, place.g * part, part)
        self.first = [
            net.plan(source, self.quarter(place.s, place.g), peer) for peer in place.line_peers
        ]
        self.second, self.third = [], [net.plan(shard, self.block(place.s), place.twin)]
        for k in range(1, place.chips):
            s = lax.rem(place.z + place.chips - k, place.chips) * 2 + place.core
            view, passed = self.quarter(s, place.g), self.quarter(s, place.near)
            self.second.append(
                [
                    net.plan(view, view, (place.near, place.s)),
                    net.plan(view, view, (place.far, place.s)),
                    net.plan(passed, passed, (place.far, place.s)),
                ]
            )
            self.third.append(net.plan(self.block(s), self.block(s), place.twin))

    def cut(self, ref, start, size):
        at = pl.ds(pl.multiple_of(start, size), size)
        return ref.at[at] if self.dim == 0 else ref.at[:, at]

    def block(self, s):
        return self.cut(self.whole, s * self.rows, self.rows)

    def quarter(self, s, g):
        part = self.rows // self.place.groups
        return self.cut(self.whole, s * self.rows + g * part, part)

    def line(self):
        for copy in self.first:
            copy.start()
        self.own.start()
        self.third[0].start()

    def batch(self, *turns):
        for k in turns or range(len(self.first)):
            self.first[k].wait_recv()
            for copy in self.second[k][:2]:
                copy.start()

    def forward(self, *turns):
        for k in turns or range(len(self.first)):
            self.second[k][0].wait_recv()
            self.second[k][2].start()

    def pair(self):
        for k, copies in enumerate(self.second):
            for copy in copies[1:]:
                copy.wait_recv()
            self.third[k + 1].start()

    def sent(self):
        return self.first + self.third + [c for copies in self.second for c in copies]

    def ready(self):
        self.own.wait()
        for copy in self.third:
            copy.wait_recv()


def moments(total, width, total_count):
    centre = gathered(total, 0, width // 4) / total_count
    square = gathered(total, 1, width // 4) / total_count
    return centre, lax.rsqrt(square - centre * centre + 1e-05)


def sigma(value):
    return 0.5 * jnp.tanh(0.5 * value) + 0.5


def step_kernel(geometry, r):
    cells, d_in, d_mid, columns, total_count, capacity, entries, samples, clips = geometry
    place = Place()
    net = Wires(r.send, r.recv)
    ranks, groups = place.ranks, place.groups
    half, size = d_in // 2, 2 * capacity
    depth = d_in // ranks
    entry = r.bank16.shape[0]
    local = r.local
    load_x = pltpu.make_async_copy(r.features, r.x, local.at[0])
    load_x.start()
    kv_weights = [rows_of(r.low_b, n, depth) for n in range(2)]
    load_kv = [
        pltpu.make_async_copy(source, target, local.at[9 + n])
        for n, (source, target) in enumerate(zip((r.w_key, r.w_value), kv_weights))
    ]
    for copy in load_kv:
        copy.start()
    greet(place.row_peers + place.batch_peers)
    a, b, c, q, o, h = (
        Gather(net, place, shard, whole, local.at[n + 1], n // 5)
        for n, (shard, whole) in enumerate(
            (
                (r.w_reduce, r.w_a),
                (r.w_spatial, r.w_b),
                (r.w_expand, r.w_c),
                (r.w_query, r.w_q),
                (r.w_out, r.w_o),
                (r.w_head, r.w_h),
            )
        )
    )
    sums = [
        Total(net, place, *refs)
        for refs in (
            (r.own1, r.rows1, r.mid1, r.batch1),
            (r.own2, r.rows2, r.mid2, r.batch2),
            (r.own3, r.rows3, r.mid3, r.batch3),
            (r.own4, r.rows4, r.mid4, r.batch4),
            (r.own5, r.rows5, r.mid5, r.batch5),
            (r.own6, r.rows6, r.mid6, r.batch6),
        )
    ]
    a.line()
    b.line()

    def at_block(s):
        return pl.ds(pl.multiple_of(s * entry, entry), entry)

    def at_depth(s):
        return pl.ds(pl.multiple_of(s * depth, depth), depth)

    r.bank16[...] = jnp.zeros_like(r.bank16)
    r.bank16[0:entries, :] = r.bank[...]
    for n in range(ranks):
        r.box16[n, 0:1, 0:capacity] = r.piece_box[n : n + 1, :]
    owner = lax.broadcasted_iota(jnp.int32, (ranks, 1), 0)
    count = jnp.zeros((ranks, 1), jnp.int32)
    for n in range(ranks):
        count = jnp.where(owner == n, r.send_count[n], count)
    for k in range(capacity):
        on = slice(k * samples, (k + 1) * samples)
        r.slot_cells[k] = r.sample_pos[:, on] + r.piece_clip[:, k : k + 1] * (cells // clips)
        r.slot_weights[k] = jnp.where(k < count, r.sample_weight[:, on], 0.0)
    asked = [
        net.push(r.bank16.at[:, at_depth(peer[1])], rows_of(r.bank_cols, place.s, entry), peer)
        for peer in place.row_peers
    ]
    named = [
        net.push(r.box16.at[peer[1]], r.box_in.at[place.s], peer) for peer in place.row_peers
    ]
    r.bank_cols[at_block(place.s), :] = r.bank16[:, at_depth(place.s)]
    mine = pl.ds(pl.multiple_of(place.s * size, size), size)
    r.box_in[place.s] = r.box16[place.s]

    by_rank = (capacity * ranks, ranks * size)
    row, slot = (lax.broadcasted_iota(jnp.int32, by_rank, n) for n in range(2))
    goal = lax.rem(row, ranks) * size + row // ranks
    perms = [jnp.where(slot == goal + n * capacity, 1.0, 0.0).astype(LOW) for n in range(2)]

    @pl.loop(0, capacity)
    def _(k):
        cell = lax.broadcasted_iota(jnp.int32, (ranks, cells), 1)
        spots, weights = r.slot_cells[k], r.slot_weights[k]
        total = jnp.zeros((ranks, cells), F32)
        for j in range(samples):
            total = total + jnp.where(cell == spots[:, j : j + 1], weights[:, j : j + 1], 0.0)
        r.pieces[pl.ds(pl.multiple_of(k * ranks, ranks), ranks), 0:cells] = total

    for n in range(2):
        r.et[n] = tdot(r.pieces[0 : capacity * ranks, 0:cells].astype(LOW), perms[n]).astype(LOW)

    a.batch()
    a.forward()
    b.batch(0)
    a.pair()
    load_x.wait()
    a.ready()

    acc = r.acc
    acc[...] = jnp.zeros_like(acc)
    big = 256
    tiles = cells // big

    @pl.loop(0, tiles)
    def _(t):
        at = pl.ds(pl.multiple_of(t * big, big), big)
        value = jnp.dot(r.x[at, :], r.w_a[...], preferred_element_type=F32)
        r.middle[at, :] = value
        acc[0, :, 0:d_mid] += folded(value)
        acc[1, :, 0:d_mid] += folded(value * value)

    spread(r.own1, [jnp.sum(acc[n, :, 0:d_mid], axis=0, keepdims=True) for n in range(2)])
    b.batch(1)
    sums[0].start()
    c.line()

    def more_b():
        b.batch(2)
        b.forward(0, 1)

    total = sums[0].finish(more_b)
    centre, inverse = moments(total, d_mid, total_count)
    gain, bias = r.gain_a[...], r.bias_a[...]
    for n, value in enumerate((gain, bias, gain * inverse)):
        r.norm_a[n : n + 1, :] = value

    first, last = place.s == 0, place.s == ranks - 1
    low_a, low_up, low_down = r.low_a, r.low_up, r.low_down

    def halo(t, way):
        at = pl.ds(pl.multiple_of(t * big, big), big)
        return pltpu.make_async_remote_copy(
            src_ref=low_a.at[at],
            dst_ref=(low_up if way == 0 else low_down).at[at],
            send_sem=r.halo_send.at[way, t],
            recv_sem=r.halo_recv.at[way, t],
            device_id=(place.g, place.s + 1 if way == 0 else place.s - 1),
            device_id_type=MESH,
        )

    @pl.when(first)
    def _():
        low_up[...] = jnp.zeros_like(low_up)

    @pl.when(last)
    def _():
        low_down[...] = jnp.zeros_like(low_down)

    @pl.loop(0, tiles)
    def _(t):
        at = pl.ds(pl.multiple_of(t * big, big), big)
        hat = (r.middle[at, :] - centre) * inverse
        r.hat_a[at, :] = hat.astype(LOW)
        act = gain * hat + bias
        low_a[at, :] = (act * sigma(act)).astype(LOW)

        @pl.when(jnp.logical_not(last))
        def _():
            halo(t, 0).start()

        @pl.when(jnp.logical_not(first))
        def _():
            halo(t, 1).start()

    keep_hat_a = pltpu.make_async_copy(r.hat_a, r.far_hat_a, local.at[8])
    keep_hat_a.start()
    c.batch()
    b.forward(2)
    for copy in asked:
        copy.wait_recv()
    for copy in load_kv:
        copy.wait()
    for n, weight in enumerate(kv_weights):
        r.kv_part[n] = jnp.dot(
            r.bank_cols[...], weight[...], preferred_element_type=F32
        ).astype(LOW)

    @pl.loop(0, tiles)
    def _(t):
        at = pl.ds(pl.multiple_of(t * big, big), big)
        r.low_t[1, :, at] = jnp.transpose(low_a[at, :].astype(F32)).astype(LOW)

    b.pair()
    c.forward()
    b.ready()
    acc[...] = jnp.zeros_like(acc)

    @pl.loop(0, tiles)
    def _(t):
        at = pl.ds(pl.multiple_of(t * big, big), big)

        @pl.when(jnp.logical_not(first))
        def _():
            halo(t, 0).wait_recv()

        @pl.when(jnp.logical_not(last))
        def _():
            halo(t, 1).wait_recv()

        parts = []
        for j in range(3):
            taps = [r.w_b[(3 * i + j) * d_mid : (3 * i + j + 1) * d_mid, :] for i in range(3)]
            parts.append(
                jnp.dot(low_up[at, :], taps[0], preferred_element_type=F32)
                + jnp.dot(low_a[at, :], taps[1], preferred_element_type=F32)
                + jnp.dot(low_down[at, :], taps[2], preferred_element_type=F32)
            )
        value = from_left(parts[0], columns) + parts[1] + from_right(parts[2], columns)
        r.middle[at, :] = value
        acc[0, :, 0:d_mid] += folded(value)
        acc[1, :, 0:d_mid] += folded(value * value)

    spread(r.own2, [jnp.sum(acc[n, :, 0:d_mid], axis=0, keepdims=True) for n in range(2)])
    sums[1].start()
    q.line()
    o.line()
    h.line()

    @pl.loop(0, tiles)
    def _(t):
        at = pl.ds(pl.multiple_of(t * big, big), big)
        r.low_t[0, :, at] = jnp.transpose(low_up[at, :].astype(F32)).astype(LOW)
        r.low_t[2, :, at] = jnp.transpose(low_down[at, :].astype(F32)).astype(LOW)

    total = sums[1].finish()
    centre, inverse = moments(total, d_mid, total_count)
    gain, bias = r.gain_b[...], r.bias_b[...]
    for n, value in enumerate((gain, bias, gain * inverse)):
        r.norm_b[n : n + 1, :] = value
    kv = [
        net.plan(r.kv_part.at[:, at_block(peer[1])], r.kv_in.at[k], peer)
        for k, peer in enumerate(place.row_peers)
    ]
    every = [
        net.plan(r.kv_own, r.kv_all.at[:, at_block(place.s)], peer) for peer in place.row_peers
    ]

    def third_norm(pre_c):
        c.pair()
        c.ready()
        acc[...] = jnp.zeros_like(acc)

        @pl.loop(0, tiles)
        def _(t):
            at = pl.ds(pl.multiple_of(t * big, big), big)
            hat = (r.middle[at, :] - centre) * inverse
            r.hat_b[at, :] = hat.astype(LOW)
            act = gain * hat + bias
            low = (act * sigma(act)).astype(LOW)
            r.low_b[at, :] = low
            for k in range(4):
                on = slice(k * (d_in // 4), (k + 1) * (d_in // 4))
                value = jnp.dot(low, r.w_c[:, on], preferred_element_type=F32)
                pre_c[at, on] = value
                acc[0, :, on] += folded(value)
                acc[1, :, on] += folded(value * value)

        spread(r.own3, [jnp.sum(acc[n], axis=0, keepdims=True) for n in range(2)])
        q.batch()
        sums[2].start()
        for copy in kv:
            copy.start()

        @pl.loop(0, tiles)
        def _(t):
            at = pl.ds(pl.multiple_of(t * big, big), big)
            r.low_bt[:, at] = jnp.transpose(r.low_b[at, :].astype(F32)).astype(LOW)


        def rest():
            o.batch()
            h.batch()
            q.forward()

        total = sums[2].finish(rest)
        centre_wide, inverse_wide = moments(total, d_in, total_count)
        r.scale_c[...] = r.gain_c[...] * inverse_wide
        r.centre_c[0:1, :] = centre_wide
        r.centre_c[1:2, :] = inverse_wide
        for copy in kv:
            copy.wait_recv()
        for n in range(2):
            total = r.kv_part[n, at_block(place.s), :].astype(F32)
            for k in range(ranks - 1):
                total = total + r.kv_in[k, n].astype(F32)
            r.kv_own[n] = total.astype(LOW)
            r.kv_all[n, at_block(place.s), :] = total.astype(LOW)
        for copy in every:
            copy.start()

        q.pair()
        o.forward()
        h.forward()
        r.pieces[...] = jnp.zeros_like(r.pieces)
        tile = 128

        @pl.loop(0, cells // tile)
        def _(t):
            at = pl.ds(pl.multiple_of(t * tile, tile), tile)
            for k in range(4):
                on = slice(k * (d_in // 4), (k + 1) * (d_in // 4))
                into = slice((k % 2) * (d_in // 4), (k % 2 + 1) * (d_in // 4))
                hat = (pre_c[at, on] - r.centre_c[0:1, on]) * r.centre_c[1:2, on]
                r.hat_c[at, on] = hat.astype(LOW)
                value = r.gain_c[:, on] * hat + r.bias_c[:, on] + r.x[at, on].astype(F32)
                sig = sigma(value)
                fmap = value * sig
                r.x[at, on] = (sig + fmap * (1.0 - sig)).astype(LOW)
                r.pieces[:, into] += tdot(r.et[k // 2, at, :], fmap.astype(LOW))


    pl.run_scoped(third_norm, pltpu.VMEM((cells, d_in), F32))
    r.blocks[...] = r.pieces[...].astype(LOW)
    pushed = [
        net.push(rows_of(r.blocks, peer[1], size), rows_of(r.arrived, place.s, size), peer)
        for peer in place.row_peers
    ]
    r.arrived[mine, :] = r.blocks[mine, :]
    o.pair()
    h.pair()
    for copy in named + every + pushed:
        copy.wait_recv()

    def block_rows(ref, count):
        return lambda s: rows_of(ref, s, ref.shape[0] // count)

    def by_columns(width):
        return lambda view, g: view.at[:, pl.ds(pl.multiple_of(g * width, width), width)]

    def by_rows(height):
        return lambda view, g: view.at[pl.ds(pl.multiple_of(g * height, height), height)]

    def scatter(key, shard, part, landing):
        return Scatter(
            net, place, shard, part, landing, *(getattr(r, n + key) for n in ("ba_", "pa_", "li_", "out_"))
        )

    per = cells // depth

    def shard_a(s):
        at = pl.ds(pl.multiple_of(lax.rem(s, per) * depth, depth), depth)
        return r.low_t.at[s // per, :, at]

    sc = {
        "q": scatter("q", block_rows(r.w_q, ranks), by_columns(d_mid // groups), Corner(r.tw_q, depth, d_mid)),
        "o": scatter("o", block_rows(r.w_o, ranks), by_columns(d_in // groups), r.tw_o.at),
        "h": scatter("h", lambda s: r.g_h.at[s], by_rows(r.g_h.shape[1] // groups), r.tw_h.at),
        "c": scatter("c", block_rows(r.w_c, ranks), by_columns(d_in // groups), r.tw_c.at),
        "a": scatter("a", shard_a, by_rows(d_mid // groups), Corner(r.tw_q, r.tw_q.shape[0] // 2, depth)),
    }
    returned = [
        net.plan(rows_of(r.blocks, peer[1], size), rows_of(r.back_in, place.s, size), peer)
        for peer in place.row_peers
    ]
    asked_back = [
        net.plan(r.kv_part.at[:, at_block(peer[1])], r.kv_in.at[k], peer)
        for k, peer in enumerate(place.row_peers)
    ]

    def own_boxes(pooled, joined, d_branch, d_pooled):
        boxes = r.cotangent.shape[1]
        number = jnp.concatenate([r.box_in[n, 0:1, :] for n in range(ranks)], axis=0)
        box = lax.broadcasted_iota(jnp.int32, (ranks, boxes), 1)
        hits = jnp.concatenate(
            [jnp.where(number[:, k : k + 1] == box, 1.0, 0.0) for k in range(capacity)], axis=0
        ).astype(LOW)
        picks = [tdot(perm, hits).astype(LOW) for perm in perms]
        across = lax.broadcasted_iota(jnp.int32, (boxes, boxes), 0) == lax.broadcasted_iota(
            jnp.int32, (boxes, boxes), 1
        )

        def upright(value):
            wide = jnp.broadcast_to(value.astype(F32), (boxes, boxes))
            return jnp.sum(jnp.where(across, wide, 0.0), axis=1, keepdims=True)

        bank_row = lax.broadcasted_iota(jnp.int32, (boxes, ranks * entry), 1)
        inner = lax.rem(bank_row, entry)
        spot = (bank_row // entry * entries + inner).astype(F32)
        start, length = upright(r.win_start[...]), upright(r.win_len[...])
        window = (inner < entries) & (spot >= start) & (spot < start + length)
        for k in range(2):
            pooled[:, k * half : (k + 1) * half] = tdot(picks[k], r.arrived[...])
        joined[:, 0:d_in] = pooled[...].astype(LOW)
        pooled_low = joined.at[:, 0:d_in]
        keys, vals = r.kv_all.at[0], r.kv_all.at[1]
        scale = d_mid ** (-0.5)
        q.ready()
        queries = jnp.dot(pooled_low[...], r.w_q[...], preferred_element_type=F32).astype(LOW)
        scores = jnp.where(window, ndot(queries, keys[...]) * scale, -1e30)
        raised = jnp.exp(scores - jnp.max(scores, axis=1, keepdims=True))
        attend = raised / jnp.sum(raised, axis=1, keepdims=True)
        attend_low = attend.astype(LOW)
        mixture = jnp.dot(attend_low, vals[...], preferred_element_type=F32)
        centred = mixture - jnp.mean(mixture, axis=1, keepdims=True)
        inverse_z = lax.rsqrt(jnp.mean(centred * centred, axis=1, keepdims=True) + 1e-05)
        hat_z = centred * inverse_z
        pre_ln = r.ln_gain[...] * hat_z + r.ln_bias[...]
        sig_z = sigma(pre_ln)
        low_r = (pre_ln * sig_z).astype(LOW)
        slope_z = sig_z * (1.0 + pre_ln * (1.0 - sig_z))
        o.ready()
        for k in range(4):
            on = slice(k * (d_in // 4), (k + 1) * (d_in // 4))
            into = slice(d_in + k * (d_in // 4), d_in + (k + 1) * (d_in // 4))
            joined[:, into] = (
                pooled[:, on] + jnp.dot(low_r, r.w_o[:, on], preferred_element_type=F32)
            ).astype(LOW)
        h.ready()
        logits = (
            ndot(joined[...], r.w_h[...]) + r.head_bias[...]
        )
        likely = jax.nn.sigmoid(logits)
        r.out_probs[...] = likely
        d_logit = (jnp.transpose(r.cotangent[...]) * (likely * (1.0 - likely))).astype(LOW)
        for k in range(4):
            on = slice(k * (d_in // 4), (k + 1) * (d_in // 4))
            below = slice(d_in + k * (d_in // 4), d_in + (k + 1) * (d_in // 4))
            upper = jnp.dot(d_logit, r.w_h[:, below], preferred_element_type=F32)
            d_branch[:, on] = upper.astype(LOW)
            pooled[:, on] = (
                jnp.dot(d_logit, r.w_h[:, on], preferred_element_type=F32) + upper
            )
        d_ln = ndot(d_branch[...], r.w_o[...]) * slope_z
        d_hat = d_ln * r.ln_gain[...]
        d_mixture = (
            inverse_z
            * (
                d_hat
                - jnp.mean(d_hat, axis=1, keepdims=True)
                - hat_z * jnp.mean(d_hat * hat_z, axis=1, keepdims=True)
            )
        ).astype(LOW)
        d_attend = ndot(d_mixture, vals[...])
        d_scores = (attend * (d_attend - jnp.sum(d_attend * attend, axis=1, keepdims=True))).astype(LOW)
        d_queries = (jnp.dot(d_scores, keys[...], preferred_element_type=F32) * scale).astype(LOW)
        for k in range(4):
            on = slice(k * (d_in // 4), (k + 1) * (d_in // 4))
            d_pooled[:, on] = (pooled[:, on] + ndot(d_queries, r.w_q[on, :])).astype(LOW)
        net.settle(pushed)
        r.blocks[...] = (
            jnp.dot(picks[0], d_pooled[:, 0:half], preferred_element_type=F32)
            + jnp.dot(picks[1], d_pooled[:, half:d_in], preferred_element_type=F32)
        ).astype(LOW)
        for copy in returned:
            copy.start()
        r.back_in[mine, :] = r.blocks[mine, :]

        net.settle(q.sent() + o.sent() + kv + every)
        r.kv_part[0] = (tdot(d_scores, queries) * scale).astype(LOW)
        r.kv_part[1] = tdot(attend_low, d_mixture).astype(LOW)
        for k in range(4):
            on = slice(k * (d_in // 4), (k + 1) * (d_in // 4))
            r.w_q[on, :] = tdot(joined[:, on], d_queries).astype(LOW)
            r.w_o[:, on] = tdot(low_r, d_branch[:, on]).astype(LOW)
        width = 2 * depth
        classes = d_logit.shape[1]
        share = classes // groups
        held, kind = (
            lax.broadcasted_iota(jnp.int32, (classes, r.g_h.shape[1]), n) for n in range(2)
        )
        padded_class = held // share * (r.g_h.shape[1] // groups) + lax.rem(held, share)
        spaced = jnp.where(kind == padded_class, 1.0, 0.0).astype(LOW)
        d_spaced = jnp.dot(d_logit, spaced, preferred_element_type=F32).astype(LOW)
        for s in range(ranks):
            r.g_h[s] = tdot(d_spaced, joined[:, s * width : (s + 1) * width]).astype(LOW)
        quarter = d_mid // 4
        r.own4[...] = jnp.zeros_like(r.own4)
        for n, value in enumerate(
            (jnp.sum(d_ln * hat_z, axis=0, keepdims=True), jnp.sum(d_ln, axis=0, keepdims=True))
        ):
            for k in range(4):
                r.own4[4 * n + k : 4 * n + k + 1, d_in // 4 : d_in // 4 + quarter] = value[
                    :, k * quarter : (k + 1) * quarter
                ]
        r.own4[0:1, d_in // 4 + quarter : d_in // 4 + quarter + classes] = jnp.sum(
            d_logit.astype(F32), axis=0, keepdims=True
        )
        sc["h"].pair()
        sc["q"].pair()
        sc["o"].pair()
        for copy in asked_back:
            copy.start()
        sc["h"].batch()
        sc["q"].batch()


    boxes = r.cotangent.shape[1]
    pl.run_scoped(
        own_boxes,
        pltpu.VMEM((boxes, d_in), F32),
        pltpu.VMEM((boxes, 2 * d_in), LOW),
        pltpu.VMEM((boxes, d_in), LOW),
        pltpu.VMEM((boxes, d_in), LOW),
    )
    keep_hat_a.wait()
    for copy in returned:
        copy.wait_recv()

    @pl.loop(0, tiles)
    def _(t):
        @pl.when(jnp.logical_not(last))
        def _():
            halo(t, 0).wait_send()

        @pl.when(jnp.logical_not(first))
        def _():
            halo(t, 1).wait_send()

    chips = place.chips
    dkv, dkv_in, dkv_own, dkv_all = r.kv_part, r.kv_in, r.kv_own, r.kv_all

    def backward(d_pre, g_b):
        sc["b"] = scatter("b", block_rows(g_b, ranks), by_columns(d_mid // groups), r.tw_b.at)
        hat_c, slope, d_c, back = r.hat_c, r.x, r.x, r.back_in
        acc = r.acc
        acc[...] = jnp.zeros_like(acc)
        tile = 128

        @pl.loop(0, cells // tile)
        def _(t):
            at = pl.ds(pl.multiple_of(t * tile, tile), tile)
            for h in range(2):
                on = slice(h * half, (h + 1) * half)
                grad = jnp.dot(
                    r.et[h, at, :], back[...], preferred_element_type=F32
                ) * slope[at, on].astype(F32)
                d_pre[at, on] = grad.astype(LOW)
                acc[0, :, on] += folded(grad)
                acc[1, :, on] += folded(grad * hat_c[at, on].astype(F32))

        own4 = r.own4
        spread(own4, [jnp.sum(acc[n], axis=0, keepdims=True) for n in range(2)])
        sums[3].start()
        sc["h"].forward()
        sc["q"].forward()
        for copy in asked_back:
            copy.wait_recv()
        own = pl.ds(pl.multiple_of(place.s * entry, entry), entry)
        for n in range(2):
            total = dkv[n, own, :].astype(F32)
            for k in range(ranks - 1):
                total = total + dkv_in[k, n].astype(F32)
            dkv_own[n] = total.astype(LOW)
            dkv_all[n, own, :] = total.astype(LOW)
        shared = [
            net.push(dkv_own, dkv_all.at[:, own], peer)
            for peer in place.row_peers
        ]

        total = sums[3].finish(sc["o"].batch)
        r.out_head[...] = total
        shift_c = gathered(total, 0, d_in // 4) / total_count
        gain_c = gathered(total, 1, d_in // 4) / total_count
        scale_c = r.scale_c[...]

        w_c, hat_b, d_act = r.w_c, r.hat_b, r.middle
        acc[...] = jnp.zeros_like(acc)
        norm_b, norm_a = r.norm_b, r.norm_a

        @pl.loop(0, cells // tile)
        def _(t):
            at = pl.ds(pl.multiple_of(t * tile, tile), tile)
            grad = scale_c * (
                d_pre[at, :].astype(F32) - shift_c - hat_c[at, :].astype(F32) * gain_c
            )
            low = grad.astype(LOW)
            d_c[at, :] = low
            hat = hat_b[at, :].astype(F32)
            back_b = ndot(low, w_c[...]) * slope_of(norm_b[0:1, :] * hat + norm_b[1:2, :])
            d_act[at, :] = back_b
            acc[0, :, 0:d_mid] += folded(back_b)
            acc[1, :, 0:d_mid] += folded(back_b * hat)

        reload = pltpu.make_async_copy(r.features, r.hat_c, local.at[20])
        reload.start()
        own5 = r.own5
        spread(own5, [jnp.sum(acc[n, :, 0:d_mid], axis=0, keepdims=True) for n in range(2)])
        sums[4].start()
        net.settle(c.sent())
        wide = 256

        @pl.loop(0, d_in // wide)
        def _(t):
            at = pl.ds(pl.multiple_of(t * wide, wide), wide)
            w_c[:, at] = jnp.dot(
                r.low_bt[...], d_c[:, at], preferred_element_type=F32
            ).astype(LOW)

        sc["c"].pair()
        sc["h"].line()
        sc["q"].line()
        for copy in shared:
            copy.wait_recv()
        kv_out, kv_in = r.kv_out, r.kv_back
        for n in range(2):
            kv_out[n] = tdot(r.bank_cols[...], dkv_all[n]).astype(LOW)
        share = d_mid // groups
        crossing = [
            net.push(
                kv_out.at[:, :, pl.ds(pl.multiple_of(peer[0] * share, share), share)], kv_in.at[k], peer
            )
            for k, peer in enumerate(place.batch_peers)
        ]


        def middle():
            sc["o"].forward()
            sc["c"].batch()

        total = sums[4].finish(middle)
        r.out_b_sums[...] = total
        shift_b = gathered(total, 0, d_mid // 4) / total_count
        gain_b = gathered(total, 1, d_mid // 4) / total_count

        d_b, d_up, d_down = (r.low_up, r.low_a, r.low_down), r.low_b, r.hat_a

        def halo_back(t, way):
            at = pl.ds(pl.multiple_of(t * big, big), big)
            return pltpu.make_async_remote_copy(
                src_ref=d_b[1].at[at],
                dst_ref=(d_up if way == 0 else d_down).at[at],
                send_sem=r.back_send.at[way, t],
                recv_sem=r.back_recv.at[way, t],
                device_id=(place.g, place.s + 1 if way == 0 else place.s - 1),
                device_id_type=MESH,
            )

        @pl.when(first)
        def _():
            d_up[...] = jnp.zeros_like(d_up)

        @pl.when(last)
        def _():
            d_down[...] = jnp.zeros_like(d_down)

        @pl.loop(0, tiles)
        def _(t):
            at = pl.ds(pl.multiple_of(t * big, big), big)
            grad = norm_b[2:3, :] * (
                d_act[at, :] - shift_b - hat_b[at, :].astype(F32) * gain_b
            )
            d_b[1][at, :] = grad.astype(LOW)

            @pl.when(jnp.logical_not(last))
            def _():
                halo_back(t, 0).start()

            @pl.when(jnp.logical_not(first))
            def _():
                halo_back(t, 1).start()

            d_b[0][at, :] = from_right(grad, columns).astype(LOW)
            d_b[2][at, :] = from_left(grad, columns).astype(LOW)

        @pl.loop(0, 3)
        def _(i):
            for j in range(3):
                at = pl.ds(pl.multiple_of((3 * i + j) * d_mid, d_mid), d_mid)
                g_b[at, :] = jnp.dot(
                    r.low_t[i], d_b[j][...], preferred_element_type=F32
                ).astype(LOW)

        more = pltpu.make_async_copy(r.far_hat_a, hat_b, local.at[18])
        more.start()
        sc["b"].pair()
        sc["c"].forward()
        sc["o"].line()
        sc["b"].batch()

        more.wait()
        w_b, hat_a = r.w_b, hat_b
        acc[...] = jnp.zeros_like(acc)

        @pl.loop(0, tiles)
        def _(t):
            at = pl.ds(pl.multiple_of(t * big, big), big)

            @pl.when(jnp.logical_not(first))
            def _():
                halo_back(t, 0).wait_recv()

            @pl.when(jnp.logical_not(last))
            def _():
                halo_back(t, 1).wait_recv()

            parts = []
            for j in range(3):
                taps = [w_b[(3 * i + j) * d_mid : (3 * i + j + 1) * d_mid, :] for i in range(3)]
                parts.append(
                    ndot(d_down[at, :], taps[0]) + ndot(d_b[1][at, :], taps[1]) + ndot(d_up[at, :], taps[2])
                )
            grad = from_right(parts[0], columns) + parts[1] + from_left(parts[2], columns)
            hat = hat_a[at, :].astype(F32)
            grad = grad * slope_of(norm_a[0:1, :] * hat + norm_a[1:2, :])
            d_act[at, :] = grad
            acc[0, :, 0:d_mid] += folded(grad)
            acc[1, :, 0:d_mid] += folded(grad * hat)

        own6 = r.own6
        spread(own6, [jnp.sum(acc[n, :, 0:d_mid], axis=0, keepdims=True) for n in range(2)])
        sums[5].start()
        sc["c"].line()

        def late():
            sc["b"].forward()

        total = sums[5].finish(late)
        r.out_a_sums[...] = total
        shift_a = gathered(total, 0, d_mid // 4) / total_count
        gain_a = gathered(total, 1, d_mid // 4) / total_count
        d_a, d_at = d_b[0], r.low_bt

        @pl.loop(0, tiles)
        def _(t):
            at = pl.ds(pl.multiple_of(t * big, big), big)
            grad = norm_a[2:3, :] * (
                d_act[at, :] - shift_a - hat_a[at, :].astype(F32) * gain_a
            )
            d_a[at, :] = grad.astype(LOW)
            d_at[:, at] = jnp.transpose(grad).astype(LOW)

        reload.wait()
        x = r.hat_c

        @pl.loop(0, ranks)
        def _(s):
            shard_a(s)[...] = jnp.dot(
                d_at[...],
                x[:, pl.ds(pl.multiple_of(s * depth, depth), depth)],
                preferred_element_type=F32,
            ).astype(LOW)

        sc["a"].pair()
        sc["b"].line()
        sc["a"].batch()
        out_x = r.out_x

        def leave(t):
            at = pl.ds(pl.multiple_of(t * tile, tile), tile)
            return pltpu.make_async_copy(d_pre.at[at], out_x.at[at], local.at[21 + t])

        @pl.loop(0, cells // tile)
        def _(t):
            at = pl.ds(pl.multiple_of(t * tile, tile), tile)
            d_pre[at, :] = (
                ndot(d_a[at, :], r.w_a[...]) + d_pre[at, :].astype(F32)
            ).astype(LOW)
            leave(t).start()

        sc["a"].forward()
        for key in "qohcb":
            sc[key].finish()
        sc["a"].line()
        for copy in crossing:
            copy.wait_recv()
        for n, key in enumerate((r.out_k, r.out_v)):
            total = kv_out[n, :, pl.ds(pl.multiple_of(place.g * share, share), share)].astype(F32)
            for k in range(groups - 1):
                total = total + kv_in[k, n].astype(F32)
            key[...] = total
        sc["a"].finish()

        @pl.loop(0, cells // tile)
        def _(t):
            leave(t).wait()

        @pl.loop(0, tiles)
        def _(t):
            @pl.when(jnp.logical_not(last))
            def _():
                halo_back(t, 0).wait_send()

            @pl.when(jnp.logical_not(first))
            def _():
                halo_back(t, 1).wait_send()

        net.close()

    pl.run_scoped(
        backward,
        pltpu.VMEM((cells, d_in), LOW),
        pltpu.VMEM(r.w_b.shape, LOW),
    )


class Refs:
    def __init__(self, names, refs, **more):
        self.__dict__.update(zip(names, refs), **more)


def run_kernel(body, geometry, channel, held, far, outs, far_outs, scratch):
    anywhere = pl.BlockSpec(memory_space=pl.ANY)
    inside = pl.BlockSpec(memory_space=pltpu.VMEM)
    names = [*held, *far, *outs, *far_outs, *scratch]
    scalars = pl.BlockSpec(memory_space=pltpu.SMEM)
    results = pl.pallas_call(
        lambda *refs: body(geometry, Refs(names, refs)),
        out_shape=(*outs.values(), *far_outs.values()),
        in_specs=[scalars if v.ndim == 1 else inside for v in held.values()] + [anywhere] * len(far),
        out_specs=(inside,) * len(outs) + (anywhere,) * len(far_outs),
        scratch_shapes=[*scratch.values()],
        compiler_params=pltpu.CompilerParams(
            collective_id=channel, has_side_effects=True, vmem_limit_bytes=64 << 20
        ),
    )(*held.values(), *far.values())
    return Refs([*outs, *far_outs], results)


def shape(kind, *sizes):
    return jax.ShapeDtypeStruct(sizes, kind)


def room(kind, *sizes):
    return pltpu.VMEM(sizes, kind)


def run_step(geometry, held, far):
    cells, d_in, d_mid, columns, total_count, capacity, entries, samples, clips = geometry
    groups, ranks = lax.axis_size("batch"), lax.axis_size("rows")
    chips, dma = ranks // 2, pltpu.SemaphoreType.DMA
    slots = ranks * 2 * capacity
    entry = -(-entries // 16) * 16
    bank = ranks * entry
    classes, boxes = held["cotangent"].shape
    spaced = groups * (-(-classes // groups // 16) * 16)
    spatial = far["w_spatial"].shape[0] * ranks
    half, depth = d_in // 2, d_in // ranks
    head = d_in // 4 + d_mid // 4 + spaced
    share = dict(
        q=(d_in // ranks, d_mid // groups),
        o=(d_mid // ranks, d_in // groups),
        h=(spaced // groups, 2 * d_in // ranks),
        c=(d_mid // ranks, d_in // groups),
        b=(spatial // ranks, d_mid // groups),
        a=(d_mid // groups, d_in // ranks),
    )
    block = dict(
        q=(d_in // ranks, d_mid),
        o=(d_mid // ranks, d_in),
        h=(spaced, 2 * d_in // ranks),
        c=(d_mid // ranks, d_in),
        b=(spatial // ranks, d_mid),
        a=(d_mid, d_in // ranks),
    )
    outs = dict(
        out_probs=shape(F32, boxes, classes),
        out_head=shape(F32, 8, head),
        out_b_sums=shape(F32, 8, d_mid // 4),
        out_a_sums=shape(F32, 8, d_mid // 4),
        out_k=shape(F32, depth, d_mid // groups),
        out_v=shape(F32, depth, d_mid // groups),
    )
    far_outs = dict(out_x=shape(LOW, cells, d_in), far_hat_a=shape(LOW, cells, d_mid))
    scratch = dict(
        x=room(LOW, cells, d_in),
        hat_c=room(LOW, cells, d_in),
        w_a=room(LOW, d_in, d_mid),
        w_b=room(LOW, spatial, d_mid),
        w_c=room(LOW, d_mid, d_in),
        w_q=room(LOW, d_in, d_mid),
        w_o=room(LOW, d_mid, d_in),
        w_h=room(LOW, classes, 2 * d_in),
        g_h=room(LOW, ranks, spaced, 2 * d_in // ranks),
        middle=room(F32, cells, d_mid),
        hat_a=room(LOW, cells, d_mid),
        hat_b=room(LOW, cells, d_mid),
        low_a=room(LOW, cells, d_mid),
        low_up=room(LOW, cells, d_mid),
        low_down=room(LOW, cells, d_mid),
        low_b=room(LOW, cells, d_mid),
        low_t=room(LOW, 3, d_mid, cells),
        low_bt=room(LOW, d_mid, cells),
        bank16=room(LOW, entry, d_in),
        bank_cols=room(LOW, bank, depth),
        box16=room(jnp.int32, ranks, 8, 128),
        box_in=room(jnp.int32, ranks, 8, 128),
        slot_cells=room(jnp.int32, capacity, ranks, samples),
        slot_weights=room(F32, capacity, ranks, samples),
        et=room(LOW, 2, cells, slots),
        kv_part=room(LOW, 2, bank, d_mid),
        kv_in=room(LOW, ranks - 1, 2, entry, d_mid),
        kv_own=room(LOW, 2, entry, d_mid),
        kv_all=room(LOW, 2, bank, d_mid),
        kv_out=room(LOW, 2, depth, d_mid),
        kv_back=room(LOW, groups - 1, 2, depth, d_mid // groups),
        norm_a=room(F32, 8, d_mid),
        norm_b=room(F32, 8, d_mid),
        scale_c=room(F32, 1, d_in),
        centre_c=room(F32, 8, d_in),
        acc=room(F32, 2, 8, d_in),
        pieces=room(F32, slots, half),
        blocks=room(LOW, slots, half),
        arrived=room(LOW, slots, half),
        back_in=room(LOW, slots, half),
        halo_send=dma((2, cells // 256)),
        halo_recv=dma((2, cells // 256)),
        back_send=dma((2, cells // 256)),
        back_recv=dma((2, cells // 256)),
        local=dma((32,)),
        send=dma((400,)),
        recv=dma((400,)),
    )
    scratch.update(tw_q=room(LOW, chips * depth, d_mid))
    narrow = d_mid // 4
    for n, width in enumerate((narrow, narrow, d_in // 4, head, narrow, narrow)):
        scratch["own%d" % (n + 1)] = room(F32, 8, width)
        scratch["mid%d" % (n + 1)] = room(F32, 8, width)
        scratch["rows%d" % (n + 1)] = room(F32, ranks - 1, 8, width)
        scratch["batch%d" % (n + 1)] = room(F32, groups - 1, 8, width)
    for key in share:
        outs["out_" + key] = shape(F32, *share[key])
        if key not in "qa":
            scratch["tw_" + key] = room(LOW, chips, *block[key])
        scratch["ba_" + key] = room(LOW, groups - 1, chips, *share[key])
        scratch["pa_" + key] = room(LOW, chips, *share[key])
        scratch["li_" + key] = room(LOW, chips - 1, *share[key])
    return run_kernel(step_kernel, geometry, 11, held, far, outs, far_outs, scratch)


def finish_kernel(r):
    chunk = r.in_x.shape[0] // 8

    def across(n, leave):
        at = pl.ds(n * chunk, chunk)
        source, target = (r.stage, r.x) if leave else (r.in_x, r.stage)
        return pltpu.make_async_copy(source.at[at], target.at[at], r.local.at[leave, n])

    for n in range(8):
        across(n, 0).start()
    for n in range(8):
        across(n, 0).wait()
        across(n, 1).start()
    r.probs[...] = jnp.transpose(r.in_probs[...])
    r.a[...] = jnp.transpose(r.in_a[...])
    r.b[...] = r.in_b[...]
    r.c[...] = r.in_c[...]
    r.q[...] = r.in_q[...]
    r.k[...] = r.in_k[...]
    r.v[...] = r.in_v[...]
    r.o[...] = r.in_o[...]
    r.h[...] = r.in_h[0 : r.h.shape[0], :]
    r.bias_a[...], r.gain_a[...] = r.in_a_sums[0:4, :], r.in_a_sums[4:8, :]
    r.bias_b[...], r.gain_b[...] = r.in_b_sums[0:4, :], r.in_b_sums[4:8, :]
    lanes = r.ln_gain.shape[1]
    per = r.gain_c.shape[0] // 4
    for n in range(4):
        for k in range(per):
            on = slice(k * lanes, (k + 1) * lanes)
            r.bias_c[per * n + k : per * n + k + 1, :] = r.in_head[n : n + 1, on]
            r.gain_c[per * n + k : per * n + k + 1, :] = r.in_head[4 + n : 5 + n, on]
    on = slice(per * lanes, (per + 1) * lanes)
    r.ln_gain[...], r.ln_bias[...] = r.in_head[0:4, on], r.in_head[4:8, on]
    at = (per + 1) * lanes
    r.head_bias[...] = r.in_head[0:1, at : at + r.head_bias.shape[1]]
    for n in range(8):
        across(n, 1).wait()


def run_finish(probs, two, groups, d_mid, classes):
    held = dict(
        in_probs=probs,
        in_a=two.out_a,
        in_b=two.out_b,
        in_c=two.out_c,
        in_q=two.out_q,
        in_k=two.out_k,
        in_v=two.out_v,
        in_o=two.out_o,
        in_h=two.out_h,
        in_a_sums=two.out_a_sums,
        in_b_sums=two.out_b_sums,
        in_head=two.out_head,
    )
    like = lambda v: shape(F32, *v.shape)
    lanes = two.out_a_sums.shape[1]
    row = shape(F32, 4, lanes)
    wide = shape(F32, 4 * (two.out_x.shape[1] // 4 // lanes), lanes)
    outs = dict(
        probs=shape(F32, *probs.shape[::-1]),
        a=shape(F32, *two.out_a.shape[::-1]),
        b=like(two.out_b),
        c=like(two.out_c),
        q=like(two.out_q),
        k=like(two.out_k),
        v=like(two.out_v),
        o=like(two.out_o),
        h=shape(F32, classes // groups, two.out_h.shape[1]),
        gain_a=row,
        bias_a=row,
        gain_b=row,
        bias_b=row,
        gain_c=wide,
        bias_c=wide,
        ln_gain=row,
        ln_bias=row,
        head_bias=shape(F32, 1, classes),
    )
    far_outs = dict(x=shape(LOW, *two.out_x.shape))
    anywhere = pl.BlockSpec(memory_space=pl.ANY)
    inside = pl.BlockSpec(memory_space=pltpu.VMEM)
    names = [*held, "in_x", *outs, *far_outs, "stage", "local"]
    results = pl.pallas_call(
        lambda *refs: finish_kernel(Refs(names, refs)),
        out_shape=(*outs.values(), *far_outs.values()),
        in_specs=[inside] * len(held) + [anywhere],
        out_specs=(inside,) * len(outs) + (anywhere,),
        scratch_shapes=[room(LOW, *two.out_x.shape), pltpu.SemaphoreType.DMA((2, 8))],
        compiler_params=pltpu.CompilerParams(vmem_limit_bytes=64 << 20),
    )(*held.values(), two.out_x)
    return Refs([*outs, *far_outs], results)


def fused_device(
    features,
    w_reduce,
    w_spatial,
    w_expand,
    query_weight,
    w_key,
    w_value,
    w_out,
    w_head,
    gain_a,
    bias_a,
    gain_b,
    bias_b,
    gain_c,
    bias_c,
    ln_gain,
    ln_bias,
    head_bias,
    bank,
    piece_box,
    piece_clip,
    send_count,
    sample_pos,
    sample_weight,
    win_start,
    win_len,
    prob_cotangent,
):
    groups, ranks = lax.axis_size("batch"), lax.axis_size("rows")
    clip_dev, row_dev, columns, d_in = features.shape
    d_mid = w_reduce.shape[1]
    cells = clip_dev * row_dev * columns
    total_count = cells * ranks * groups
    capacity = piece_box.shape[1]
    samples = sample_pos.shape[1] // capacity
    entries = bank.shape[0]
    geometry = (cells, d_in, d_mid, columns, total_count, capacity, entries, samples, clip_dev)
    line = lambda v: v.reshape(1, -1)
    held = dict(
        bank=bank,
        piece_box=piece_box,
        piece_clip=piece_clip,
        send_count=send_count,
        sample_pos=sample_pos,
        sample_weight=sample_weight,
        gain_a=line(gain_a),
        bias_a=line(bias_a),
        gain_b=line(gain_b),
        bias_b=line(bias_b),
        gain_c=line(gain_c),
        bias_c=line(bias_c),
        ln_gain=line(ln_gain),
        ln_bias=line(ln_bias),
        win_start=line(win_start),
        win_len=line(win_len),
        head_bias=line(head_bias),
        cotangent=prob_cotangent.T,
    )
    far = dict(
        features=features.reshape(cells, d_in),
        w_reduce=w_reduce,
        w_spatial=w_spatial,
        w_expand=w_expand,
        w_query=query_weight,
        w_out=w_out,
        w_head=w_head.T,
        w_key=w_key,
        w_value=w_value,
    )
    done = run_step(geometry, held, far)
    last = run_finish(done.out_probs, done, groups, d_mid, prob_cotangent.shape[1])
    flat = lambda v: v.reshape(-1)
    return (
        last.probs.T,
        last.x.reshape(features.shape),
        last.a,
        last.b,
        last.c,
        last.q,
        last.k,
        last.v,
        last.o,
        last.h.T,
        flat(last.gain_a),
        flat(last.bias_a),
        flat(last.gain_b),
        flat(last.bias_b),
        flat(last.gain_c),
        flat(last.bias_c),
        flat(last.ln_gain),
        flat(last.ln_bias),
        flat(last.head_bias),
    )


def plain_normalize(field, total_count):
    sums, squares = lax.psum((jnp.sum(field, 0), jnp.sum(field * field, 0)), ("batch", "rows"))
    centre_value = sums / total_count
    inverse = lax.rsqrt(squares / total_count - centre_value * centre_value + 1e-05)
    return ((field - centre_value) * inverse, inverse)


def plain_totals(grad, normed):
    return lax.psum((jnp.sum(grad, 0), jnp.sum(grad * normed, 0)), ("batch", "rows"))


def plain_device(
    features,
    w_reduce,
    w_spatial,
    w_expand,
    query_weight,
    w_key,
    w_value,
    w_out,
    w_head,
    gain_a,
    bias_a,
    gain_b,
    bias_b,
    gain_c,
    bias_c,
    ln_gain,
    ln_bias,
    head_bias,
    bank,
    piece_box,
    piece_clip,
    send_count,
    sample_pos,
    sample_weight,
    win_start,
    win_len,
    prob_cotangent,
):
    owners = lax.axis_size("rows")
    clip_dev, row_dev, col_count, d_in = features.shape
    cell_count = clip_dev * row_dev * col_count
    total_count = cell_count * owners * lax.axis_size("batch")
    w_a, w_b, w_c, w_q, w_k, w_v, w_o, w_h = (
        lax.all_gather(w_reduce, "rows", axis=0, tiled=True),
        lax.all_gather(w_spatial, "rows", axis=0, tiled=True),
        lax.all_gather(w_expand, "rows", axis=0, tiled=True),
        lax.all_gather(query_weight, "rows", axis=0, tiled=True),
        lax.all_gather(w_key, "rows", axis=0, tiled=True),
        lax.all_gather(w_value, "rows", axis=0, tiled=True),
        lax.all_gather(w_out, "rows", axis=0, tiled=True),
        lax.all_gather(w_head, "rows", axis=0, tiled=True),
    )
    d_mid = w_a.shape[1]
    flat_x = features.reshape(cell_count, d_in)
    pre_a = jnp.dot(flat_x, w_a, preferred_element_type=jnp.float32)
    hat_a, inverse_a = plain_normalize(pre_a, total_count)
    act_a = gain_a * hat_a + bias_a
    low_a = jax.nn.silu(act_a).astype(jnp.bfloat16)
    halo_a = padded(low_a.reshape(clip_dev, row_dev, col_count, d_mid), (("rows", 1),), 1)
    halo_a = jnp.pad(halo_a, ((0, 0), (0, 0), (1, 1), (0, 0)))
    window_a = jnp.concatenate(
        [
            halo_a[:, row_step : row_step + row_dev, col_step : col_step + col_count]
            for row_step in range(3)
            for col_step in range(3)
        ],
        axis=3,
    ).reshape(cell_count, 9 * d_mid)
    pre_b = jnp.dot(window_a, w_b, preferred_element_type=jnp.float32)
    hat_b, inverse_b = plain_normalize(pre_b, total_count)
    act_b = gain_b * hat_b + bias_b
    low_b = jax.nn.silu(act_b).astype(jnp.bfloat16)
    pre_c = jnp.dot(low_b, w_c, preferred_element_type=jnp.float32)
    hat_c, inverse_c = plain_normalize(pre_c, total_count)
    pre_out = gain_c * hat_c + bias_c + flat_x.astype(jnp.float32)
    fmap = jax.nn.silu(pre_out).astype(jnp.bfloat16)
    capacity = piece_box.shape[1]
    samples = sample_pos.shape[1] // capacity
    slot_count = owners * capacity
    sample_cells = (
        piece_clip[:, :, None] * (row_dev * col_count)
        + sample_pos.reshape(owners, capacity, samples)
    ).reshape(slot_count, samples)
    is_live = (jnp.arange(capacity)[None, :] < send_count[:, None]).reshape(slot_count)
    slot_weights = sample_weight.reshape(slot_count, samples) * is_live[:, None].astype(jnp.float32)
    cell_ids = jnp.arange(cell_count)[None, :]
    interp_sum = jnp.zeros((slot_count, cell_count), jnp.float32)
    for sample_index in range(samples):
        interp_sum = interp_sum + jnp.where(
            sample_cells[:, sample_index, None] == cell_ids,
            slot_weights[:, sample_index, None],
            0.0,
        )
    interpolated_value = interp_sum.astype(jnp.bfloat16)
    region_parts = (
        jnp.dot(interpolated_value, fmap, preferred_element_type=jnp.float32)
        .astype(jnp.bfloat16)
        .reshape(owners, capacity, d_in)
    )
    arrived, arrived_box = (
        lax.all_to_all(region_parts, "rows", split_axis=0, concat_axis=0, tiled=True),
        lax.all_to_all(piece_box, "rows", split_axis=0, concat_axis=0, tiled=True),
    )
    box_dev = win_start.shape[0]
    flat_box = arrived_box.reshape(slot_count)
    owner_hits = (flat_box[None, :] == jnp.arange(box_dev)[:, None]).astype(jnp.bfloat16)
    pooled = jnp.dot(
        owner_hits, arrived.reshape(slot_count, d_in), preferred_element_type=jnp.float32
    )
    pooled_low = pooled.astype(jnp.bfloat16)
    keys_own = jnp.dot(bank, w_k, preferred_element_type=jnp.float32).astype(jnp.bfloat16)
    values_own = jnp.dot(bank, w_v, preferred_element_type=jnp.float32).astype(jnp.bfloat16)
    key_rows, value_rows = (
        lax.all_gather(keys_own, "rows", axis=0, tiled=True),
        lax.all_gather(values_own, "rows", axis=0, tiled=True),
    )
    bank_length = key_rows.shape[0]
    queries = jnp.dot(pooled_low, w_q, preferred_element_type=jnp.float32).astype(jnp.bfloat16)
    score_scale = d_mid ** (-0.5)
    scores = ndot(queries, key_rows) * score_scale
    positions = jnp.arange(bank_length)[None, :]
    window_mask = (positions >= win_start[:, None]) & (positions < (win_start + win_len)[:, None])
    attend = jax.nn.softmax(jnp.where(window_mask, scores, -1e30), axis=-1)
    attend_low = attend.astype(jnp.bfloat16)
    mixture = jnp.dot(attend_low, value_rows, preferred_element_type=jnp.float32)
    centred = mixture - jnp.mean(mixture, axis=-1, keepdims=True)
    inverse_z = lax.rsqrt(jnp.mean(centred * centred, axis=-1, keepdims=True) + 1e-05)
    hat_z = centred * inverse_z
    pre_ln = ln_gain * hat_z + ln_bias
    low_r = jax.nn.silu(pre_ln).astype(jnp.bfloat16)
    branch = jnp.dot(low_r, w_o, preferred_element_type=jnp.float32)
    joined = jnp.concatenate([pooled, pooled + branch], axis=1).astype(jnp.bfloat16)
    logits = jnp.dot(joined, w_h, preferred_element_type=jnp.float32) + head_bias
    likely = jax.nn.sigmoid(logits)
    d_logit = (prob_cotangent * (likely * (1.0 - likely))).astype(jnp.bfloat16)
    grad_head_bias = jnp.sum(d_logit.astype(jnp.float32), 0)
    grad_wh = tdot(joined, d_logit)
    d_joined = ndot(d_logit, w_h)
    d_pooled = d_joined[:, :d_in] + d_joined[:, d_in:]
    d_branch = d_joined[:, d_in:].astype(jnp.bfloat16)
    grad_wo = tdot(low_r, d_branch)
    d_ln = ndot(d_branch, w_o) * silu_slope(pre_ln)
    grad_ln_gain = jnp.sum(d_ln * hat_z, 0)
    grad_ln_bias = jnp.sum(d_ln, 0)
    d_hat = d_ln * ln_gain
    d_mixture = (
        inverse_z
        * (
            d_hat
            - jnp.mean(d_hat, axis=-1, keepdims=True)
            - hat_z * jnp.mean(d_hat * hat_z, axis=-1, keepdims=True)
        )
    ).astype(jnp.bfloat16)
    d_attend = ndot(d_mixture, value_rows)
    d_values = tdot(attend_low, d_mixture)
    d_scores = (attend * (d_attend - jnp.sum(d_attend * attend, axis=-1, keepdims=True))).astype(
        jnp.bfloat16
    )
    d_queries = (
        jnp.dot(d_scores, key_rows, preferred_element_type=jnp.float32) * score_scale
    ).astype(jnp.bfloat16)
    d_keys = tdot(d_scores, queries) * score_scale
    grad_wq = tdot(pooled_low, d_queries)
    d_pooled = d_pooled + ndot(d_queries, w_q)
    key_sum, value_sum = side_by_side(
        (d_keys.astype(jnp.bfloat16), d_values.astype(jnp.bfloat16)), "rows", 0, 1
    )
    grad_wk = tdot(bank, key_sum.astype(jnp.bfloat16))
    grad_wv = tdot(bank, value_sum.astype(jnp.bfloat16))
    back_pieces = jnp.take(d_pooled.astype(jnp.bfloat16), flat_box, axis=0).reshape(
        owners, capacity, d_in
    )
    returned = lax.all_to_all(back_pieces, "rows", split_axis=0, concat_axis=0, tiled=True)
    d_fmap = tdot(interpolated_value, returned.reshape(slot_count, d_in))
    d_pre = d_fmap * silu_slope(pre_out)
    head_sums = lax.psum(
        (jnp.sum(d_pre, 0), jnp.sum(d_pre * hat_c, 0), grad_ln_gain, grad_ln_bias, grad_head_bias),
        ("batch", "rows"),
    )
    d_c = norm_back(
        d_pre, hat_c, inverse_c, gain_c, head_sums[0], head_sums[1], total_count
    ).astype(jnp.bfloat16)
    grad_wc = tdot(low_b, d_c)
    d_act_b = ndot(d_c, w_c) * silu_slope(act_b)
    shift_b_sum, gain_b_sum = plain_totals(d_act_b, hat_b)
    d_b = norm_back(d_act_b, hat_b, inverse_b, gain_b, shift_b_sum, gain_b_sum, total_count).astype(
        jnp.bfloat16
    )
    grad_wb = tdot(window_a, d_b)
    halo_d = padded(d_b.reshape(clip_dev, row_dev, col_count, d_mid), (("rows", 1),), 1)
    halo_d = jnp.pad(halo_d, ((0, 0), (0, 0), (1, 1), (0, 0)))
    window_d = jnp.concatenate(
        [
            halo_d[
                :, 2 - row_step : 2 - row_step + row_dev, 2 - col_step : 2 - col_step + col_count
            ]
            for row_step in range(3)
            for col_step in range(3)
        ],
        axis=3,
    ).reshape(cell_count, 9 * d_mid)
    flipped = w_b.reshape(9, d_mid, d_mid).transpose(0, 2, 1).reshape(9 * d_mid, d_mid)
    d_act_a = jnp.dot(window_d, flipped, preferred_element_type=jnp.float32) * silu_slope(act_a)
    shift_a_sum, gain_a_sum = plain_totals(d_act_a, hat_a)
    d_a = norm_back(d_act_a, hat_a, inverse_a, gain_a, shift_a_sum, gain_a_sum, total_count).astype(
        jnp.bfloat16
    )
    grad_wa = tdot(flat_x, d_a)
    grad_input = (ndot(d_a, w_a) + d_pre).astype(jnp.bfloat16).reshape(features.shape)
    partial_sums = (
        lax.psum_scatter(grad_wa, "rows", scatter_dimension=0, tiled=True),
        lax.psum_scatter(grad_wb, "rows", scatter_dimension=0, tiled=True),
        lax.psum_scatter(grad_wc, "rows", scatter_dimension=0, tiled=True),
        lax.psum_scatter(grad_wq, "rows", scatter_dimension=0, tiled=True),
        lax.psum_scatter(grad_wk, "rows", scatter_dimension=0, tiled=True),
        lax.psum_scatter(grad_wv, "rows", scatter_dimension=0, tiled=True),
        lax.psum_scatter(grad_wo, "rows", scatter_dimension=0, tiled=True),
        lax.psum_scatter(grad_wh, "rows", scatter_dimension=0, tiled=True),
    )
    finished = (
        lax.psum_scatter(
            partial_sums[0].astype(jnp.bfloat16), "batch", scatter_dimension=1, tiled=True
        ).astype(jnp.float32),
        lax.psum_scatter(
            partial_sums[1].astype(jnp.bfloat16), "batch", scatter_dimension=1, tiled=True
        ).astype(jnp.float32),
        lax.psum_scatter(
            partial_sums[2].astype(jnp.bfloat16), "batch", scatter_dimension=1, tiled=True
        ).astype(jnp.float32),
        lax.psum_scatter(
            partial_sums[3].astype(jnp.bfloat16), "batch", scatter_dimension=1, tiled=True
        ).astype(jnp.float32),
        lax.psum_scatter(
            partial_sums[4].astype(jnp.bfloat16), "batch", scatter_dimension=1, tiled=True
        ).astype(jnp.float32),
        lax.psum_scatter(
            partial_sums[5].astype(jnp.bfloat16), "batch", scatter_dimension=1, tiled=True
        ).astype(jnp.float32),
        lax.psum_scatter(
            partial_sums[6].astype(jnp.bfloat16), "batch", scatter_dimension=1, tiled=True
        ).astype(jnp.float32),
        lax.psum_scatter(
            partial_sums[7].astype(jnp.bfloat16), "batch", scatter_dimension=1, tiled=True
        ).astype(jnp.float32),
    )
    return (
        likely,
        grad_input,
        finished[0],
        finished[1],
        finished[2],
        finished[3],
        finished[4],
        finished[5],
        finished[6],
        finished[7],
        gain_a_sum,
        shift_a_sum,
        gain_b_sum,
        shift_b_sum,
        head_sums[1],
        head_sums[0],
        head_sums[2],
        head_sums[3],
        head_sums[4],
    )


def on_device(*args):
    fits = all(a.shape[0] % 64 == 0 for a in args[1:9]) and lax.axis_size("rows") % 2 == 0
    return (fused_device if fits else plain_device)(*args)


def solution(mesh):
    return jax.shard_map(
        on_device,
        mesh=mesh,
        in_specs=(
            P("batch", "rows", None, None),
            P("rows", None),
            P("rows", None),
            P("rows", None),
            P("rows", None),
            P("rows", None),
            P("rows", None),
            P("rows", None),
            P("rows", None),
            P(),
            P(),
            P(),
            P(),
            P(),
            P(),
            P(),
            P(),
            P(),
            P(("batch", "rows"), None),
            P(("batch", "rows"), None),
            P(("batch", "rows"), None),
            P(("batch", "rows")),
            P(("batch", "rows"), None),
            P(("batch", "rows"), None),
            P(("batch", "rows")),
            P(("batch", "rows")),
            P(("batch", "rows"), None),
        ),
        out_specs=(
            P(("batch", "rows"), None),
            P("batch", "rows", None, None),
            P("rows", "batch"),
            P("rows", "batch"),
            P("rows", "batch"),
            P("rows", "batch"),
            P("rows", "batch"),
            P("rows", "batch"),
            P("rows", "batch"),
            P("rows", "batch"),
            P(),
            P(),
            P(),
            P(),
            P(),
            P(),
            P(),
            P(),
            P(),
        ),
        check_vma=False,
    )
```

```python
import jax
import jax.numpy as jnp
from jax import lax
from jax.experimental import pallas as pl
from jax.experimental.pallas import tpu as pltpu
from jax.sharding import PartitionSpec as P


def padded(cells, sides, width):
    for axis, dim in sides:
        count = lax.axis_size(axis)
        ends = count - 1
        head = lax.slice_in_dim(cells, 0, width, axis=dim)
        tail = lax.slice_in_dim(cells, cells.shape[dim] - width, cells.shape[dim], axis=dim)
        cells = jnp.concatenate(
            [
                lax.ppermute(tail, axis, [(i, (i + 1) % count) for i in range(ends)]),
                cells,
                lax.ppermute(head, axis, [((i + 1) % count, i) for i in range(ends)]),
            ],
            axis=dim,
        )
    return cells


def split_up(value, dim, peers):
    shape = value.shape
    parts = value.reshape(*shape[:dim], peers, shape[dim] // peers, *shape[dim + 1 :])
    return jnp.moveaxis(parts, dim, 0)


def sum_at_owner(value, axis, dim):
    peers = lax.axis_size(axis)
    parts = lax.all_to_all(split_up(value, dim, peers), axis, 0, 0, tiled=True)
    return jnp.sum(parts.astype(jnp.float32), axis=0)


def side_by_side(arrays, axis, dim, along):
    ends, at = ([], 0)
    for a in arrays[:-1]:
        at += a.shape[along]
        ends.append(at)
    both = jnp.concatenate(arrays, axis=along)
    return tuple(jnp.split(sum_at_owner(both, axis, dim), ends, axis=along))


def tdot(left, right):
    return lax.dot_general(
        left, right, (((0,), (0,)), ((), ())), preferred_element_type=jnp.float32
    )


def ndot(left, right):
    return lax.dot_general(
        left, right, (((1,), (1,)), ((), ())), preferred_element_type=jnp.float32
    )


def silu_slope(value):
    sig = jax.nn.sigmoid(value)
    return sig * (1.0 + value * (1.0 - sig))


def norm_back(grad, normed, inverse, gain, shift_sum, gain_total_grad, total_count):
    return (
        gain * inverse * (grad - shift_sum / total_count - normed * gain_total_grad / total_count)
    )


MESH = pl.DeviceIdType.MESH
LOW = jnp.bfloat16
F32 = jnp.float32


class Wires:
    def __init__(self, send, recv):
        self.send, self.recv, self.at, self.open, self.some = send, recv, 0, [], []

    def plan(self, source, target, peer, land=None):
        copy = pltpu.make_async_remote_copy(
            src_ref=source,
            dst_ref=target,
            send_sem=self.send.at[self.at],
            recv_sem=self.recv.at[self.at if land is None else land],
            device_id=peer,
            device_id_type=MESH,
        )
        self.at += 1
        self.open.append(copy)
        return copy

    def waiter(self, like, land, peer):
        return pltpu.make_async_remote_copy(
            src_ref=like,
            dst_ref=like,
            send_sem=self.send.at[0],
            recv_sem=self.recv.at[land],
            device_id=peer,
            device_id_type=MESH,
        )

    def only_where(self, where, copy):
        self.open.pop()
        self.some.append((where, copy))
        return where, copy

    def push(self, source, target, peer):
        return start(self.plan(source, target, peer))

    def settle(self, copies):
        for copy in copies:
            copy.wait_send()
        done = {id(copy) for copy in copies}
        self.open = [copy for copy in self.open if id(copy) not in done]

    def settle_some(self, pairs):
        for where, copy in pairs:

            @pl.when(where)
            def _():
                copy.wait_send()

        done = {id(copy) for where, copy in pairs}
        self.some = [pair for pair in self.some if id(pair[1]) not in done]

    def close(self):
        for copy in self.open:
            copy.wait_send()
        self.settle_some(self.some)


def start(copy):
    copy.start()
    return copy


def greet(peers):
    barrier = pltpu.get_barrier_semaphore()
    for peer in peers:
        pl.semaphore_signal(barrier, inc=1, device_id=peer, device_id_type=MESH)
    pl.semaphore_wait(barrier, len(peers))


class Place:
    def __init__(self):
        self.groups, self.ranks = lax.axis_size("batch"), lax.axis_size("rows")
        self.g, self.s = lax.axis_index("batch"), lax.axis_index("rows")
        self.chips = self.ranks // 2
        self.z, self.core = self.s // 2, lax.rem(self.s, 2)
        self.other = 1 - self.core
        self.row_peers = [(self.g, lax.rem(self.s + k, self.ranks)) for k in range(1, self.ranks)]
        self.batch_peers = [
            (lax.rem(self.g + k, self.groups), self.s) for k in range(1, self.groups)
        ]
        self.line = [lax.rem(self.z + k, self.chips) for k in range(self.chips)]
        self.line_peers = [(self.g, z * 2 + self.core) for z in self.line[1:]]
        self.twin = (self.g, self.z * 2 + self.other)
        low, high = lax.rem(self.g, 2), self.g // 2
        beside, above = high * 2 + 1 - low, (1 - high) * 2 + low
        self.near = beside + self.core * (above - beside)
        self.far, self.across = beside + above - self.near, 3 - self.g


def rows_of(ref, index, size):
    return ref.at[pl.ds(pl.multiple_of(index * size, size), size)]


class Total:
    def __init__(self, net, place, held, from_rows, second, from_batch):
        self.held, self.from_rows, self.second, self.from_batch = (
            held,
            from_rows,
            second,
            from_batch,
        )
        self.rows = [
            net.plan(held, from_rows.at[k], peer) for k, peer in enumerate(place.row_peers)
        ]
        self.batch = [
            net.plan(second, from_batch.at[k], peer) for k, peer in enumerate(place.batch_peers)
        ]

    def start(self):
        for copy in self.rows:
            copy.start()

    def sent(self):
        return self.rows + self.batch

    def finish(self, behind=None):
        for copy in self.rows:
            copy.wait_recv()
        total = self.held[...]
        for k in range(len(self.rows)):
            total = total + self.from_rows[k]
        self.second[...] = total
        for copy in self.batch:
            copy.start()
        if behind is not None:
            behind()
        for copy in self.batch:
            copy.wait_recv()
        for k in range(len(self.batch)):
            total = total + self.from_batch[k]
        return total


def spread(ref, values):
    quarter = values[0].shape[1] // 4
    for n, value in enumerate(values):
        for k in range(4):
            ref[4 * n + k : 4 * n + k + 1, 0:quarter] = value[:, k * quarter : (k + 1) * quarter]


def gathered(block, n, quarter, at=0):
    return jnp.concatenate(
        [block[4 * n + k : 4 * n + k + 1, at : at + quarter] for k in range(4)], axis=1
    )


class Corner:
    def __init__(self, ref, height, width):
        self.ref, self.height, self.width = ref, height, width

    def __getitem__(self, z):
        beside = self.ref.shape[1] // self.width
        down, along = z // beside * self.height, z % beside * self.width
        return self.ref.at[down : down + self.height, along : along + self.width]


class Scatter:
    def __init__(self, net, place, shard, part, from_twin, from_batch, partial, from_line, result):
        self.place, self.shard, self.part = place, shard, part
        self.from_twin, self.from_batch, self.partial = from_twin, from_batch, partial
        self.from_line, self.result = from_line, result
        self.first, self.second, self.last = [], [], []
        for z in range(place.chips):
            self.first.append(net.plan(shard(2 * z + place.other), from_twin[z], place.twin))
            mine = shard(2 * z + place.core)
            self.second.append(
                [
                    net.plan(part(mine, g), from_batch.at[k, z], (near, place.s))
                    for k, (g, near) in enumerate(
                        (
                            (place.near, place.near),
                            (place.across, place.near),
                            (place.far, place.far),
                        )
                    )
                ]
            )
        self.third = [
            net.plan(partial.at[k + 1], from_line.at[k], peer)
            for k, peer in enumerate(place.line_peers)
        ]

    def sent(self, steps):
        return self.first + [copy for copies in self.second for copy in copies[:steps]]

    def pair(self):
        for copy in self.first:
            copy.start()

    def batch(self, *turns):
        place = self.place
        for z in turns or range(place.chips):
            self.first[z].wait_recv()
            mine = self.shard(2 * z + place.core)
            rows = mine.shape[0]
            step = next(n for n in (64, 32, 16) if rows % n == 0)

            @pl.loop(0, rows // step)
            def _(n):
                at = pl.ds(pl.multiple_of(n * step, step), step)
                mine[at, :] = (
                    mine[at, :].astype(F32) + self.from_twin[z][at, :].astype(F32)
                ).astype(LOW)

            for copy in self.second[z][:2]:
                copy.start()

    def forward(self, *turns):
        place = self.place
        for z in turns or range(place.chips):
            for copy in self.second[z][:2]:
                copy.wait_recv()
            theirs = self.part(self.shard(2 * z + place.core), place.far)
            theirs[...] = (
                theirs[...].astype(F32) + self.from_batch[1, z].astype(F32)
            ).astype(LOW)
            self.second[z][2].start()

    def line(self):
        place = self.place
        for copies in self.second:
            copies[2].wait_recv()
        for k, z in enumerate(place.line):
            mine = self.part(self.shard(2 * z + place.core), place.g)
            total = mine[...].astype(F32)
            for n in (0, 2):
                total = total + self.from_batch[n, z].astype(F32)
            self.partial[k] = total.astype(LOW)
            if k:
                self.third[k - 1].start()

    def finish(self):
        for copy in self.third:
            copy.wait_recv()
        total = self.partial[0].astype(F32)
        for k in range(self.place.chips - 1):
            total = total + self.from_line[k].astype(F32)
        self.result[...] = total


def slope_of(value):
    sig = 0.5 * jnp.tanh(0.5 * value) + 0.5
    return sig * (1.0 + value * (1.0 - sig))


def column_of(shape, columns):
    return lax.rem(lax.broadcasted_iota(jnp.int32, shape, 0), columns)


def from_left(value, columns):
    return jnp.where(
        column_of(value.shape, columns) == 0, 0.0, pltpu.roll(value, 1, 0)
    )


def from_right(value, columns):
    return jnp.where(
        column_of(value.shape, columns) == columns - 1,
        0.0,
        pltpu.roll(value, value.shape[0] - 1, 0),
    )


def folded(value):
    rows, width = value.shape
    return jnp.sum(value.reshape(rows // 8, 8, width), axis=0)


class Gather:
    def __init__(self, net, place, shard, whole, local, dim=0, relayed=False):
        self.net, self.place, self.shard, self.whole = net, place, shard, whole
        self.dim, self.rows = dim, whole.shape[dim] // place.ranks
        self.own = pltpu.make_async_copy(shard, self.block(place.s), local)
        part = self.rows // place.groups
        source = self.cut(shard, place.g * part, part)
        self.relayed, self.some = relayed and place.chips == 4, []
        if self.relayed:
            self.plan_relay(net, source)
        else:
            self.first = [
                net.plan(source, self.quarter(place.s, place.g), peer) for peer in place.line_peers
            ]
        self.second, self.third = [], [net.plan(shard, self.block(place.s), place.twin)]
        for k in self.order if self.relayed else range(1, place.chips):
            s = lax.rem(place.z + place.chips - k, place.chips) * 2 + place.core
            view, passed = self.quarter(s, place.g), self.quarter(s, place.near)
            self.second.append(
                [
                    net.plan(view, view, (place.near, place.s)),
                    net.plan(view, view, (place.far, place.s)),
                    net.plan(passed, passed, (place.far, place.s)),
                ]
            )
            self.third.append(net.plan(self.block(s), self.block(s), place.twin))

    def plan_relay(self, net, source):
        place, z, base = self.place, self.place.z, net.at
        right, left = (
            (place.g, lax.rem(z + n, 4) * 2 + place.core) for n in (1, 3)
        )
        mine = self.quarter(place.s, place.g)
        passed = [
            self.quarter(lax.rem(z + 4 - k, 4) * 2 + place.core, place.g) for k in (1, 2, 3)
        ]
        self.inner = (z == 1) | (z == 2)
        first = 1 + (3 - z) // 3 * 2
        then = 2 + lax.rem((z + 1) // 2, 2)
        self.order = (first, then, 6 - first - then)
        self.arrivals = [net.waiter(passed[0], base + k - 1, place.twin) for k in self.order]
        steps = (
            (z < 3, source, mine, right, base),
            (self.inner, passed[0], passed[0], right, base + 1),
            (z > 0, source, mine, left, base + 2),
            (self.inner, passed[2], passed[2], left, base + 1),
            (z == 2, passed[1], passed[1], right, base + 2),
            (z == 1, passed[1], passed[1], left, base),
        )
        for where, origin, goal, peer, land in steps:
            self.some.append(net.only_where(where, net.plan(origin, goal, peer, land)))
        self.first = [copy for where, copy in self.some[:3]]

    def go(self, n):
        where, copy = self.some[n]

        @pl.when(where)
        def _():
            copy.start()

    def relay(self):
        @pl.when(self.inner)
        def _():
            self.first[0].wait_recv()
            self.some[1][1].start()
            self.first[2].wait_recv()
            self.some[3][1].start()

    def relay_last(self):
        @pl.when(self.inner)
        def _():
            self.first[1].wait_recv()

        self.go(4)
        self.go(5)

    def cut(self, ref, start, size):
        at = pl.ds(pl.multiple_of(start, size), size)
        return ref.at[at] if self.dim == 0 else ref.at[:, at]

    def block(self, s):
        return self.cut(self.whole, s * self.rows, self.rows)

    def quarter(self, s, g):
        part = self.rows // self.place.groups
        return self.cut(self.whole, s * self.rows + g * part, part)

    def line(self):
        if self.relayed:
            self.go(0)
            self.go(2)
        else:
            for copy in self.first:
                copy.start()
        self.own.start()
        self.third[0].start()

    def batch(self, *turns):
        for k in turns or range(len(self.first)):
            if self.relayed:

                @pl.when(jnp.logical_not(self.inner))
                def _():
                    self.arrivals[k].wait_recv()

            else:
                self.first[k].wait_recv()
            for copy in self.second[k][:2]:
                copy.start()

    def forward(self, *turns):
        for k in turns or range(len(self.first)):
            self.second[k][0].wait_recv()
            self.second[k][2].start()

    def pair(self):
        for k, copies in enumerate(self.second):
            for copy in copies[1:]:
                copy.wait_recv()
            self.third[k + 1].start()

    def sent(self):
        return ([] if self.relayed else self.first) + self.third + [c for copies in self.second for c in copies]

    def ready(self):
        self.own.wait()
        for copy in self.third:
            copy.wait_recv()


def moments(total, width, total_count):
    centre = gathered(total, 0, width // 4) / total_count
    square = gathered(total, 1, width // 4) / total_count
    return centre, lax.rsqrt(square - centre * centre + 1e-05)


def sigma(value):
    return 0.5 * jnp.tanh(0.5 * value) + 0.5


def step_kernel(geometry, r):
    cells, d_in, d_mid, columns, total_count, capacity, entries, samples, clips = geometry
    place = Place()
    net = Wires(r.send, r.recv)
    ranks, groups = place.ranks, place.groups
    half, size = d_in // 2, 2 * capacity
    depth = d_in // ranks
    entry = r.bank16.shape[0]
    local = r.local
    load_x = pltpu.make_async_copy(r.features, r.x, local.at[0])
    load_x.start()
    kv_weights = [rows_of(r.low_b, n, depth) for n in range(2)]
    load_kv = [
        pltpu.make_async_copy(source, target, local.at[9 + n])
        for n, (source, target) in enumerate(zip((r.w_key, r.w_value), kv_weights))
    ]
    for copy in load_kv:
        copy.start()
    greet(place.row_peers + place.batch_peers)
    a, b, c, q, o, h = (
        Gather(net, place, shard, whole, local.at[n + 1], n // 5, n in (1, 3, 4, 5))
        for n, (shard, whole) in enumerate(
            (
                (r.w_reduce, r.w_a),
                (r.w_spatial, r.w_b),
                (r.w_expand, r.w_c),
                (r.w_query, r.w_q),
                (r.w_out, r.w_o),
                (r.w_head, r.w_h),
            )
        )
    )
    sums = [
        Total(net, place, *refs)
        for refs in (
            (r.own1, r.rows1, r.mid1, r.batch1),
            (r.own2, r.rows2, r.mid2, r.batch2),
            (r.own3, r.rows3, r.mid3, r.batch3),
            (r.own4, r.rows4, r.mid4, r.batch4),
            (r.own5, r.rows5, r.mid5, r.batch5),
            (r.own6, r.rows6, r.mid6, r.batch6),
        )
    ]
    a.line()

    def at_block(s):
        return pl.ds(pl.multiple_of(s * entry, entry), entry)

    def at_depth(s):
        return pl.ds(pl.multiple_of(s * depth, depth), depth)

    r.bank16[...] = jnp.zeros_like(r.bank16)
    r.bank16[0:entries, :] = r.bank[...]
    asked = [
        net.push(r.bank16.at[:, at_depth(peer[1])], rows_of(r.bank_cols, place.s, entry), peer)
        for peer in place.row_peers
    ]
    b.line()
    for n in range(ranks):
        r.box16[n, 0:1, 0:capacity] = r.piece_box[n : n + 1, :]
    owner = lax.broadcasted_iota(jnp.int32, (ranks, 1), 0)
    count = jnp.zeros((ranks, 1), jnp.int32)
    for n in range(ranks):
        count = jnp.where(owner == n, r.send_count[n], count)
    for k in range(capacity):
        on = slice(k * samples, (k + 1) * samples)
        r.slot_cells[k] = r.sample_pos[:, on] + r.piece_clip[:, k : k + 1] * (cells // clips)
        r.slot_weights[k] = jnp.where(k < count, r.sample_weight[:, on], 0.0)
    named = [
        net.push(r.box16.at[peer[1]], r.box_in.at[place.s], peer) for peer in place.row_peers
    ]
    r.bank_cols[at_block(place.s), :] = r.bank16[:, at_depth(place.s)]
    mine = pl.ds(pl.multiple_of(place.s * size, size), size)
    r.box_in[place.s] = r.box16[place.s]

    by_rank = (capacity * ranks, ranks * size)
    row, slot = (lax.broadcasted_iota(jnp.int32, by_rank, n) for n in range(2))
    goal = lax.rem(row, ranks) * size + row // ranks
    perms = [jnp.where(slot == goal + n * capacity, 1.0, 0.0).astype(LOW) for n in range(2)]

    @pl.loop(0, capacity)
    def _(k):
        cell = lax.broadcasted_iota(jnp.int32, (ranks, cells), 1)
        spots, weights = r.slot_cells[k], r.slot_weights[k]
        total = jnp.zeros((ranks, cells), F32)
        for j in range(samples):
            total = total + jnp.where(cell == spots[:, j : j + 1], weights[:, j : j + 1], 0.0)
        r.pieces[pl.ds(pl.multiple_of(k * ranks, ranks), ranks), 0:cells] = total

    for n in range(2):
        r.et[n] = tdot(r.pieces[0 : capacity * ranks, 0:cells].astype(LOW), perms[n]).astype(LOW)

    a.batch()
    b.relay()
    a.forward()
    b.batch(0)
    a.pair()
    b.relay_last()
    b.batch(1)
    for copy in asked:
        copy.wait_recv()
    for copy in load_kv:
        copy.wait()
    for n, weight in enumerate(kv_weights):
        r.kv_part[n] = jnp.dot(
            r.bank_cols[...], weight[...], preferred_element_type=F32
        ).astype(LOW)
    load_x.wait()
    a.ready()

    acc = r.acc
    acc[...] = jnp.zeros_like(acc)
    big = 256
    tiles = cells // big

    @pl.loop(0, tiles)
    def _(t):
        at = pl.ds(pl.multiple_of(t * big, big), big)
        value = jnp.dot(r.x[at, :], r.w_a[...], preferred_element_type=F32)
        r.middle[at, :] = value
        acc[0, :, 0:d_mid] += folded(value)
        acc[1, :, 0:d_mid] += folded(value * value)

    spread(r.own1, [jnp.sum(acc[n, :, 0:d_mid], axis=0, keepdims=True) for n in range(2)])
    own_mean = jnp.sum(acc[0, :, 0:d_mid], axis=0, keepdims=True) / cells

    first, last = place.s == 0, place.s == ranks - 1
    low_a, low_up, low_down = r.low_a, r.low_up, r.low_down

    def halo(t, way):
        at = pl.ds(pl.multiple_of(t * big, big), big)
        return pltpu.make_async_remote_copy(
            src_ref=r.low_b.at[at],
            dst_ref=(low_up if way == 0 else low_down).at[at],
            send_sem=r.halo_send.at[way, t],
            recv_sem=r.halo_recv.at[way, t],
            device_id=(place.g, place.s + 1 if way == 0 else place.s - 1),
            device_id_type=MESH,
        )

    @pl.when(first)
    def _():
        low_up[...] = jnp.zeros_like(low_up)

    @pl.when(last)
    def _():
        low_down[...] = jnp.zeros_like(low_down)

    @pl.loop(0, tiles)
    def _(t):
        at = pl.ds(pl.multiple_of(t * big, big), big)
        r.low_b[at, :] = (r.middle[at, :] - own_mean).astype(LOW)

    b.forward(0)
    b.batch(2)
    sums[0].start()
    c.line()

    @pl.loop(0, tiles)
    def _(t):
        @pl.when(jnp.logical_not(last))
        def _():
            halo(t, 0).start()

        @pl.when(jnp.logical_not(first))
        def _():
            halo(t, 1).start()


    def more_b():
        b.forward(1)

    total = sums[0].finish(more_b)
    centre, inverse = moments(total, d_mid, total_count)
    gain, bias = r.gain_a[...], r.bias_a[...]
    for n, value in enumerate((gain, bias, gain * inverse)):
        r.norm_a[n : n + 1, :] = value

    @pl.loop(0, tiles)
    def _(t):
        at = pl.ds(pl.multiple_of(t * big, big), big)
        hat = (r.middle[at, :] - centre) * inverse
        r.hat_a[at, :] = hat.astype(LOW)
        act = gain * hat + bias
        low_a[at, :] = (act * sigma(act)).astype(LOW)

    beyond = [
        (
            low,
            gathered(r.rows1[n], 0, d_mid // 4) / cells - centre,
            jnp.where(edge, 0.0, 1.0),
        )
        for low, n, edge in ((low_up, 0, first), (low_down, ranks - 2, last))
    ]

    keep_hat_a = pltpu.make_async_copy(r.hat_a, r.far_hat_a, local.at[8])
    keep_hat_a.start()
    b.forward(2)
    c.batch()
    @pl.loop(0, tiles)
    def _(t):
        at = pl.ds(pl.multiple_of(t * big, big), big)
        r.low_t[1, :, at] = jnp.transpose(low_a[at, :].astype(F32)).astype(LOW)

    b.pair()
    c.forward()
    b.ready()
    acc[...] = jnp.zeros_like(acc)

    @pl.loop(0, tiles)
    def _(t):
        at = pl.ds(pl.multiple_of(t * big, big), big)

        @pl.when(jnp.logical_not(first))
        def _():
            halo(t, 0).wait_recv()

        @pl.when(jnp.logical_not(last))
        def _():
            halo(t, 1).wait_recv()

        for low, offset, inside in beyond:
            act = gain * ((low[at, :].astype(F32) + offset) * inverse) + bias
            low[at, :] = (act * sigma(act) * inside).astype(LOW)
        parts = []
        for j in range(3):
            taps = [r.w_b[(3 * i + j) * d_mid : (3 * i + j + 1) * d_mid, :] for i in range(3)]
            parts.append(
                jnp.dot(low_up[at, :], taps[0], preferred_element_type=F32)
                + jnp.dot(low_a[at, :], taps[1], preferred_element_type=F32)
                + jnp.dot(low_down[at, :], taps[2], preferred_element_type=F32)
            )
        value = from_left(parts[0], columns) + parts[1] + from_right(parts[2], columns)
        r.middle[at, :] = value
        acc[0, :, 0:d_mid] += folded(value)
        acc[1, :, 0:d_mid] += folded(value * value)

    spread(r.own2, [jnp.sum(acc[n, :, 0:d_mid], axis=0, keepdims=True) for n in range(2)])
    sums[1].start()
    net.settle(sums[0].sent() + asked + named + a.sent())
    q.line()
    o.line()
    h.line()

    @pl.loop(0, tiles)
    def _(t):
        at = pl.ds(pl.multiple_of(t * big, big), big)
        r.low_t[0, :, at] = jnp.transpose(low_up[at, :].astype(F32)).astype(LOW)
        r.low_t[2, :, at] = jnp.transpose(low_down[at, :].astype(F32)).astype(LOW)

    total = sums[1].finish()
    for gather in (q, o, h):
        gather.relay()
    centre, inverse = moments(total, d_mid, total_count)
    gain, bias = r.gain_b[...], r.bias_b[...]
    for n, value in enumerate((gain, bias, gain * inverse)):
        r.norm_b[n : n + 1, :] = value
    kv = [
        net.plan(r.kv_part.at[:, at_block(peer[1])], r.kv_in.at[k], peer)
        for k, peer in enumerate(place.row_peers)
    ]
    every = [
        net.plan(r.kv_own, r.kv_all.at[:, at_block(place.s)], peer) for peer in place.row_peers
    ]

    @pl.loop(0, tiles)
    def _(t):
        @pl.when(jnp.logical_not(last))
        def _():
            halo(t, 0).wait_send()

        @pl.when(jnp.logical_not(first))
        def _():
            halo(t, 1).wait_send()

    def third_norm(pre_c):
        c.pair()
        c.ready()
        acc[...] = jnp.zeros_like(acc)

        @pl.loop(0, tiles)
        def _(t):
            at = pl.ds(pl.multiple_of(t * big, big), big)
            hat = (r.middle[at, :] - centre) * inverse
            r.hat_b[at, :] = hat.astype(LOW)
            act = gain * hat + bias
            low = (act * sigma(act)).astype(LOW)
            r.low_b[at, :] = low
            for k in range(4):
                on = slice(k * (d_in // 4), (k + 1) * (d_in // 4))
                value = jnp.dot(low, r.w_c[:, on], preferred_element_type=F32)
                pre_c[at, on] = value
                acc[0, :, on] += folded(value)
                acc[1, :, on] += folded(value * value)

        spread(r.own3, [jnp.sum(acc[n], axis=0, keepdims=True) for n in range(2)])
        for gather in (q, o, h):
            gather.relay_last()
        sums[2].start()
        net.settle(sums[1].sent() + b.sent())
        net.settle_some(b.some)
        for copy in kv:
            copy.start()

        @pl.loop(0, tiles)
        def _(t):
            at = pl.ds(pl.multiple_of(t * big, big), big)
            r.low_bt[:, at] = jnp.transpose(r.low_b[at, :].astype(F32)).astype(LOW)


        def rest():
            for gather in (q, o, h):
                gather.batch()

        total = sums[2].finish(rest)
        centre_wide, inverse_wide = moments(total, d_in, total_count)
        r.scale_c[...] = r.gain_c[...] * inverse_wide
        r.centre_c[0:1, :] = centre_wide
        r.centre_c[1:2, :] = inverse_wide
        for copy in kv:
            copy.wait_recv()
        for n in range(2):
            total = r.kv_part[n, at_block(place.s), :].astype(F32)
            for k in range(ranks - 1):
                total = total + r.kv_in[k, n].astype(F32)
            r.kv_own[n] = total.astype(LOW)
            r.kv_all[n, at_block(place.s), :] = total.astype(LOW)
        for copy in every:
            copy.start()

        q.forward()
        r.pieces[...] = jnp.zeros_like(r.pieces)
        tile = 128

        @pl.loop(0, cells // 256)
        def _(t):
            at = pl.ds(pl.multiple_of(t * 256, 256), 256)
            for k in range(4):
                on = slice(k * (d_in // 4), (k + 1) * (d_in // 4))
                into = slice((k % 2) * (d_in // 4), (k % 2 + 1) * (d_in // 4))
                hat = (pre_c[at, on] - r.centre_c[0:1, on]) * r.centre_c[1:2, on]
                r.hat_c[at, on] = hat.astype(LOW)
                value = r.gain_c[:, on] * hat + r.bias_c[:, on] + r.x[at, on].astype(F32)
                sig = sigma(value)
                fmap = value * sig
                r.x[at, on] = (sig + fmap * (1.0 - sig)).astype(LOW)
                r.pieces[:, into] += tdot(r.et[k // 2, at, :], fmap.astype(LOW))


    pl.run_scoped(third_norm, pltpu.VMEM((cells, d_in), F32))
    o.forward()
    h.forward()
    r.blocks[...] = r.pieces[...].astype(LOW)
    pushed = [
        net.push(rows_of(r.blocks, peer[1], size), rows_of(r.arrived, place.s, size), peer)
        for peer in place.row_peers
    ]
    r.arrived[mine, :] = r.blocks[mine, :]
    q.pair()
    o.pair()
    h.pair()
    for copy in named + every + pushed:
        copy.wait_recv()

    def block_rows(ref, count):
        return lambda s: rows_of(ref, s, ref.shape[0] // count)

    def by_columns(width):
        return lambda view, g: view.at[:, pl.ds(pl.multiple_of(g * width, width), width)]

    def by_rows(height):
        return lambda view, g: view.at[pl.ds(pl.multiple_of(g * height, height), height)]

    def scatter(key, shard, part, landing):
        return Scatter(
            net, place, shard, part, landing, *(getattr(r, n + key) for n in ("ba_", "pa_", "li_", "out_"))
        )

    per = cells // depth

    def shard_a(s):
        at = pl.ds(pl.multiple_of(lax.rem(s, per) * depth, depth), depth)
        return r.low_t.at[s // per, :, at]

    sc = {
        "q": scatter("q", block_rows(r.w_q, ranks), by_columns(d_mid // groups), Corner(r.tw_q, depth, d_mid)),
        "o": scatter("o", block_rows(r.w_o, ranks), by_columns(d_in // groups), r.tw_o.at),
        "h": scatter("h", lambda s: r.g_h.at[s], by_rows(r.g_h.shape[1] // groups), r.tw_h.at),
        "c": scatter("c", block_rows(r.w_c, ranks), by_columns(d_in // groups), r.tw_c.at),
        "a": scatter("a", shard_a, by_rows(d_mid // groups), Corner(r.tw_q, r.tw_q.shape[0] // 2, depth)),
    }
    returned = [
        net.plan(rows_of(r.blocks, peer[1], size), rows_of(r.back_in, place.s, size), peer)
        for peer in place.row_peers
    ]
    asked_back = [
        net.plan(r.kv_part.at[:, at_block(peer[1])], r.kv_in.at[k], peer)
        for k, peer in enumerate(place.row_peers)
    ]

    def own_boxes(pooled, joined, d_branch, d_pooled):
        boxes = r.cotangent.shape[1]
        number = jnp.concatenate([r.box_in[n, 0:1, :] for n in range(ranks)], axis=0)
        box = lax.broadcasted_iota(jnp.int32, (ranks, boxes), 1)
        hits = jnp.concatenate(
            [jnp.where(number[:, k : k + 1] == box, 1.0, 0.0) for k in range(capacity)], axis=0
        ).astype(LOW)
        picks = [tdot(perm, hits).astype(LOW) for perm in perms]
        across = lax.broadcasted_iota(jnp.int32, (boxes, boxes), 0) == lax.broadcasted_iota(
            jnp.int32, (boxes, boxes), 1
        )

        def upright(value):
            wide = jnp.broadcast_to(value.astype(F32), (boxes, boxes))
            return jnp.sum(jnp.where(across, wide, 0.0), axis=1, keepdims=True)

        bank_row = lax.broadcasted_iota(jnp.int32, (boxes, ranks * entry), 1)
        inner = lax.rem(bank_row, entry)
        spot = (bank_row // entry * entries + inner).astype(F32)
        start, length = upright(r.win_start[...]), upright(r.win_len[...])
        window = (inner < entries) & (spot >= start) & (spot < start + length)
        for k in range(2):
            pooled[:, k * half : (k + 1) * half] = tdot(picks[k], r.arrived[...])
        joined[:, 0:d_in] = pooled[...].astype(LOW)
        pooled_low = joined.at[:, 0:d_in]
        keys, vals = r.kv_all.at[0], r.kv_all.at[1]
        scale = d_mid ** (-0.5)
        q.ready()
        queries = jnp.dot(pooled_low[...], r.w_q[...], preferred_element_type=F32).astype(LOW)
        scores = jnp.where(window, ndot(queries, keys[...]) * scale, -1e30)
        raised = jnp.exp(scores - jnp.max(scores, axis=1, keepdims=True))
        attend = raised / jnp.sum(raised, axis=1, keepdims=True)
        attend_low = attend.astype(LOW)
        mixture = jnp.dot(attend_low, vals[...], preferred_element_type=F32)
        centred = mixture - jnp.mean(mixture, axis=1, keepdims=True)
        inverse_z = lax.rsqrt(jnp.mean(centred * centred, axis=1, keepdims=True) + 1e-05)
        hat_z = centred * inverse_z
        pre_ln = r.ln_gain[...] * hat_z + r.ln_bias[...]
        sig_z = sigma(pre_ln)
        low_r = (pre_ln * sig_z).astype(LOW)
        slope_z = sig_z * (1.0 + pre_ln * (1.0 - sig_z))
        o.ready()
        for k in range(4):
            on = slice(k * (d_in // 4), (k + 1) * (d_in // 4))
            into = slice(d_in + k * (d_in // 4), d_in + (k + 1) * (d_in // 4))
            joined[:, into] = (
                pooled[:, on] + jnp.dot(low_r, r.w_o[:, on], preferred_element_type=F32)
            ).astype(LOW)
        h.ready()
        logits = (
            ndot(joined[...], r.w_h[...]) + r.head_bias[...]
        )
        likely = jax.nn.sigmoid(logits)
        r.out_probs[...] = likely
        d_logit = (jnp.transpose(r.cotangent[...]) * (likely * (1.0 - likely))).astype(LOW)
        for k in range(4):
            on = slice(k * (d_in // 4), (k + 1) * (d_in // 4))
            below = slice(d_in + k * (d_in // 4), d_in + (k + 1) * (d_in // 4))
            upper = jnp.dot(d_logit, r.w_h[:, below], preferred_element_type=F32)
            d_branch[:, on] = upper.astype(LOW)
            pooled[:, on] = (
                jnp.dot(d_logit, r.w_h[:, on], preferred_element_type=F32) + upper
            )
        d_ln = ndot(d_branch[...], r.w_o[...]) * slope_z
        d_hat = d_ln * r.ln_gain[...]
        d_mixture = (
            inverse_z
            * (
                d_hat
                - jnp.mean(d_hat, axis=1, keepdims=True)
                - hat_z * jnp.mean(d_hat * hat_z, axis=1, keepdims=True)
            )
        ).astype(LOW)
        d_attend = ndot(d_mixture, vals[...])
        d_scores = (attend * (d_attend - jnp.sum(d_attend * attend, axis=1, keepdims=True))).astype(LOW)
        d_queries = (jnp.dot(d_scores, keys[...], preferred_element_type=F32) * scale).astype(LOW)
        for k in range(4):
            on = slice(k * (d_in // 4), (k + 1) * (d_in // 4))
            d_pooled[:, on] = (pooled[:, on] + ndot(d_queries, r.w_q[on, :])).astype(LOW)
        net.settle(pushed)
        r.blocks[...] = (
            jnp.dot(picks[0], d_pooled[:, 0:half], preferred_element_type=F32)
            + jnp.dot(picks[1], d_pooled[:, half:d_in], preferred_element_type=F32)
        ).astype(LOW)
        for copy in returned:
            copy.start()
        r.back_in[mine, :] = r.blocks[mine, :]

        net.settle(q.sent() + o.sent() + kv + every)
        net.settle_some(q.some + o.some)
        r.kv_part[0] = (tdot(d_scores, queries) * scale).astype(LOW)
        r.kv_part[1] = tdot(attend_low, d_mixture).astype(LOW)
        for k in range(4):
            on = slice(k * (d_in // 4), (k + 1) * (d_in // 4))
            r.w_q[on, :] = tdot(joined[:, on], d_queries).astype(LOW)
            r.w_o[:, on] = tdot(low_r, d_branch[:, on]).astype(LOW)
        width = 2 * depth
        classes = d_logit.shape[1]
        share = classes // groups
        held, kind = (
            lax.broadcasted_iota(jnp.int32, (classes, r.g_h.shape[1]), n) for n in range(2)
        )
        padded_class = held // share * (r.g_h.shape[1] // groups) + lax.rem(held, share)
        spaced = jnp.where(kind == padded_class, 1.0, 0.0).astype(LOW)
        d_spaced = jnp.dot(d_logit, spaced, preferred_element_type=F32).astype(LOW)
        for s in range(ranks):
            r.g_h[s] = tdot(d_spaced, joined[:, s * width : (s + 1) * width]).astype(LOW)
        quarter = d_mid // 4
        r.own4[...] = jnp.zeros_like(r.own4)
        for n, value in enumerate(
            (jnp.sum(d_ln * hat_z, axis=0, keepdims=True), jnp.sum(d_ln, axis=0, keepdims=True))
        ):
            for k in range(4):
                r.own4[4 * n + k : 4 * n + k + 1, d_in // 4 : d_in // 4 + quarter] = value[
                    :, k * quarter : (k + 1) * quarter
                ]
        r.own4[0:1, d_in // 4 + quarter : d_in // 4 + quarter + classes] = jnp.sum(
            d_logit.astype(F32), axis=0, keepdims=True
        )
        sc["h"].pair()
        sc["q"].pair()
        sc["o"].pair()
        for copy in asked_back:
            copy.start()
        sc["h"].batch()
        sc["q"].batch()


    boxes = r.cotangent.shape[1]
    pl.run_scoped(
        own_boxes,
        pltpu.VMEM((boxes, d_in), F32),
        pltpu.VMEM((boxes, 2 * d_in), LOW),
        pltpu.VMEM((boxes, d_in), LOW),
        pltpu.VMEM((boxes, d_in), LOW),
    )
    keep_hat_a.wait()
    for copy in returned:
        copy.wait_recv()

    chips = place.chips
    dkv, dkv_in, dkv_own, dkv_all = r.kv_part, r.kv_in, r.kv_own, r.kv_all

    def backward(d_pre, g_b):
        sc["b"] = scatter("b", block_rows(g_b, ranks), by_columns(d_mid // groups), r.tw_b.at)
        hat_c, slope, d_c, back = r.hat_c, r.x, r.x, r.back_in
        acc = r.acc
        acc[...] = jnp.zeros_like(acc)
        tile = 128

        @pl.loop(0, cells // tile)
        def _(t):
            at = pl.ds(pl.multiple_of(t * tile, tile), tile)
            for h in range(2):
                on = slice(h * half, (h + 1) * half)
                grad = jnp.dot(
                    r.et[h, at, :], back[...], preferred_element_type=F32
                ) * slope[at, on].astype(F32)
                d_pre[at, on] = grad.astype(LOW)
                acc[0, :, on] += folded(grad)
                acc[1, :, on] += folded(grad * hat_c[at, on].astype(F32))

        own4 = r.own4
        spread(own4, [jnp.sum(acc[n], axis=0, keepdims=True) for n in range(2)])
        sums[3].start()
        net.settle(sums[2].sent() + returned + h.sent())
        net.settle_some(h.some)
        sc["h"].forward()
        sc["q"].forward()
        for copy in asked_back:
            copy.wait_recv()
        own = pl.ds(pl.multiple_of(place.s * entry, entry), entry)
        for n in range(2):
            total = dkv[n, own, :].astype(F32)
            for k in range(ranks - 1):
                total = total + dkv_in[k, n].astype(F32)
            dkv_own[n] = total.astype(LOW)
            dkv_all[n, own, :] = total.astype(LOW)
        shared = [
            net.push(dkv_own, dkv_all.at[:, own], peer)
            for peer in place.row_peers
        ]

        total = sums[3].finish(sc["o"].batch)
        r.out_head[...] = total
        shift_c = gathered(total, 0, d_in // 4) / total_count
        gain_c = gathered(total, 1, d_in // 4) / total_count
        scale_c = r.scale_c[...]

        w_c, hat_b, d_act = r.w_c, r.hat_b, r.middle
        acc[...] = jnp.zeros_like(acc)
        norm_b, norm_a = r.norm_b, r.norm_a

        @pl.loop(0, cells // 256)
        def _(t):
            at = pl.ds(pl.multiple_of(t * 256, 256), 256)
            grad = scale_c * (
                d_pre[at, :].astype(F32) - shift_c - hat_c[at, :].astype(F32) * gain_c
            )
            low = grad.astype(LOW)
            d_c[at, :] = low
            hat = hat_b[at, :].astype(F32)
            back_b = ndot(low, w_c[...]) * slope_of(norm_b[0:1, :] * hat + norm_b[1:2, :])
            d_act[at, :] = back_b
            acc[0, :, 0:d_mid] += folded(back_b)
            acc[1, :, 0:d_mid] += folded(back_b * hat)

        reload = pltpu.make_async_copy(r.features, r.hat_c, local.at[20])
        reload.start()
        own5 = r.own5
        spread(own5, [jnp.sum(acc[n, :, 0:d_mid], axis=0, keepdims=True) for n in range(2)])
        sums[4].start()
        net.settle(sums[3].sent() + asked_back)
        net.settle([copy for key in "hqo" for copy in sc[key].sent(3 if key in "hq" else 2)])
        net.settle(c.sent())
        wide = 256

        @pl.loop(0, d_in // wide)
        def _(t):
            at = pl.ds(pl.multiple_of(t * wide, wide), wide)
            w_c[:, at] = jnp.dot(
                r.low_bt[...], d_c[:, at], preferred_element_type=F32
            ).astype(LOW)

        sc["c"].pair()
        sc["h"].line()
        sc["q"].line()
        for copy in shared:
            copy.wait_recv()
        kv_out, kv_in = r.kv_out, r.kv_back
        for n in range(2):
            kv_out[n] = tdot(r.bank_cols[...], dkv_all[n]).astype(LOW)


        share = d_mid // groups
        crossing = [
            net.plan(
                kv_out.at[:, :, pl.ds(pl.multiple_of(peer[0] * share, share), share)],
                kv_in.at[k],
                peer,
            )
            for k, peer in enumerate(place.batch_peers)
        ]

        def middle():
            for copy in crossing:
                copy.start()
            sc["o"].forward()
            sc["c"].batch()

        total = sums[4].finish(middle)
        r.out_b_sums[...] = total
        shift_b = gathered(total, 0, d_mid // 4) / total_count
        gain_b = gathered(total, 1, d_mid // 4) / total_count

        d_b, d_up, d_down = (r.low_up, r.low_a, r.low_down), r.low_b, r.hat_a

        def halo_back(t, way):
            at = pl.ds(pl.multiple_of(t * big, big), big)
            return pltpu.make_async_remote_copy(
                src_ref=d_b[1].at[at],
                dst_ref=(d_up if way == 0 else d_down).at[at],
                send_sem=r.back_send.at[way, t],
                recv_sem=r.back_recv.at[way, t],
                device_id=(place.g, place.s + 1 if way == 0 else place.s - 1),
                device_id_type=MESH,
            )

        @pl.when(first)
        def _():
            d_up[...] = jnp.zeros_like(d_up)

        @pl.when(last)
        def _():
            d_down[...] = jnp.zeros_like(d_down)

        @pl.loop(0, tiles)
        def _(t):
            at = pl.ds(pl.multiple_of(t * big, big), big)
            grad = norm_b[2:3, :] * (
                d_act[at, :] - shift_b - hat_b[at, :].astype(F32) * gain_b
            )
            d_b[1][at, :] = grad.astype(LOW)

            @pl.when(jnp.logical_not(last))
            def _():
                halo_back(t, 0).start()

            @pl.when(jnp.logical_not(first))
            def _():
                halo_back(t, 1).start()

            d_b[0][at, :] = from_right(grad, columns).astype(LOW)
            d_b[2][at, :] = from_left(grad, columns).astype(LOW)

        @pl.loop(0, 3)
        def _(i):
            for j in range(3):
                at = pl.ds(pl.multiple_of((3 * i + j) * d_mid, d_mid), d_mid)
                g_b[at, :] = jnp.dot(
                    r.low_t[i], d_b[j][...], preferred_element_type=F32
                ).astype(LOW)

        more = pltpu.make_async_copy(r.far_hat_a, hat_b, local.at[18])
        more.start()
        sc["b"].pair()
        sc["c"].forward()
        sc["o"].line()
        sc["b"].batch()

        more.wait()
        w_b, hat_a = r.w_b, hat_b
        acc[...] = jnp.zeros_like(acc)

        @pl.loop(0, tiles)
        def _(t):
            at = pl.ds(pl.multiple_of(t * big, big), big)

            @pl.when(jnp.logical_not(first))
            def _():
                halo_back(t, 0).wait_recv()

            @pl.when(jnp.logical_not(last))
            def _():
                halo_back(t, 1).wait_recv()

            parts = []
            for j in range(3):
                taps = [w_b[(3 * i + j) * d_mid : (3 * i + j + 1) * d_mid, :] for i in range(3)]
                parts.append(
                    ndot(d_down[at, :], taps[0]) + ndot(d_b[1][at, :], taps[1]) + ndot(d_up[at, :], taps[2])
                )
            grad = from_right(parts[0], columns) + parts[1] + from_left(parts[2], columns)
            hat = hat_a[at, :].astype(F32)
            grad = grad * slope_of(norm_a[0:1, :] * hat + norm_a[1:2, :])
            d_act[at, :] = grad
            acc[0, :, 0:d_mid] += folded(grad)
            acc[1, :, 0:d_mid] += folded(grad * hat)

        own6 = r.own6
        spread(own6, [jnp.sum(acc[n, :, 0:d_mid], axis=0, keepdims=True) for n in range(2)])
        sums[5].start()
        net.settle(sums[4].sent() + shared + crossing)
        net.settle(sc["c"].sent(3) + sc["b"].sent(2) + sc["h"].third + sc["q"].third)
        net.settle([copies[2] for copies in sc["o"].second])
        sc["c"].line()

        def late():
            sc["b"].forward()

        total = sums[5].finish(late)
        r.out_a_sums[...] = total
        shift_a = gathered(total, 0, d_mid // 4) / total_count
        gain_a = gathered(total, 1, d_mid // 4) / total_count
        d_a, d_at = d_b[0], r.low_bt

        @pl.loop(0, tiles)
        def _(t):
            at = pl.ds(pl.multiple_of(t * big, big), big)
            grad = norm_a[2:3, :] * (
                d_act[at, :] - shift_a - hat_a[at, :].astype(F32) * gain_a
            )
            d_a[at, :] = grad.astype(LOW)
            d_at[:, at] = jnp.transpose(grad).astype(LOW)

        reload.wait()
        x = r.hat_c

        @pl.loop(0, ranks)
        def _(s):
            shard_a(s)[...] = jnp.dot(
                d_at[...],
                x[:, pl.ds(pl.multiple_of(s * depth, depth), depth)],
                preferred_element_type=F32,
            ).astype(LOW)

        sc["a"].pair()
        sc["b"].line()
        sc["a"].batch()
        out_x = r.out_x

        def leave(t):
            at = pl.ds(pl.multiple_of(t * tile, tile), tile)
            return pltpu.make_async_copy(d_pre.at[at], out_x.at[at], local.at[21 + t])

        @pl.loop(0, cells // tile)
        def _(t):
            at = pl.ds(pl.multiple_of(t * tile, tile), tile)
            d_pre[at, :] = (
                ndot(d_a[at, :], r.w_a[...]) + d_pre[at, :].astype(F32)
            ).astype(LOW)
            leave(t).start()

        sc["a"].forward()
        for key in "qohc":
            sc[key].finish()
        sc["a"].line()
        sc["b"].finish()
        for copy in crossing:
            copy.wait_recv()
        for n, key in enumerate((r.out_k, r.out_v)):
            total = kv_out[n, :, pl.ds(pl.multiple_of(place.g * share, share), share)].astype(F32)
            for k in range(groups - 1):
                total = total + kv_in[k, n].astype(F32)
            key[...] = total
        sc["a"].finish()

        @pl.loop(0, cells // tile)
        def _(t):
            leave(t).wait()

        @pl.loop(0, tiles)
        def _(t):
            @pl.when(jnp.logical_not(last))
            def _():
                halo_back(t, 0).wait_send()

            @pl.when(jnp.logical_not(first))
            def _():
                halo_back(t, 1).wait_send()

        net.close()

    pl.run_scoped(
        backward,
        pltpu.VMEM((cells, d_in), LOW),
        pltpu.VMEM(r.w_b.shape, LOW),
    )


class Refs:
    def __init__(self, names, refs, **more):
        self.__dict__.update(zip(names, refs), **more)


def run_kernel(body, geometry, channel, held, far, outs, far_outs, scratch):
    anywhere = pl.BlockSpec(memory_space=pl.ANY)
    inside = pl.BlockSpec(memory_space=pltpu.VMEM)
    names = [*held, *far, *outs, *far_outs, *scratch]
    scalars = pl.BlockSpec(memory_space=pltpu.SMEM)
    results = pl.pallas_call(
        lambda *refs: body(geometry, Refs(names, refs)),
        out_shape=(*outs.values(), *far_outs.values()),
        in_specs=[scalars if v.ndim == 1 else inside for v in held.values()] + [anywhere] * len(far),
        out_specs=(inside,) * len(outs) + (anywhere,) * len(far_outs),
        scratch_shapes=[*scratch.values()],
        compiler_params=pltpu.CompilerParams(
            collective_id=channel, has_side_effects=True, vmem_limit_bytes=64 << 20
        ),
    )(*held.values(), *far.values())
    return Refs([*outs, *far_outs], results)


def shape(kind, *sizes):
    return jax.ShapeDtypeStruct(sizes, kind)


def room(kind, *sizes):
    return pltpu.VMEM(sizes, kind)


def run_step(geometry, held, far):
    cells, d_in, d_mid, columns, total_count, capacity, entries, samples, clips = geometry
    groups, ranks = lax.axis_size("batch"), lax.axis_size("rows")
    chips, dma = ranks // 2, pltpu.SemaphoreType.DMA
    slots = ranks * 2 * capacity
    entry = -(-entries // 16) * 16
    bank = ranks * entry
    classes, boxes = held["cotangent"].shape
    spaced = groups * (-(-classes // groups // 16) * 16)
    spatial = far["w_spatial"].shape[0] * ranks
    half, depth = d_in // 2, d_in // ranks
    head = d_in // 4 + d_mid // 4 + spaced
    share = dict(
        q=(d_in // ranks, d_mid // groups),
        o=(d_mid // ranks, d_in // groups),
        h=(spaced // groups, 2 * d_in // ranks),
        c=(d_mid // ranks, d_in // groups),
        b=(spatial // ranks, d_mid // groups),
        a=(d_mid // groups, d_in // ranks),
    )
    block = dict(
        q=(d_in // ranks, d_mid),
        o=(d_mid // ranks, d_in),
        h=(spaced, 2 * d_in // ranks),
        c=(d_mid // ranks, d_in),
        b=(spatial // ranks, d_mid),
        a=(d_mid, d_in // ranks),
    )
    outs = dict(
        out_probs=shape(F32, boxes, classes),
        out_head=shape(F32, 8, head),
        out_b_sums=shape(F32, 8, d_mid // 4),
        out_a_sums=shape(F32, 8, d_mid // 4),
        out_k=shape(F32, depth, d_mid // groups),
        out_v=shape(F32, depth, d_mid // groups),
    )
    far_outs = dict(out_x=shape(LOW, cells, d_in), far_hat_a=shape(LOW, cells, d_mid))
    scratch = dict(
        x=room(LOW, cells, d_in),
        hat_c=room(LOW, cells, d_in),
        w_a=room(LOW, d_in, d_mid),
        w_b=room(LOW, spatial, d_mid),
        w_c=room(LOW, d_mid, d_in),
        w_q=room(LOW, d_in, d_mid),
        w_o=room(LOW, d_mid, d_in),
        w_h=room(LOW, classes, 2 * d_in),
        g_h=room(LOW, ranks, spaced, 2 * d_in // ranks),
        middle=room(F32, cells, d_mid),
        hat_a=room(LOW, cells, d_mid),
        hat_b=room(LOW, cells, d_mid),
        low_a=room(LOW, cells, d_mid),
        low_up=room(LOW, cells, d_mid),
        low_down=room(LOW, cells, d_mid),
        low_b=room(LOW, cells, d_mid),
        low_t=room(LOW, 3, d_mid, cells),
        low_bt=room(LOW, d_mid, cells),
        bank16=room(LOW, entry, d_in),
        bank_cols=room(LOW, bank, depth),
        box16=room(jnp.int32, ranks, 8, 128),
        box_in=room(jnp.int32, ranks, 8, 128),
        slot_cells=room(jnp.int32, capacity, ranks, samples),
        slot_weights=room(F32, capacity, ranks, samples),
        et=room(LOW, 2, cells, slots),
        kv_part=room(LOW, 2, bank, d_mid),
        kv_in=room(LOW, ranks - 1, 2, entry, d_mid),
        kv_own=room(LOW, 2, entry, d_mid),
        kv_all=room(LOW, 2, bank, d_mid),
        kv_out=room(LOW, 2, depth, d_mid),
        kv_back=room(LOW, groups - 1, 2, depth, d_mid // groups),
        norm_a=room(F32, 8, d_mid),
        norm_b=room(F32, 8, d_mid),
        scale_c=room(F32, 1, d_in),
        centre_c=room(F32, 8, d_in),
        acc=room(F32, 2, 8, d_in),
        pieces=room(F32, slots, half),
        blocks=room(LOW, slots, half),
        arrived=room(LOW, slots, half),
        back_in=room(LOW, slots, half),
        halo_send=dma((2, cells // 256)),
        halo_recv=dma((2, cells // 256)),
        back_send=dma((2, cells // 256)),
        back_recv=dma((2, cells // 256)),
        local=dma((32,)),
        send=dma((400,)),
        recv=dma((400,)),
    )
    scratch.update(tw_q=room(LOW, chips * depth, d_mid))
    narrow = d_mid // 4
    for n, width in enumerate((narrow, narrow, d_in // 4, head, narrow, narrow)):
        scratch["own%d" % (n + 1)] = room(F32, 8, width)
        scratch["mid%d" % (n + 1)] = room(F32, 8, width)
        scratch["rows%d" % (n + 1)] = room(F32, ranks - 1, 8, width)
        scratch["batch%d" % (n + 1)] = room(F32, groups - 1, 8, width)
    for key in share:
        outs["out_" + key] = shape(F32, *share[key])
        if key not in "qa":
            scratch["tw_" + key] = room(LOW, chips, *block[key])
        scratch["ba_" + key] = room(LOW, groups - 1, chips, *share[key])
        scratch["pa_" + key] = room(LOW, chips, *share[key])
        scratch["li_" + key] = room(LOW, chips - 1, *share[key])
    return run_kernel(step_kernel, geometry, 11, held, far, outs, far_outs, scratch)


def finish_kernel(r):
    chunk = r.in_x.shape[0] // 8

    def across(n, leave):
        at = pl.ds(n * chunk, chunk)
        source, target = (r.stage, r.x) if leave else (r.in_x, r.stage)
        return pltpu.make_async_copy(source.at[at], target.at[at], r.local.at[leave, n])

    for n in range(8):
        across(n, 0).start()
    for n in range(8):
        across(n, 0).wait()
        across(n, 1).start()
    r.probs[...] = jnp.transpose(r.in_probs[...])
    r.a[...] = jnp.transpose(r.in_a[...])
    r.b[...] = r.in_b[...]
    r.c[...] = r.in_c[...]
    r.q[...] = r.in_q[...]
    r.k[...] = r.in_k[...]
    r.v[...] = r.in_v[...]
    r.o[...] = r.in_o[...]
    r.h[...] = r.in_h[0 : r.h.shape[0], :]
    r.bias_a[...], r.gain_a[...] = r.in_a_sums[0:4, :], r.in_a_sums[4:8, :]
    r.bias_b[...], r.gain_b[...] = r.in_b_sums[0:4, :], r.in_b_sums[4:8, :]
    lanes = r.ln_gain.shape[1]
    per = r.gain_c.shape[0] // 4
    for n in range(4):
        for k in range(per):
            on = slice(k * lanes, (k + 1) * lanes)
            r.bias_c[per * n + k : per * n + k + 1, :] = r.in_head[n : n + 1, on]
            r.gain_c[per * n + k : per * n + k + 1, :] = r.in_head[4 + n : 5 + n, on]
    on = slice(per * lanes, (per + 1) * lanes)
    r.ln_gain[...], r.ln_bias[...] = r.in_head[0:4, on], r.in_head[4:8, on]
    at = (per + 1) * lanes
    r.head_bias[...] = r.in_head[0:1, at : at + r.head_bias.shape[1]]
    for n in range(8):
        across(n, 1).wait()


def run_finish(probs, two, groups, d_mid, classes):
    held = dict(
        in_probs=probs,
        in_a=two.out_a,
        in_b=two.out_b,
        in_c=two.out_c,
        in_q=two.out_q,
        in_k=two.out_k,
        in_v=two.out_v,
        in_o=two.out_o,
        in_h=two.out_h,
        in_a_sums=two.out_a_sums,
        in_b_sums=two.out_b_sums,
        in_head=two.out_head,
    )
    like = lambda v: shape(F32, *v.shape)
    lanes = two.out_a_sums.shape[1]
    row = shape(F32, 4, lanes)
    wide = shape(F32, 4 * (two.out_x.shape[1] // 4 // lanes), lanes)
    outs = dict(
        probs=shape(F32, *probs.shape[::-1]),
        a=shape(F32, *two.out_a.shape[::-1]),
        b=like(two.out_b),
        c=like(two.out_c),
        q=like(two.out_q),
        k=like(two.out_k),
        v=like(two.out_v),
        o=like(two.out_o),
        h=shape(F32, classes // groups, two.out_h.shape[1]),
        gain_a=row,
        bias_a=row,
        gain_b=row,
        bias_b=row,
        gain_c=wide,
        bias_c=wide,
        ln_gain=row,
        ln_bias=row,
        head_bias=shape(F32, 1, classes),
    )
    far_outs = dict(x=shape(LOW, *two.out_x.shape))
    anywhere = pl.BlockSpec(memory_space=pl.ANY)
    inside = pl.BlockSpec(memory_space=pltpu.VMEM)
    names = [*held, "in_x", *outs, *far_outs, "stage", "local"]
    results = pl.pallas_call(
        lambda *refs: finish_kernel(Refs(names, refs)),
        out_shape=(*outs.values(), *far_outs.values()),
        in_specs=[inside] * len(held) + [anywhere],
        out_specs=(inside,) * len(outs) + (anywhere,),
        scratch_shapes=[room(LOW, *two.out_x.shape), pltpu.SemaphoreType.DMA((2, 8))],
        compiler_params=pltpu.CompilerParams(vmem_limit_bytes=64 << 20),
    )(*held.values(), two.out_x)
    return Refs([*outs, *far_outs], results)


def fused_device(
    features,
    w_reduce,
    w_spatial,
    w_expand,
    query_weight,
    w_key,
    w_value,
    w_out,
    w_head,
    gain_a,
    bias_a,
    gain_b,
    bias_b,
    gain_c,
    bias_c,
    ln_gain,
    ln_bias,
    head_bias,
    bank,
    piece_box,
    piece_clip,
    send_count,
    sample_pos,
    sample_weight,
    win_start,
    win_len,
    prob_cotangent,
):
    groups, ranks = lax.axis_size("batch"), lax.axis_size("rows")
    clip_dev, row_dev, columns, d_in = features.shape
    d_mid = w_reduce.shape[1]
    cells = clip_dev * row_dev * columns
    total_count = cells * ranks * groups
    capacity = piece_box.shape[1]
    samples = sample_pos.shape[1] // capacity
    entries = bank.shape[0]
    geometry = (cells, d_in, d_mid, columns, total_count, capacity, entries, samples, clip_dev)
    line = lambda v: v.reshape(1, -1)
    held = dict(
        bank=bank,
        piece_box=piece_box,
        piece_clip=piece_clip,
        send_count=send_count,
        sample_pos=sample_pos,
        sample_weight=sample_weight,
        gain_a=line(gain_a),
        bias_a=line(bias_a),
        gain_b=line(gain_b),
        bias_b=line(bias_b),
        gain_c=line(gain_c),
        bias_c=line(bias_c),
        ln_gain=line(ln_gain),
        ln_bias=line(ln_bias),
        win_start=line(win_start),
        win_len=line(win_len),
        head_bias=line(head_bias),
        cotangent=prob_cotangent.T,
    )
    far = dict(
        features=features.reshape(cells, d_in),
        w_reduce=w_reduce,
        w_spatial=w_spatial,
        w_expand=w_expand,
        w_query=query_weight,
        w_out=w_out,
        w_head=w_head.T,
        w_key=w_key,
        w_value=w_value,
    )
    done = run_step(geometry, held, far)
    last = run_finish(done.out_probs, done, groups, d_mid, prob_cotangent.shape[1])
    flat = lambda v: v.reshape(-1)
    return (
        last.probs.T,
        last.x.reshape(features.shape),
        last.a,
        last.b,
        last.c,
        last.q,
        last.k,
        last.v,
        last.o,
        last.h.T,
        flat(last.gain_a),
        flat(last.bias_a),
        flat(last.gain_b),
        flat(last.bias_b),
        flat(last.gain_c),
        flat(last.bias_c),
        flat(last.ln_gain),
        flat(last.ln_bias),
        flat(last.head_bias),
    )


def plain_normalize(field, total_count):
    sums, squares = lax.psum((jnp.sum(field, 0), jnp.sum(field * field, 0)), ("batch", "rows"))
    centre_value = sums / total_count
    inverse = lax.rsqrt(squares / total_count - centre_value * centre_value + 1e-05)
    return ((field - centre_value) * inverse, inverse)


def plain_totals(grad, normed):
    return lax.psum((jnp.sum(grad, 0), jnp.sum(grad * normed, 0)), ("batch", "rows"))


def plain_device(
    features,
    w_reduce,
    w_spatial,
    w_expand,
    query_weight,
    w_key,
    w_value,
    w_out,
    w_head,
    gain_a,
    bias_a,
    gain_b,
    bias_b,
    gain_c,
    bias_c,
    ln_gain,
    ln_bias,
    head_bias,
    bank,
    piece_box,
    piece_clip,
    send_count,
    sample_pos,
    sample_weight,
    win_start,
    win_len,
    prob_cotangent,
):
    owners = lax.axis_size("rows")
    clip_dev, row_dev, col_count, d_in = features.shape
    cell_count = clip_dev * row_dev * col_count
    total_count = cell_count * owners * lax.axis_size("batch")
    w_a, w_b, w_c, w_q, w_k, w_v, w_o, w_h = (
        lax.all_gather(w_reduce, "rows", axis=0, tiled=True),
        lax.all_gather(w_spatial, "rows", axis=0, tiled=True),
        lax.all_gather(w_expand, "rows", axis=0, tiled=True),
        lax.all_gather(query_weight, "rows", axis=0, tiled=True),
        lax.all_gather(w_key, "rows", axis=0, tiled=True),
        lax.all_gather(w_value, "rows", axis=0, tiled=True),
        lax.all_gather(w_out, "rows", axis=0, tiled=True),
        lax.all_gather(w_head, "rows", axis=0, tiled=True),
    )
    d_mid = w_a.shape[1]
    flat_x = features.reshape(cell_count, d_in)
    pre_a = jnp.dot(flat_x, w_a, preferred_element_type=jnp.float32)
    hat_a, inverse_a = plain_normalize(pre_a, total_count)
    act_a = gain_a * hat_a + bias_a
    low_a = jax.nn.silu(act_a).astype(jnp.bfloat16)
    halo_a = padded(low_a.reshape(clip_dev, row_dev, col_count, d_mid), (("rows", 1),), 1)
    halo_a = jnp.pad(halo_a, ((0, 0), (0, 0), (1, 1), (0, 0)))
    window_a = jnp.concatenate(
        [
            halo_a[:, row_step : row_step + row_dev, col_step : col_step + col_count]
            for row_step in range(3)
            for col_step in range(3)
        ],
        axis=3,
    ).reshape(cell_count, 9 * d_mid)
    pre_b = jnp.dot(window_a, w_b, preferred_element_type=jnp.float32)
    hat_b, inverse_b = plain_normalize(pre_b, total_count)
    act_b = gain_b * hat_b + bias_b
    low_b = jax.nn.silu(act_b).astype(jnp.bfloat16)
    pre_c = jnp.dot(low_b, w_c, preferred_element_type=jnp.float32)
    hat_c, inverse_c = plain_normalize(pre_c, total_count)
    pre_out = gain_c * hat_c + bias_c + flat_x.astype(jnp.float32)
    fmap = jax.nn.silu(pre_out).astype(jnp.bfloat16)
    capacity = piece_box.shape[1]
    samples = sample_pos.shape[1] // capacity
    slot_count = owners * capacity
    sample_cells = (
        piece_clip[:, :, None] * (row_dev * col_count)
        + sample_pos.reshape(owners, capacity, samples)
    ).reshape(slot_count, samples)
    is_live = (jnp.arange(capacity)[None, :] < send_count[:, None]).reshape(slot_count)
    slot_weights = sample_weight.reshape(slot_count, samples) * is_live[:, None].astype(jnp.float32)
    cell_ids = jnp.arange(cell_count)[None, :]
    interp_sum = jnp.zeros((slot_count, cell_count), jnp.float32)
    for sample_index in range(samples):
        interp_sum = interp_sum + jnp.where(
            sample_cells[:, sample_index, None] == cell_ids,
            slot_weights[:, sample_index, None],
            0.0,
        )
    interpolated_value = interp_sum.astype(jnp.bfloat16)
    region_parts = (
        jnp.dot(interpolated_value, fmap, preferred_element_type=jnp.float32)
        .astype(jnp.bfloat16)
        .reshape(owners, capacity, d_in)
    )
    arrived, arrived_box = (
        lax.all_to_all(region_parts, "rows", split_axis=0, concat_axis=0, tiled=True),
        lax.all_to_all(piece_box, "rows", split_axis=0, concat_axis=0, tiled=True),
    )
    box_dev = win_start.shape[0]
    flat_box = arrived_box.reshape(slot_count)
    owner_hits = (flat_box[None, :] == jnp.arange(box_dev)[:, None]).astype(jnp.bfloat16)
    pooled = jnp.dot(
        owner_hits, arrived.reshape(slot_count, d_in), preferred_element_type=jnp.float32
    )
    pooled_low = pooled.astype(jnp.bfloat16)
    keys_own = jnp.dot(bank, w_k, preferred_element_type=jnp.float32).astype(jnp.bfloat16)
    values_own = jnp.dot(bank, w_v, preferred_element_type=jnp.float32).astype(jnp.bfloat16)
    key_rows, value_rows = (
        lax.all_gather(keys_own, "rows", axis=0, tiled=True),
        lax.all_gather(values_own, "rows", axis=0, tiled=True),
    )
    bank_length = key_rows.shape[0]
    queries = jnp.dot(pooled_low, w_q, preferred_element_type=jnp.float32).astype(jnp.bfloat16)
    score_scale = d_mid ** (-0.5)
    scores = ndot(queries, key_rows) * score_scale
    positions = jnp.arange(bank_length)[None, :]
    window_mask = (positions >= win_start[:, None]) & (positions < (win_start + win_len)[:, None])
    attend = jax.nn.softmax(jnp.where(window_mask, scores, -1e30), axis=-1)
    attend_low = attend.astype(jnp.bfloat16)
    mixture = jnp.dot(attend_low, value_rows, preferred_element_type=jnp.float32)
    centred = mixture - jnp.mean(mixture, axis=-1, keepdims=True)
    inverse_z = lax.rsqrt(jnp.mean(centred * centred, axis=-1, keepdims=True) + 1e-05)
    hat_z = centred * inverse_z
    pre_ln = ln_gain * hat_z + ln_bias
    low_r = jax.nn.silu(pre_ln).astype(jnp.bfloat16)
    branch = jnp.dot(low_r, w_o, preferred_element_type=jnp.float32)
    joined = jnp.concatenate([pooled, pooled + branch], axis=1).astype(jnp.bfloat16)
    logits = jnp.dot(joined, w_h, preferred_element_type=jnp.float32) + head_bias
    likely = jax.nn.sigmoid(logits)
    d_logit = (prob_cotangent * (likely * (1.0 - likely))).astype(jnp.bfloat16)
    grad_head_bias = jnp.sum(d_logit.astype(jnp.float32), 0)
    grad_wh = tdot(joined, d_logit)
    d_joined = ndot(d_logit, w_h)
    d_pooled = d_joined[:, :d_in] + d_joined[:, d_in:]
    d_branch = d_joined[:, d_in:].astype(jnp.bfloat16)
    grad_wo = tdot(low_r, d_branch)
    d_ln = ndot(d_branch, w_o) * silu_slope(pre_ln)
    grad_ln_gain = jnp.sum(d_ln * hat_z, 0)
    grad_ln_bias = jnp.sum(d_ln, 0)
    d_hat = d_ln * ln_gain
    d_mixture = (
        inverse_z
        * (
            d_hat
            - jnp.mean(d_hat, axis=-1, keepdims=True)
            - hat_z * jnp.mean(d_hat * hat_z, axis=-1, keepdims=True)
        )
    ).astype(jnp.bfloat16)
    d_attend = ndot(d_mixture, value_rows)
    d_values = tdot(attend_low, d_mixture)
    d_scores = (attend * (d_attend - jnp.sum(d_attend * attend, axis=-1, keepdims=True))).astype(
        jnp.bfloat16
    )
    d_queries = (
        jnp.dot(d_scores, key_rows, preferred_element_type=jnp.float32) * score_scale
    ).astype(jnp.bfloat16)
    d_keys = tdot(d_scores, queries) * score_scale
    grad_wq = tdot(pooled_low, d_queries)
    d_pooled = d_pooled + ndot(d_queries, w_q)
    key_sum, value_sum = side_by_side(
        (d_keys.astype(jnp.bfloat16), d_values.astype(jnp.bfloat16)), "rows", 0, 1
    )
    grad_wk = tdot(bank, key_sum.astype(jnp.bfloat16))
    grad_wv = tdot(bank, value_sum.astype(jnp.bfloat16))
    back_pieces = jnp.take(d_pooled.astype(jnp.bfloat16), flat_box, axis=0).reshape(
        owners, capacity, d_in
    )
    returned = lax.all_to_all(back_pieces, "rows", split_axis=0, concat_axis=0, tiled=True)
    d_fmap = tdot(interpolated_value, returned.reshape(slot_count, d_in))
    d_pre = d_fmap * silu_slope(pre_out)
    head_sums = lax.psum(
        (jnp.sum(d_pre, 0), jnp.sum(d_pre * hat_c, 0), grad_ln_gain, grad_ln_bias, grad_head_bias),
        ("batch", "rows"),
    )
    d_c = norm_back(
        d_pre, hat_c, inverse_c, gain_c, head_sums[0], head_sums[1], total_count
    ).astype(jnp.bfloat16)
    grad_wc = tdot(low_b, d_c)
    d_act_b = ndot(d_c, w_c) * silu_slope(act_b)
    shift_b_sum, gain_b_sum = plain_totals(d_act_b, hat_b)
    d_b = norm_back(d_act_b, hat_b, inverse_b, gain_b, shift_b_sum, gain_b_sum, total_count).astype(
        jnp.bfloat16
    )
    grad_wb = tdot(window_a, d_b)
    halo_d = padded(d_b.reshape(clip_dev, row_dev, col_count, d_mid), (("rows", 1),), 1)
    halo_d = jnp.pad(halo_d, ((0, 0), (0, 0), (1, 1), (0, 0)))
    window_d = jnp.concatenate(
        [
            halo_d[
                :, 2 - row_step : 2 - row_step + row_dev, 2 - col_step : 2 - col_step + col_count
            ]
            for row_step in range(3)
            for col_step in range(3)
        ],
        axis=3,
    ).reshape(cell_count, 9 * d_mid)
    flipped = w_b.reshape(9, d_mid, d_mid).transpose(0, 2, 1).reshape(9 * d_mid, d_mid)
    d_act_a = jnp.dot(window_d, flipped, preferred_element_type=jnp.float32) * silu_slope(act_a)
    shift_a_sum, gain_a_sum = plain_totals(d_act_a, hat_a)
    d_a = norm_back(d_act_a, hat_a, inverse_a, gain_a, shift_a_sum, gain_a_sum, total_count).astype(
        jnp.bfloat16
    )
    grad_wa = tdot(flat_x, d_a)
    grad_input = (ndot(d_a, w_a) + d_pre).astype(jnp.bfloat16).reshape(features.shape)
    partial_sums = (
        lax.psum_scatter(grad_wa, "rows", scatter_dimension=0, tiled=True),
        lax.psum_scatter(grad_wb, "rows", scatter_dimension=0, tiled=True),
        lax.psum_scatter(grad_wc, "rows", scatter_dimension=0, tiled=True),
        lax.psum_scatter(grad_wq, "rows", scatter_dimension=0, tiled=True),
        lax.psum_scatter(grad_wk, "rows", scatter_dimension=0, tiled=True),
        lax.psum_scatter(grad_wv, "rows", scatter_dimension=0, tiled=True),
        lax.psum_scatter(grad_wo, "rows", scatter_dimension=0, tiled=True),
        lax.psum_scatter(grad_wh, "rows", scatter_dimension=0, tiled=True),
    )
    finished = (
        lax.psum_scatter(
            partial_sums[0].astype(jnp.bfloat16), "batch", scatter_dimension=1, tiled=True
        ).astype(jnp.float32),
        lax.psum_scatter(
            partial_sums[1].astype(jnp.bfloat16), "batch", scatter_dimension=1, tiled=True
        ).astype(jnp.float32),
        lax.psum_scatter(
            partial_sums[2].astype(jnp.bfloat16), "batch", scatter_dimension=1, tiled=True
        ).astype(jnp.float32),
        lax.psum_scatter(
            partial_sums[3].astype(jnp.bfloat16), "batch", scatter_dimension=1, tiled=True
        ).astype(jnp.float32),
        lax.psum_scatter(
            partial_sums[4].astype(jnp.bfloat16), "batch", scatter_dimension=1, tiled=True
        ).astype(jnp.float32),
        lax.psum_scatter(
            partial_sums[5].astype(jnp.bfloat16), "batch", scatter_dimension=1, tiled=True
        ).astype(jnp.float32),
        lax.psum_scatter(
            partial_sums[6].astype(jnp.bfloat16), "batch", scatter_dimension=1, tiled=True
        ).astype(jnp.float32),
        lax.psum_scatter(
            partial_sums[7].astype(jnp.bfloat16), "batch", scatter_dimension=1, tiled=True
        ).astype(jnp.float32),
    )
    return (
        likely,
        grad_input,
        finished[0],
        finished[1],
        finished[2],
        finished[3],
        finished[4],
        finished[5],
        finished[6],
        finished[7],
        gain_a_sum,
        shift_a_sum,
        gain_b_sum,
        shift_b_sum,
        head_sums[1],
        head_sums[0],
        head_sums[2],
        head_sums[3],
        head_sums[4],
    )


def on_device(*args):
    fits = all(a.shape[0] % 64 == 0 for a in args[1:9]) and lax.axis_size("rows") % 2 == 0
    return (fused_device if fits else plain_device)(*args)


def solution(mesh):
    return jax.shard_map(
        on_device,
        mesh=mesh,
        in_specs=(
            P("batch", "rows", None, None),
            P("rows", None),
            P("rows", None),
            P("rows", None),
            P("rows", None),
            P("rows", None),
            P("rows", None),
            P("rows", None),
            P("rows", None),
            P(),
            P(),
            P(),
            P(),
            P(),
            P(),
            P(),
            P(),
            P(),
            P(("batch", "rows"), None),
            P(("batch", "rows"), None),
            P(("batch", "rows"), None),
            P(("batch", "rows")),
            P(("batch", "rows"), None),
            P(("batch", "rows"), None),
            P(("batch", "rows")),
            P(("batch", "rows")),
            P(("batch", "rows"), None),
        ),
        out_specs=(
            P(("batch", "rows"), None),
            P("batch", "rows", None, None),
            P("rows", "batch"),
            P("rows", "batch"),
            P("rows", "batch"),
            P("rows", "batch"),
            P("rows", "batch"),
            P("rows", "batch"),
            P("rows", "batch"),
            P("rows", "batch"),
            P(),
            P(),
            P(),
            P(),
            P(),
            P(),
            P(),
            P(),
            P(),
        ),
        check_vma=False,
    )
```

```python
import jax
import jax.numpy as jnp
from jax import lax
from jax.experimental import pallas as pl
from jax.experimental.pallas import tpu as pltpu
from jax.sharding import PartitionSpec as P


def padded(cells, sides, width):
    for axis, dim in sides:
        count = lax.axis_size(axis)
        ends = count - 1
        head = lax.slice_in_dim(cells, 0, width, axis=dim)
        tail = lax.slice_in_dim(cells, cells.shape[dim] - width, cells.shape[dim], axis=dim)
        cells = jnp.concatenate(
            [
                lax.ppermute(tail, axis, [(i, (i + 1) % count) for i in range(ends)]),
                cells,
                lax.ppermute(head, axis, [((i + 1) % count, i) for i in range(ends)]),
            ],
            axis=dim,
        )
    return cells


def split_up(value, dim, peers):
    shape = value.shape
    parts = value.reshape(*shape[:dim], peers, shape[dim] // peers, *shape[dim + 1 :])
    return jnp.moveaxis(parts, dim, 0)


def sum_at_owner(value, axis, dim):
    peers = lax.axis_size(axis)
    parts = lax.all_to_all(split_up(value, dim, peers), axis, 0, 0, tiled=True)
    return jnp.sum(parts.astype(jnp.float32), axis=0)


def side_by_side(arrays, axis, dim, along):
    ends, at = ([], 0)
    for a in arrays[:-1]:
        at += a.shape[along]
        ends.append(at)
    both = jnp.concatenate(arrays, axis=along)
    return tuple(jnp.split(sum_at_owner(both, axis, dim), ends, axis=along))


def tdot(left, right):
    return lax.dot_general(
        left, right, (((0,), (0,)), ((), ())), preferred_element_type=jnp.float32
    )


def ndot(left, right):
    return lax.dot_general(
        left, right, (((1,), (1,)), ((), ())), preferred_element_type=jnp.float32
    )


def silu_slope(value):
    sig = jax.nn.sigmoid(value)
    return sig * (1.0 + value * (1.0 - sig))


def norm_back(grad, normed, inverse, gain, shift_sum, gain_total_grad, total_count):
    return (
        gain * inverse * (grad - shift_sum / total_count - normed * gain_total_grad / total_count)
    )


MESH = pl.DeviceIdType.MESH
LOW = jnp.bfloat16
F32 = jnp.float32


class Wires:
    def __init__(self, send, recv):
        self.send, self.recv, self.at, self.open, self.some = send, recv, 0, [], []

    def plan(self, source, target, peer, land=None):
        copy = pltpu.make_async_remote_copy(
            src_ref=source,
            dst_ref=target,
            send_sem=self.send.at[self.at],
            recv_sem=self.recv.at[self.at if land is None else land],
            device_id=peer,
            device_id_type=MESH,
        )
        self.at += 1
        self.open.append(copy)
        return copy

    def waiter(self, like, land, peer):
        return pltpu.make_async_remote_copy(
            src_ref=like,
            dst_ref=like,
            send_sem=self.send.at[0],
            recv_sem=self.recv.at[land],
            device_id=peer,
            device_id_type=MESH,
        )

    def only_where(self, where, copy):
        self.open.pop()
        self.some.append((where, copy))
        return where, copy

    def push(self, source, target, peer):
        return start(self.plan(source, target, peer))

    def settle(self, copies):
        for copy in copies:
            copy.wait_send()
        done = {id(copy) for copy in copies}
        self.open = [copy for copy in self.open if id(copy) not in done]

    def settle_some(self, pairs):
        for where, copy in pairs:

            @pl.when(where)
            def _():
                copy.wait_send()

        done = {id(copy) for where, copy in pairs}
        self.some = [pair for pair in self.some if id(pair[1]) not in done]

    def close(self):
        for copy in self.open:
            copy.wait_send()
        self.settle_some(self.some)


def start(copy):
    copy.start()
    return copy


def greet(peers):
    barrier = pltpu.get_barrier_semaphore()
    for peer in peers:
        pl.semaphore_signal(barrier, inc=1, device_id=peer, device_id_type=MESH)
    pl.semaphore_wait(barrier, len(peers))


class Place:
    def __init__(self):
        self.groups, self.ranks = lax.axis_size("batch"), lax.axis_size("rows")
        self.g, self.s = lax.axis_index("batch"), lax.axis_index("rows")
        self.chips = self.ranks // 2
        self.z, self.core = self.s // 2, lax.rem(self.s, 2)
        self.other = 1 - self.core
        self.row_peers = [(self.g, lax.rem(self.s + k, self.ranks)) for k in range(1, self.ranks)]
        self.batch_peers = [
            (lax.rem(self.g + k, self.groups), self.s) for k in range(1, self.groups)
        ]
        self.line = [lax.rem(self.z + k, self.chips) for k in range(self.chips)]
        self.line_peers = [(self.g, z * 2 + self.core) for z in self.line[1:]]
        self.twin = (self.g, self.z * 2 + self.other)
        low, high = lax.rem(self.g, 2), self.g // 2
        beside, above = high * 2 + 1 - low, (1 - high) * 2 + low
        self.near = beside + self.core * (above - beside)
        self.far, self.across = beside + above - self.near, 3 - self.g


def rows_of(ref, index, size):
    return ref.at[pl.ds(pl.multiple_of(index * size, size), size)]


class Total:
    def __init__(self, net, place, held, from_rows, second, from_batch):
        self.held, self.from_rows, self.second, self.from_batch = (
            held,
            from_rows,
            second,
            from_batch,
        )
        self.rows = [
            net.plan(held, from_rows.at[k], peer) for k, peer in enumerate(place.row_peers)
        ]
        self.batch = [
            net.plan(second, from_batch.at[k], peer) for k, peer in enumerate(place.batch_peers)
        ]

    def start(self):
        for copy in self.rows:
            copy.start()

    def sent(self):
        return self.rows + self.batch

    def finish(self, behind=None):
        for copy in self.rows:
            copy.wait_recv()
        total = self.held[...]
        for k in range(len(self.rows)):
            total = total + self.from_rows[k]
        self.second[...] = total
        for copy in self.batch:
            copy.start()
        if behind is not None:
            behind()
        for copy in self.batch:
            copy.wait_recv()
        for k in range(len(self.batch)):
            total = total + self.from_batch[k]
        return total


def spread(ref, values):
    quarter = values[0].shape[1] // 4
    for n, value in enumerate(values):
        for k in range(4):
            ref[4 * n + k : 4 * n + k + 1, 0:quarter] = value[:, k * quarter : (k + 1) * quarter]


def gathered(block, n, quarter, at=0):
    return jnp.concatenate(
        [block[4 * n + k : 4 * n + k + 1, at : at + quarter] for k in range(4)], axis=1
    )


class Corner:
    def __init__(self, ref, height, width):
        self.ref, self.height, self.width = ref, height, width

    def __getitem__(self, z):
        beside = self.ref.shape[1] // self.width
        down, along = z // beside * self.height, z % beside * self.width
        return self.ref.at[down : down + self.height, along : along + self.width]


class Scatter:
    def __init__(self, net, place, shard, part, from_twin, from_batch, partial, from_line, result):
        self.place, self.shard, self.part = place, shard, part
        self.from_twin, self.from_batch, self.partial = from_twin, from_batch, partial
        self.from_line, self.result = from_line, result
        self.first, self.second, self.last = [], [], []
        for z in range(place.chips):
            self.first.append(net.plan(shard(2 * z + place.other), from_twin[z], place.twin))
            mine = shard(2 * z + place.core)
            self.second.append(
                [
                    net.plan(part(mine, g), from_batch.at[k, z], (near, place.s))
                    for k, (g, near) in enumerate(
                        (
                            (place.near, place.near),
                            (place.across, place.near),
                            (place.far, place.far),
                        )
                    )
                ]
            )
        self.third = [
            net.plan(partial.at[k + 1], from_line.at[k], peer)
            for k, peer in enumerate(place.line_peers)
        ]

    def sent(self, steps):
        return self.first + [copy for copies in self.second for copy in copies[:steps]]

    def pair(self):
        for copy in self.first:
            copy.start()

    def batch(self, *turns):
        place = self.place
        for z in turns or range(place.chips):
            self.first[z].wait_recv()
            mine = self.shard(2 * z + place.core)
            rows = mine.shape[0]
            step = next(n for n in (64, 32, 16) if rows % n == 0)

            @pl.loop(0, rows // step)
            def _(n):
                at = pl.ds(pl.multiple_of(n * step, step), step)
                mine[at, :] = (
                    mine[at, :].astype(F32) + self.from_twin[z][at, :].astype(F32)
                ).astype(LOW)

            for copy in self.second[z][:2]:
                copy.start()

    def forward(self, *turns):
        place = self.place
        for z in turns or range(place.chips):
            for copy in self.second[z][:2]:
                copy.wait_recv()
            theirs = self.part(self.shard(2 * z + place.core), place.far)
            theirs[...] = (
                theirs[...].astype(F32) + self.from_batch[1, z].astype(F32)
            ).astype(LOW)
            self.second[z][2].start()

    def line(self):
        place = self.place
        for copies in self.second:
            copies[2].wait_recv()
        for k, z in enumerate(place.line):
            mine = self.part(self.shard(2 * z + place.core), place.g)
            total = mine[...].astype(F32)
            for n in (0, 2):
                total = total + self.from_batch[n, z].astype(F32)
            self.partial[k] = total.astype(LOW)
            if k:
                self.third[k - 1].start()

    def finish(self):
        for copy in self.third:
            copy.wait_recv()
        total = self.partial[0].astype(F32)
        for k in range(self.place.chips - 1):
            total = total + self.from_line[k].astype(F32)
        self.result[...] = total


def slope_of(value):
    sig = 0.5 * jnp.tanh(0.5 * value) + 0.5
    return sig * (1.0 + value * (1.0 - sig))


def column_of(shape, columns):
    return lax.rem(lax.broadcasted_iota(jnp.int32, shape, 0), columns)


def from_left(value, columns):
    return jnp.where(
        column_of(value.shape, columns) == 0, 0.0, pltpu.roll(value, 1, 0)
    )


def from_right(value, columns):
    return jnp.where(
        column_of(value.shape, columns) == columns - 1,
        0.0,
        pltpu.roll(value, value.shape[0] - 1, 0),
    )


def folded(value):
    rows, width = value.shape
    return jnp.sum(value.reshape(rows // 8, 8, width), axis=0)


class Gather:
    def __init__(self, net, place, shard, whole, local, dim=0, relayed=False):
        self.net, self.place, self.shard, self.whole = net, place, shard, whole
        self.dim, self.rows = dim, whole.shape[dim] // place.ranks
        self.own = pltpu.make_async_copy(shard, self.block(place.s), local)
        part = self.rows // place.groups
        source = self.cut(shard, place.g * part, part)
        self.relayed, self.some = relayed and place.chips == 4, []
        if self.relayed:
            self.plan_relay(net, source)
        else:
            self.first = [
                net.plan(source, self.quarter(place.s, place.g), peer) for peer in place.line_peers
            ]
        self.second, self.third = [], [net.plan(shard, self.block(place.s), place.twin)]
        for k in self.order if self.relayed else range(1, place.chips):
            s = lax.rem(place.z + place.chips - k, place.chips) * 2 + place.core
            view, passed = self.quarter(s, place.g), self.quarter(s, place.near)
            self.second.append(
                [
                    net.plan(view, view, (place.near, place.s)),
                    net.plan(view, view, (place.far, place.s)),
                    net.plan(passed, passed, (place.far, place.s)),
                ]
            )
            self.third.append(net.plan(self.block(s), self.block(s), place.twin))

    def plan_relay(self, net, source):
        place, z, base = self.place, self.place.z, net.at
        right, left = (
            (place.g, lax.rem(z + n, 4) * 2 + place.core) for n in (1, 3)
        )
        mine = self.quarter(place.s, place.g)
        passed = [
            self.quarter(lax.rem(z + 4 - k, 4) * 2 + place.core, place.g) for k in (1, 2, 3)
        ]
        self.inner = (z == 1) | (z == 2)
        first = 1 + (3 - z) // 3 * 2
        then = 2 + lax.rem((z + 1) // 2, 2)
        self.order = (first, then, 6 - first - then)
        self.arrivals = [net.waiter(passed[0], base + k - 1, place.twin) for k in self.order]
        steps = (
            (z < 3, source, mine, right, base),
            (self.inner, passed[0], passed[0], right, base + 1),
            (z > 0, source, mine, left, base + 2),
            (self.inner, passed[2], passed[2], left, base + 1),
            (z == 2, passed[1], passed[1], right, base + 2),
            (z == 1, passed[1], passed[1], left, base),
        )
        for where, origin, goal, peer, land in steps:
            self.some.append(net.only_where(where, net.plan(origin, goal, peer, land)))
        self.first = [copy for where, copy in self.some[:3]]

    def go(self, n):
        where, copy = self.some[n]

        @pl.when(where)
        def _():
            copy.start()

    def relay(self):
        @pl.when(self.inner)
        def _():
            self.first[0].wait_recv()
            self.some[1][1].start()
            self.first[2].wait_recv()
            self.some[3][1].start()

    def relay_last(self):
        @pl.when(self.inner)
        def _():
            self.first[1].wait_recv()

        self.go(4)
        self.go(5)

    def cut(self, ref, start, size):
        at = pl.ds(pl.multiple_of(start, size), size)
        return ref.at[at] if self.dim == 0 else ref.at[:, at]

    def block(self, s):
        return self.cut(self.whole, s * self.rows, self.rows)

    def quarter(self, s, g):
        part = self.rows // self.place.groups
        return self.cut(self.whole, s * self.rows + g * part, part)

    def line(self):
        if self.relayed:
            self.go(0)
            self.go(2)
        else:
            for copy in self.first:
                copy.start()
        self.own.start()
        self.third[0].start()

    def batch(self, *turns):
        for k in turns or range(len(self.first)):
            if self.relayed:

                @pl.when(jnp.logical_not(self.inner))
                def _():
                    self.arrivals[k].wait_recv()

            else:
                self.first[k].wait_recv()
            for copy in self.second[k][:2]:
                copy.start()

    def forward(self, *turns):
        for k in turns or range(len(self.first)):
            self.second[k][0].wait_recv()
            self.second[k][2].start()

    def pair(self):
        for k, copies in enumerate(self.second):
            for copy in copies[1:]:
                copy.wait_recv()
            self.third[k + 1].start()

    def sent(self):
        return ([] if self.relayed else self.first) + self.third + [c for copies in self.second for c in copies]

    def ready(self):
        self.own.wait()
        for copy in self.third:
            copy.wait_recv()


def moments(total, width, total_count):
    centre = gathered(total, 0, width // 4) / total_count
    square = gathered(total, 1, width // 4) / total_count
    return centre, lax.rsqrt(square - centre * centre + 1e-05)


def sigma(value):
    return 0.5 * jnp.tanh(0.5 * value) + 0.5


def step_kernel(geometry, r):
    cells, d_in, d_mid, columns, total_count, capacity, entries, samples, clips = geometry
    place = Place()
    net = Wires(r.send, r.recv)
    ranks, groups = place.ranks, place.groups
    half, size = d_in // 2, 2 * capacity
    depth = d_in // ranks
    entry = r.bank16.shape[0]
    local = r.local
    load_x = pltpu.make_async_copy(r.features, r.x, local.at[0])
    load_x.start()
    kv_weights = [rows_of(r.low_b, n, depth) for n in range(2)]
    load_kv = [
        pltpu.make_async_copy(source, target, local.at[9 + n])
        for n, (source, target) in enumerate(zip((r.w_key, r.w_value), kv_weights))
    ]
    for copy in load_kv:
        copy.start()
    greet(place.row_peers + place.batch_peers)
    a, b, c, q, o, h = (
        Gather(net, place, shard, whole, local.at[n + 1], n // 5, n in (1, 3, 4, 5))
        for n, (shard, whole) in enumerate(
            (
                (r.w_reduce, r.w_a),
                (r.w_spatial, r.w_b),
                (r.w_expand, r.w_c),
                (r.w_query, r.w_q),
                (r.w_out, r.w_o),
                (r.w_head, r.w_h),
            )
        )
    )
    sums = [
        Total(net, place, *refs)
        for refs in (
            (r.own1, r.rows1, r.mid1, r.batch1),
            (r.own2, r.rows2, r.mid2, r.batch2),
            (r.own3, r.rows3, r.mid3, r.batch3),
            (r.own4, r.rows4, r.mid4, r.batch4),
            (r.own5, r.rows5, r.mid5, r.batch5),
            (r.own6, r.rows6, r.mid6, r.batch6),
        )
    ]
    a.line()

    def at_block(s):
        return pl.ds(pl.multiple_of(s * entry, entry), entry)

    def at_depth(s):
        return pl.ds(pl.multiple_of(s * depth, depth), depth)

    r.bank16[...] = jnp.zeros_like(r.bank16)
    r.bank16[0:entries, :] = r.bank[...]
    asked = [
        net.push(r.bank16.at[:, at_depth(peer[1])], rows_of(r.bank_cols, place.s, entry), peer)
        for peer in place.row_peers
    ]
    b.line()
    for n in range(ranks):
        r.box16[n, 0:1, 0:capacity] = r.piece_box[n : n + 1, :]
    owner = lax.broadcasted_iota(jnp.int32, (ranks, 1), 0)
    count = jnp.zeros((ranks, 1), jnp.int32)
    for n in range(ranks):
        count = jnp.where(owner == n, r.send_count[n], count)
    for k in range(capacity):
        on = slice(k * samples, (k + 1) * samples)
        r.slot_cells[k] = r.sample_pos[:, on] + r.piece_clip[:, k : k + 1] * (cells // clips)
        r.slot_weights[k] = jnp.where(k < count, r.sample_weight[:, on], 0.0)
    named = [
        net.push(r.box16.at[peer[1]], r.box_in.at[place.s], peer) for peer in place.row_peers
    ]
    r.bank_cols[at_block(place.s), :] = r.bank16[:, at_depth(place.s)]
    mine = pl.ds(pl.multiple_of(place.s * size, size), size)
    r.box_in[place.s] = r.box16[place.s]

    by_rank = (capacity * ranks, ranks * size)
    row, slot = (lax.broadcasted_iota(jnp.int32, by_rank, n) for n in range(2))
    goal = lax.rem(row, ranks) * size + row // ranks
    perms = [jnp.where(slot == goal + n * capacity, 1.0, 0.0).astype(LOW) for n in range(2)]

    @pl.loop(0, capacity)
    def _(k):
        cell = lax.broadcasted_iota(jnp.int32, (ranks, cells), 1)
        spots, weights = r.slot_cells[k], r.slot_weights[k]
        total = jnp.zeros((ranks, cells), F32)
        for j in range(samples):
            total = total + jnp.where(cell == spots[:, j : j + 1], weights[:, j : j + 1], 0.0)
        r.pieces[pl.ds(pl.multiple_of(k * ranks, ranks), ranks), 0:cells] = total

    for n in range(2):
        r.et[n] = tdot(r.pieces[0 : capacity * ranks, 0:cells].astype(LOW), perms[n]).astype(LOW)

    a.batch()
    b.relay()
    a.forward()
    b.batch(0)
    a.pair()
    b.relay_last()
    b.batch(1)
    for copy in asked:
        copy.wait_recv()
    for copy in load_kv:
        copy.wait()
    for n, weight in enumerate(kv_weights):
        r.kv_part[n] = jnp.dot(
            r.bank_cols[...], weight[...], preferred_element_type=F32
        ).astype(LOW)
    load_x.wait()
    a.ready()

    acc = r.acc
    acc[...] = jnp.zeros_like(acc)
    big = 256
    tiles = cells // big

    @pl.loop(0, tiles)
    def _(t):
        at = pl.ds(pl.multiple_of(t * big, big), big)
        value = jnp.dot(r.x[at, :], r.w_a[...], preferred_element_type=F32)
        r.middle[at, :] = value
        acc[0, :, 0:d_mid] += folded(value)
        acc[1, :, 0:d_mid] += folded(value * value)

    spread(r.own1, [jnp.sum(acc[n, :, 0:d_mid], axis=0, keepdims=True) for n in range(2)])
    own_mean = jnp.sum(acc[0, :, 0:d_mid], axis=0, keepdims=True) / cells

    first, last = place.s == 0, place.s == ranks - 1
    low_a, low_up, low_down = r.low_a, r.low_up, r.low_down

    def halo(t, way):
        at = pl.ds(pl.multiple_of(t * big, big), big)
        return pltpu.make_async_remote_copy(
            src_ref=r.low_b.at[at],
            dst_ref=(low_up if way == 0 else low_down).at[at],
            send_sem=r.halo_send.at[way, t],
            recv_sem=r.halo_recv.at[way, t],
            device_id=(place.g, place.s + 1 if way == 0 else place.s - 1),
            device_id_type=MESH,
        )

    @pl.when(first)
    def _():
        low_up[...] = jnp.zeros_like(low_up)

    @pl.when(last)
    def _():
        low_down[...] = jnp.zeros_like(low_down)

    @pl.loop(0, tiles)
    def _(t):
        at = pl.ds(pl.multiple_of(t * big, big), big)
        r.low_b[at, :] = (r.middle[at, :] - own_mean).astype(LOW)

    b.forward(0)
    b.batch(2)
    sums[0].start()
    c.line()

    @pl.loop(0, tiles)
    def _(t):
        @pl.when(jnp.logical_not(last))
        def _():
            halo(t, 0).start()

        @pl.when(jnp.logical_not(first))
        def _():
            halo(t, 1).start()

    for gather in (q, o, h):
        gather.line()

    def more_b():
        b.forward(1)

    total = sums[0].finish(more_b)
    centre, inverse = moments(total, d_mid, total_count)
    gain, bias = r.gain_a[...], r.bias_a[...]
    for n, value in enumerate((gain, bias, gain * inverse)):
        r.norm_a[n : n + 1, :] = value

    @pl.loop(0, tiles)
    def _(t):
        at = pl.ds(pl.multiple_of(t * big, big), big)
        hat = (r.middle[at, :] - centre) * inverse
        r.hat_a[at, :] = hat.astype(LOW)
        act = gain * hat + bias
        low_a[at, :] = (act * sigma(act)).astype(LOW)

    beyond = [
        (
            low,
            gathered(r.rows1[n], 0, d_mid // 4) / cells - centre,
            jnp.where(edge, 0.0, 1.0),
        )
        for low, n, edge in ((low_up, 0, first), (low_down, ranks - 2, last))
    ]

    keep_hat_a = pltpu.make_async_copy(r.hat_a, r.far_hat_a, local.at[8])
    keep_hat_a.start()
    b.forward(2)
    c.batch()
    @pl.loop(0, tiles)
    def _(t):
        at = pl.ds(pl.multiple_of(t * big, big), big)
        r.low_t[1, :, at] = jnp.transpose(low_a[at, :].astype(F32)).astype(LOW)

    b.pair()
    c.forward()
    b.ready()
    acc[...] = jnp.zeros_like(acc)

    @pl.loop(0, tiles)
    def _(t):
        at = pl.ds(pl.multiple_of(t * big, big), big)

        @pl.when(jnp.logical_not(first))
        def _():
            halo(t, 0).wait_recv()

        @pl.when(jnp.logical_not(last))
        def _():
            halo(t, 1).wait_recv()

        for low, offset, inside in beyond:
            act = gain * ((low[at, :].astype(F32) + offset) * inverse) + bias
            low[at, :] = (act * sigma(act) * inside).astype(LOW)
        parts = []
        for j in range(3):
            taps = [r.w_b[(3 * i + j) * d_mid : (3 * i + j + 1) * d_mid, :] for i in range(3)]
            parts.append(
                jnp.dot(low_up[at, :], taps[0], preferred_element_type=F32)
                + jnp.dot(low_a[at, :], taps[1], preferred_element_type=F32)
                + jnp.dot(low_down[at, :], taps[2], preferred_element_type=F32)
            )
        value = from_left(parts[0], columns) + parts[1] + from_right(parts[2], columns)
        r.middle[at, :] = value
        acc[0, :, 0:d_mid] += folded(value)
        acc[1, :, 0:d_mid] += folded(value * value)

    spread(r.own2, [jnp.sum(acc[n, :, 0:d_mid], axis=0, keepdims=True) for n in range(2)])
    sums[1].start()
    net.settle(sums[0].sent() + asked + named + a.sent())
    for gather in (q, o, h):
        gather.relay()

    @pl.loop(0, tiles)
    def _(t):
        at = pl.ds(pl.multiple_of(t * big, big), big)
        r.low_t[0, :, at] = jnp.transpose(low_up[at, :].astype(F32)).astype(LOW)
        r.low_t[2, :, at] = jnp.transpose(low_down[at, :].astype(F32)).astype(LOW)


    def begin():
        for gather in (q, o, h):
            gather.batch(0)

    total = sums[1].finish(begin)
    for gather in (q, o, h):
        gather.relay_last()
    centre, inverse = moments(total, d_mid, total_count)
    gain, bias = r.gain_b[...], r.bias_b[...]
    for n, value in enumerate((gain, bias, gain * inverse)):
        r.norm_b[n : n + 1, :] = value
    kv = [
        net.plan(r.kv_part.at[:, at_block(peer[1])], r.kv_in.at[k], peer)
        for k, peer in enumerate(place.row_peers)
    ]
    every = [
        net.plan(r.kv_own, r.kv_all.at[:, at_block(place.s)], peer) for peer in place.row_peers
    ]

    @pl.loop(0, tiles)
    def _(t):
        @pl.when(jnp.logical_not(last))
        def _():
            halo(t, 0).wait_send()

        @pl.when(jnp.logical_not(first))
        def _():
            halo(t, 1).wait_send()

    def third_norm(pre_c):
        c.pair()
        c.ready()
        acc[...] = jnp.zeros_like(acc)

        @pl.loop(0, tiles)
        def _(t):
            at = pl.ds(pl.multiple_of(t * big, big), big)
            hat = (r.middle[at, :] - centre) * inverse
            r.hat_b[at, :] = hat.astype(LOW)
            act = gain * hat + bias
            low = (act * sigma(act)).astype(LOW)
            r.low_b[at, :] = low
            for k in range(4):
                on = slice(k * (d_in // 4), (k + 1) * (d_in // 4))
                value = jnp.dot(low, r.w_c[:, on], preferred_element_type=F32)
                pre_c[at, on] = value
                acc[0, :, on] += folded(value)
                acc[1, :, on] += folded(value * value)

        spread(r.own3, [jnp.sum(acc[n], axis=0, keepdims=True) for n in range(2)])
        for gather in (q, o, h):
            gather.batch(1)
        sums[2].start()
        net.settle(sums[1].sent() + b.sent())
        net.settle_some(b.some)
        for copy in kv:
            copy.start()

        @pl.loop(0, tiles)
        def _(t):
            at = pl.ds(pl.multiple_of(t * big, big), big)
            r.low_bt[:, at] = jnp.transpose(r.low_b[at, :].astype(F32)).astype(LOW)


        def rest():
            for gather in (q, o, h):
                gather.batch(2)
                gather.forward(0)

        total = sums[2].finish(rest)
        centre_wide, inverse_wide = moments(total, d_in, total_count)
        r.scale_c[...] = r.gain_c[...] * inverse_wide
        r.centre_c[0:1, :] = centre_wide
        r.centre_c[1:2, :] = inverse_wide
        for copy in kv:
            copy.wait_recv()
        for n in range(2):
            total = r.kv_part[n, at_block(place.s), :].astype(F32)
            for k in range(ranks - 1):
                total = total + r.kv_in[k, n].astype(F32)
            r.kv_own[n] = total.astype(LOW)
            r.kv_all[n, at_block(place.s), :] = total.astype(LOW)
        for copy in every:
            copy.start()

        for gather in (q, o, h):
            gather.forward(1)
        r.pieces[...] = jnp.zeros_like(r.pieces)
        tile = 128

        @pl.loop(0, cells // 256)
        def _(t):
            at = pl.ds(pl.multiple_of(t * 256, 256), 256)
            for k in range(4):
                on = slice(k * (d_in // 4), (k + 1) * (d_in // 4))
                into = slice((k % 2) * (d_in // 4), (k % 2 + 1) * (d_in // 4))
                hat = (pre_c[at, on] - r.centre_c[0:1, on]) * r.centre_c[1:2, on]
                r.hat_c[at, on] = hat.astype(LOW)
                value = r.gain_c[:, on] * hat + r.bias_c[:, on] + r.x[at, on].astype(F32)
                sig = sigma(value)
                fmap = value * sig
                r.x[at, on] = (sig + fmap * (1.0 - sig)).astype(LOW)
                r.pieces[:, into] += tdot(r.et[k // 2, at, :], fmap.astype(LOW))


    pl.run_scoped(third_norm, pltpu.VMEM((cells, d_in), F32))
    for gather in (q, o, h):
        gather.forward(2)
    r.blocks[...] = r.pieces[...].astype(LOW)
    pushed = [
        net.push(rows_of(r.blocks, peer[1], size), rows_of(r.arrived, place.s, size), peer)
        for peer in place.row_peers
    ]
    r.arrived[mine, :] = r.blocks[mine, :]
    q.pair()
    o.pair()
    h.pair()
    for copy in named + every + pushed:
        copy.wait_recv()

    def block_rows(ref, count):
        return lambda s: rows_of(ref, s, ref.shape[0] // count)

    def by_columns(width):
        return lambda view, g: view.at[:, pl.ds(pl.multiple_of(g * width, width), width)]

    def by_rows(height):
        return lambda view, g: view.at[pl.ds(pl.multiple_of(g * height, height), height)]

    def scatter(key, shard, part, landing):
        return Scatter(
            net, place, shard, part, landing, *(getattr(r, n + key) for n in ("ba_", "pa_", "li_", "out_"))
        )

    per = cells // depth

    def shard_a(s):
        at = pl.ds(pl.multiple_of(lax.rem(s, per) * depth, depth), depth)
        return r.low_t.at[s // per, :, at]

    sc = {
        "q": scatter("q", block_rows(r.w_q, ranks), by_columns(d_mid // groups), Corner(r.tw_q, depth, d_mid)),
        "o": scatter("o", block_rows(r.w_o, ranks), by_columns(d_in // groups), r.tw_o.at),
        "h": scatter("h", lambda s: r.g_h.at[s], by_rows(r.g_h.shape[1] // groups), r.tw_h.at),
        "c": scatter("c", block_rows(r.w_c, ranks), by_columns(d_in // groups), r.tw_c.at),
        "a": scatter("a", shard_a, by_rows(d_mid // groups), Corner(r.tw_q, r.tw_q.shape[0] // 2, depth)),
    }
    returned = [
        net.plan(rows_of(r.blocks, peer[1], size), rows_of(r.back_in, place.s, size), peer)
        for peer in place.row_peers
    ]
    asked_back = [
        net.plan(r.kv_part.at[:, at_block(peer[1])], r.kv_in.at[k], peer)
        for k, peer in enumerate(place.row_peers)
    ]

    def own_boxes(pooled, joined, d_branch, d_pooled):
        boxes = r.cotangent.shape[1]
        number = jnp.concatenate([r.box_in[n, 0:1, :] for n in range(ranks)], axis=0)
        box = lax.broadcasted_iota(jnp.int32, (ranks, boxes), 1)
        hits = jnp.concatenate(
            [jnp.where(number[:, k : k + 1] == box, 1.0, 0.0) for k in range(capacity)], axis=0
        ).astype(LOW)
        picks = [tdot(perm, hits).astype(LOW) for perm in perms]
        across = lax.broadcasted_iota(jnp.int32, (boxes, boxes), 0) == lax.broadcasted_iota(
            jnp.int32, (boxes, boxes), 1
        )

        def upright(value):
            wide = jnp.broadcast_to(value.astype(F32), (boxes, boxes))
            return jnp.sum(jnp.where(across, wide, 0.0), axis=1, keepdims=True)

        bank_row = lax.broadcasted_iota(jnp.int32, (boxes, ranks * entry), 1)
        inner = lax.rem(bank_row, entry)
        spot = (bank_row // entry * entries + inner).astype(F32)
        start, length = upright(r.win_start[...]), upright(r.win_len[...])
        window = (inner < entries) & (spot >= start) & (spot < start + length)
        for k in range(2):
            pooled[:, k * half : (k + 1) * half] = tdot(picks[k], r.arrived[...])
        joined[:, 0:d_in] = pooled[...].astype(LOW)
        pooled_low = joined.at[:, 0:d_in]
        keys, vals = r.kv_all.at[0], r.kv_all.at[1]
        scale = d_mid ** (-0.5)
        q.ready()
        queries = jnp.dot(pooled_low[...], r.w_q[...], preferred_element_type=F32).astype(LOW)
        scores = jnp.where(window, ndot(queries, keys[...]) * scale, -1e30)
        raised = jnp.exp(scores - jnp.max(scores, axis=1, keepdims=True))
        attend = raised / jnp.sum(raised, axis=1, keepdims=True)
        attend_low = attend.astype(LOW)
        mixture = jnp.dot(attend_low, vals[...], preferred_element_type=F32)
        centred = mixture - jnp.mean(mixture, axis=1, keepdims=True)
        inverse_z = lax.rsqrt(jnp.mean(centred * centred, axis=1, keepdims=True) + 1e-05)
        hat_z = centred * inverse_z
        pre_ln = r.ln_gain[...] * hat_z + r.ln_bias[...]
        sig_z = sigma(pre_ln)
        low_r = (pre_ln * sig_z).astype(LOW)
        slope_z = sig_z * (1.0 + pre_ln * (1.0 - sig_z))
        o.ready()
        for k in range(4):
            on = slice(k * (d_in // 4), (k + 1) * (d_in // 4))
            into = slice(d_in + k * (d_in // 4), d_in + (k + 1) * (d_in // 4))
            joined[:, into] = (
                pooled[:, on] + jnp.dot(low_r, r.w_o[:, on], preferred_element_type=F32)
            ).astype(LOW)
        h.ready()
        logits = (
            ndot(joined[...], r.w_h[...]) + r.head_bias[...]
        )
        likely = jax.nn.sigmoid(logits)
        r.out_probs[...] = likely
        d_logit = (jnp.transpose(r.cotangent[...]) * (likely * (1.0 - likely))).astype(LOW)
        for k in range(4):
            on = slice(k * (d_in // 4), (k + 1) * (d_in // 4))
            below = slice(d_in + k * (d_in // 4), d_in + (k + 1) * (d_in // 4))
            upper = jnp.dot(d_logit, r.w_h[:, below], preferred_element_type=F32)
            d_branch[:, on] = upper.astype(LOW)
            pooled[:, on] = (
                jnp.dot(d_logit, r.w_h[:, on], preferred_element_type=F32) + upper
            )
        d_ln = ndot(d_branch[...], r.w_o[...]) * slope_z
        d_hat = d_ln * r.ln_gain[...]
        d_mixture = (
            inverse_z
            * (
                d_hat
                - jnp.mean(d_hat, axis=1, keepdims=True)
                - hat_z * jnp.mean(d_hat * hat_z, axis=1, keepdims=True)
            )
        ).astype(LOW)
        d_attend = ndot(d_mixture, vals[...])
        d_scores = (attend * (d_attend - jnp.sum(d_attend * attend, axis=1, keepdims=True))).astype(LOW)
        d_queries = (jnp.dot(d_scores, keys[...], preferred_element_type=F32) * scale).astype(LOW)
        for k in range(4):
            on = slice(k * (d_in // 4), (k + 1) * (d_in // 4))
            d_pooled[:, on] = (pooled[:, on] + ndot(d_queries, r.w_q[on, :])).astype(LOW)
        net.settle(pushed)
        r.blocks[...] = (
            jnp.dot(picks[0], d_pooled[:, 0:half], preferred_element_type=F32)
            + jnp.dot(picks[1], d_pooled[:, half:d_in], preferred_element_type=F32)
        ).astype(LOW)
        for copy in returned:
            copy.start()
        r.back_in[mine, :] = r.blocks[mine, :]

        net.settle(q.sent() + o.sent() + kv + every)
        net.settle_some(q.some + o.some)
        r.kv_part[0] = (tdot(d_scores, queries) * scale).astype(LOW)
        r.kv_part[1] = tdot(attend_low, d_mixture).astype(LOW)
        for k in range(4):
            on = slice(k * (d_in // 4), (k + 1) * (d_in // 4))
            r.w_q[on, :] = tdot(joined[:, on], d_queries).astype(LOW)
            r.w_o[:, on] = tdot(low_r, d_branch[:, on]).astype(LOW)
        width = 2 * depth
        classes = d_logit.shape[1]
        share = classes // groups
        held, kind = (
            lax.broadcasted_iota(jnp.int32, (classes, r.g_h.shape[1]), n) for n in range(2)
        )
        padded_class = held // share * (r.g_h.shape[1] // groups) + lax.rem(held, share)
        spaced = jnp.where(kind == padded_class, 1.0, 0.0).astype(LOW)
        d_spaced = jnp.dot(d_logit, spaced, preferred_element_type=F32).astype(LOW)
        for s in range(ranks):
            r.g_h[s] = tdot(d_spaced, joined[:, s * width : (s + 1) * width]).astype(LOW)
        quarter = d_mid // 4
        r.own4[...] = jnp.zeros_like(r.own4)
        for n, value in enumerate(
            (jnp.sum(d_ln * hat_z, axis=0, keepdims=True), jnp.sum(d_ln, axis=0, keepdims=True))
        ):
            for k in range(4):
                r.own4[4 * n + k : 4 * n + k + 1, d_in // 4 : d_in // 4 + quarter] = value[
                    :, k * quarter : (k + 1) * quarter
                ]
        r.own4[0:1, d_in // 4 + quarter : d_in // 4 + quarter + classes] = jnp.sum(
            d_logit.astype(F32), axis=0, keepdims=True
        )
        sc["h"].pair()
        sc["q"].pair()
        sc["o"].pair()
        for copy in asked_back:
            copy.start()
        sc["h"].batch()
        sc["q"].batch()


    boxes = r.cotangent.shape[1]
    pl.run_scoped(
        own_boxes,
        pltpu.VMEM((boxes, d_in), F32),
        pltpu.VMEM((boxes, 2 * d_in), LOW),
        pltpu.VMEM((boxes, d_in), LOW),
        pltpu.VMEM((boxes, d_in), LOW),
    )
    keep_hat_a.wait()
    for copy in returned:
        copy.wait_recv()

    chips = place.chips
    dkv, dkv_in, dkv_own, dkv_all = r.kv_part, r.kv_in, r.kv_own, r.kv_all

    def backward(d_pre, g_b):
        sc["b"] = scatter("b", block_rows(g_b, ranks), by_columns(d_mid // groups), r.tw_b.at)
        hat_c, slope, d_c, back = r.hat_c, r.x, r.x, r.back_in
        acc = r.acc
        acc[...] = jnp.zeros_like(acc)
        tile = 128

        @pl.loop(0, cells // tile)
        def _(t):
            at = pl.ds(pl.multiple_of(t * tile, tile), tile)
            for h in range(2):
                on = slice(h * half, (h + 1) * half)
                grad = jnp.dot(
                    r.et[h, at, :], back[...], preferred_element_type=F32
                ) * slope[at, on].astype(F32)
                d_pre[at, on] = grad.astype(LOW)
                acc[0, :, on] += folded(grad)
                acc[1, :, on] += folded(grad * hat_c[at, on].astype(F32))

        own4 = r.own4
        spread(own4, [jnp.sum(acc[n], axis=0, keepdims=True) for n in range(2)])
        sums[3].start()
        net.settle(sums[2].sent() + returned + h.sent())
        net.settle_some(h.some)
        sc["h"].forward()
        sc["q"].forward()
        for copy in asked_back:
            copy.wait_recv()
        own = pl.ds(pl.multiple_of(place.s * entry, entry), entry)
        for n in range(2):
            total = dkv[n, own, :].astype(F32)
            for k in range(ranks - 1):
                total = total + dkv_in[k, n].astype(F32)
            dkv_own[n] = total.astype(LOW)
            dkv_all[n, own, :] = total.astype(LOW)
        shared = [
            net.push(dkv_own, dkv_all.at[:, own], peer)
            for peer in place.row_peers
        ]

        total = sums[3].finish(sc["o"].batch)
        r.out_head[...] = total
        shift_c = gathered(total, 0, d_in // 4) / total_count
        gain_c = gathered(total, 1, d_in // 4) / total_count
        scale_c = r.scale_c[...]

        w_c, hat_b, d_act = r.w_c, r.hat_b, r.middle
        acc[...] = jnp.zeros_like(acc)
        norm_b, norm_a = r.norm_b, r.norm_a

        @pl.loop(0, cells // 256)
        def _(t):
            at = pl.ds(pl.multiple_of(t * 256, 256), 256)
            grad = scale_c * (
                d_pre[at, :].astype(F32) - shift_c - hat_c[at, :].astype(F32) * gain_c
            )
            low = grad.astype(LOW)
            d_c[at, :] = low
            hat = hat_b[at, :].astype(F32)
            back_b = ndot(low, w_c[...]) * slope_of(norm_b[0:1, :] * hat + norm_b[1:2, :])
            d_act[at, :] = back_b
            acc[0, :, 0:d_mid] += folded(back_b)
            acc[1, :, 0:d_mid] += folded(back_b * hat)

        reload = pltpu.make_async_copy(r.features, r.hat_c, local.at[20])
        reload.start()
        own5 = r.own5
        spread(own5, [jnp.sum(acc[n, :, 0:d_mid], axis=0, keepdims=True) for n in range(2)])
        sums[4].start()
        net.settle(sums[3].sent() + asked_back)
        net.settle([copy for key in "hqo" for copy in sc[key].sent(3 if key in "hq" else 2)])
        net.settle(c.sent())
        wide = 256

        @pl.loop(0, d_in // wide)
        def _(t):
            at = pl.ds(pl.multiple_of(t * wide, wide), wide)
            w_c[:, at] = jnp.dot(
                r.low_bt[...], d_c[:, at], preferred_element_type=F32
            ).astype(LOW)

        sc["c"].pair()
        sc["h"].line()
        sc["q"].line()
        for copy in shared:
            copy.wait_recv()
        kv_out, kv_in = r.kv_out, r.kv_back
        for n in range(2):
            kv_out[n] = tdot(r.bank_cols[...], dkv_all[n]).astype(LOW)


        share = d_mid // groups
        crossing = [
            net.plan(
                kv_out.at[:, :, pl.ds(pl.multiple_of(peer[0] * share, share), share)],
                kv_in.at[k],
                peer,
            )
            for k, peer in enumerate(place.batch_peers)
        ]

        def middle():
            for copy in crossing:
                copy.start()
            sc["o"].forward()
            sc["c"].batch()

        total = sums[4].finish(middle)
        r.out_b_sums[...] = total
        shift_b = gathered(total, 0, d_mid // 4) / total_count
        gain_b = gathered(total, 1, d_mid // 4) / total_count

        d_b, d_up, d_down = (r.low_up, r.low_a, r.low_down), r.low_b, r.hat_a

        def halo_back(t, way):
            at = pl.ds(pl.multiple_of(t * big, big), big)
            return pltpu.make_async_remote_copy(
                src_ref=d_b[1].at[at],
                dst_ref=(d_up if way == 0 else d_down).at[at],
                send_sem=r.back_send.at[way, t],
                recv_sem=r.back_recv.at[way, t],
                device_id=(place.g, place.s + 1 if way == 0 else place.s - 1),
                device_id_type=MESH,
            )

        @pl.when(first)
        def _():
            d_up[...] = jnp.zeros_like(d_up)

        @pl.when(last)
        def _():
            d_down[...] = jnp.zeros_like(d_down)

        @pl.loop(0, tiles)
        def _(t):
            at = pl.ds(pl.multiple_of(t * big, big), big)
            grad = norm_b[2:3, :] * (
                d_act[at, :] - shift_b - hat_b[at, :].astype(F32) * gain_b
            )
            d_b[1][at, :] = grad.astype(LOW)

            @pl.when(jnp.logical_not(last))
            def _():
                halo_back(t, 0).start()

            @pl.when(jnp.logical_not(first))
            def _():
                halo_back(t, 1).start()

            d_b[0][at, :] = from_right(grad, columns).astype(LOW)
            d_b[2][at, :] = from_left(grad, columns).astype(LOW)

        @pl.loop(0, 3)
        def _(i):
            for j in range(3):
                at = pl.ds(pl.multiple_of((3 * i + j) * d_mid, d_mid), d_mid)
                g_b[at, :] = jnp.dot(
                    r.low_t[i], d_b[j][...], preferred_element_type=F32
                ).astype(LOW)

        more = pltpu.make_async_copy(r.far_hat_a, hat_b, local.at[18])
        more.start()
        sc["b"].pair()
        sc["c"].forward()
        sc["o"].line()
        sc["b"].batch()

        more.wait()
        w_b, hat_a = r.w_b, hat_b
        acc[...] = jnp.zeros_like(acc)

        @pl.loop(0, tiles)
        def _(t):
            at = pl.ds(pl.multiple_of(t * big, big), big)

            @pl.when(jnp.logical_not(first))
            def _():
                halo_back(t, 0).wait_recv()

            @pl.when(jnp.logical_not(last))
            def _():
                halo_back(t, 1).wait_recv()

            parts = []
            for j in range(3):
                taps = [w_b[(3 * i + j) * d_mid : (3 * i + j + 1) * d_mid, :] for i in range(3)]
                parts.append(
                    ndot(d_down[at, :], taps[0]) + ndot(d_b[1][at, :], taps[1]) + ndot(d_up[at, :], taps[2])
                )
            grad = from_right(parts[0], columns) + parts[1] + from_left(parts[2], columns)
            hat = hat_a[at, :].astype(F32)
            grad = grad * slope_of(norm_a[0:1, :] * hat + norm_a[1:2, :])
            d_act[at, :] = grad
            acc[0, :, 0:d_mid] += folded(grad)
            acc[1, :, 0:d_mid] += folded(grad * hat)

        own6 = r.own6
        spread(own6, [jnp.sum(acc[n, :, 0:d_mid], axis=0, keepdims=True) for n in range(2)])
        sums[5].start()
        net.settle(sums[4].sent() + shared + crossing)
        net.settle(sc["c"].sent(3) + sc["b"].sent(2) + sc["h"].third + sc["q"].third)
        net.settle([copies[2] for copies in sc["o"].second])
        sc["c"].line()

        def late():
            sc["b"].forward()

        total = sums[5].finish(late)
        r.out_a_sums[...] = total
        shift_a = gathered(total, 0, d_mid // 4) / total_count
        gain_a = gathered(total, 1, d_mid // 4) / total_count
        d_a, d_at = d_b[0], r.low_bt

        @pl.loop(0, tiles)
        def _(t):
            at = pl.ds(pl.multiple_of(t * big, big), big)
            grad = norm_a[2:3, :] * (
                d_act[at, :] - shift_a - hat_a[at, :].astype(F32) * gain_a
            )
            d_a[at, :] = grad.astype(LOW)
            d_at[:, at] = jnp.transpose(grad).astype(LOW)

        reload.wait()
        x = r.hat_c

        def block_a(s):
            shard_a(s)[...] = jnp.dot(
                d_at[...],
                x[:, pl.ds(pl.multiple_of(s * depth, depth), depth)],
                preferred_element_type=F32,
            ).astype(LOW)

        for z in range(chips):
            block_a(2 * z + place.other)
            sc["a"].first[z].start()

        @pl.loop(0, chips)
        def _(z):
            block_a(2 * z + place.core)

        sc["b"].line()
        sc["a"].batch()
        out_x = r.out_x

        def leave(t):
            at = pl.ds(pl.multiple_of(t * tile, tile), tile)
            return pltpu.make_async_copy(d_pre.at[at], out_x.at[at], local.at[21 + t])

        @pl.loop(0, cells // tile)
        def _(t):
            at = pl.ds(pl.multiple_of(t * tile, tile), tile)
            d_pre[at, :] = (
                ndot(d_a[at, :], r.w_a[...]) + d_pre[at, :].astype(F32)
            ).astype(LOW)
            leave(t).start()

        sc["a"].forward()
        for key in "qohc":
            sc[key].finish()
        sc["a"].line()
        sc["b"].finish()
        for copy in crossing:
            copy.wait_recv()
        for n, key in enumerate((r.out_k, r.out_v)):
            total = kv_out[n, :, pl.ds(pl.multiple_of(place.g * share, share), share)].astype(F32)
            for k in range(groups - 1):
                total = total + kv_in[k, n].astype(F32)
            key[...] = total
        sc["a"].finish()

        @pl.loop(0, cells // tile)
        def _(t):
            leave(t).wait()

        @pl.loop(0, tiles)
        def _(t):
            @pl.when(jnp.logical_not(last))
            def _():
                halo_back(t, 0).wait_send()

            @pl.when(jnp.logical_not(first))
            def _():
                halo_back(t, 1).wait_send()

        net.close()

    pl.run_scoped(
        backward,
        pltpu.VMEM((cells, d_in), LOW),
        pltpu.VMEM(r.w_b.shape, LOW),
    )


class Refs:
    def __init__(self, names, refs, **more):
        self.__dict__.update(zip(names, refs), **more)


def run_kernel(body, geometry, channel, held, far, outs, far_outs, scratch):
    anywhere = pl.BlockSpec(memory_space=pl.ANY)
    inside = pl.BlockSpec(memory_space=pltpu.VMEM)
    names = [*held, *far, *outs, *far_outs, *scratch]
    scalars = pl.BlockSpec(memory_space=pltpu.SMEM)
    results = pl.pallas_call(
        lambda *refs: body(geometry, Refs(names, refs)),
        out_shape=(*outs.values(), *far_outs.values()),
        in_specs=[scalars if v.ndim == 1 else inside for v in held.values()] + [anywhere] * len(far),
        out_specs=(inside,) * len(outs) + (anywhere,) * len(far_outs),
        scratch_shapes=[*scratch.values()],
        compiler_params=pltpu.CompilerParams(
            collective_id=channel, has_side_effects=True, vmem_limit_bytes=64 << 20
        ),
    )(*held.values(), *far.values())
    return Refs([*outs, *far_outs], results)


def shape(kind, *sizes):
    return jax.ShapeDtypeStruct(sizes, kind)


def room(kind, *sizes):
    return pltpu.VMEM(sizes, kind)


def run_step(geometry, held, far):
    cells, d_in, d_mid, columns, total_count, capacity, entries, samples, clips = geometry
    groups, ranks = lax.axis_size("batch"), lax.axis_size("rows")
    chips, dma = ranks // 2, pltpu.SemaphoreType.DMA
    slots = ranks * 2 * capacity
    entry = -(-entries // 16) * 16
    bank = ranks * entry
    classes, boxes = held["cotangent"].shape
    spaced = groups * (-(-classes // groups // 16) * 16)
    spatial = far["w_spatial"].shape[0] * ranks
    half, depth = d_in // 2, d_in // ranks
    head = d_in // 4 + d_mid // 4 + spaced
    share = dict(
        q=(d_in // ranks, d_mid // groups),
        o=(d_mid // ranks, d_in // groups),
        h=(spaced // groups, 2 * d_in // ranks),
        c=(d_mid // ranks, d_in // groups),
        b=(spatial // ranks, d_mid // groups),
        a=(d_mid // groups, d_in // ranks),
    )
    block = dict(
        q=(d_in // ranks, d_mid),
        o=(d_mid // ranks, d_in),
        h=(spaced, 2 * d_in // ranks),
        c=(d_mid // ranks, d_in),
        b=(spatial // ranks, d_mid),
        a=(d_mid, d_in // ranks),
    )
    outs = dict(
        out_probs=shape(F32, boxes, classes),
        out_head=shape(F32, 8, head),
        out_b_sums=shape(F32, 8, d_mid // 4),
        out_a_sums=shape(F32, 8, d_mid // 4),
        out_k=shape(F32, depth, d_mid // groups),
        out_v=shape(F32, depth, d_mid // groups),
    )
    far_outs = dict(out_x=shape(LOW, cells, d_in), far_hat_a=shape(LOW, cells, d_mid))
    scratch = dict(
        x=room(LOW, cells, d_in),
        hat_c=room(LOW, cells, d_in),
        w_a=room(LOW, d_in, d_mid),
        w_b=room(LOW, spatial, d_mid),
        w_c=room(LOW, d_mid, d_in),
        w_q=room(LOW, d_in, d_mid),
        w_o=room(LOW, d_mid, d_in),
        w_h=room(LOW, classes, 2 * d_in),
        g_h=room(LOW, ranks, spaced, 2 * d_in // ranks),
        middle=room(F32, cells, d_mid),
        hat_a=room(LOW, cells, d_mid),
        hat_b=room(LOW, cells, d_mid),
        low_a=room(LOW, cells, d_mid),
        low_up=room(LOW, cells, d_mid),
        low_down=room(LOW, cells, d_mid),
        low_b=room(LOW, cells, d_mid),
        low_t=room(LOW, 3, d_mid, cells),
        low_bt=room(LOW, d_mid, cells),
        bank16=room(LOW, entry, d_in),
        bank_cols=room(LOW, bank, depth),
        box16=room(jnp.int32, ranks, 8, 128),
        box_in=room(jnp.int32, ranks, 8, 128),
        slot_cells=room(jnp.int32, capacity, ranks, samples),
        slot_weights=room(F32, capacity, ranks, samples),
        et=room(LOW, 2, cells, slots),
        kv_part=room(LOW, 2, bank, d_mid),
        kv_in=room(LOW, ranks - 1, 2, entry, d_mid),
        kv_own=room(LOW, 2, entry, d_mid),
        kv_all=room(LOW, 2, bank, d_mid),
        kv_out=room(LOW, 2, depth, d_mid),
        kv_back=room(LOW, groups - 1, 2, depth, d_mid // groups),
        norm_a=room(F32, 8, d_mid),
        norm_b=room(F32, 8, d_mid),
        scale_c=room(F32, 1, d_in),
        centre_c=room(F32, 8, d_in),
        acc=room(F32, 2, 8, d_in),
        pieces=room(F32, slots, half),
        blocks=room(LOW, slots, half),
        arrived=room(LOW, slots, half),
        back_in=room(LOW, slots, half),
        halo_send=dma((2, cells // 256)),
        halo_recv=dma((2, cells // 256)),
        back_send=dma((2, cells // 256)),
        back_recv=dma((2, cells // 256)),
        local=dma((32,)),
        send=dma((400,)),
        recv=dma((400,)),
    )
    scratch.update(tw_q=room(LOW, chips * depth, d_mid))
    narrow = d_mid // 4
    for n, width in enumerate((narrow, narrow, d_in // 4, head, narrow, narrow)):
        scratch["own%d" % (n + 1)] = room(F32, 8, width)
        scratch["mid%d" % (n + 1)] = room(F32, 8, width)
        scratch["rows%d" % (n + 1)] = room(F32, ranks - 1, 8, width)
        scratch["batch%d" % (n + 1)] = room(F32, groups - 1, 8, width)
    for key in share:
        outs["out_" + key] = shape(F32, *share[key])
        if key not in "qa":
            scratch["tw_" + key] = room(LOW, chips, *block[key])
        scratch["ba_" + key] = room(LOW, groups - 1, chips, *share[key])
        scratch["pa_" + key] = room(LOW, chips, *share[key])
        scratch["li_" + key] = room(LOW, chips - 1, *share[key])
    return run_kernel(step_kernel, geometry, 11, held, far, outs, far_outs, scratch)


def finish_kernel(r):
    chunk = r.in_x.shape[0] // 8

    def across(n, leave):
        at = pl.ds(n * chunk, chunk)
        source, target = (r.stage, r.x) if leave else (r.in_x, r.stage)
        return pltpu.make_async_copy(source.at[at], target.at[at], r.local.at[leave, n])

    for n in range(8):
        across(n, 0).start()
    for n in range(8):
        across(n, 0).wait()
        across(n, 1).start()
    r.probs[...] = jnp.transpose(r.in_probs[...])
    r.a[...] = jnp.transpose(r.in_a[...])
    r.b[...] = r.in_b[...]
    r.c[...] = r.in_c[...]
    r.q[...] = r.in_q[...]
    r.k[...] = r.in_k[...]
    r.v[...] = r.in_v[...]
    r.o[...] = r.in_o[...]
    r.h[...] = r.in_h[0 : r.h.shape[0], :]
    r.bias_a[...], r.gain_a[...] = r.in_a_sums[0:4, :], r.in_a_sums[4:8, :]
    r.bias_b[...], r.gain_b[...] = r.in_b_sums[0:4, :], r.in_b_sums[4:8, :]
    lanes = r.ln_gain.shape[1]
    per = r.gain_c.shape[0] // 4
    for n in range(4):
        for k in range(per):
            on = slice(k * lanes, (k + 1) * lanes)
            r.bias_c[per * n + k : per * n + k + 1, :] = r.in_head[n : n + 1, on]
            r.gain_c[per * n + k : per * n + k + 1, :] = r.in_head[4 + n : 5 + n, on]
    on = slice(per * lanes, (per + 1) * lanes)
    r.ln_gain[...], r.ln_bias[...] = r.in_head[0:4, on], r.in_head[4:8, on]
    at = (per + 1) * lanes
    r.head_bias[...] = r.in_head[0:1, at : at + r.head_bias.shape[1]]
    for n in range(8):
        across(n, 1).wait()


def run_finish(probs, two, groups, d_mid, classes):
    held = dict(
        in_probs=probs,
        in_a=two.out_a,
        in_b=two.out_b,
        in_c=two.out_c,
        in_q=two.out_q,
        in_k=two.out_k,
        in_v=two.out_v,
        in_o=two.out_o,
        in_h=two.out_h,
        in_a_sums=two.out_a_sums,
        in_b_sums=two.out_b_sums,
        in_head=two.out_head,
    )
    like = lambda v: shape(F32, *v.shape)
    lanes = two.out_a_sums.shape[1]
    row = shape(F32, 4, lanes)
    wide = shape(F32, 4 * (two.out_x.shape[1] // 4 // lanes), lanes)
    outs = dict(
        probs=shape(F32, *probs.shape[::-1]),
        a=shape(F32, *two.out_a.shape[::-1]),
        b=like(two.out_b),
        c=like(two.out_c),
        q=like(two.out_q),
        k=like(two.out_k),
        v=like(two.out_v),
        o=like(two.out_o),
        h=shape(F32, classes // groups, two.out_h.shape[1]),
        gain_a=row,
        bias_a=row,
        gain_b=row,
        bias_b=row,
        gain_c=wide,
        bias_c=wide,
        ln_gain=row,
        ln_bias=row,
        head_bias=shape(F32, 1, classes),
    )
    far_outs = dict(x=shape(LOW, *two.out_x.shape))
    anywhere = pl.BlockSpec(memory_space=pl.ANY)
    inside = pl.BlockSpec(memory_space=pltpu.VMEM)
    names = [*held, "in_x", *outs, *far_outs, "stage", "local"]
    results = pl.pallas_call(
        lambda *refs: finish_kernel(Refs(names, refs)),
        out_shape=(*outs.values(), *far_outs.values()),
        in_specs=[inside] * len(held) + [anywhere],
        out_specs=(inside,) * len(outs) + (anywhere,),
        scratch_shapes=[room(LOW, *two.out_x.shape), pltpu.SemaphoreType.DMA((2, 8))],
        compiler_params=pltpu.CompilerParams(vmem_limit_bytes=64 << 20),
    )(*held.values(), two.out_x)
    return Refs([*outs, *far_outs], results)


def fused_device(
    features,
    w_reduce,
    w_spatial,
    w_expand,
    query_weight,
    w_key,
    w_value,
    w_out,
    w_head,
    gain_a,
    bias_a,
    gain_b,
    bias_b,
    gain_c,
    bias_c,
    ln_gain,
    ln_bias,
    head_bias,
    bank,
    piece_box,
    piece_clip,
    send_count,
    sample_pos,
    sample_weight,
    win_start,
    win_len,
    prob_cotangent,
):
    groups, ranks = lax.axis_size("batch"), lax.axis_size("rows")
    clip_dev, row_dev, columns, d_in = features.shape
    d_mid = w_reduce.shape[1]
    cells = clip_dev * row_dev * columns
    total_count = cells * ranks * groups
    capacity = piece_box.shape[1]
    samples = sample_pos.shape[1] // capacity
    entries = bank.shape[0]
    geometry = (cells, d_in, d_mid, columns, total_count, capacity, entries, samples, clip_dev)
    line = lambda v: v.reshape(1, -1)
    held = dict(
        bank=bank,
        piece_box=piece_box,
        piece_clip=piece_clip,
        send_count=send_count,
        sample_pos=sample_pos,
        sample_weight=sample_weight,
        gain_a=line(gain_a),
        bias_a=line(bias_a),
        gain_b=line(gain_b),
        bias_b=line(bias_b),
        gain_c=line(gain_c),
        bias_c=line(bias_c),
        ln_gain=line(ln_gain),
        ln_bias=line(ln_bias),
        win_start=line(win_start),
        win_len=line(win_len),
        head_bias=line(head_bias),
        cotangent=prob_cotangent.T,
    )
    far = dict(
        features=features.reshape(cells, d_in),
        w_reduce=w_reduce,
        w_spatial=w_spatial,
        w_expand=w_expand,
        w_query=query_weight,
        w_out=w_out,
        w_head=w_head.T,
        w_key=w_key,
        w_value=w_value,
    )
    done = run_step(geometry, held, far)
    last = run_finish(done.out_probs, done, groups, d_mid, prob_cotangent.shape[1])
    flat = lambda v: v.reshape(-1)
    return (
        last.probs.T,
        last.x.reshape(features.shape),
        last.a,
        last.b,
        last.c,
        last.q,
        last.k,
        last.v,
        last.o,
        last.h.T,
        flat(last.gain_a),
        flat(last.bias_a),
        flat(last.gain_b),
        flat(last.bias_b),
        flat(last.gain_c),
        flat(last.bias_c),
        flat(last.ln_gain),
        flat(last.ln_bias),
        flat(last.head_bias),
    )


def plain_normalize(field, total_count):
    sums, squares = lax.psum((jnp.sum(field, 0), jnp.sum(field * field, 0)), ("batch", "rows"))
    centre_value = sums / total_count
    inverse = lax.rsqrt(squares / total_count - centre_value * centre_value + 1e-05)
    return ((field - centre_value) * inverse, inverse)


def plain_totals(grad, normed):
    return lax.psum((jnp.sum(grad, 0), jnp.sum(grad * normed, 0)), ("batch", "rows"))


def plain_device(
    features,
    w_reduce,
    w_spatial,
    w_expand,
    query_weight,
    w_key,
    w_value,
    w_out,
    w_head,
    gain_a,
    bias_a,
    gain_b,
    bias_b,
    gain_c,
    bias_c,
    ln_gain,
    ln_bias,
    head_bias,
    bank,
    piece_box,
    piece_clip,
    send_count,
    sample_pos,
    sample_weight,
    win_start,
    win_len,
    prob_cotangent,
):
    owners = lax.axis_size("rows")
    clip_dev, row_dev, col_count, d_in = features.shape
    cell_count = clip_dev * row_dev * col_count
    total_count = cell_count * owners * lax.axis_size("batch")
    w_a, w_b, w_c, w_q, w_k, w_v, w_o, w_h = (
        lax.all_gather(w_reduce, "rows", axis=0, tiled=True),
        lax.all_gather(w_spatial, "rows", axis=0, tiled=True),
        lax.all_gather(w_expand, "rows", axis=0, tiled=True),
        lax.all_gather(query_weight, "rows", axis=0, tiled=True),
        lax.all_gather(w_key, "rows", axis=0, tiled=True),
        lax.all_gather(w_value, "rows", axis=0, tiled=True),
        lax.all_gather(w_out, "rows", axis=0, tiled=True),
        lax.all_gather(w_head, "rows", axis=0, tiled=True),
    )
    d_mid = w_a.shape[1]
    flat_x = features.reshape(cell_count, d_in)
    pre_a = jnp.dot(flat_x, w_a, preferred_element_type=jnp.float32)
    hat_a, inverse_a = plain_normalize(pre_a, total_count)
    act_a = gain_a * hat_a + bias_a
    low_a = jax.nn.silu(act_a).astype(jnp.bfloat16)
    halo_a = padded(low_a.reshape(clip_dev, row_dev, col_count, d_mid), (("rows", 1),), 1)
    halo_a = jnp.pad(halo_a, ((0, 0), (0, 0), (1, 1), (0, 0)))
    window_a = jnp.concatenate(
        [
            halo_a[:, row_step : row_step + row_dev, col_step : col_step + col_count]
            for row_step in range(3)
            for col_step in range(3)
        ],
        axis=3,
    ).reshape(cell_count, 9 * d_mid)
    pre_b = jnp.dot(window_a, w_b, preferred_element_type=jnp.float32)
    hat_b, inverse_b = plain_normalize(pre_b, total_count)
    act_b = gain_b * hat_b + bias_b
    low_b = jax.nn.silu(act_b).astype(jnp.bfloat16)
    pre_c = jnp.dot(low_b, w_c, preferred_element_type=jnp.float32)
    hat_c, inverse_c = plain_normalize(pre_c, total_count)
    pre_out = gain_c * hat_c + bias_c + flat_x.astype(jnp.float32)
    fmap = jax.nn.silu(pre_out).astype(jnp.bfloat16)
    capacity = piece_box.shape[1]
    samples = sample_pos.shape[1] // capacity
    slot_count = owners * capacity
    sample_cells = (
        piece_clip[:, :, None] * (row_dev * col_count)
        + sample_pos.reshape(owners, capacity, samples)
    ).reshape(slot_count, samples)
    is_live = (jnp.arange(capacity)[None, :] < send_count[:, None]).reshape(slot_count)
    slot_weights = sample_weight.reshape(slot_count, samples) * is_live[:, None].astype(jnp.float32)
    cell_ids = jnp.arange(cell_count)[None, :]
    interp_sum = jnp.zeros((slot_count, cell_count), jnp.float32)
    for sample_index in range(samples):
        interp_sum = interp_sum + jnp.where(
            sample_cells[:, sample_index, None] == cell_ids,
            slot_weights[:, sample_index, None],
            0.0,
        )
    interpolated_value = interp_sum.astype(jnp.bfloat16)
    region_parts = (
        jnp.dot(interpolated_value, fmap, preferred_element_type=jnp.float32)
        .astype(jnp.bfloat16)
        .reshape(owners, capacity, d_in)
    )
    arrived, arrived_box = (
        lax.all_to_all(region_parts, "rows", split_axis=0, concat_axis=0, tiled=True),
        lax.all_to_all(piece_box, "rows", split_axis=0, concat_axis=0, tiled=True),
    )
    box_dev = win_start.shape[0]
    flat_box = arrived_box.reshape(slot_count)
    owner_hits = (flat_box[None, :] == jnp.arange(box_dev)[:, None]).astype(jnp.bfloat16)
    pooled = jnp.dot(
        owner_hits, arrived.reshape(slot_count, d_in), preferred_element_type=jnp.float32
    )
    pooled_low = pooled.astype(jnp.bfloat16)
    keys_own = jnp.dot(bank, w_k, preferred_element_type=jnp.float32).astype(jnp.bfloat16)
    values_own = jnp.dot(bank, w_v, preferred_element_type=jnp.float32).astype(jnp.bfloat16)
    key_rows, value_rows = (
        lax.all_gather(keys_own, "rows", axis=0, tiled=True),
        lax.all_gather(values_own, "rows", axis=0, tiled=True),
    )
    bank_length = key_rows.shape[0]
    queries = jnp.dot(pooled_low, w_q, preferred_element_type=jnp.float32).astype(jnp.bfloat16)
    score_scale = d_mid ** (-0.5)
    scores = ndot(queries, key_rows) * score_scale
    positions = jnp.arange(bank_length)[None, :]
    window_mask = (positions >= win_start[:, None]) & (positions < (win_start + win_len)[:, None])
    attend = jax.nn.softmax(jnp.where(window_mask, scores, -1e30), axis=-1)
    attend_low = attend.astype(jnp.bfloat16)
    mixture = jnp.dot(attend_low, value_rows, preferred_element_type=jnp.float32)
    centred = mixture - jnp.mean(mixture, axis=-1, keepdims=True)
    inverse_z = lax.rsqrt(jnp.mean(centred * centred, axis=-1, keepdims=True) + 1e-05)
    hat_z = centred * inverse_z
    pre_ln = ln_gain * hat_z + ln_bias
    low_r = jax.nn.silu(pre_ln).astype(jnp.bfloat16)
    branch = jnp.dot(low_r, w_o, preferred_element_type=jnp.float32)
    joined = jnp.concatenate([pooled, pooled + branch], axis=1).astype(jnp.bfloat16)
    logits = jnp.dot(joined, w_h, preferred_element_type=jnp.float32) + head_bias
    likely = jax.nn.sigmoid(logits)
    d_logit = (prob_cotangent * (likely * (1.0 - likely))).astype(jnp.bfloat16)
    grad_head_bias = jnp.sum(d_logit.astype(jnp.float32), 0)
    grad_wh = tdot(joined, d_logit)
    d_joined = ndot(d_logit, w_h)
    d_pooled = d_joined[:, :d_in] + d_joined[:, d_in:]
    d_branch = d_joined[:, d_in:].astype(jnp.bfloat16)
    grad_wo = tdot(low_r, d_branch)
    d_ln = ndot(d_branch, w_o) * silu_slope(pre_ln)
    grad_ln_gain = jnp.sum(d_ln * hat_z, 0)
    grad_ln_bias = jnp.sum(d_ln, 0)
    d_hat = d_ln * ln_gain
    d_mixture = (
        inverse_z
        * (
            d_hat
            - jnp.mean(d_hat, axis=-1, keepdims=True)
            - hat_z * jnp.mean(d_hat * hat_z, axis=-1, keepdims=True)
        )
    ).astype(jnp.bfloat16)
    d_attend = ndot(d_mixture, value_rows)
    d_values = tdot(attend_low, d_mixture)
    d_scores = (attend * (d_attend - jnp.sum(d_attend * attend, axis=-1, keepdims=True))).astype(
        jnp.bfloat16
    )
    d_queries = (
        jnp.dot(d_scores, key_rows, preferred_element_type=jnp.float32) * score_scale
    ).astype(jnp.bfloat16)
    d_keys = tdot(d_scores, queries) * score_scale
    grad_wq = tdot(pooled_low, d_queries)
    d_pooled = d_pooled + ndot(d_queries, w_q)
    key_sum, value_sum = side_by_side(
        (d_keys.astype(jnp.bfloat16), d_values.astype(jnp.bfloat16)), "rows", 0, 1
    )
    grad_wk = tdot(bank, key_sum.astype(jnp.bfloat16))
    grad_wv = tdot(bank, value_sum.astype(jnp.bfloat16))
    back_pieces = jnp.take(d_pooled.astype(jnp.bfloat16), flat_box, axis=0).reshape(
        owners, capacity, d_in
    )
    returned = lax.all_to_all(back_pieces, "rows", split_axis=0, concat_axis=0, tiled=True)
    d_fmap = tdot(interpolated_value, returned.reshape(slot_count, d_in))
    d_pre = d_fmap * silu_slope(pre_out)
    head_sums = lax.psum(
        (jnp.sum(d_pre, 0), jnp.sum(d_pre * hat_c, 0), grad_ln_gain, grad_ln_bias, grad_head_bias),
        ("batch", "rows"),
    )
    d_c = norm_back(
        d_pre, hat_c, inverse_c, gain_c, head_sums[0], head_sums[1], total_count
    ).astype(jnp.bfloat16)
    grad_wc = tdot(low_b, d_c)
    d_act_b = ndot(d_c, w_c) * silu_slope(act_b)
    shift_b_sum, gain_b_sum = plain_totals(d_act_b, hat_b)
    d_b = norm_back(d_act_b, hat_b, inverse_b, gain_b, shift_b_sum, gain_b_sum, total_count).astype(
        jnp.bfloat16
    )
    grad_wb = tdot(window_a, d_b)
    halo_d = padded(d_b.reshape(clip_dev, row_dev, col_count, d_mid), (("rows", 1),), 1)
    halo_d = jnp.pad(halo_d, ((0, 0), (0, 0), (1, 1), (0, 0)))
    window_d = jnp.concatenate(
        [
            halo_d[
                :, 2 - row_step : 2 - row_step + row_dev, 2 - col_step : 2 - col_step + col_count
            ]
            for row_step in range(3)
            for col_step in range(3)
        ],
        axis=3,
    ).reshape(cell_count, 9 * d_mid)
    flipped = w_b.reshape(9, d_mid, d_mid).transpose(0, 2, 1).reshape(9 * d_mid, d_mid)
    d_act_a = jnp.dot(window_d, flipped, preferred_element_type=jnp.float32) * silu_slope(act_a)
    shift_a_sum, gain_a_sum = plain_totals(d_act_a, hat_a)
    d_a = norm_back(d_act_a, hat_a, inverse_a, gain_a, shift_a_sum, gain_a_sum, total_count).astype(
        jnp.bfloat16
    )
    grad_wa = tdot(flat_x, d_a)
    grad_input = (ndot(d_a, w_a) + d_pre).astype(jnp.bfloat16).reshape(features.shape)
    partial_sums = (
        lax.psum_scatter(grad_wa, "rows", scatter_dimension=0, tiled=True),
        lax.psum_scatter(grad_wb, "rows", scatter_dimension=0, tiled=True),
        lax.psum_scatter(grad_wc, "rows", scatter_dimension=0, tiled=True),
        lax.psum_scatter(grad_wq, "rows", scatter_dimension=0, tiled=True),
        lax.psum_scatter(grad_wk, "rows", scatter_dimension=0, tiled=True),
        lax.psum_scatter(grad_wv, "rows", scatter_dimension=0, tiled=True),
        lax.psum_scatter(grad_wo, "rows", scatter_dimension=0, tiled=True),
        lax.psum_scatter(grad_wh, "rows", scatter_dimension=0, tiled=True),
    )
    finished = (
        lax.psum_scatter(
            partial_sums[0].astype(jnp.bfloat16), "batch", scatter_dimension=1, tiled=True
        ).astype(jnp.float32),
        lax.psum_scatter(
            partial_sums[1].astype(jnp.bfloat16), "batch", scatter_dimension=1, tiled=True
        ).astype(jnp.float32),
        lax.psum_scatter(
            partial_sums[2].astype(jnp.bfloat16), "batch", scatter_dimension=1, tiled=True
        ).astype(jnp.float32),
        lax.psum_scatter(
            partial_sums[3].astype(jnp.bfloat16), "batch", scatter_dimension=1, tiled=True
        ).astype(jnp.float32),
        lax.psum_scatter(
            partial_sums[4].astype(jnp.bfloat16), "batch", scatter_dimension=1, tiled=True
        ).astype(jnp.float32),
        lax.psum_scatter(
            partial_sums[5].astype(jnp.bfloat16), "batch", scatter_dimension=1, tiled=True
        ).astype(jnp.float32),
        lax.psum_scatter(
            partial_sums[6].astype(jnp.bfloat16), "batch", scatter_dimension=1, tiled=True
        ).astype(jnp.float32),
        lax.psum_scatter(
            partial_sums[7].astype(jnp.bfloat16), "batch", scatter_dimension=1, tiled=True
        ).astype(jnp.float32),
    )
    return (
        likely,
        grad_input,
        finished[0],
        finished[1],
        finished[2],
        finished[3],
        finished[4],
        finished[5],
        finished[6],
        finished[7],
        gain_a_sum,
        shift_a_sum,
        gain_b_sum,
        shift_b_sum,
        head_sums[1],
        head_sums[0],
        head_sums[2],
        head_sums[3],
        head_sums[4],
    )


def on_device(*args):
    fits = all(a.shape[0] % 64 == 0 for a in args[1:9]) and lax.axis_size("rows") % 2 == 0
    return (fused_device if fits else plain_device)(*args)


def solution(mesh):
    return jax.shard_map(
        on_device,
        mesh=mesh,
        in_specs=(
            P("batch", "rows", None, None),
            P("rows", None),
            P("rows", None),
            P("rows", None),
            P("rows", None),
            P("rows", None),
            P("rows", None),
            P("rows", None),
            P("rows", None),
            P(),
            P(),
            P(),
            P(),
            P(),
            P(),
            P(),
            P(),
            P(),
            P(("batch", "rows"), None),
            P(("batch", "rows"), None),
            P(("batch", "rows"), None),
            P(("batch", "rows")),
            P(("batch", "rows"), None),
            P(("batch", "rows"), None),
            P(("batch", "rows")),
            P(("batch", "rows")),
            P(("batch", "rows"), None),
        ),
        out_specs=(
            P(("batch", "rows"), None),
            P("batch", "rows", None, None),
            P("rows", "batch"),
            P("rows", "batch"),
            P("rows", "batch"),
            P("rows", "batch"),
            P("rows", "batch"),
            P("rows", "batch"),
            P("rows", "batch"),
            P("rows", "batch"),
            P(),
            P(),
            P(),
            P(),
            P(),
            P(),
            P(),
            P(),
            P(),
        ),
        check_vma=False,
    )
```
